32 devices in a mesh: dp: 8 (over y, x, core), mp: 4 (over z).
Axes of the slice: x: 2, y: 2, z: 4, core: 2. Of those that a mesh axis runs over, the one named last changes fastest.
Arguments:
- tokens: bfloat16 [8192, 2048], P(('dp', 'mp')), may hold values from -6 to 6
- cotangent: bfloat16 [8192, 2048], P(('dp', 'mp')), may hold values from -6 to 6
- valid_counts: int32 [8], P('dp'), may hold values from 1 to 1024, 7168 in all
- w_qkv: float32 [2048, 3, 2048], P('dp', None, 'mp'), may hold values from -0.1875 to 0.1875
- w_out: float32 [2048, 2048], P('mp', 'dp'), may hold values from -0.1875 to 0.1875
- w_gu: float32 [2048, 2, 8192], P('dp', None, 'mp'), may hold values from -0.125 to 0.125
- w_down: float32 [8192, 2048], P('mp', 'dp'), may hold values from -0.0625 to 0.0625
- gains: float32 [2, 2048], P(None, ('dp', 'mp')), may hold values from 0.5 to 1.5
- mom_qkv: float32 [2048, 3, 2048], P('dp', None, 'mp'), may hold values from -28 to 28
- mom_out: float32 [2048, 2048], P('mp', 'dp'), may hold values from -28 to 28
- mom_gu: float32 [2048, 2, 8192], P('dp', None, 'mp'), may hold values from -16 to 16
- mom_down: float32 [8192, 2048], P('mp', 'dp'), may hold values from -28 to 28
- mom_gains: float32 [2, 2048], P(None, ('dp', 'mp')), may hold values from -28 to 28
- avg_qkv: float32 [2048, 3, 2048], P('dp', None, 'mp'), may hold values from -0.1875 to 0.1875
- avg_out: float32 [2048, 2048], P('mp', 'dp'), may hold values from -0.1875 to 0.1875
- avg_gu: float32 [2048, 2, 8192], P('dp', None, 'mp'), may hold values from -0.125 to 0.125
- avg_down: float32 [8192, 2048], P('mp', 'dp'), may hold values from -0.0625 to 0.0625
- avg_gains: float32 [2, 2048], P(None, ('dp', 'mp')), may hold values from 0.5 to 1.5
Outputs:
- block_out: bfloat16 [8192, 2048], P(('dp', 'mp'))
- input_grad: float32 [8192, 2048], P(('dp', 'mp'))
- new_qkv: float32 [2048, 3, 2048], P('dp', None, 'mp')
- new_out: float32 [2048, 2048], P('mp', 'dp')
- new_gu: float32 [2048, 2, 8192], P('dp', None, 'mp')
- new_down: float32 [8192, 2048], P('mp', 'dp')
- new_gains: float32 [2, 2048], P(None, ('dp', 'mp'))
- next_mom_qkv: float32 [2048, 3, 2048], P('dp', None, 'mp')
- next_mom_out: float32 [2048, 2048], P('mp', 'dp')
- next_mom_gu: float32 [2048, 2, 8192], P('dp', None, 'mp')
- next_mom_down: float32 [8192, 2048], P('mp', 'dp')
- next_mom_gains: float32 [2, 2048], P(None, ('dp', 'mp'))
- next_avg_qkv: float32 [2048, 3, 2048], P('dp', None, 'mp')
- next_avg_out: float32 [2048, 2048], P('mp', 'dp')
- next_avg_gu: float32 [2048, 2, 8192], P('dp', None, 'mp')
- next_avg_down: float32 [8192, 2048], P('mp', 'dp')
- next_avg_gains: float32 [2, 2048], P(None, ('dp', 'mp'))
- copy_qkv: bfloat16 [2048, 3, 2048], P('dp', None, 'mp')
- copy_out: bfloat16 [2048, 2048], P('mp', 'dp')
- copy_gu: bfloat16 [2048, 2, 8192], P('dp', None, 'mp')
- copy_down: bfloat16 [8192, 2048], P('mp', 'dp')
The draws below stay inside these ranges and needn't reach their ends.
Inputs may be any that keep to these rules, and one draw needn't show every extreme that they name: `valid_counts`: each slot's valid tokens are its first rows; the counts sum to 7168 and the largest equals 1024.
All inputs are finite; a program needn't handle non-finite values. No bound on the sum of `valid_counts` on one device may be relied on, other than what follows from the above.
Results may differ from the reference program's by a relative error of at most 0.017.
Values may be sent and summed in bfloat16 or wider, within the bound.
A program may use at most 256 MiB of HBM per device.

```python
import math
import jax
import jax.numpy as jnp
import numpy as np
from jax import lax

D = 2048
HEADS = 16
HDIM = 128
FF = 8192
SEQ = 1024
TOKENS = 8192
N_DP = 8


def level_of(key, shape, split, low, high):
    factor_of = 1.0
    for position, blocks in split:
        draws = jax.random.uniform(jax.random.fold_in(jax.random.fold_in(key, 6), position), (blocks,), jnp.float32, low / len(split), high / len(split))
        factor_of = factor_of * jnp.repeat(jnp.exp(draws), shape[position] // blocks).reshape((-1,) + (1,) * (len(shape) - 1 - position))
    return factor_of


def profile(amount, total, limit, skew):
    portions = [(1 << 20) // math.isqrt(standing ** skew) + 1 for standing in range(2, amount + 1)]
    spare, holding = total - limit - (amount - 1), [1] * (amount - 1)
    while spare > 0:
        candidates = [i for i in range(amount - 1) if holding[i] < limit]
        mass, remaining = sum([portions[i] for i in candidates]), spare
        for i in candidates:
            more = min(limit - holding[i], max(1, remaining * portions[i] // mass), spare)
            holding[i] = holding[i] + more
            spare = spare - more
    return np.array([limit] + holding)


def ragged(own_key, number_of, total, limit, skew):
    if number_of == 2:
        one = jax.random.randint(own_key, (), max(1, total - limit), min(limit, total - 1) + 1)
        return jnp.stack([one, total - one])
    tallies = jnp.asarray(profile(number_of, total, limit, skew), jnp.int32)
    pairs = (number_of - 1) // 2
    giver, receiver = tallies[1:1 + 2 * pairs:2], tallies[2:2 + 2 * pairs:2]
    slack = jnp.minimum(giver - 1, limit - receiver)
    moved = jax.random.randint(jax.random.fold_in(own_key, 1), (pairs,), 0, 1 << 20) % (slack + 1)
    tallies = tallies.at[1:1 + 2 * pairs:2].set(giver - moved).at[2:2 + 2 * pairs:2].set(receiver + moved)
    return tallies[jax.random.permutation(jax.random.fold_in(own_key, 2), number_of)]


def bell_draw(rng, shape, width, reach, split=(), kind=jnp.bfloat16):
    factor_of = level_of(rng, shape, split, -0.22, 0.18) if split else 1.0
    values = jax.random.normal(rng, shape, jnp.float32) * width * factor_of
    return jnp.minimum(jnp.maximum(values, -reach), reach).astype(kind)


def setup_inputs(seed: int = 0) -> dict:
    key_of = jax.random.split(jax.random.key(seed), 19)
    return {
        "tokens": bell_draw(key_of[0], (TOKENS, D), 1.0, 6.0, ((0, 32),)),
        "cotangent": bell_draw(key_of[1], (TOKENS, D), 1.0, 6.0, ((0, 32),)),
        "valid_counts": ragged(key_of[2], N_DP, SEQ * N_DP * 7 // 8, SEQ, 0).astype(jnp.int32),
        "w_qkv": bell_draw(key_of[3], (D, 3, D), (D // 2) ** -0.5, 0.1875, ((0, 8), (2, 4)), jnp.float32),
        "w_out": bell_draw(key_of[4], (D, D), (D // 2) ** -0.5, 0.1875, ((0, 4), (1, 8)), jnp.float32),
        "w_gu": bell_draw(key_of[5], (D, 2, FF), D ** -0.5, 0.125, ((0, 8), (2, 4)), jnp.float32),
        "w_down": bell_draw(key_of[6], (FF, D), FF ** -0.5, 0.0625, ((0, 4), (1, 8)), jnp.float32),
        "gains": jnp.clip(1.0 + 0.1 * jax.random.normal(key_of[7], (2, D), jnp.float32), 0.5, 1.5),
        "mom_qkv": bell_draw(key_of[8], (D, 3, D), (0.05 * TOKENS ** 0.5), 28.0, ((0, 8), (2, 4)), jnp.float32),
        "mom_out": bell_draw(key_of[9], (D, D), (0.05 * TOKENS ** 0.5), 28.0, ((0, 4), (1, 8)), jnp.float32),
        "mom_gu": bell_draw(key_of[10], (D, 2, FF), (0.03 * TOKENS ** 0.5), 16.0, ((0, 8), (2, 4)), jnp.float32),
        "mom_down": bell_draw(key_of[11], (FF, D), (0.05 * TOKENS ** 0.5), 28.0, ((0, 4), (1, 8)), jnp.float32),
        "mom_gains": bell_draw(key_of[12], (2, D), (0.05 * TOKENS ** 0.5), 28.0, ((1, 32),), jnp.float32),
        "avg_qkv": bell_draw(key_of[13], (D, 3, D), (D // 2) ** -0.5, 0.1875, ((0, 8), (2, 4)), jnp.float32),
        "avg_out": bell_draw(key_of[14], (D, D), (D // 2) ** -0.5, 0.1875, ((0, 4), (1, 8)), jnp.float32),
        "avg_gu": bell_draw(key_of[15], (D, 2, FF), D ** -0.5, 0.125, ((0, 8), (2, 4)), jnp.float32),
        "avg_down": bell_draw(key_of[16], (FF, D), FF ** -0.5, 0.0625, ((0, 4), (1, 8)), jnp.float32),
        "avg_gains": jnp.clip(1.0 + 0.1 * jax.random.normal(key_of[17], (2, D), jnp.float32), 0.5, 1.5),
    }


norm_eps = 1e-05
rope_base = 10000.0
momentum_decay = 0.9
average_decay = 0.9
step_rate = 0.05
gain_rate = 0.5

@jax.custom_vjp
def low(v):
    return lax.optimization_barrier(v.astype(jnp.bfloat16)).astype(jnp.float32)

@jax.custom_vjp
def low_back(v):
    return v

def low_keep(v):
    return (low(v), None)

def low_pass(kept, grad):
    return (grad,)

def back_keep(v):
    return (v, None)

def back_low(kept, grad):
    return (low(grad),)
low.defvjp(low_keep, low_pass)
low_back.defvjp(back_keep, back_low)

def rope_tables(length, half_dim):
    positions = jnp.arange(length, dtype=jnp.float32)[:, None]
    inverse_freq = rope_base ** (-jnp.arange(half_dim, dtype=jnp.float32) / half_dim)
    angles = positions * inverse_freq[None, :]
    return (jnp.cos(angles)[:, None, :], jnp.sin(angles)[:, None, :])

def rotate(values, cosine, sine_tab):
    half_dim = values.shape[-1] // 2
    first, second = (values[..., :half_dim], values[..., half_dim:])
    return jnp.concatenate([first * cosine - second * sine_tab, second * cosine + first * sine_tab], axis=-1)

def rms_unit(rows):
    return rows * lax.rsqrt(lax.optimization_barrier(jnp.mean(rows * rows, axis=1, keepdims=True)) + norm_eps)

def forward(xf, w_qkv, w_out, w_gu, w_down, gains, valid_counts):
    highest = lax.Precision.HIGHEST
    h_first = low(rms_unit(xf) * gains[0][None, :])
    joined = low_back(jnp.dot(h_first, low(w_qkv).reshape(D, 3 * D), precision=highest))
    joined = joined.reshape(N_DP, SEQ, 3, HEADS, HDIM)
    cosine, sine_tab = rope_tables(SEQ, HDIM // 2)
    score_scale = 1.0 / math.sqrt(HDIM)
    score_shift = -math.log(SEQ)
    positions = jnp.arange(SEQ, dtype=jnp.int32)

    def one_slot(inputs):
        slot_qkv, valid_len = inputs
        queries = low(rotate(slot_qkv[:, 0], cosine, sine_tab))
        keys = low(rotate(slot_qkv[:, 1], cosine, sine_tab))
        values = low(slot_qkv[:, 2])
        raw = low_back(jnp.einsum('qhd,khd->hqk', queries, keys, precision=highest))
        allowed = (positions[None, :] <= positions[:, None]) & (positions[None, :] < valid_len)
        attn_prob = low(jax.nn.sigmoid(raw * score_scale + score_shift) * allowed.astype(jnp.float32)[None])
        return low(low_back(jnp.einsum('hqk,khd->qhd', attn_prob, values, precision=highest)))
    mixed = lax.map(jax.checkpoint(one_slot), (joined, valid_counts)).reshape(TOKENS, D)
    second = xf + low_back(jnp.dot(mixed, low(w_out), precision=highest))
    h_second = low(rms_unit(second) * gains[1][None, :])
    gate_up = low_back(jnp.dot(h_second, low(w_gu).reshape(D, 2 * FF), precision=highest)).reshape(TOKENS, 2, FF)
    act = low(jax.nn.silu(gate_up[:, 0]) * gate_up[:, 1])
    return second + low_back(jnp.dot(act, low(w_down), precision=highest))

def update(weight, moment, average, gradient, step_size):
    moment_new = momentum_decay * moment + (1.0 - momentum_decay) * gradient
    weight_new = weight - step_size * ((1.0 - momentum_decay) * gradient + momentum_decay * moment_new)
    average_new = average_decay * average + (1.0 - average_decay) * weight_new
    return (weight_new, moment_new, average_new)

def reference(tokens, cotangent, valid_counts, w_qkv, w_out, w_gu, w_down, gains, mom_qkv, mom_out, mom_gu, mom_down, mom_gains, avg_qkv, avg_out, avg_gu, avg_down, avg_gains):
    xf = tokens.astype(jnp.float32)
    live = (jnp.arange(SEQ, dtype=jnp.int32)[None, :] < valid_counts[:, None]).astype(jnp.float32).reshape(TOKENS, 1)

    def wrapped(xf, w_qkv, w_out, w_gu, w_down, gains):
        return forward(xf, w_qkv, w_out, w_gu, w_down, gains, valid_counts)
    result, pullback = jax.vjp(wrapped, xf, w_qkv, w_out, w_gu, w_down, gains)
    grads = pullback(cotangent.astype(jnp.float32) * live)
    matrix_rate = step_rate / math.sqrt(TOKENS)
    scale_rate = gain_rate / math.sqrt(TOKENS)
    new_qkv, next_mom_qkv, next_avg_qkv = update(w_qkv, mom_qkv, avg_qkv, grads[1], matrix_rate)
    new_out, next_mom_out, next_avg_out = update(w_out, mom_out, avg_out, grads[2], matrix_rate)
    new_gu, next_mom_gu, next_avg_gu = update(w_gu, mom_gu, avg_gu, grads[3], matrix_rate)
    new_down, next_mom_down, next_avg_down = update(w_down, mom_down, avg_down, grads[4], matrix_rate)
    new_gains, next_mom_gains, next_avg_gains = update(gains, mom_gains, avg_gains, grads[5], scale_rate)
    return (result.astype(jnp.bfloat16), grads[0], new_qkv, new_out, new_gu, new_down, new_gains, next_mom_qkv, next_mom_out, next_mom_gu, next_mom_down, next_mom_gains, next_avg_qkv, next_avg_out, next_avg_gu, next_avg_down, next_avg_gains, new_qkv.astype(jnp.bfloat16), new_out.astype(jnp.bfloat16), new_gu.astype(jnp.bfloat16), new_down.astype(jnp.bfloat16))
```

```python
import functools
import math

import jax
import jax.numpy as jnp
from jax import lax
from jax.experimental import pallas as pl
from jax.experimental.pallas import tpu as pltpu
from jax.sharding import PartitionSpec as P

HDIM = 128
SEQ = 1024
MESH = pl.DeviceIdType.MESH
ANY = pl.BlockSpec(memory_space=pl.ANY)
VMEM = pl.BlockSpec(memory_space=pltpu.VMEM)
VMEM_LIMIT = 60 * 1024 * 1024

norm_eps = 1e-05
rope_base = 10000.0
momentum_decay = 0.9
average_decay = 0.9
step_rate = 0.05
gain_rate = 0.5


def rows_at(start, size):
    return pl.ds(pl.multiple_of(start, size), size)


def remote(src, dst, send_sem, recv_sem, peer):
    return pltpu.make_async_remote_copy(
        src_ref=src,
        dst_ref=dst,
        send_sem=send_sem,
        recv_sem=recv_sem,
        device_id={"mp": peer},
        device_id_type=MESH,
    )


def neighbour_barrier(n):
    me = lax.axis_index("mp")
    barrier = pltpu.get_barrier_semaphore()

    @pl.when(me > 0)
    def _():
        pl.semaphore_signal(barrier, inc=1, device_id={"mp": me - 1}, device_id_type=MESH)

    @pl.when(me < n - 1)
    def _():
        pl.semaphore_signal(barrier, inc=1, device_id={"mp": me + 1}, device_id_type=MESH)

    pl.semaphore_wait(barrier, jnp.where(me > 0, 1, 0) + jnp.where(me < n - 1, 1, 0))


class LineGather:
    def __init__(self, n, rows, chunks, own, whole, sems):
        self.n, self.rows, self.chunks = n, rows, chunks
        self.size = rows // chunks
        self.own, self.whole, self.sems = own, whole, sems
        self.me = lax.axis_index("mp")

    def at(self, block, chunk):
        return self.whole.at[rows_at(block * self.rows + chunk * self.size, self.size)]

    def copies(self, step, chunk, first):
        me, n = self.me, self.n
        send_r, recv_r, send_l, recv_l = self.sems
        out = []
        for block, peer, has, send, recv in (
            (me - step, me + 1, (me - step >= 0) & (me < n - 1), send_r, recv_r),
            (me + step, me - 1, (me + step <= n - 1) & (me > 0), send_l, recv_l),
        ):
            src = (
                self.own.at[pl.ds(chunk * self.size, self.size)]
                if first
                else self.at(block, chunk)
            )
            index = step * self.chunks + chunk
            out.append(
                (has, remote(src, self.at(block, chunk), send.at[index], recv.at[index], peer))
            )
        return out

    def arrivals(self, step, chunk):
        me, n = self.me, self.n
        send_r, recv_r, send_l, recv_l = self.sems
        index = step * self.chunks + chunk
        out = []
        for block, has, send, recv in (
            (me - 1 - step, me - 1 - step >= 0, send_r, recv_r),
            (me + 1 + step, me + 1 + step <= n - 1, send_l, recv_l),
        ):
            ref = self.at(block, chunk)
            out.append((has, remote(ref, ref, send.at[index], recv.at[index], me)))
        return out

    def send_own(self, chunk):
        for has, copy in self.copies(0, chunk, True):
            pl.when(has)(copy.start)

    def forward(self, step):
        for chunk in range(self.chunks):
            for (got, arrival), (has, copy) in zip(
                self.arrivals(step - 1, chunk), self.copies(step, chunk, False)
            ):
                pl.when(got)(arrival.wait_recv)
                pl.when(has)(copy.start)

    def finish(self):
        for chunk in range(self.chunks):
            for got, arrival in self.arrivals(self.n - 2, chunk):
                pl.when(got)(arrival.wait_recv)
        for chunk in range(self.chunks):
            for has, copy in self.copies(0, chunk, True):
                pl.when(has)(copy.wait_send)

        def waits(step, carry):
            for chunk in range(self.chunks):
                for has, copy in self.copies(step, chunk, False):
                    pl.when(has)(copy.wait_send)
            return carry

        lax.fori_loop(1, self.n - 1, waits, 0)

    def forward_all(self):
        def step_of(step, carry):
            self.forward(step)
            return carry

        lax.fori_loop(1, self.n - 1, step_of, 0)


def gather_sems(n, chunks):
    return [pltpu.SemaphoreType.DMA(((n - 1) * chunks,))] * 4


def gather_rows(n, own, collective_id):
    rows, width = own.shape

    def kernel(own_ref, whole_ref, local_sem, *sems):
        me = lax.axis_index("mp")
        stream = LineGather(n, rows, 1, own_ref, whole_ref, sems)
        local = pltpu.make_async_copy(own_ref, stream.at(me, 0), local_sem)
        local.start()
        neighbour_barrier(n)
        stream.send_own(0)
        stream.forward_all()
        stream.finish()
        local.wait()

    return pl.pallas_call(
        kernel,
        out_shape=jax.ShapeDtypeStruct((n * rows, width), own.dtype),
        in_specs=[ANY],
        out_specs=ANY,
        scratch_shapes=[pltpu.SemaphoreType.DMA] + gather_sems(n, 1),
        compiler_params=pltpu.CompilerParams(collective_id=collective_id, has_side_effects=True),
        cost_estimate=pl.CostEstimate(
            flops=0, bytes_accessed=200 * own.size * own.dtype.itemsize, transcendentals=0
        ),
        name="gather_rows",
    )(own)


def scatter_rows(n, pairs, own_rows, epilogue, gains_row, collective_id, extra=None, chunks=2):
    total_rows = pairs[0][0].shape[0]
    rows = total_rows // n
    width = gains_row.shape[1]
    size = rows // chunks
    tile = 512
    gathers = epilogue != "last"
    lhs_args = [p[0] for p in pairs]
    rhs_args = [p[1] for p in pairs]
    flips = [p[2] for p in pairs]
    count = len(pairs)
    block = 32

    def kernel(*refs):
        refs = list(refs)
        take = lambda k: [refs.pop(0) for _ in range(k)]
        lhs, rhs = take(count), take(count)
        (gain_ref,) = take(1)
        own = take(len(own_rows))
        extra_ref = take(1)[0] if extra is not None else None
        outs = take(2 if epilogue != "forward" else 1)
        whole = take(1)[0] if gathers else None
        extra_whole = take(1)[0] if extra is not None else None
        held, sent, part = take(3)
        normed = take(1)[0] if gathers else None
        send_sems, recv_sems = take(2)
        gather = extra_gather = None
        me = lax.axis_index("mp")
        if gathers:
            (local_sem,) = take(1)
            gather = LineGather(n, rows, chunks, normed, whole, take(4))
        if extra is not None:
            (extra_sem,) = take(1)
            extra_gather = LineGather(n, rows, 1, extra_ref, extra_whole, take(4))
            extra_local = pltpu.make_async_copy(extra_ref, extra_gather.at(me, 0), extra_sem)
            extra_local.start()
        neighbour_barrier(n)
        if extra is not None:
            extra_gather.send_own(0)

        def product(block_id):
            def column(ct, carry):
                cols = rows_at(ct * tile, tile)
                total = None
                for a, b, flip in zip(lhs, rhs, flips):
                    left = a[rows_at(block_id * rows, rows), :]
                    if flip:
                        term = lax.dot_general(
                            left,
                            b[cols, :],
                            (((1,), (1,)), ((), ())),
                            preferred_element_type=jnp.float32,
                        )
                    else:
                        term = jnp.dot(left, b[:, cols], preferred_element_type=jnp.float32)
                    total = term if total is None else total + term
                part[:, cols] = total
                return carry

            lax.fori_loop(0, width // tile, column, 0)

        def hop(block_id, chunk, rightward):
            peer = me + 1 if rightward else me - 1
            slot = block_id if rightward else jnp.where(block_id == peer, n, block_id)
            return remote(
                sent.at[block_id, pl.ds(chunk * size, size)],
                held.at[slot, pl.ds(chunk * size, size)],
                send_sems.at[block_id * chunks + chunk],
                recv_sems.at[slot * chunks + chunk],
                peer,
            )

        def arrival(slot, chunk):
            ref = held.at[slot, pl.ds(chunk * size, size)]
            return remote(
                ref, ref, send_sems.at[chunk], recv_sems.at[slot * chunks + chunk], me
            )

        def add_rows(block_id, chunk, slots):
            def body(i, carry):
                span = rows_at(chunk * size + i * block, block)
                value = part[span, :]
                for slot in slots:
                    value = value + held[slot, span, :].astype(jnp.float32)
                sent[block_id, span, :] = value.astype(jnp.bfloat16)
                return carry

            lax.fori_loop(0, size // block, body, 0)

        def relay(block_id, rightward, inner):
            product(block_id)
            for chunk in range(chunks):

                @pl.when(inner)
                def _():
                    arrival(block_id, chunk).wait_recv()
                    add_rows(block_id, chunk, [block_id])

                @pl.when(jnp.logical_not(inner))
                def _():
                    add_rows(block_id, chunk, [])

                hop(block_id, chunk, rightward).start()

        def step_of(step, carry):
            @pl.when((step >= me + 1) & (me < n - 1))
            def _():
                relay(me + n - step, True, me > 0)

            @pl.when((step >= n - me) & (me > 0))
            def _():
                relay(me - n + step, False, me < n - 1)

            if extra is not None:

                @pl.when(step < n - 1)
                def _():
                    extra_gather.forward(step)

            return carry

        lax.fori_loop(1, n, step_of, 0)
        product(me)
        if epilogue != "forward":
            outs[1][...] = jnp.zeros_like(outs[1])
        for chunk in range(chunks):

            @pl.when(me > 0)
            def _():
                arrival(me, chunk).wait_recv()

            @pl.when(me < n - 1)
            def _():
                arrival(n, chunk).wait_recv()

            def body(i, carry):
                span = rows_at(chunk * size + i * block, block)
                total = part[span, :]
                zero = jnp.zeros_like(total)
                total = total + jnp.where(me > 0, held[me, span, :].astype(jnp.float32), zero)
                total = total + jnp.where(
                    me < n - 1, held[n, span, :].astype(jnp.float32), zero
                )
                gain = gain_ref[...]
                if epilogue == "forward":
                    value = own[0][span, :] + total
                    outs[0][span, :] = value
                    inverse = lax.rsqrt(
                        jnp.mean(value * value, axis=1, keepdims=True) + norm_eps
                    )
                    normed[span, :] = (value * inverse * gain).astype(jnp.bfloat16)
                else:
                    value = own[0][span, :]
                    inverse = lax.rsqrt(
                        jnp.mean(value * value, axis=1, keepdims=True) + norm_eps
                    )
                    unit = value * inverse
                    scaled = total * gain
                    inner = jnp.mean(scaled * unit, axis=1, keepdims=True)
                    result = own[1][span, :] + inverse * (scaled - unit * inner)
                    outs[0][span, :] = result
                    outs[1][...] += jnp.sum(
                        (total * unit).reshape(block // 8, 8, width), axis=0
                    )
                    if gathers:
                        normed[span, :] = result.astype(jnp.bfloat16)
                return carry

            lax.fori_loop(0, size // block, body, 0)
            if gathers:
                gather.send_own(chunk)
        if gathers:
            local = pltpu.make_async_copy(
                normed, whole.at[rows_at(me * rows, rows)], local_sem
            )
            local.start()
        if extra is not None:
            extra_gather.finish()
            extra_local.wait()
        if gathers:
            gather.forward_all()
            gather.finish()
            local.wait()

        def sends(step, carry):
            for chunk in range(chunks):

                @pl.when((step >= me + 1) & (me < n - 1))
                def _():
                    hop(me + n - step, chunk, True).wait_send()

                @pl.when((step >= n - me) & (me > 0))
                def _():
                    hop(me - n + step, chunk, False).wait_send()

            return carry

        lax.fori_loop(1, n, sends, 0)

    out_shape = [jax.ShapeDtypeStruct((rows, width), jnp.float32)]
    out_specs = [VMEM]
    if epilogue != "forward":
        out_shape.append(jax.ShapeDtypeStruct((8, width), jnp.float32))
        out_specs.append(VMEM)
    scratch = [
        pltpu.VMEM((n + 1, rows, width), jnp.bfloat16),
        pltpu.VMEM((n, rows, width), jnp.bfloat16),
        pltpu.VMEM((rows, width), jnp.float32),
    ]
    if gathers:
        out_shape.append(jax.ShapeDtypeStruct((total_rows, width), jnp.bfloat16))
        out_specs.append(ANY)
        scratch.append(pltpu.VMEM((rows, width), jnp.bfloat16))
    scratch += [
        pltpu.SemaphoreType.DMA((n * chunks,)),
        pltpu.SemaphoreType.DMA(((n + 1) * chunks,)),
    ]
    if gathers:
        scratch += [pltpu.SemaphoreType.DMA] + gather_sems(n, chunks)
    extra_args = []
    if extra is not None:
        out_shape.append(jax.ShapeDtypeStruct((total_rows, width), jnp.bfloat16))
        out_specs.append(ANY)
        scratch += [pltpu.SemaphoreType.DMA] + gather_sems(n, 1)
        extra_args = [extra]
    flops = sum(2 * a.size * width for a in lhs_args)
    return pl.pallas_call(
        kernel,
        out_shape=out_shape,
        in_specs=[VMEM] * (2 * count + 1 + len(own_rows)) + [ANY] * len(extra_args),
        out_specs=out_specs,
        scratch_shapes=scratch,
        compiler_params=pltpu.CompilerParams(
            collective_id=collective_id, has_side_effects=True, vmem_limit_bytes=VMEM_LIMIT
        ),
        cost_estimate=pl.CostEstimate(
            flops=flops, bytes_accessed=300_000_000, transcendentals=0
        ),
        name="scatter_" + epilogue,
    )(*lhs_args, *rhs_args, gains_row, *own_rows, *extra_args)


def small_exchange(n_dp, n_mp, table, reduces, collective_id):
    peers_mp, peers_dp = n_mp - 1, n_dp - 1

    def kernel(in_ref, out_ref, first, second, mid, s_mp, r_mp, s_dp, r_dp):
        dp, mp = lax.axis_index("dp"), lax.axis_index("mp")
        barrier = pltpu.get_barrier_semaphore()
        for k in range(1, n_mp):
            pl.semaphore_signal(
                barrier, inc=1, device_id={"mp": lax.rem(mp + k, n_mp)}, device_id_type=MESH
            )
        for k in range(1, n_dp):
            pl.semaphore_signal(
                barrier, inc=1, device_id={"dp": lax.rem(dp + k, n_dp)}, device_id_type=MESH
            )
        pl.semaphore_wait(barrier, peers_mp + peers_dp)
        if reduces:
            first[mp] = in_ref[mp]
        else:
            first[mp] = in_ref[...]
        copies = []
        for k in range(1, n_mp):
            peer = lax.rem(mp + k, n_mp)
            copies.append(
                pltpu.make_async_remote_copy(
                    src_ref=in_ref.at[peer] if reduces else in_ref,
                    dst_ref=first.at[mp],
                    send_sem=s_mp.at[k - 1],
                    recv_sem=r_mp.at[k - 1],
                    device_id={"mp": peer},
                    device_id_type=MESH,
                )
            )
        for copy in copies:
            copy.start()
        for copy in copies:
            copy.wait()
        if reduces:
            total = first[0]
            for k in range(1, n_mp):
                total = total + first[k]
            mid[...] = total
        else:
            mid[...] = first[...]
        second[dp] = mid[dp] if reduces else mid[...]
        copies = []
        for k in range(1, n_dp):
            peer = lax.rem(dp + k, n_dp)
            copies.append(
                pltpu.make_async_remote_copy(
                    src_ref=mid.at[peer] if reduces else mid,
                    dst_ref=second.at[dp],
                    send_sem=s_dp.at[k - 1],
                    recv_sem=r_dp.at[k - 1],
                    device_id={"dp": peer},
                    device_id_type=MESH,
                )
            )
        for copy in copies:
            copy.start()
        for copy in copies:
            copy.wait()
        if reduces:
            total = second[0]
            for k in range(1, n_dp):
                total = total + second[k]
            out_ref[...] = total
        else:
            out_ref[...] = second[...]

    if reduces:
        out = (8, 128)
        first, mid, second = (n_mp, n_dp, 8, 128), (n_dp, 8, 128), (n_dp, 8, 128)
    else:
        out = (n_dp, n_mp, 8, 128)
        first, mid, second = (n_mp, 8, 128), (n_mp, 8, 128), (n_dp, n_mp, 8, 128)
    return pl.pallas_call(
        kernel,
        out_shape=jax.ShapeDtypeStruct(out, jnp.float32),
        in_specs=[VMEM],
        out_specs=VMEM,
        scratch_shapes=[
            pltpu.VMEM(first, jnp.float32),
            pltpu.VMEM(second, jnp.float32),
            pltpu.VMEM(mid, jnp.float32),
            pltpu.SemaphoreType.DMA((peers_mp,)),
            pltpu.SemaphoreType.DMA((peers_mp,)),
            pltpu.SemaphoreType.DMA((peers_dp,)),
            pltpu.SemaphoreType.DMA((peers_dp,)),
        ],
        compiler_params=pltpu.CompilerParams(collective_id=collective_id, has_side_effects=True),
        name="sum_small" if reduces else "gather_small",
    )(table)


def gather_gains(n_dp, n_mp, gains, collective_id):
    local = gains.shape[1]
    flat = jnp.pad(gains.reshape(1, 2 * local), ((0, 7), (0, 128 - 2 * local)))
    whole = small_exchange(n_dp, n_mp, flat, False, collective_id)
    rows = whole[:, :, 0, : 2 * local].reshape(n_dp * n_mp, 2, local)
    return rows.transpose(1, 0, 2).reshape(2, n_dp * n_mp * local)


def scatter_gains(n_dp, n_mp, partial, collective_id):
    local = partial.shape[1] // (n_dp * n_mp)
    table = partial.reshape(2, n_dp, n_mp, local).transpose(2, 1, 0, 3)
    table = table.reshape(n_mp, n_dp, 1, 2 * local)
    table = jnp.pad(table, ((0, 0), (0, 0), (0, 7), (0, 128 - 2 * local)))
    out = small_exchange(n_dp, n_mp, table, True, collective_id)
    return out[0, : 2 * local].reshape(2, local)


def rope_tables(length, half_dim):
    positions = jnp.arange(length, dtype=jnp.float32)[:, None]
    inverse_freq = rope_base ** (-jnp.arange(half_dim, dtype=jnp.float32) / half_dim)
    angles = positions * inverse_freq[None, :]
    return (jnp.cos(angles)[:, None, :], jnp.sin(angles)[:, None, :])


def rotate(values, cosine, sine_tab):
    half_dim = values.shape[-1] // 2
    first, second = (values[..., :half_dim], values[..., half_dim:])
    return jnp.concatenate(
        [first * cosine - second * sine_tab, second * cosine + first * sine_tab], axis=-1
    )


def unrotate(gradient, cosine, sine_tab):
    half_dim = gradient.shape[-1] // 2
    first, second = (gradient[..., :half_dim], gradient[..., half_dim:])
    return jnp.concatenate(
        [first * cosine + second * sine_tab, second * cosine - first * sine_tab], axis=-1
    )


def update(weight, moment, average, gradient, step_size):
    moment_new = momentum_decay * moment + (1.0 - momentum_decay) * gradient
    weight_new = weight - step_size * (
        (1.0 - momentum_decay) * gradient + momentum_decay * moment_new
    )
    average_new = average_decay * average + (1.0 - average_decay) * weight_new
    return (weight_new, moment_new, average_new)


def dot_t(left, right):
    return lax.dot_general(
        left, right, (((1,), (1,)), ((), ())), preferred_element_type=jnp.float32
    )


def t_dot(left, right):
    return lax.dot_general(
        left, right, (((0,), (0,)), ((), ())), preferred_element_type=jnp.float32
    )


def dot(left, right):
    return jnp.dot(left, right, preferred_element_type=jnp.float32)


def per_device(
    n_dp,
    n_mp,
    tokens,
    cotangent,
    valid_counts,
    w_qkv,
    w_out,
    w_gu,
    w_down,
    gains,
    mom_qkv,
    mom_out,
    mom_gu,
    mom_down,
    mom_gains,
    avg_qkv,
    avg_out,
    avg_gu,
    avg_down,
    avg_gains,
):
    half = jnp.bfloat16
    row_count, width = tokens.shape
    owned, _, local_width = w_qkv.shape
    hidden = w_gu.shape[2]
    heads_here = local_width // HDIM
    block_len = min(512, SEQ)
    block_total = SEQ // block_len
    score_scale = 1.0 / math.sqrt(HDIM)
    score_shift = -math.log(SEQ)
    valid_len = valid_counts[0]

    attn_part = jnp.concatenate(
        [w_qkv.reshape(owned, 3 * local_width), w_out.T], axis=1
    ).astype(half)
    attn_w = lax.all_gather(attn_part, "dp", axis=0, tiled=True)
    ffn_part = jnp.concatenate([w_gu.reshape(owned, 2 * hidden), w_down.T], axis=1).astype(half)
    ffn_w = lax.all_gather(ffn_part, "dp", axis=0, tiled=True)
    qkv_w, out_wt = attn_w[:, : 3 * local_width], attn_w[:, 3 * local_width :]
    gu_w, down_wt = ffn_w[:, : 2 * hidden], ffn_w[:, 2 * hidden :]

    gain_all = gather_gains(n_dp, n_mp, gains, 0)
    row_ids = lax.axis_index("mp") * row_count + jnp.arange(row_count, dtype=jnp.int32)
    live_rows = (row_ids < valid_len).astype(jnp.float32)[:, None]
    xin = tokens.astype(jnp.float32)
    inverse = lax.rsqrt(jnp.mean(xin * xin, axis=1, keepdims=True) + norm_eps)
    normed_first = (xin * inverse * gain_all[0][None, :]).astype(half)
    h_first = gather_rows(n_mp, normed_first, 1)
    out_grad = cotangent.astype(jnp.float32) * live_rows
    branch_grad = lax.all_gather(out_grad.astype(half), "mp", axis=0, tiled=True)

    joined = dot(h_first, qkv_w)
    cosine, sine_tab = rope_tables(SEQ, HDIM // 2)
    parts = [
        joined[:, k * local_width : (k + 1) * local_width].reshape(SEQ, heads_here, HDIM)
        for k in range(3)
    ]
    queries = rotate(parts[0], cosine, sine_tab).astype(half)
    keys = rotate(parts[1], cosine, sine_tab).astype(half)
    values = parts[2].astype(half)
    key_pos = jnp.arange(SEQ, dtype=jnp.int32)

    def probabilities(query_blk, offset):
        raw = jnp.einsum("qhd,khd->hqk", query_blk, keys, preferred_element_type=jnp.float32)
        query_pos = offset + jnp.arange(block_len, dtype=jnp.int32)
        allowed = (key_pos[None, :] <= query_pos[:, None]) & (key_pos[None, :] < valid_len)
        return jax.nn.sigmoid(raw * score_scale + score_shift) * allowed.astype(jnp.float32)[None]

    def attend(block_idx):
        offset = block_idx * block_len
        query_blk = lax.dynamic_slice_in_dim(queries, offset, block_len, 0)
        attn_prob = probabilities(query_blk, offset).astype(half)
        return jnp.einsum(
            "hqk,khd->qhd", attn_prob, values, preferred_element_type=jnp.float32
        ).astype(half)

    mixed = lax.map(attend, jnp.arange(block_total, dtype=jnp.int32)).reshape(SEQ, local_width)
    second, h_second = scatter_rows(
        n_mp, [(mixed, out_wt, True)], [xin], "forward", gain_all[1:2], 2
    )

    gate_up = dot(h_second, gu_w)
    gate_val, up_val = gate_up[:, :hidden], gate_up[:, hidden:]
    act = (jax.nn.silu(gate_val) * up_val).astype(half)
    ffn_out = lax.psum_scatter(
        dot_t(act, down_wt).astype(half), "mp", scatter_dimension=0, tiled=True
    )
    block_out = (second + ffn_out.astype(jnp.float32)).astype(half)
    act_grad = dot(branch_grad, down_wt)
    sigma = jax.nn.sigmoid(gate_val)
    gate_grad = act_grad * up_val * sigma * (1.0 + gate_val * (1.0 - sigma))
    up_grad = act_grad * gate_val * sigma
    gu_grad = jnp.concatenate([gate_grad, up_grad], axis=1).astype(half)
    grad_ffn = jnp.concatenate(
        [t_dot(h_second, gu_grad).astype(half), t_dot(branch_grad, act).astype(half)], axis=1
    )
    sum_ffn = lax.psum_scatter(grad_ffn, "dp", scatter_dimension=0, tiled=True)
    second_grad, gain_two, attn_grad = scatter_rows(
        n_mp, [(gu_grad, gu_w, True)], [second, out_grad], "backward", gain_all[1:2], 3
    )

    mixed_grad = dot(attn_grad, out_wt).astype(half).reshape(SEQ, heads_here, HDIM)
    grad_out = t_dot(attn_grad, mixed).astype(half)

    def back_block(carried, block_idx):
        key_grad, value_grad = carried
        offset = block_idx * block_len
        query_blk = lax.dynamic_slice_in_dim(queries, offset, block_len, 0)
        mixed_blk = lax.dynamic_slice_in_dim(mixed_grad, offset, block_len, 0)
        attn_prob = probabilities(query_blk, offset)
        prob_grad = jnp.einsum(
            "qhd,khd->hqk", mixed_blk, values, preferred_element_type=jnp.float32
        )
        value_grad = value_grad + jnp.einsum(
            "hqk,qhd->khd",
            attn_prob.astype(half),
            mixed_blk,
            preferred_element_type=jnp.float32,
        )
        score_grad = (prob_grad * attn_prob * (1.0 - attn_prob) * score_scale).astype(half)
        query_grad = jnp.einsum(
            "hqk,khd->qhd", score_grad, keys, preferred_element_type=jnp.float32
        )
        key_grad = key_grad + jnp.einsum(
            "hqk,qhd->khd", score_grad, query_blk, preferred_element_type=jnp.float32
        )
        return ((key_grad, value_grad), query_grad)

    zeros_kv = jnp.zeros((SEQ, heads_here, HDIM), jnp.float32)
    (key_total, value_total), query_blocks = lax.scan(
        back_block, (zeros_kv, zeros_kv), jnp.arange(block_total, dtype=jnp.int32)
    )
    query_total = query_blocks.reshape(SEQ, heads_here, HDIM)
    joined_grad = jnp.concatenate(
        [
            unrotate(query_total, cosine, sine_tab).reshape(SEQ, local_width),
            unrotate(key_total, cosine, sine_tab).reshape(SEQ, local_width),
            value_total.reshape(SEQ, local_width),
        ],
        axis=1,
    ).astype(half)
    grad_attn = jnp.concatenate([t_dot(h_first, joined_grad).astype(half), grad_out], axis=1)
    sum_attn = lax.psum_scatter(grad_attn, "dp", scatter_dimension=0, tiled=True)
    input_grad, gain_one = scatter_rows(
        n_mp, [(joined_grad, qkv_w, True)], [xin, second_grad], "last", gain_all[0:1], 4
    )
    gain_partial = jnp.stack([gain_one.sum(axis=0), gain_two.sum(axis=0)], axis=0)
    sum_gains = scatter_gains(n_dp, n_mp, gain_partial, 5)

    total_rows = SEQ * n_dp
    matrix_rate = step_rate / math.sqrt(total_rows)
    scale_rate = gain_rate / math.sqrt(total_rows)
    sum_attn = sum_attn.astype(jnp.float32)
    sum_ffn = sum_ffn.astype(jnp.float32)
    sum_qkv = sum_attn[:, : 3 * local_width].reshape(owned, 3, local_width)
    sum_out = sum_attn[:, 3 * local_width :].T
    sum_gu = sum_ffn[:, : 2 * hidden].reshape(owned, 2, hidden)
    sum_down = sum_ffn[:, 2 * hidden :].T
    new_qkv, next_mom_qkv, next_avg_qkv = update(w_qkv, mom_qkv, avg_qkv, sum_qkv, matrix_rate)
    new_out, next_mom_out, next_avg_out = update(w_out, mom_out, avg_out, sum_out, matrix_rate)
    new_gu, next_mom_gu, next_avg_gu = update(w_gu, mom_gu, avg_gu, sum_gu, matrix_rate)
    new_down, next_mom_down, next_avg_down = update(
        w_down, mom_down, avg_down, sum_down, matrix_rate
    )
    new_gains, next_mom_gains, next_avg_gains = update(
        gains, mom_gains, avg_gains, sum_gains, scale_rate
    )
    return (
        block_out,
        input_grad,
        new_qkv,
        new_out,
        new_gu,
        new_down,
        new_gains,
        next_mom_qkv,
        next_mom_out,
        next_mom_gu,
        next_mom_down,
        next_mom_gains,
        next_avg_qkv,
        next_avg_out,
        next_avg_gu,
        next_avg_down,
        next_avg_gains,
        new_qkv.astype(half),
        new_out.astype(half),
        new_gu.astype(half),
        new_down.astype(half),
    )


def solution(mesh):
    rows, one = P(("dp", "mp"), None), P("dp")
    tall, wide, spread = P("dp", None, "mp"), P("mp", "dp"), P(None, ("dp", "mp"))
    weights = (tall, wide, tall, wide)
    return jax.shard_map(
        functools.partial(per_device, mesh.shape["dp"], mesh.shape["mp"]),
        mesh=mesh,
        in_specs=(rows, rows, one, *((*weights, spread) * 3)),
        out_specs=(rows, rows, *((*weights, spread) * 3), *weights),
        check_vma=False,
    )
```

```python
import functools
import math

import jax
import jax.numpy as jnp
from jax import lax
from jax.experimental import pallas as pl
from jax.experimental.pallas import tpu as pltpu
from jax.sharding import PartitionSpec as P

HDIM = 128
SEQ = 1024
MESH = pl.DeviceIdType.MESH
ANY = pl.BlockSpec(memory_space=pl.ANY)
VMEM = pl.BlockSpec(memory_space=pltpu.VMEM)
VMEM_LIMIT = 60 * 1024 * 1024

norm_eps = 1e-05
rope_base = 10000.0
momentum_decay = 0.9
average_decay = 0.9
step_rate = 0.05
gain_rate = 0.5


def rows_at(start, size):
    return pl.ds(pl.multiple_of(start, size), size)


def remote(src, dst, send_sem, recv_sem, peer):
    return pltpu.make_async_remote_copy(
        src_ref=src,
        dst_ref=dst,
        send_sem=send_sem,
        recv_sem=recv_sem,
        device_id={"mp": peer},
        device_id_type=MESH,
    )


def neighbour_barrier(n):
    me = lax.axis_index("mp")
    barrier = pltpu.get_barrier_semaphore()

    @pl.when(me > 0)
    def _():
        pl.semaphore_signal(barrier, inc=1, device_id={"mp": me - 1}, device_id_type=MESH)

    @pl.when(me < n - 1)
    def _():
        pl.semaphore_signal(barrier, inc=1, device_id={"mp": me + 1}, device_id_type=MESH)

    pl.semaphore_wait(barrier, jnp.where(me > 0, 1, 0) + jnp.where(me < n - 1, 1, 0))


class LineGather:
    def __init__(self, n, rows, chunks, own, whole, sems):
        self.n, self.rows, self.chunks = n, rows, chunks
        self.size = rows // chunks
        self.own, self.whole, self.sems = own, whole, sems
        self.me = lax.axis_index("mp")

    def at(self, block, chunk):
        return self.whole.at[rows_at(block * self.rows + chunk * self.size, self.size)]

    def copies(self, step, chunk, first):
        me, n = self.me, self.n
        send_r, recv_r, send_l, recv_l = self.sems
        out = []
        for block, peer, has, send, recv in (
            (me - step, me + 1, (me - step >= 0) & (me < n - 1), send_r, recv_r),
            (me + step, me - 1, (me + step <= n - 1) & (me > 0), send_l, recv_l),
        ):
            src = (
                self.own.at[pl.ds(chunk * self.size, self.size)]
                if first
                else self.at(block, chunk)
            )
            index = step * self.chunks + chunk
            out.append(
                (has, remote(src, self.at(block, chunk), send.at[index], recv.at[index], peer))
            )
        return out

    def arrivals(self, step, chunk):
        me, n = self.me, self.n
        send_r, recv_r, send_l, recv_l = self.sems
        index = step * self.chunks + chunk
        out = []
        for block, has, send, recv in (
            (me - 1 - step, me - 1 - step >= 0, send_r, recv_r),
            (me + 1 + step, me + 1 + step <= n - 1, send_l, recv_l),
        ):
            ref = self.at(block, chunk)
            out.append((has, remote(ref, ref, send.at[index], recv.at[index], me)))
        return out

    def send_own(self, chunk):
        for has, copy in self.copies(0, chunk, True):
            pl.when(has)(copy.start)

    def forward(self, step):
        for chunk in range(self.chunks):
            for (got, arrival), (has, copy) in zip(
                self.arrivals(step - 1, chunk), self.copies(step, chunk, False)
            ):
                pl.when(got)(arrival.wait_recv)
                pl.when(has)(copy.start)

    def finish(self):
        for chunk in range(self.chunks):
            for got, arrival in self.arrivals(self.n - 2, chunk):
                pl.when(got)(arrival.wait_recv)
        for chunk in range(self.chunks):
            for has, copy in self.copies(0, chunk, True):
                pl.when(has)(copy.wait_send)

        def waits(step, carry):
            for chunk in range(self.chunks):
                for has, copy in self.copies(step, chunk, False):
                    pl.when(has)(copy.wait_send)
            return carry

        lax.fori_loop(1, self.n - 1, waits, 0)

    def forward_all(self):
        def step_of(step, carry):
            self.forward(step)
            return carry

        lax.fori_loop(1, self.n - 1, step_of, 0)


def gather_sems(n, chunks):
    return [pltpu.SemaphoreType.DMA(((n - 1) * chunks,))] * 4


def gather_rows(n, own, collective_id):
    rows, width = own.shape

    def kernel(own_ref, whole_ref, local_sem, *sems):
        me = lax.axis_index("mp")
        stream = LineGather(n, rows, 1, own_ref, whole_ref, sems)
        local = pltpu.make_async_copy(own_ref, stream.at(me, 0), local_sem)
        local.start()
        neighbour_barrier(n)
        stream.send_own(0)
        stream.forward_all()
        stream.finish()
        local.wait()

    return pl.pallas_call(
        kernel,
        out_shape=jax.ShapeDtypeStruct((n * rows, width), own.dtype),
        in_specs=[ANY],
        out_specs=ANY,
        scratch_shapes=[pltpu.SemaphoreType.DMA] + gather_sems(n, 1),
        compiler_params=pltpu.CompilerParams(collective_id=collective_id, has_side_effects=True),
        cost_estimate=pl.CostEstimate(
            flops=0, bytes_accessed=200 * own.size * own.dtype.itemsize, transcendentals=0
        ),
        name="gather_rows",
    )(own)


def dot_t(left, right):
    return lax.dot_general(
        left, right, (((1,), (1,)), ((), ())), preferred_element_type=jnp.float32
    )


def t_dot(left, right):
    return lax.dot_general(
        left, right, (((0,), (0,)), ((), ())), preferred_element_type=jnp.float32
    )


def dot(left, right):
    return jnp.dot(left, right, preferred_element_type=jnp.float32)


def probability(raw):
    return 1.0 / (1.0 + jnp.exp(math.log(SEQ) - raw * (1.0 / math.sqrt(HDIM))))


def rotated(values, cosine, sine, backward=False):
    turned = pltpu.roll(values, HDIM // 2, 1) * sine
    return values * cosine - turned if backward else values * cosine + turned


def scatter_rows(
    n, lhs, rhs, rhs_start, own_rows, epilogue, gains_row, collective_id, heads=None, extra=None, chunks=2
):
    total_rows = lhs[0].shape[0]
    rows = total_rows // n
    width = gains_row.shape[1]
    size = rows // chunks
    tile = 512
    has_norm, has_gain = epilogue in ("forward", "backward"), epilogue in ("backward", "last")
    count = len(lhs)
    block = 32
    if heads is not None:
        inner_width = lhs[0].shape[1] // 3
        head_count = inner_width // HDIM
        pieces = [inner_width]
    else:
        pieces = [a.shape[1] for a in lhs]
    depth = sum(pieces)

    def kernel(*refs):
        refs = list(refs)

        def take(k):
            return [refs.pop(0) for _ in range(k)]

        left_refs = take(count)
        (right_hbm,) = take(1)
        (gain_ref,) = take(1)
        own = take(len(own_rows))
        if heads is not None:
            cosine_ref, sine_ref, mask_ref = take(3)
        extra_ref = take(1)[0] if extra is not None else None
        outs = take(1 + has_gain)
        normed = take(1)[0] if has_norm else None
        if heads is not None:
            query_ref, key_ref, value_ref, mixed_ref = take(4)
        extra_whole = take(1)[0] if extra is not None else None
        right, held, sent, part = take(4)
        right_sem, send_sems, recv_sems = take(3)
        me = lax.axis_index("mp")
        fetch = pltpu.make_async_copy(
            right_hbm.at[:, pl.ds(rhs_start, depth)], right, right_sem
        )
        fetch.start()
        if extra is not None:
            (extra_sem,) = take(1)
            extra_gather = LineGather(n, rows, 1, extra_ref, extra_whole, take(4))
            extra_local = pltpu.make_async_copy(extra_ref, extra_gather.at(me, 0), extra_sem)
            extra_local.start()
        neighbour_barrier(n)
        if extra is not None:
            extra_gather.send_own(0)
        if heads is not None:
            turn = 128

            def enter(i, carry):
                span = rows_at(i * turn, turn)
                cosine, sine = cosine_ref[span, :], sine_ref[span, :]
                for h in range(head_count):
                    cols = pl.ds(h * HDIM, HDIM)
                    for k, target in ((0, query_ref), (1, key_ref)):
                        piece = left_refs[0][span, pl.ds(k * inner_width + h * HDIM, HDIM)]
                        target[span, cols] = rotated(piece, cosine, sine).astype(jnp.bfloat16)
                value_ref[span, :] = left_refs[0][
                    span, pl.ds(2 * inner_width, inner_width)
                ].astype(jnp.bfloat16)
                return carry

            lax.fori_loop(0, total_rows // turn, enter, 0)
        fetch.wait()

        def attend(block_id):
            span = rows_at(block_id * rows, rows)
            row_pos = block_id * rows + lax.broadcasted_iota(jnp.int32, (rows, rows), 0)

            def against(kb, totals):
                other = rows_at(kb * rows, rows)
                col_pos = kb * rows + lax.broadcasted_iota(jnp.int32, (rows, rows), 1)
                allowed = jnp.where(col_pos <= row_pos, mask_ref[:, other], 0.0)
                out = []
                for h in range(head_count):
                    cols = pl.ds(h * HDIM, HDIM)
                    raw = dot_t(query_ref[span, cols], key_ref[other, cols])
                    prob = probability(raw) * allowed
                    out.append(
                        totals[h]
                        + jnp.dot(
                            prob.astype(jnp.bfloat16),
                            value_ref[other, cols],
                            preferred_element_type=jnp.float32,
                        )
                    )
                return tuple(out)

            start = tuple(jnp.zeros((rows, HDIM), jnp.float32) for _ in range(head_count))
            totals = lax.fori_loop(0, block_id + 1, against, start)
            for h in range(head_count):
                mixed_ref[span, pl.ds(h * HDIM, HDIM)] = totals[h].astype(jnp.bfloat16)

        def product(block_id):
            if heads is not None:
                attend(block_id)
            sources = [mixed_ref] if heads is not None else left_refs

            def column(ct, carry):
                cols = rows_at(ct * tile, tile)
                total, start = None, 0
                for source, piece in zip(sources, pieces):
                    term = dot_t(
                        source[rows_at(block_id * rows, rows), :],
                        right[cols, pl.ds(start, piece)],
                    )
                    start += piece
                    total = term if total is None else total + term
                part[:, cols] = total
                return carry

            lax.fori_loop(0, width // tile, column, 0)

        def hop(block_id, chunk, rightward):
            peer = me + 1 if rightward else me - 1
            slot = block_id if rightward else jnp.where(block_id == peer, n, block_id)
            return remote(
                sent.at[block_id, pl.ds(chunk * size, size)],
                held.at[slot, pl.ds(chunk * size, size)],
                send_sems.at[block_id * chunks + chunk],
                recv_sems.at[slot * chunks + chunk],
                peer,
            )

        def arrival(slot, chunk):
            ref = held.at[slot, pl.ds(chunk * size, size)]
            return remote(
                ref, ref, send_sems.at[chunk], recv_sems.at[slot * chunks + chunk], me
            )

        def add_rows(block_id, chunk, slots):
            def body(i, carry):
                span = rows_at(chunk * size + i * block, block)
                value = part[span, :]
                for slot in slots:
                    value = value + held[slot, span, :].astype(jnp.float32)
                sent[block_id, span, :] = value.astype(jnp.bfloat16)
                return carry

            lax.fori_loop(0, size // block, body, 0)

        def relay(block_id, rightward, inner):
            product(block_id)
            for chunk in range(chunks):

                @pl.when(inner)
                def _():
                    arrival(block_id, chunk).wait_recv()
                    add_rows(block_id, chunk, [block_id])

                @pl.when(jnp.logical_not(inner))
                def _():
                    add_rows(block_id, chunk, [])

                hop(block_id, chunk, rightward).start()

        def step_of(step, carry):
            @pl.when((step >= me + 1) & (me < n - 1))
            def _():
                relay(me + n - step, True, me > 0)

            @pl.when((step >= n - me) & (me > 0))
            def _():
                relay(me - n + step, False, me < n - 1)

            if extra is not None:

                @pl.when(step < n - 1)
                def _():
                    extra_gather.forward(step)

            return carry

        lax.fori_loop(1, n, step_of, 0)
        product(me)
        if has_gain:
            outs[1][...] = jnp.zeros_like(outs[1])
        for chunk in range(chunks):

            @pl.when(me > 0)
            def _():
                arrival(me, chunk).wait_recv()

            @pl.when(me < n - 1)
            def _():
                arrival(n, chunk).wait_recv()

            def body(i, carry):
                span = rows_at(chunk * size + i * block, block)
                total = part[span, :]
                zero = jnp.zeros_like(total)
                total = total + jnp.where(me > 0, held[me, span, :].astype(jnp.float32), zero)
                total = total + jnp.where(
                    me < n - 1, held[n, span, :].astype(jnp.float32), zero
                )
                gain = gain_ref[...]
                if epilogue == "residual":
                    outs[0][span, :] = (own[0][span, :] + total).astype(jnp.bfloat16)
                elif epilogue == "forward":
                    value = own[0][span, :] + total
                    outs[0][span, :] = value
                    inverse = lax.rsqrt(
                        jnp.mean(value * value, axis=1, keepdims=True) + norm_eps
                    )
                    normed[span, :] = (value * inverse * gain).astype(jnp.bfloat16)
                else:
                    value = own[0][span, :]
                    inverse = lax.rsqrt(
                        jnp.mean(value * value, axis=1, keepdims=True) + norm_eps
                    )
                    unit = value * inverse
                    scaled = total * gain
                    inner = jnp.mean(scaled * unit, axis=1, keepdims=True)
                    result = own[1][span, :] + inverse * (scaled - unit * inner)
                    outs[0][span, :] = result
                    outs[1][...] += jnp.sum(
                        (total * unit).reshape(block // 8, 8, width), axis=0
                    )
                    if has_norm:
                        normed[span, :] = result.astype(jnp.bfloat16)
                return carry

            lax.fori_loop(0, size // block, body, 0)
        if extra is not None:
            extra_gather.finish()
            extra_local.wait()

        def sends(step, carry):
            for chunk in range(chunks):

                @pl.when((step >= me + 1) & (me < n - 1))
                def _():
                    hop(me + n - step, chunk, True).wait_send()

                @pl.when((step >= n - me) & (me > 0))
                def _():
                    hop(me - n + step, chunk, False).wait_send()

            return carry

        lax.fori_loop(1, n, sends, 0)

    out_type = jnp.bfloat16 if epilogue == "residual" else jnp.float32
    out_shape = [jax.ShapeDtypeStruct((rows, width), out_type)]
    out_specs = [VMEM]
    if has_gain:
        out_shape.append(jax.ShapeDtypeStruct((8, width), jnp.float32))
        out_specs.append(VMEM)
    scratch = [
        pltpu.VMEM((width, depth), jnp.bfloat16),
        pltpu.VMEM((n + 1, rows, width), jnp.bfloat16),
        pltpu.VMEM((n, rows, width), jnp.bfloat16),
        pltpu.VMEM((rows, width), jnp.float32),
    ]
    if has_norm:
        out_shape.append(jax.ShapeDtypeStruct((rows, width), jnp.bfloat16))
        out_specs.append(VMEM)
    scratch += [
        pltpu.SemaphoreType.DMA,
        pltpu.SemaphoreType.DMA((n * chunks,)),
        pltpu.SemaphoreType.DMA(((n + 1) * chunks,)),
    ]
    head_args = []
    if heads is not None:
        head_args = list(heads)
        out_shape += [jax.ShapeDtypeStruct((total_rows, inner_width), jnp.bfloat16)] * 4
        out_specs += [VMEM] * 4
    extra_args = []
    if extra is not None:
        out_shape.append(jax.ShapeDtypeStruct((total_rows, width), jnp.bfloat16))
        out_specs.append(ANY)
        scratch += [pltpu.SemaphoreType.DMA] + gather_sems(n, 1)
        extra_args = [extra]
    flops = 2 * total_rows * depth * width
    return pl.pallas_call(
        kernel,
        out_shape=out_shape,
        in_specs=[VMEM] * count
        + [ANY]
        + [VMEM] * (1 + len(own_rows) + len(head_args))
        + [ANY] * len(extra_args),
        out_specs=out_specs,
        scratch_shapes=scratch,
        compiler_params=pltpu.CompilerParams(
            collective_id=collective_id, has_side_effects=True, vmem_limit_bytes=VMEM_LIMIT
        ),
        cost_estimate=pl.CostEstimate(
            flops=flops, bytes_accessed=300_000_000, transcendentals=0
        ),
        name="scatter_" + epilogue,
    )(*lhs, rhs, gains_row, *own_rows, *head_args, *extra_args)


def attention_backward(queries, keys, values, mixed_grad, cosine, sine, key_mask):
    total_rows, inner_width = queries.shape
    block = min(256, total_rows)

    def kernel(q_ref, k_ref, v_ref, do_ref, cos_ref, sin_ref, mask_ref, dq_out, dk_out, dv_out, dk_ref, dv_ref):
        dk_ref[...] = jnp.zeros_like(dk_ref)
        dv_ref[...] = jnp.zeros_like(dv_ref)
        for i in range(total_rows // block):
            span = pl.ds(i * block, block)
            upto = (i + 1) * block
            shape = (upto, block)
            key_pos = lax.broadcasted_iota(jnp.int32, shape, 0)
            query_pos = i * block + lax.broadcasted_iota(jnp.int32, shape, 1)
            allowed = jnp.where(key_pos <= query_pos, mask_ref[:upto, :], 0.0)
            query, grad = q_ref[span, :], do_ref[span, :]
            key = k_ref[:upto, :]
            prob = probability(dot_t(key, query)) * allowed
            prob_grad = dot_t(v_ref[:upto, :], grad)
            dv_ref[:upto, :] += jnp.dot(
                prob.astype(jnp.bfloat16), grad, preferred_element_type=jnp.float32
            )
            score_grad = (prob_grad * prob * (1.0 - prob) * (1.0 / math.sqrt(HDIM))).astype(
                jnp.bfloat16
            )
            dk_ref[:upto, :] += jnp.dot(score_grad, query, preferred_element_type=jnp.float32)
            dq = t_dot(score_grad, key)
            dq_out[span, :] = rotated(
                dq, cos_ref[span, :], sin_ref[span, :], True
            ).astype(jnp.bfloat16)
        dk_out[...] = rotated(dk_ref[...], cos_ref[...], sin_ref[...], True).astype(jnp.bfloat16)
        dv_out[...] = dv_ref[...].astype(jnp.bfloat16)

    head = pl.BlockSpec((total_rows, HDIM), lambda h: (0, h))
    table = pl.BlockSpec((total_rows, HDIM), lambda h: (0, 0))
    return pl.pallas_call(
        kernel,
        grid=(inner_width // HDIM,),
        out_shape=[jax.ShapeDtypeStruct((total_rows, inner_width), jnp.bfloat16)] * 3,
        in_specs=[head] * 4 + [table] * 2 + [pl.BlockSpec((total_rows, 1), lambda h: (0, 0))],
        out_specs=[head] * 3,
        scratch_shapes=[pltpu.VMEM((total_rows, HDIM), jnp.float32)] * 2,
        compiler_params=pltpu.CompilerParams(vmem_limit_bytes=VMEM_LIMIT),
        cost_estimate=pl.CostEstimate(
            flops=8 * total_rows * total_rows * inner_width,
            bytes_accessed=14 * total_rows * inner_width,
            transcendentals=0,
        ),
        name="attention_backward",
    )(queries, keys, values, mixed_grad, cosine, sine, key_mask)


def small_exchange(n_dp, n_mp, table, reduces, collective_id):
    peers_mp, peers_dp = n_mp - 1, n_dp - 1

    def kernel(in_ref, out_ref, first, second, mid, s_mp, r_mp, s_dp, r_dp):
        dp, mp = lax.axis_index("dp"), lax.axis_index("mp")
        barrier = pltpu.get_barrier_semaphore()
        for k in range(1, n_mp):
            pl.semaphore_signal(
                barrier, inc=1, device_id={"mp": lax.rem(mp + k, n_mp)}, device_id_type=MESH
            )
        for k in range(1, n_dp):
            pl.semaphore_signal(
                barrier, inc=1, device_id={"dp": lax.rem(dp + k, n_dp)}, device_id_type=MESH
            )
        pl.semaphore_wait(barrier, peers_mp + peers_dp)
        if reduces:
            first[mp] = in_ref[mp]
        else:
            first[mp] = in_ref[...]
        copies = []
        for k in range(1, n_mp):
            peer = lax.rem(mp + k, n_mp)
            copies.append(
                pltpu.make_async_remote_copy(
                    src_ref=in_ref.at[peer] if reduces else in_ref,
                    dst_ref=first.at[mp],
                    send_sem=s_mp.at[k - 1],
                    recv_sem=r_mp.at[k - 1],
                    device_id={"mp": peer},
                    device_id_type=MESH,
                )
            )
        for copy in copies:
            copy.start()
        for copy in copies:
            copy.wait()
        if reduces:
            total = first[0]
            for k in range(1, n_mp):
                total = total + first[k]
            mid[...] = total
        else:
            mid[...] = first[...]
        second[dp] = mid[dp] if reduces else mid[...]
        copies = []
        for k in range(1, n_dp):
            peer = lax.rem(dp + k, n_dp)
            copies.append(
                pltpu.make_async_remote_copy(
                    src_ref=mid.at[peer] if reduces else mid,
                    dst_ref=second.at[dp],
                    send_sem=s_dp.at[k - 1],
                    recv_sem=r_dp.at[k - 1],
                    device_id={"dp": peer},
                    device_id_type=MESH,
                )
            )
        for copy in copies:
            copy.start()
        for copy in copies:
            copy.wait()
        if reduces:
            total = second[0]
            for k in range(1, n_dp):
                total = total + second[k]
            out_ref[...] = total
        else:
            out_ref[...] = second[...]

    if reduces:
        out = (8, 128)
        first, mid, second = (n_mp, n_dp, 8, 128), (n_dp, 8, 128), (n_dp, 8, 128)
    else:
        out = (n_dp, n_mp, 8, 128)
        first, mid, second = (n_mp, 8, 128), (n_mp, 8, 128), (n_dp, n_mp, 8, 128)
    return pl.pallas_call(
        kernel,
        out_shape=jax.ShapeDtypeStruct(out, jnp.float32),
        in_specs=[VMEM],
        out_specs=VMEM,
        scratch_shapes=[
            pltpu.VMEM(first, jnp.float32),
            pltpu.VMEM(second, jnp.float32),
            pltpu.VMEM(mid, jnp.float32),
            pltpu.SemaphoreType.DMA((peers_mp,)),
            pltpu.SemaphoreType.DMA((peers_mp,)),
            pltpu.SemaphoreType.DMA((peers_dp,)),
            pltpu.SemaphoreType.DMA((peers_dp,)),
        ],
        compiler_params=pltpu.CompilerParams(collective_id=collective_id, has_side_effects=True),
        name="sum_small" if reduces else "gather_small",
    )(table)


def gather_gains(n_dp, n_mp, gains, collective_id):
    local = gains.shape[1]
    flat = jnp.pad(gains.reshape(1, 2 * local), ((0, 7), (0, 128 - 2 * local)))
    whole = small_exchange(n_dp, n_mp, flat, False, collective_id)
    rows = whole[:, :, 0, : 2 * local].reshape(n_dp * n_mp, 2, local)
    return rows.transpose(1, 0, 2).reshape(2, n_dp * n_mp * local)


def scatter_gains(n_dp, n_mp, partial, collective_id):
    local = partial.shape[1] // (n_dp * n_mp)
    table = partial.reshape(2, n_dp, n_mp, local).transpose(2, 1, 0, 3)
    table = table.reshape(n_mp, n_dp, 1, 2 * local)
    table = jnp.pad(table, ((0, 0), (0, 0), (0, 7), (0, 128 - 2 * local)))
    out = small_exchange(n_dp, n_mp, table, True, collective_id)
    return out[0, : 2 * local].reshape(2, local)


def rope_tables(length, half_dim):
    positions = jnp.arange(length, dtype=jnp.float32)[:, None]
    inverse_freq = rope_base ** (-jnp.arange(half_dim, dtype=jnp.float32) / half_dim)
    angles = positions * inverse_freq[None, :]
    cosine, sine = jnp.cos(angles), jnp.sin(angles)
    return jnp.concatenate([cosine, cosine], axis=1), jnp.concatenate([-sine, sine], axis=1)


def update(weight, moment, average, gradient, step_size):
    moment_new = momentum_decay * moment + (1.0 - momentum_decay) * gradient
    weight_new = weight - step_size * (
        (1.0 - momentum_decay) * gradient + momentum_decay * moment_new
    )
    average_new = average_decay * average + (1.0 - average_decay) * weight_new
    return (weight_new, moment_new, average_new)


def per_device(
    n_dp,
    n_mp,
    tokens,
    cotangent,
    valid_counts,
    w_qkv,
    w_out,
    w_gu,
    w_down,
    gains,
    mom_qkv,
    mom_out,
    mom_gu,
    mom_down,
    mom_gains,
    avg_qkv,
    avg_out,
    avg_gu,
    avg_down,
    avg_gains,
):
    half = jnp.bfloat16
    row_count, width = tokens.shape
    owned, _, local_width = w_qkv.shape
    hidden = w_gu.shape[2]
    valid_len = valid_counts[0]

    attn_part = jnp.concatenate(
        [w_qkv.reshape(owned, 3 * local_width), w_out.T], axis=1
    ).astype(half)
    attn_w = lax.all_gather(attn_part, "dp", axis=0, tiled=True)
    ffn_part = jnp.concatenate([w_gu.reshape(owned, 2 * hidden), w_down.T], axis=1).astype(half)
    ffn_w = lax.all_gather(ffn_part, "dp", axis=0, tiled=True)
    qkv_w, out_wt = attn_w[:, : 3 * local_width], attn_w[:, 3 * local_width :]
    down_wt = ffn_w[:, 2 * hidden :]

    gain_all = gather_gains(n_dp, n_mp, gains, 0)
    row_ids = lax.axis_index("mp") * row_count + jnp.arange(row_count, dtype=jnp.int32)
    live_rows = (row_ids < valid_len).astype(jnp.float32)[:, None]
    xin = tokens.astype(jnp.float32)
    inverse = lax.rsqrt(jnp.mean(xin * xin, axis=1, keepdims=True) + norm_eps)
    normed_first = (xin * inverse * gain_all[0][None, :]).astype(half)
    h_first = gather_rows(n_mp, normed_first, 1)
    out_grad = cotangent.astype(jnp.float32) * live_rows
    cosine, sine = rope_tables(SEQ, HDIM // 2)
    key_mask = (jnp.arange(SEQ, dtype=jnp.int32) < valid_len).astype(jnp.float32)

    joined = dot(h_first, qkv_w)
    second, normed_second, queries, keys, values, mixed, branch_grad = scatter_rows(
        n_mp,
        [joined],
        attn_w,
        3 * local_width,
        [xin],
        "forward",
        gain_all[1:2],
        2,
        heads=(cosine, sine, key_mask[None, :]),
        extra=out_grad.astype(half),
    )

    h_second = gather_rows(n_mp, normed_second, 6)
    gate_val = dot(h_second, ffn_w[:, :hidden])
    up_val = dot(h_second, ffn_w[:, hidden : 2 * hidden])
    act = (jax.nn.silu(gate_val) * up_val).astype(half)
    act_grad = dot(branch_grad, down_wt)
    sigma = jax.nn.sigmoid(gate_val)
    gate_grad = (act_grad * up_val * sigma * (1.0 + gate_val * (1.0 - sigma))).astype(half)
    up_grad = (act_grad * gate_val * sigma).astype(half)
    grad_ffn = jnp.zeros((width, 3 * hidden), half)
    for k, (a, b) in enumerate(
        ((h_second, gate_grad), (h_second, up_grad), (branch_grad, act))
    ):
        grad_ffn = lax.dynamic_update_slice(grad_ffn, t_dot(a, b).astype(half), (0, k * hidden))
    grad_ffn, gate_grad = lax.optimization_barrier((grad_ffn, gate_grad))
    sum_ffn = lax.psum_scatter(grad_ffn, "dp", scatter_dimension=0, tiled=True)
    second_grad, gain_two, own_grad = scatter_rows(
        n_mp, [gate_grad, up_grad], ffn_w, 0, [second, out_grad], "backward", gain_all[1:2], 3
    )
    block_out, attn_grad = scatter_rows(
        n_mp,
        [act],
        ffn_w,
        2 * hidden,
        [second],
        "residual",
        gain_all[1:2],
        7,
        extra=own_grad,
    )

    mixed_grad = dot(attn_grad, out_wt).astype(half)
    joined_grad = attention_backward(
        queries, keys, values, mixed_grad, cosine, sine, key_mask[:, None]
    )
    grad_attn = jnp.zeros((width, 4 * local_width), half)
    for k, (a, b) in enumerate(
        (
            (h_first, joined_grad[0]),
            (h_first, joined_grad[1]),
            (h_first, joined_grad[2]),
            (attn_grad, mixed),
        )
    ):
        grad_attn = lax.dynamic_update_slice(
            grad_attn, t_dot(a, b).astype(half), (0, k * local_width)
        )
    grad_attn, second_grad = lax.optimization_barrier((grad_attn, second_grad))
    grad_attn, sum_ffn = lax.optimization_barrier((grad_attn, sum_ffn))
    sum_attn = lax.psum_scatter(grad_attn, "dp", scatter_dimension=0, tiled=True)
    input_grad, gain_one = scatter_rows(
        n_mp,
        [joined_grad[0], joined_grad[1], joined_grad[2]],
        attn_w,
        0,
        [xin, second_grad],
        "last",
        gain_all[0:1],
        4,
    )
    gain_partial = jnp.stack([gain_one.sum(axis=0), gain_two.sum(axis=0)], axis=0)
    sum_gains = scatter_gains(n_dp, n_mp, gain_partial, 5)

    total_rows = SEQ * n_dp
    matrix_rate = step_rate / math.sqrt(total_rows)
    scale_rate = gain_rate / math.sqrt(total_rows)
    sum_attn = sum_attn.astype(jnp.float32)
    sum_ffn = sum_ffn.astype(jnp.float32)
    sum_qkv = sum_attn[:, : 3 * local_width].reshape(owned, 3, local_width)
    sum_out = sum_attn[:, 3 * local_width :].T
    sum_gu = sum_ffn[:, : 2 * hidden].reshape(owned, 2, hidden)
    sum_down = sum_ffn[:, 2 * hidden :].T
    new_qkv, next_mom_qkv, next_avg_qkv = update(w_qkv, mom_qkv, avg_qkv, sum_qkv, matrix_rate)
    new_out, next_mom_out, next_avg_out = update(w_out, mom_out, avg_out, sum_out, matrix_rate)
    new_gu, next_mom_gu, next_avg_gu = update(w_gu, mom_gu, avg_gu, sum_gu, matrix_rate)
    new_down, next_mom_down, next_avg_down = update(
        w_down, mom_down, avg_down, sum_down, matrix_rate
    )
    new_gains, next_mom_gains, next_avg_gains = update(
        gains, mom_gains, avg_gains, sum_gains, scale_rate
    )
    return (
        block_out,
        input_grad,
        new_qkv,
        new_out,
        new_gu,
        new_down,
        new_gains,
        next_mom_qkv,
        next_mom_out,
        next_mom_gu,
        next_mom_down,
        next_mom_gains,
        next_avg_qkv,
        next_avg_out,
        next_avg_gu,
        next_avg_down,
        next_avg_gains,
        new_qkv.astype(half),
        new_out.astype(half),
        new_gu.astype(half),
        new_down.astype(half),
    )


def solution(mesh):
    rows, one = P(("dp", "mp"), None), P("dp")
    tall, wide, spread = P("dp", None, "mp"), P("mp", "dp"), P(None, ("dp", "mp"))
    weights = (tall, wide, tall, wide)
    return jax.shard_map(
        functools.partial(per_device, mesh.shape["dp"], mesh.shape["mp"]),
        mesh=mesh,
        in_specs=(rows, rows, one, *((*weights, spread) * 3)),
        out_specs=(rows, rows, *((*weights, spread) * 3), *weights),
        check_vma=False,
    )
```

```python
import functools
import math

import jax
import jax.numpy as jnp
from jax import lax
from jax.experimental import pallas as pl
from jax.experimental.pallas import tpu as pltpu
import numpy as np
from jax.sharding import PartitionSpec as P

HDIM = 128
SEQ = 1024
MESH = pl.DeviceIdType.MESH
ANY = pl.BlockSpec(memory_space=pl.ANY)
VMEM = pl.BlockSpec(memory_space=pltpu.VMEM)
VMEM_LIMIT = 60 * 1024 * 1024

norm_eps = 1e-05
rope_base = 10000.0
momentum_decay = 0.9
average_decay = 0.9
step_rate = 0.05
gain_rate = 0.5


def rows_at(start, size):
    return pl.ds(pl.multiple_of(start, size), size)


def remote(src, dst, send_sem, recv_sem, peer):
    return pltpu.make_async_remote_copy(
        src_ref=src,
        dst_ref=dst,
        send_sem=send_sem,
        recv_sem=recv_sem,
        device_id={"mp": peer},
        device_id_type=MESH,
    )


def neighbour_barrier(n):
    me = lax.axis_index("mp")
    barrier = pltpu.get_barrier_semaphore()

    @pl.when(me > 0)
    def _():
        pl.semaphore_signal(barrier, inc=1, device_id={"mp": me - 1}, device_id_type=MESH)

    @pl.when(me < n - 1)
    def _():
        pl.semaphore_signal(barrier, inc=1, device_id={"mp": me + 1}, device_id_type=MESH)

    pl.semaphore_wait(barrier, jnp.where(me > 0, 1, 0) + jnp.where(me < n - 1, 1, 0))


class LineGather:
    def __init__(self, n, rows, chunks, own, whole, sems):
        self.n, self.rows, self.chunks = n, rows, chunks
        self.size = rows // chunks
        self.own, self.whole, self.sems = own, whole, sems
        self.me = lax.axis_index("mp")

    def at(self, block, chunk):
        return self.whole.at[rows_at(block * self.rows + chunk * self.size, self.size)]

    def copies(self, step, chunk, first):
        me, n = self.me, self.n
        send_r, recv_r, send_l, recv_l = self.sems
        out = []
        for block, peer, has, send, recv in (
            (me - step, me + 1, (me - step >= 0) & (me < n - 1), send_r, recv_r),
            (me + step, me - 1, (me + step <= n - 1) & (me > 0), send_l, recv_l),
        ):
            src = (
                self.own.at[pl.ds(chunk * self.size, self.size)]
                if first
                else self.at(block, chunk)
            )
            index = step * self.chunks + chunk
            out.append(
                (has, remote(src, self.at(block, chunk), send.at[index], recv.at[index], peer))
            )
        return out

    def arrivals(self, step, chunk):
        me, n = self.me, self.n
        send_r, recv_r, send_l, recv_l = self.sems
        index = step * self.chunks + chunk
        out = []
        for block, has, send, recv in (
            (me - 1 - step, me - 1 - step >= 0, send_r, recv_r),
            (me + 1 + step, me + 1 + step <= n - 1, send_l, recv_l),
        ):
            ref = self.at(block, chunk)
            out.append((has, remote(ref, ref, send.at[index], recv.at[index], me)))
        return out

    def send_own(self, chunk):
        for has, copy in self.copies(0, chunk, True):
            pl.when(has)(copy.start)

    def forward(self, step):
        for chunk in range(self.chunks):
            self.forward_chunk(step, chunk, True)

    def forward_chunk(self, step, chunk, more):
        for (got, arrival), (has, copy) in zip(
            self.arrivals(step - 1, chunk), self.copies(step, chunk, False)
        ):
            pl.when(got)(arrival.wait_recv)
            pl.when(has & more)(copy.start)

    def finish(self, arrivals=True):
        for chunk in range(self.chunks if arrivals else 0):
            for got, arrival in self.arrivals(self.n - 2, chunk):
                pl.when(got)(arrival.wait_recv)
        for chunk in range(self.chunks):
            for has, copy in self.copies(0, chunk, True):
                pl.when(has)(copy.wait_send)

        def waits(step, carry):
            for chunk in range(self.chunks):
                for has, copy in self.copies(step, chunk, False):
                    pl.when(has)(copy.wait_send)
            return carry

        lax.fori_loop(1, self.n - 1, waits, 0)

    def forward_all(self):
        def step_of(step, carry):
            self.forward(step)
            return carry

        lax.fori_loop(1, self.n - 1, step_of, 0)


def gather_sems(n, chunks):
    return [pltpu.SemaphoreType.DMA(((n - 1) * chunks,))] * 4


class Exchange:
    def __init__(self, n_dp, n_mp, sems):
        self.n_dp, self.n_mp = n_dp, n_mp
        self.s_mp, self.r_mp, self.s_dp, self.r_dp = sems
        self.dp, self.mp = lax.axis_index("dp"), lax.axis_index("mp")

    def barrier(self):
        barrier = pltpu.get_barrier_semaphore()
        for axis, here, count in (("mp", self.mp, self.n_mp), ("dp", self.dp, self.n_dp)):
            for k in range(1, count):
                pl.semaphore_signal(
                    barrier,
                    inc=1,
                    device_id={axis: lax.rem(here + k, count)},
                    device_id_type=MESH,
                )
        pl.semaphore_wait(barrier, self.n_mp + self.n_dp - 2)

    def swap(self, axis, source_of, target):
        if axis == "mp":
            here, count, send, recv = self.mp, self.n_mp, self.s_mp, self.r_mp
        else:
            here, count, send, recv = self.dp, self.n_dp, self.s_dp, self.r_dp
        copies = []
        for k in range(1, count):
            peer = lax.rem(here + k, count)
            copies.append(
                pltpu.make_async_remote_copy(
                    src_ref=source_of(peer),
                    dst_ref=target.at[here],
                    send_sem=send.at[k - 1],
                    recv_sem=recv.at[k - 1],
                    device_id={axis: peer},
                    device_id_type=MESH,
                )
            )
        for copy in copies:
            copy.start()
        return copies


def exchange_sems(n_dp, n_mp):
    return [pltpu.SemaphoreType.DMA((n_mp - 1,))] * 2 + [pltpu.SemaphoreType.DMA((n_dp - 1,))] * 2


def tile_of(dp, mp, n_mp, local):
    return (dp * n_mp + mp) * local // 128


def flat_pairs(x):
    high, parts, wide = x.shape
    return x.reshape(high, parts, wide // 128, 128).transpose(0, 2, 1, 3).reshape(-1, 128)


def round_shares(w_gu, w_down):
    high, parts, hidden = w_gu.shape
    tiles = hidden // 128
    step = 128
    turn = min(256, hidden)

    def kernel(gu_ref, down_ref, out_ref):
        for part in range(parts):
            for tile in range(tiles):
                cols = pl.ds(part * hidden + tile * 128, 128)
                out_ref[:, cols] = gu_ref[
                    pl.ds(tile * parts + part, step, stride=tiles * parts), :
                ].astype(jnp.bfloat16)
        for i in range(hidden // turn):
            piece = down_ref[pl.ds(i * turn, turn), :]
            out_ref[:, pl.ds(parts * hidden + i * turn, turn)] = piece.T.astype(jnp.bfloat16)

    return pl.pallas_call(
        kernel,
        grid=(high // step,),
        out_shape=jax.ShapeDtypeStruct((high, (parts + 1) * hidden), jnp.bfloat16),
        in_specs=[
            pl.BlockSpec((step * tiles * parts, 128), lambda i: (i, 0)),
            pl.BlockSpec((hidden, step), lambda i: (0, i)),
        ],
        out_specs=pl.BlockSpec((step, (parts + 1) * hidden), lambda i: (i, 0)),
        compiler_params=pltpu.CompilerParams(vmem_limit_bytes=VMEM_LIMIT),
        cost_estimate=pl.CostEstimate(
            flops=0, bytes_accessed=6 * (w_gu.size + w_down.size), transcendentals=0
        ),
        name="round_shares",
    )(flat_pairs(w_gu), w_down)


def gather_first(n_dp, n_mp, own, gains, cotangent, live, collective_id, chunks=2):
    rows, width = own.shape
    local = gains.shape[1]
    lanes = jnp.arange(128, dtype=jnp.int32) // local
    place = lax.rem(lax.axis_index("mp"), 128 // local)
    if n_mp * local < 128:
        place = lax.rem(lax.axis_index("dp") * n_mp + lax.axis_index("mp"), 128 // local)
    tile = jnp.where(
        (lanes == place)[None, :], jnp.tile(gains, (1, 128 // local)), 0.0
    )
    tile = jnp.concatenate([tile, jnp.zeros((6, 128), jnp.float32)], axis=0)

    block = 64 if rows % 64 == 0 else rows

    def kernel(
        own_ref,
        tile_ref,
        cotangent_ref,
        live_ref,
        normed_ref,
        gain_ref,
        base_ref,
        branch_ref,
        all_ref,
        first,
        second,
        *sems,
    ):
        me = lax.axis_index("mp")
        exchange = Exchange(n_dp, n_mp, sems[:4])
        stream = LineGather(n_mp, rows, chunks, own_ref, all_ref, sems[4:])
        exchange.barrier()
        first[me] = tile_ref[...]
        copies = exchange.swap("mp", lambda peer: tile_ref, first)
        for chunk in range(chunks):
            stream.send_own(chunk)
        all_ref[rows_at(me * rows, rows), :] = own_ref[...]
        for copy in copies:
            copy.wait()
        dp = lax.axis_index("dp")
        second[dp] = first[...]
        copies = exchange.swap("dp", lambda peer: first, second)

        def enter(i, carry):
            span = rows_at(i * block, block)
            value = cotangent_ref[span, :].astype(jnp.float32) * live_ref[span, :]
            base_ref[span, :] = value
            branch_ref[span, :] = value.astype(jnp.bfloat16)
            return carry

        lax.fori_loop(0, rows // block, enter, 0)
        for copy in copies:
            copy.wait()
        gain_ref[...] = jnp.zeros_like(gain_ref)
        for d in range(n_dp):
            for m in range(n_mp):
                cols = pl.ds(tile_of(d, m, n_mp, local) * 128, 128)
                gain_ref[:, cols] += second[d, m]
        def norm(block_id):
            def body(i, carry):
                span = rows_at(block_id * rows + i * block, block)
                value = all_ref[span, :].astype(jnp.float32)
                inverse = lax.rsqrt(jnp.mean(value * value, axis=1, keepdims=True) + norm_eps)
                normed_ref[span, :] = (value * inverse * gain_ref[0:1, :]).astype(jnp.bfloat16)
                return carry

            lax.fori_loop(0, rows // block, body, 0)

        def step_of(step, carry):
            @pl.when(step > 0)
            def _():
                for chunk in range(chunks):
                    stream.forward_chunk(step, chunk, step < n_mp - 1)

            @pl.when(me + step < n_mp)
            def _():
                norm(me + step)

            @pl.when((me - step >= 0) & (step > 0))
            def _():
                norm(me - step)

            return carry

        lax.fori_loop(0, n_mp, step_of, 0)
        stream.finish(False)

    half = jnp.bfloat16
    return pl.pallas_call(
        kernel,
        out_shape=[
            jax.ShapeDtypeStruct((n_mp * rows, width), half),
            jax.ShapeDtypeStruct((8, width), jnp.float32),
            jax.ShapeDtypeStruct((rows, width), jnp.float32),
            jax.ShapeDtypeStruct((rows, width), half),
        ],
        in_specs=[VMEM] * 4,
        out_specs=[VMEM] * 4,
        scratch_shapes=[
            pltpu.VMEM((n_mp * rows, width), half),
            pltpu.VMEM((n_mp, 8, 128), jnp.float32),
            pltpu.VMEM((n_dp, n_mp, 8, 128), jnp.float32),
        ]
        + exchange_sems(n_dp, n_mp)
        + gather_sems(n_mp, chunks),
        compiler_params=pltpu.CompilerParams(
            collective_id=collective_id, has_side_effects=True, vmem_limit_bytes=VMEM_LIMIT
        ),
        cost_estimate=pl.CostEstimate(
            flops=0, bytes_accessed=200 * own.size * own.dtype.itemsize, transcendentals=0
        ),
        name="gather_first",
    )(own, tile, cotangent, live)


def dot_t(left, right):
    return lax.dot_general(
        left, right, (((1,), (1,)), ((), ())), preferred_element_type=jnp.float32
    )


def t_dot(left, right):
    return lax.dot_general(
        left, right, (((0,), (0,)), ((), ())), preferred_element_type=jnp.float32
    )


def dot(left, right):
    return jnp.dot(left, right, preferred_element_type=jnp.float32)


def probability(raw):
    return 1.0 / (1.0 + jnp.exp(math.log(SEQ) - raw * (1.0 / math.sqrt(HDIM))))


def rotated(values, cosine, sine, backward=False):
    turned = pltpu.roll(values, HDIM // 2, 1) * sine
    return values * cosine - turned if backward else values * cosine + turned


def scatter_rows(
    n,
    lhs,
    rhs,
    rhs_start,
    own_rows,
    epilogue,
    gains_row,
    collective_id,
    heads=None,
    extra=None,
    other_gain=None,
    grad_lefts=None,
    grad_right=None,
    n_dp=1,
    chunks=2,
):
    total_rows = lhs[0].shape[0]
    rows = total_rows // n
    width = gains_row.shape[1]
    size = rows // chunks
    tile = 512
    has_norm, has_gain = epilogue in ("forward", "backward"), epilogue in ("backward", "last")
    count = len(lhs)
    block = 32
    if heads is not None:
        inner_width = rhs_start // 3
        head_count = inner_width // HDIM
        pieces = [inner_width]
    else:
        pieces = [a.shape[1] for a in lhs]
    depth = sum(pieces)

    def kernel(*refs):
        refs = list(refs)

        def take(k):
            return [refs.pop(0) for _ in range(k)]

        left_refs = take(count)
        (right_hbm,) = take(1)
        (gain_ref,) = take(1)
        own = take(len(own_rows))
        if heads is not None:
            cosine_ref, sine_ref, mask_ref = take(3)
        if other_gain is not None:
            (other_ref,) = take(1)
            grad_left_refs, grad_right_ref = take(2), take(1)[0]
        extra_ref = take(1)[0] if extra is not None else None
        outs = take(1 + has_gain)
        owned_ref = take(1)[0] if other_gain is not None else None
        normed = take(1)[0] if has_norm else None
        if heads is not None:
            query_ref, key_ref, value_ref, mixed_ref = take(4)
        extra_whole = take(1)[0] if extra is not None else None
        right, held, sent, part = take(4)
        joined_ref = take(1)[0] if heads is not None else None
        right_sem, send_sems, recv_sems = take(3)
        me = lax.axis_index("mp")
        fetch = pltpu.make_async_copy(
            right_hbm.at[:, pl.ds(rhs_start, depth)], right, right_sem
        )
        fetch.start()
        if heads is not None:
            (joined_sem,) = take(1)
            fetch_joined = pltpu.make_async_copy(
                right_hbm.at[:, pl.ds(0, rhs_start)], joined_ref, joined_sem
            )
            fetch_joined.start()
        if extra is not None:
            (extra_sem,) = take(1)
            extra_gather = LineGather(n, rows, 1, extra_ref, extra_whole, take(4))
            extra_local = pltpu.make_async_copy(extra_ref, extra_gather.at(me, 0), extra_sem)
            extra_local.start()
        if other_gain is not None:
            gain_sum, table, first, middle, second = take(5)
            exchange = Exchange(n_dp, n, take(4))
            grads, paired, landed = take(3)
            pair_send, pair_recv, land_send, land_recv = take(4)
            dp = lax.axis_index("dp")
            core, chip = lax.rem(dp, 2), dp // 2
            chips, share = n_dp // 2, landed.shape[1]
            exchange.barrier()
            pair_copies = [
                pltpu.make_async_remote_copy(
                    src_ref=grads.at[rows_at((2 * q + 1 - core) * share, share)],
                    dst_ref=paired.at[q],
                    send_sem=pair_send.at[q],
                    recv_sem=pair_recv.at[q],
                    device_id={"dp": dp + 1 - 2 * core},
                    device_id_type=MESH,
                )
                for q in range(chips)
            ]
            land_copies = [
                pltpu.make_async_remote_copy(
                    src_ref=paired.at[lax.rem(chip + k, chips)],
                    dst_ref=landed.at[k - 1],
                    send_sem=land_send.at[k - 1],
                    recv_sem=land_recv.at[k - 1],
                    device_id={"dp": 2 * lax.rem(chip + k, chips) + core},
                    device_id_type=MESH,
                )
                for k in range(1, chips)
            ]

            def make_grads():
                start, narrow = 0, 256
                for k, right_ref in enumerate([*left_refs, grad_right_ref]):
                    left_ref = grad_left_refs[0 if k < count else 1]

                    def column(i, carry, start=start, left_ref=left_ref, right_ref=right_ref):
                        grads[:, rows_at(start + i * narrow, narrow)] = t_dot(
                            left_ref[...], right_ref[:, rows_at(i * narrow, narrow)]
                        ).astype(jnp.bfloat16)
                        return carry

                    lax.fori_loop(0, right_ref.shape[1] // narrow, column, 0)
                    start += right_ref.shape[1]
                for copy in pair_copies:
                    copy.start()

            def pair_up():
                for copy in pair_copies:
                    copy.wait()

                def add(i, carry):
                    span = rows_at(i * block, block)
                    for q in range(chips):
                        own_span = rows_at((2 * q + core) * share + i * block, block)
                        paired[q, span, :] = (
                            paired[q, span, :].astype(jnp.float32)
                            + grads[own_span, :].astype(jnp.float32)
                        ).astype(jnp.bfloat16)
                    return carry

                lax.fori_loop(0, share // block, add, 0)
                for copy in land_copies:
                    copy.start()

            def land():
                for copy in land_copies:
                    copy.wait()

                def add(i, carry):
                    span = rows_at(i * block, block)
                    total = paired[chip, span, :].astype(jnp.float32)
                    for k in range(chips - 1):
                        total = total + landed[k, span, :].astype(jnp.float32)
                    owned_ref[span, :] = total
                    return carry

                lax.fori_loop(0, share // block, add, 0)

        else:
            gain_sum = outs[1] if has_gain else None
            neighbour_barrier(n)
        if extra is not None:
            extra_gather.send_own(0)
        if heads is not None:
            turn = 256
            fetch_joined.wait()

            def enter(i, carry):
                span = rows_at(i * turn, turn)
                cosine, sine = cosine_ref[span, :], sine_ref[span, :]
                row_vals = left_refs[0][span, :]
                for k, target in ((0, query_ref), (1, key_ref), (2, value_ref)):
                    piece = dot(row_vals, joined_ref[:, pl.ds(k * inner_width, inner_width)])
                    for h in range(head_count):
                        value = piece[:, h * HDIM : (h + 1) * HDIM]
                        if k < 2:
                            value = rotated(value, cosine, sine)
                        target[span, pl.ds(h * HDIM, HDIM)] = value.astype(jnp.bfloat16)
                return carry

            lax.fori_loop(0, total_rows // turn, enter, 0)
        fetch.wait()

        def attend(block_id):
            span = rows_at(block_id * rows, rows)
            row_pos = block_id * rows + lax.broadcasted_iota(jnp.int32, (rows, rows), 0)

            def against(kb, totals):
                other = rows_at(kb * rows, rows)
                col_pos = kb * rows + lax.broadcasted_iota(jnp.int32, (rows, rows), 1)
                allowed = jnp.where(col_pos <= row_pos, mask_ref[:, other], 0.0)
                out = []
                for h in range(head_count):
                    cols = pl.ds(h * HDIM, HDIM)
                    raw = dot_t(query_ref[span, cols], key_ref[other, cols])
                    prob = probability(raw) * allowed
                    out.append(
                        totals[h]
                        + jnp.dot(
                            prob.astype(jnp.bfloat16),
                            value_ref[other, cols],
                            preferred_element_type=jnp.float32,
                        )
                    )
                return tuple(out)

            start = tuple(jnp.zeros((rows, HDIM), jnp.float32) for _ in range(head_count))
            totals = lax.fori_loop(0, block_id + 1, against, start)
            for h in range(head_count):
                mixed_ref[span, pl.ds(h * HDIM, HDIM)] = totals[h].astype(jnp.bfloat16)

        def product(block_id):
            if heads is not None:
                attend(block_id)
            sources = [mixed_ref] if heads is not None else left_refs

            def column(ct, carry):
                cols = rows_at(ct * tile, tile)
                total, start = None, 0
                for source, piece in zip(sources, pieces):
                    term = dot_t(
                        source[rows_at(block_id * rows, rows), :],
                        right[cols, pl.ds(start, piece)],
                    )
                    start += piece
                    total = term if total is None else total + term
                part[:, cols] = total
                return carry

            lax.fori_loop(0, width // tile, column, 0)

        def hop(block_id, chunk, rightward):
            peer = me + 1 if rightward else me - 1
            slot = block_id if rightward else jnp.where(block_id == peer, n, block_id)
            return remote(
                sent.at[block_id, pl.ds(chunk * size, size)],
                held.at[slot, pl.ds(chunk * size, size)],
                send_sems.at[block_id * chunks + chunk],
                recv_sems.at[slot * chunks + chunk],
                peer,
            )

        def arrival(slot, chunk):
            ref = held.at[slot, pl.ds(chunk * size, size)]
            return remote(
                ref, ref, send_sems.at[chunk], recv_sems.at[slot * chunks + chunk], me
            )

        def add_rows(block_id, chunk, slots):
            def body(i, carry):
                span = rows_at(chunk * size + i * block, block)
                value = part[span, :]
                for slot in slots:
                    value = value + held[slot, span, :].astype(jnp.float32)
                sent[block_id, span, :] = value.astype(jnp.bfloat16)
                return carry

            lax.fori_loop(0, size // block, body, 0)

        def relay(block_id, rightward, inner):
            product(block_id)
            for chunk in range(chunks):

                @pl.when(inner)
                def _():
                    arrival(block_id, chunk).wait_recv()
                    add_rows(block_id, chunk, [block_id])

                @pl.when(jnp.logical_not(inner))
                def _():
                    add_rows(block_id, chunk, [])

                hop(block_id, chunk, rightward).start()

        def step_of(step, carry):
            @pl.when((step >= me + 1) & (me < n - 1))
            def _():
                relay(me + n - step, True, me > 0)

            @pl.when((step >= n - me) & (me > 0))
            def _():
                relay(me - n + step, False, me < n - 1)

            if extra is not None:

                @pl.when(step < n - 1)
                def _():
                    extra_gather.forward(step)

            if other_gain is not None:
                pl.when(step == 1)(make_grads)
                pl.when(step == 2)(pair_up)

            return carry

        lax.fori_loop(1, n, step_of, 0)
        product(me)
        if has_gain:
            gain_sum[...] = jnp.zeros_like(gain_sum)
        for chunk in range(chunks):

            @pl.when(me > 0)
            def _():
                arrival(me, chunk).wait_recv()

            @pl.when(me < n - 1)
            def _():
                arrival(n, chunk).wait_recv()

            def body(i, carry):
                span = rows_at(chunk * size + i * block, block)
                total = part[span, :]
                zero = jnp.zeros_like(total)
                total = total + jnp.where(me > 0, held[me, span, :].astype(jnp.float32), zero)
                total = total + jnp.where(
                    me < n - 1, held[n, span, :].astype(jnp.float32), zero
                )
                gain = gain_ref[...]
                if epilogue == "residual":
                    outs[0][span, :] = (own[0][span, :] + total).astype(jnp.bfloat16)
                elif epilogue == "forward":
                    value = own[0][span, :] + total
                    outs[0][span, :] = value
                    inverse = lax.rsqrt(
                        jnp.mean(value * value, axis=1, keepdims=True) + norm_eps
                    )
                    normed[span, :] = (value * inverse * gain).astype(jnp.bfloat16)
                else:
                    value = own[0][span, :]
                    inverse = lax.rsqrt(
                        jnp.mean(value * value, axis=1, keepdims=True) + norm_eps
                    )
                    unit = value * inverse
                    scaled = total * gain
                    inner = jnp.mean(scaled * unit, axis=1, keepdims=True)
                    result = own[1][span, :] + inverse * (scaled - unit * inner)
                    outs[0][span, :] = result
                    gain_sum[...] += jnp.sum(
                        (total * unit).reshape(block // 8, 8, width), axis=0
                    )
                    if has_norm:
                        normed[span, :] = result.astype(jnp.bfloat16)
                return carry

            lax.fori_loop(0, size // block, body, 0)
        if extra is not None:
            extra_gather.finish()
            extra_local.wait()
        if other_gain is not None:
            local = width // (n * n_dp)
            for source, rows_of in ((gain_sum, pl.ds(0, 8)), (other_ref, pl.ds(8, 8))):
                for d in range(n_dp):
                    for m in range(n):
                        cols = pl.ds(tile_of(d, m, n, local) * 128, 128)
                        table[m, d, rows_of, :] = source[:, cols]
            copies = exchange.swap("mp", lambda peer: table.at[peer], first)
            first[me] = table[me]
            for copy in copies:
                copy.wait()
            total = first[0]
            for m in range(1, n):
                total = total + first[m]
            middle[...] = total
            copies = exchange.swap("dp", lambda peer: middle.at[peer], second)
            second[dp] = middle[dp]
            land()
            for copy in copies:
                copy.wait()
            total = second[0]
            for d in range(1, n_dp):
                total = total + second[d]
            outs[1][...] = total

        def sends(step, carry):
            for chunk in range(chunks):

                @pl.when((step >= me + 1) & (me < n - 1))
                def _():
                    hop(me + n - step, chunk, True).wait_send()

                @pl.when((step >= n - me) & (me > 0))
                def _():
                    hop(me - n + step, chunk, False).wait_send()

            return carry

        lax.fori_loop(1, n, sends, 0)

    out_type = jnp.bfloat16 if epilogue == "residual" else jnp.float32
    out_shape = [jax.ShapeDtypeStruct((rows, width), out_type)]
    out_specs = [VMEM]
    if has_gain:
        out_shape.append(
            jax.ShapeDtypeStruct((8, width) if other_gain is None else (16, 128), jnp.float32)
        )
        out_specs.append(VMEM)
    if other_gain is not None:
        share = width // n_dp
        grad_width = sum(pieces) + grad_right.shape[1]
        out_shape.append(jax.ShapeDtypeStruct((share, grad_width), jnp.float32))
        out_specs.append(VMEM)
    scratch = [
        pltpu.VMEM((width, depth), jnp.bfloat16),
        pltpu.VMEM((n + 1, rows, width), jnp.bfloat16),
        pltpu.VMEM((n, rows, width), jnp.bfloat16),
        pltpu.VMEM((rows, width), jnp.float32),
    ]
    if heads is not None:
        scratch.append(pltpu.VMEM((width, rhs_start), jnp.bfloat16))
    if has_norm:
        out_shape.append(jax.ShapeDtypeStruct((rows, width), jnp.bfloat16))
        out_specs.append(VMEM)
    scratch += [
        pltpu.SemaphoreType.DMA,
        pltpu.SemaphoreType.DMA((n * chunks,)),
        pltpu.SemaphoreType.DMA(((n + 1) * chunks,)),
    ]
    head_args = []
    if heads is not None:
        scratch.append(pltpu.SemaphoreType.DMA)
        head_args = list(heads)
        out_shape += [jax.ShapeDtypeStruct((total_rows, inner_width), jnp.bfloat16)] * 4
        out_specs += [VMEM] * 4
    extra_args = []
    if extra is not None:
        out_shape.append(jax.ShapeDtypeStruct((total_rows, width), jnp.bfloat16))
        out_specs.append(ANY)
        scratch += [pltpu.SemaphoreType.DMA] + gather_sems(n, 1)
        extra_args = [extra]
    if other_gain is not None:
        head_args += [other_gain, *grad_lefts, grad_right]
        scratch += [
            pltpu.VMEM((8, width), jnp.float32),
            pltpu.VMEM((n, n_dp, 16, 128), jnp.float32),
            pltpu.VMEM((n, n_dp, 16, 128), jnp.float32),
            pltpu.VMEM((n_dp, 16, 128), jnp.float32),
            pltpu.VMEM((n_dp, 16, 128), jnp.float32),
        ] + exchange_sems(n_dp, n)
        chips = n_dp // 2
        scratch.append(pltpu.VMEM((width, grad_width), jnp.bfloat16))
        scratch.append(pltpu.VMEM((chips, share, grad_width), jnp.bfloat16))
        scratch.append(pltpu.VMEM((chips - 1, share, grad_width), jnp.bfloat16))
        scratch += [pltpu.SemaphoreType.DMA((chips,))] * 2
        scratch += [pltpu.SemaphoreType.DMA((chips - 1,))] * 2
    flops = 2 * total_rows * depth * width
    return pl.pallas_call(
        kernel,
        out_shape=out_shape,
        in_specs=[VMEM] * count
        + [ANY]
        + [VMEM] * (1 + len(own_rows) + len(head_args))
        + [ANY] * len(extra_args),
        out_specs=out_specs,
        scratch_shapes=scratch,
        compiler_params=pltpu.CompilerParams(
            collective_id=collective_id, has_side_effects=True, vmem_limit_bytes=VMEM_LIMIT
        ),
        cost_estimate=pl.CostEstimate(
            flops=flops, bytes_accessed=300_000_000, transcendentals=0
        ),
        name="scatter_" + epilogue,
    )(*lhs, rhs, gains_row, *own_rows, *head_args, *extra_args)


def feed_forward(n, normed, branch_grad, weights, own_rows, gains_row, collective_id, chunks=1, hops=4):
    rows, width = normed.shape
    total_rows = n * rows
    hidden = weights.shape[1] // 3
    size = rows // chunks
    part_size = size // hops
    count = chunks * hops
    tile = min(1024, hidden)
    block = min(32, part_size)

    def kernel(
        normed_ref,
        branch_hbm,
        weights_hbm,
        second_ref,
        base_ref,
        gain_ref,
        result_ref,
        rounded_ref,
        gain_sum,
        whole_hbm,
        act_hbm,
        gate_hbm,
        up_hbm,
        weight_ref,
        branch_ref,
        all_ref,
        held,
        sent,
        own_part,
        act_ref,
        gate_ref,
        up_ref,
        load_sems,
        stage_sems,
        send_sems,
        recv_sems,
        *gather_refs,
    ):
        me = lax.axis_index("mp")
        middle = (me > 0) & (me < n - 1)
        loads = [
            pltpu.make_async_copy(weights_hbm, weight_ref, load_sems.at[0]),
            pltpu.make_async_copy(branch_hbm, branch_ref, load_sems.at[1]),
        ]
        for load in loads:
            load.start()
        gather = LineGather(n, rows, chunks, normed_ref, all_ref, gather_refs)
        neighbour_barrier(n)
        for chunk in range(chunks):
            gather.send_own(chunk)
        all_ref[rows_at(me * rows, rows), :] = normed_ref[...]
        for load in loads:
            load.wait()

        def hop(block_id, chunk, rightward):
            peer = me + 1 if rightward else me - 1
            slot = block_id if rightward else jnp.where(block_id == peer, n, block_id)
            return remote(
                sent.at[block_id, pl.ds(chunk * part_size, part_size)],
                held.at[slot, pl.ds(chunk * part_size, part_size)],
                send_sems.at[block_id * count + chunk],
                recv_sems.at[slot * count + chunk],
                peer,
            )

        def arrival(slot, chunk):
            ref = held.at[slot, pl.ds(chunk * part_size, part_size)]
            return remote(
                ref, ref, send_sems.at[chunk], recv_sems.at[slot * count + chunk], me
            )

        def stages(block_id, chunk):
            span = rows_at(block_id * rows + chunk * size, size)
            return [
                pltpu.make_async_copy(ref.at[chunk], hbm.at[span], stage_sems.at[chunk * 3 + k])
                for k, (ref, hbm) in enumerate(
                    ((act_ref, act_hbm), (gate_ref, gate_hbm), (up_ref, up_hbm))
                )
            ]

        def compute(block_id, chunk, first):
            span = rows_at(block_id * rows + chunk * size, size)

            @pl.when(jnp.logical_not(first))
            def _():
                for stage in stages(block_id, chunk):
                    stage.wait()

            def units(ct, carry):
                cols = rows_at(ct * tile, tile)
                row_vals, branch = all_ref[span, :], branch_ref[span, :]
                gate = dot(row_vals, weight_ref[:, cols])
                up = dot(row_vals, weight_ref[:, rows_at(hidden + ct * tile, tile)])
                act_grad = dot(branch, weight_ref[:, rows_at(2 * hidden + ct * tile, tile)])
                sigma = 1.0 / (1.0 + jnp.exp(-gate))
                silu = gate * sigma
                act_ref[chunk, :, cols] = (silu * up).astype(jnp.bfloat16)
                gate_ref[chunk, :, cols] = (
                    act_grad * up * sigma * (1.0 + gate * (1.0 - sigma))
                ).astype(jnp.bfloat16)
                up_ref[chunk, :, cols] = (act_grad * silu).astype(jnp.bfloat16)
                return carry

            lax.fori_loop(0, hidden // tile, units, 0)
            for stage in stages(block_id, chunk):
                stage.start()

            def columns(ct, carry):
                cols = rows_at(ct * tile, tile)
                total = dot_t(gate_ref[chunk], weight_ref[cols, pl.ds(0, hidden)])
                total += dot_t(up_ref[chunk], weight_ref[cols, pl.ds(hidden, hidden)])

                @pl.when(block_id == me)
                def _():
                    own_part[pl.ds(chunk * size, size), cols] = total

                @pl.when(block_id != me)
                def _():
                    sent[block_id, pl.ds(chunk * size, size), cols] = total.astype(jnp.bfloat16)

                return carry

            lax.fori_loop(0, width // tile, columns, 0)

            @pl.when((me == 0) & (block_id > me))
            def _():
                for k in range(hops):
                    hop(block_id, chunk * hops + k, True).start()

            @pl.when((me == n - 1) & (block_id < me))
            def _():
                for k in range(hops):
                    hop(block_id, chunk * hops + k, False).start()

        def step_of(step, carry):
            def side_of(side, carry):
                block_id = me + (1 - 2 * side) * step
                valid = (block_id >= 0) & (block_id < n) & ((step > 0) | (side == 0))
                for chunk in range(chunks):

                    @pl.when(middle & (step > 0) & (step < n - 1) & (side == 1))
                    def _():
                        gather.forward_chunk(step + 1, chunk, step < n - 2)

                    @pl.when(jnp.logical_not(middle) & valid & (step > 0))
                    def _():
                        gather.forward_chunk(step, chunk, step < n - 1)

                    @pl.when(valid)
                    def _():
                        compute(block_id, chunk, step == 0)

                    @pl.when(middle & (step == 0) & (side == 0))
                    def _():
                        gather.forward_chunk(1, chunk, 1 < n - 1)

                return carry

            return lax.fori_loop(0, 2, side_of, carry)

        lax.fori_loop(0, n, step_of, 0)
        whole_copy = pltpu.make_async_copy(all_ref, whole_hbm, load_sems.at[0])
        whole_copy.start()

        def add_rows(block_id, chunk):
            def body(i, carry):
                span = rows_at(chunk * part_size + i * block, block)
                value = sent[block_id, span, :].astype(jnp.float32)
                value = value + held[block_id, span, :].astype(jnp.float32)
                sent[block_id, span, :] = value.astype(jnp.bfloat16)
                return carry

            lax.fori_loop(0, part_size // block, body, 0)

        def relay_of(step, carry):
            for chunk in range(count):
                for rightward, block_id, has in (
                    (True, step, (me > 0) & (step > me)),
                    (False, n - 1 - step, (me < n - 1) & (n - 1 - step < me)),
                ):

                    @pl.when(has)
                    def _():
                        arrival(block_id, chunk).wait_recv()
                        add_rows(block_id, chunk)
                        hop(block_id, chunk, rightward).start()

            return carry

        lax.fori_loop(1, n, relay_of, 0)
        gain_sum[...] = jnp.zeros_like(gain_sum)
        for chunk in range(count):

            @pl.when(me > 0)
            def _():
                arrival(me, chunk).wait_recv()

            @pl.when(me < n - 1)
            def _():
                arrival(n, chunk).wait_recv()

            def body(i, carry):
                span = rows_at(chunk * part_size + i * block, block)
                total = own_part[span, :]
                zero = jnp.zeros_like(total)
                total = total + jnp.where(me > 0, held[me, span, :].astype(jnp.float32), zero)
                total = total + jnp.where(
                    me < n - 1, held[n, span, :].astype(jnp.float32), zero
                )
                value = second_ref[span, :]
                inverse = lax.rsqrt(jnp.mean(value * value, axis=1, keepdims=True) + norm_eps)
                unit = value * inverse
                scaled = total * gain_ref[...]
                inner = jnp.mean(scaled * unit, axis=1, keepdims=True)
                result = base_ref[span, :] + inverse * (scaled - unit * inner)
                result_ref[span, :] = result
                rounded_ref[span, :] = result.astype(jnp.bfloat16)
                gain_sum[...] += jnp.sum((total * unit).reshape(block // 8, 8, width), axis=0)
                return carry

            lax.fori_loop(0, part_size // block, body, 0)
        gather.finish(False)
        for chunk in range(chunks):
            for stage in stages(me, chunk):
                stage.wait()

        def sends(block_id, carry):
            for chunk in range(count):

                @pl.when((block_id > me) & (me < n - 1))
                def _():
                    hop(block_id, chunk, True).wait_send()

                @pl.when((block_id < me) & (me > 0))
                def _():
                    hop(block_id, chunk, False).wait_send()

            return carry

        lax.fori_loop(0, n, sends, 0)
        whole_copy.wait()

    half = jnp.bfloat16
    return pl.pallas_call(
        kernel,
        out_shape=[
            jax.ShapeDtypeStruct((rows, width), jnp.float32),
            jax.ShapeDtypeStruct((rows, width), half),
            jax.ShapeDtypeStruct((8, width), jnp.float32),
            jax.ShapeDtypeStruct((total_rows, width), half),
        ]
        + [jax.ShapeDtypeStruct((total_rows, hidden), half)] * 3,
        in_specs=[VMEM, ANY, ANY, VMEM, VMEM, VMEM],
        out_specs=[VMEM] * 3 + [ANY] * 4,
        scratch_shapes=[
            pltpu.VMEM((width, 3 * hidden), half),
            pltpu.VMEM((total_rows, width), half),
            pltpu.VMEM((total_rows, width), half),
            pltpu.VMEM((n + 1, rows, width), half),
            pltpu.VMEM((n, rows, width), half),
            pltpu.VMEM((rows, width), jnp.float32),
        ]
        + [pltpu.VMEM((chunks, size, hidden), half)] * 3
        + [
            pltpu.SemaphoreType.DMA((2,)),
            pltpu.SemaphoreType.DMA((chunks * 3,)),
            pltpu.SemaphoreType.DMA((n * count,)),
            pltpu.SemaphoreType.DMA(((n + 1) * count,)),
        ]
        + gather_sems(n, chunks),
        compiler_params=pltpu.CompilerParams(
            collective_id=collective_id, has_side_effects=True, vmem_limit_bytes=VMEM_LIMIT
        ),
        cost_estimate=pl.CostEstimate(
            flops=10 * total_rows * width * hidden, bytes_accessed=300_000_000, transcendentals=0
        ),
        name="feed_forward",
    )(normed, branch_grad, weights, *own_rows, gains_row)


def attention_backward(queries, keys, values, mixed_grad, cosine, sine, key_mask):
    total_rows, inner_width = queries.shape
    block = min(256, total_rows)

    def kernel(q_ref, k_ref, v_ref, do_ref, cos_ref, sin_ref, mask_ref, dq_out, dk_out, dv_out, dk_ref, dv_ref):
        dk_ref[...] = jnp.zeros_like(dk_ref)
        dv_ref[...] = jnp.zeros_like(dv_ref)
        for i in range(total_rows // block):
            span = pl.ds(i * block, block)
            upto = (i + 1) * block
            shape = (upto, block)
            key_pos = lax.broadcasted_iota(jnp.int32, shape, 0)
            query_pos = i * block + lax.broadcasted_iota(jnp.int32, shape, 1)
            allowed = jnp.where(key_pos <= query_pos, mask_ref[:upto, :], 0.0)
            query, grad = q_ref[span, :], do_ref[span, :]
            key = k_ref[:upto, :]
            prob = probability(dot_t(key, query)) * allowed
            prob_grad = dot_t(v_ref[:upto, :], grad)
            dv_ref[:upto, :] += jnp.dot(
                prob.astype(jnp.bfloat16), grad, preferred_element_type=jnp.float32
            )
            score_grad = (prob_grad * prob * (1.0 - prob) * (1.0 / math.sqrt(HDIM))).astype(
                jnp.bfloat16
            )
            dk_ref[:upto, :] += jnp.dot(score_grad, query, preferred_element_type=jnp.float32)
            dq = t_dot(score_grad, key)
            dq_out[span, :] = rotated(
                dq, cos_ref[span, :], sin_ref[span, :], True
            ).astype(jnp.bfloat16)
        dk_out[...] = rotated(dk_ref[...], cos_ref[...], sin_ref[...], True).astype(jnp.bfloat16)
        dv_out[...] = dv_ref[...].astype(jnp.bfloat16)

    head = pl.BlockSpec((total_rows, HDIM), lambda h: (0, h))
    table = pl.BlockSpec((total_rows, HDIM), lambda h: (0, 0))
    return pl.pallas_call(
        kernel,
        grid=(inner_width // HDIM,),
        out_shape=[jax.ShapeDtypeStruct((total_rows, inner_width), jnp.bfloat16)] * 3,
        in_specs=[head] * 4 + [table] * 2 + [pl.BlockSpec((total_rows, 1), lambda h: (0, 0))],
        out_specs=[head] * 3,
        scratch_shapes=[pltpu.VMEM((total_rows, HDIM), jnp.float32)] * 2,
        compiler_params=pltpu.CompilerParams(vmem_limit_bytes=VMEM_LIMIT),
        cost_estimate=pl.CostEstimate(
            flops=8 * total_rows * total_rows * inner_width,
            bytes_accessed=14 * total_rows * inner_width,
            transcendentals=0,
        ),
        name="attention_backward",
    )(queries, keys, values, mixed_grad, cosine, sine, key_mask)


def updated(weight, moment, average, gradient, rate):
    moment_new = momentum_decay * moment + (1.0 - momentum_decay) * gradient
    weight_new = weight - rate * (
        (1.0 - momentum_decay) * gradient + momentum_decay * moment_new
    )
    average_new = average_decay * average + (1.0 - average_decay) * weight_new
    return weight_new, moment_new, average_new


def store_update(ins, gradient, outs, rate):
    weight, moment, average = updated(*[ref[...] for ref in ins], gradient, rate)
    outs[0][...] = weight
    outs[1][...] = moment
    outs[2][...] = average
    outs[3][...] = weight.astype(jnp.bfloat16)


def update_call(body, grid, arrays, spec, total, total_spec, scratch, name):
    kinds = [jnp.float32] * 3 + [jnp.bfloat16]
    shape = arrays[0].shape
    return pl.pallas_call(
        body,
        grid=grid,
        out_shape=[jax.ShapeDtypeStruct(shape, kind) for kind in kinds],
        in_specs=[spec] * 3 + [total_spec],
        out_specs=[spec] * 4,
        scratch_shapes=scratch,
        compiler_params=pltpu.CompilerParams(vmem_limit_bytes=VMEM_LIMIT),
        cost_estimate=pl.CostEstimate(
            flops=10 * arrays[0].size, bytes_accessed=28 * arrays[0].size, transcendentals=0
        ),
        name=name,
    )(*arrays, total)


def update_flipped(arrays, total, start, rate, name):
    high, wide = arrays[0].shape
    step = min(256, high)

    def body(w, m, a, g, *outs):
        store_update((w, m, a), g[...].astype(jnp.float32).T, outs, rate)

    return update_call(
        body,
        (high // step,),
        arrays,
        pl.BlockSpec((step, wide), lambda i: (i, 0)),
        total,
        pl.BlockSpec((wide, step), lambda i: (0, start // step + i)),
        [],
        name,
    )


def update_parts(arrays, total, rate, name):
    high, parts, wide = arrays[0].shape

    def body(w, m, a, g, *outs):
        store_update((w, m, a), g[...].astype(jnp.float32), outs, rate)

    turns = 2
    outs = update_call(
        body,
        (parts, turns),
        [x.transpose(1, 0, 2) for x in arrays],
        pl.BlockSpec((None, high // turns, wide), lambda i, j: (i, j, 0)),
        total,
        pl.BlockSpec((high // turns, wide), lambda i, j: (j, i)),
        [],
        name,
    )
    return [x.transpose(1, 0, 2) for x in outs]


def update_pairs(arrays, total, rate, name):
    high, parts, wide = arrays[0].shape
    tiles = wide // 128
    step = min(16, high)
    stride = tiles * parts

    def body(w, m, a, g, *rest):
        outs, spread = rest[:4], rest[4]
        for part in range(parts):
            for tile in range(tiles):
                cols = pl.ds(part * wide + tile * 128, 128)
                spread[pl.ds(tile * parts + part, step, stride=stride), :] = g[:, cols].astype(
                    jnp.float32
                )
        store_update((w, m, a), spread[...], outs, rate)

    outs = update_call(
        body,
        (high // step,),
        [flat_pairs(x) for x in arrays],
        pl.BlockSpec((step * stride, 128), lambda i: (i, 0)),
        total,
        pl.BlockSpec((step, parts * wide), lambda i: (i, 0)),
        [pltpu.VMEM((step * stride, 128), jnp.float32)],
        name,
    )
    return [
        x.reshape(high, tiles, parts, 128).transpose(0, 2, 1, 3).reshape(high, parts, wide)
        for x in outs
    ]


def weight_gradients(lefts, rights, tile=512):
    count = len(lefts)
    rows, depth = lefts[0].shape
    wide = rights[0].shape[1]
    steps = wide // tile
    distinct = []
    for left in lefts:
        if all(left is not other for other in distinct):
            distinct.append(left)
    which = [next(k for k, d in enumerate(distinct) if d is left) for left in lefts]

    def kernel(*refs):
        left_refs, right_refs = refs[: len(distinct)], refs[len(distinct) : -1]
        out_ref = refs[-1]
        pair = pl.program_id(0)
        for k in range(count):

            @pl.when(pair == k)
            def _():
                out_ref[...] = t_dot(left_refs[which[k]][...], right_refs[k][...]).astype(
                    jnp.bfloat16
                )

    def right_map(k):
        return lambda pair, i: (0, jnp.where(pair == k, i, jnp.where(pair < k, 0, steps - 1)))

    return pl.pallas_call(
        kernel,
        grid=(count, steps),
        out_shape=jax.ShapeDtypeStruct((depth, count * wide), jnp.bfloat16),
        in_specs=[VMEM] * len(distinct)
        + [pl.BlockSpec((rows, tile), right_map(k)) for k in range(count)],
        out_specs=pl.BlockSpec((depth, tile), lambda pair, i: (0, pair * steps + i)),
        compiler_params=pltpu.CompilerParams(vmem_limit_bytes=VMEM_LIMIT),
        cost_estimate=pl.CostEstimate(
            flops=2 * rows * depth * count * wide,
            bytes_accessed=2 * (len(distinct) * rows * depth + count * wide * (rows + depth)),
            transcendentals=0,
        ),
        name="weight_gradients",
    )(*distinct, *rights)


def rope_tables(length, half_dim):
    positions = np.arange(length, dtype=np.float32)[:, None]
    inverse_freq = np.power(
        np.float32(rope_base), -np.arange(half_dim, dtype=np.float32) / np.float32(half_dim)
    )
    angles = positions * inverse_freq[None, :]
    cosine, sine = np.cos(angles), np.sin(angles)
    return np.concatenate([cosine, cosine], axis=1), np.concatenate([-sine, sine], axis=1)


def per_device(
    n_dp,
    n_mp,
    tokens,
    cotangent,
    valid_counts,
    w_qkv,
    w_out,
    w_gu,
    w_down,
    gains,
    mom_qkv,
    mom_out,
    mom_gu,
    mom_down,
    mom_gains,
    avg_qkv,
    avg_out,
    avg_gu,
    avg_down,
    avg_gains,
):
    half = jnp.bfloat16
    row_count, width = tokens.shape
    owned, _, local_width = w_qkv.shape
    hidden = w_gu.shape[2]
    valid_len = valid_counts[0]

    attn_part = jnp.concatenate(
        [w_qkv.reshape(owned, 3 * local_width), w_out.T], axis=1
    ).astype(half)
    attn_w = lax.all_gather(attn_part, "dp", axis=0, tiled=True)
    row_ids = lax.axis_index("mp") * row_count + jnp.arange(row_count, dtype=jnp.int32)
    live_rows = (row_ids < valid_len).astype(jnp.float32)[:, None]
    key_mask = (jnp.arange(SEQ, dtype=jnp.int32) < valid_len).astype(jnp.float32)
    ffn_part, tokens_in = lax.optimization_barrier((round_shares(w_gu, w_down), tokens))
    h_first, gain_all, out_grad, own_branch = gather_first(
        n_dp, n_mp, tokens_in, gains, cotangent, live_rows, 1
    )
    ffn_w = lax.all_gather(ffn_part, "dp", axis=0, tiled=True)
    out_wt = attn_w[:, 3 * local_width :]
    xin = tokens.astype(jnp.float32)
    cosine, sine = (jnp.asarray(x, jnp.float32) for x in rope_tables(SEQ, HDIM // 2))

    second, normed_second, queries, keys, values, mixed, branch_grad = scatter_rows(
        n_mp,
        [h_first],
        attn_w,
        3 * local_width,
        [xin],
        "forward",
        gain_all[1:2],
        2,
        heads=(cosine, sine, key_mask[None, :]),
        extra=own_branch,
    )

    second_grad, own_grad, gain_two, h_second, act, gate_grad, up_grad = feed_forward(
        n_mp, normed_second, branch_grad, ffn_w, [second, out_grad], gain_all[1:2], 3
    )
    grad_ffn = weight_gradients(
        [h_second, h_second, branch_grad], [gate_grad, up_grad, act]
    )
    grad_ffn, own_grad = lax.optimization_barrier((grad_ffn, own_grad))
    sum_ffn = lax.psum_scatter(grad_ffn, "dp", scatter_dimension=0, tiled=True)
    block_out, attn_grad = scatter_rows(
        n_mp,
        [act],
        ffn_w,
        2 * hidden,
        [second],
        "residual",
        gain_all[1:2],
        7,
        extra=own_grad,
    )

    mixed_grad = dot(attn_grad, out_wt).astype(half)
    joined_grad = attention_backward(
        queries, keys, values, mixed_grad, cosine, sine, key_mask[:, None]
    )
    input_grad, gain_tile, sum_attn = scatter_rows(
        n_mp,
        list(joined_grad),
        attn_w,
        0,
        [xin, second_grad],
        "last",
        gain_all[0:1],
        4,
        other_gain=gain_two,
        grad_lefts=[h_first, attn_grad],
        grad_right=mixed,
        n_dp=n_dp,
    )

    total_rows = SEQ * n_dp
    matrix_rate = step_rate / math.sqrt(total_rows)
    scale_rate = gain_rate / math.sqrt(total_rows)
    local = gains.shape[1]
    place = lax.rem((lax.axis_index("dp") * n_mp + lax.axis_index("mp")) * local, 128)
    sum_gains = lax.dynamic_slice(gain_tile.reshape(2, 8, 128).sum(axis=1), (0, place), (2, local))
    new_gu, next_mom_gu, next_avg_gu, copy_gu = update_pairs(
        [w_gu, mom_gu, avg_gu], sum_ffn, matrix_rate, "update_gu"
    )
    new_down, next_mom_down, next_avg_down, copy_down = update_flipped(
        [w_down, mom_down, avg_down], sum_ffn, 2 * hidden, matrix_rate, "update_down"
    )
    new_qkv, next_mom_qkv, next_avg_qkv, copy_qkv = update_parts(
        [w_qkv, mom_qkv, avg_qkv], sum_attn, matrix_rate, "update_qkv"
    )
    new_out, next_mom_out, next_avg_out, copy_out = update_flipped(
        [w_out, mom_out, avg_out], sum_attn, 3 * local_width, matrix_rate, "update_out"
    )
    new_gains, next_mom_gains, next_avg_gains = updated(
        gains, mom_gains, avg_gains, sum_gains, scale_rate
    )
    return (
        block_out,
        input_grad,
        new_qkv,
        new_out,
        new_gu,
        new_down,
        new_gains,
        next_mom_qkv,
        next_mom_out,
        next_mom_gu,
        next_mom_down,
        next_mom_gains,
        next_avg_qkv,
        next_avg_out,
        next_avg_gu,
        next_avg_down,
        next_avg_gains,
        copy_qkv,
        copy_out,
        copy_gu,
        copy_down,
    )


def solution(mesh):
    rows, one = P(("dp", "mp"), None), P("dp")
    tall, wide, spread = P("dp", None, "mp"), P("mp", "dp"), P(None, ("dp", "mp"))
    weights = (tall, wide, tall, wide)
    return jax.shard_map(
        functools.partial(per_device, mesh.shape["dp"], mesh.shape["mp"]),
        mesh=mesh,
        in_specs=(rows, rows, one, *((*weights, spread) * 3)),
        out_specs=(rows, rows, *((*weights, spread) * 3), *weights),
        check_vma=False,
    )
```

```python
import functools
import math

import jax
import jax.numpy as jnp
from jax import lax
from jax.experimental import pallas as pl
from jax.experimental.pallas import tpu as pltpu
import numpy as np
from jax.sharding import PartitionSpec as P

HDIM = 128
SEQ = 1024
MESH = pl.DeviceIdType.MESH
ANY = pl.BlockSpec(memory_space=pl.ANY)
VMEM = pl.BlockSpec(memory_space=pltpu.VMEM)
VMEM_LIMIT = 60 * 1024 * 1024

norm_eps = 1e-05
rope_base = 10000.0
momentum_decay = 0.9
average_decay = 0.9
step_rate = 0.05
gain_rate = 0.5


def rows_at(start, size):
    return pl.ds(pl.multiple_of(start, size), size)


def remote(src, dst, send_sem, recv_sem, peer):
    return pltpu.make_async_remote_copy(
        src_ref=src,
        dst_ref=dst,
        send_sem=send_sem,
        recv_sem=recv_sem,
        device_id={"mp": peer},
        device_id_type=MESH,
    )


def neighbour_barrier(n):
    me = lax.axis_index("mp")
    barrier = pltpu.get_barrier_semaphore()

    @pl.when(me > 0)
    def _():
        pl.semaphore_signal(barrier, inc=1, device_id={"mp": me - 1}, device_id_type=MESH)

    @pl.when(me < n - 1)
    def _():
        pl.semaphore_signal(barrier, inc=1, device_id={"mp": me + 1}, device_id_type=MESH)

    pl.semaphore_wait(barrier, jnp.where(me > 0, 1, 0) + jnp.where(me < n - 1, 1, 0))


class LineGather:
    def __init__(self, n, rows, chunks, own, whole, sems):
        self.n, self.rows, self.chunks = n, rows, chunks
        self.size = rows // chunks
        self.own, self.whole, self.sems = own, whole, sems
        self.me = lax.axis_index("mp")

    def at(self, block, chunk):
        return self.whole.at[rows_at(block * self.rows + chunk * self.size, self.size)]

    def copies(self, step, chunk, first):
        me, n = self.me, self.n
        send_r, recv_r, send_l, recv_l = self.sems
        out = []
        for block, peer, has, send, recv in (
            (me - step, me + 1, (me - step >= 0) & (me < n - 1), send_r, recv_r),
            (me + step, me - 1, (me + step <= n - 1) & (me > 0), send_l, recv_l),
        ):
            src = (
                self.own.at[pl.ds(chunk * self.size, self.size)]
                if first
                else self.at(block, chunk)
            )
            index = step * self.chunks + chunk
            out.append(
                (has, remote(src, self.at(block, chunk), send.at[index], recv.at[index], peer))
            )
        return out

    def arrivals(self, step, chunk):
        me, n = self.me, self.n
        send_r, recv_r, send_l, recv_l = self.sems
        index = step * self.chunks + chunk
        out = []
        for block, has, send, recv in (
            (me - 1 - step, me - 1 - step >= 0, send_r, recv_r),
            (me + 1 + step, me + 1 + step <= n - 1, send_l, recv_l),
        ):
            ref = self.at(block, chunk)
            out.append((has, remote(ref, ref, send.at[index], recv.at[index], me)))
        return out

    def send_own(self, chunk):
        for has, copy in self.copies(0, chunk, True):
            pl.when(has)(copy.start)

    def forward(self, step):
        for chunk in range(self.chunks):
            self.forward_chunk(step, chunk, True)

    def forward_chunk(self, step, chunk, more):
        for (got, arrival), (has, copy) in zip(
            self.arrivals(step - 1, chunk), self.copies(step, chunk, False)
        ):
            pl.when(got)(arrival.wait_recv)
            pl.when(has & more)(copy.start)

    def finish(self, arrivals=True):
        for chunk in range(self.chunks if arrivals else 0):
            for got, arrival in self.arrivals(self.n - 2, chunk):
                pl.when(got)(arrival.wait_recv)
        for chunk in range(self.chunks):
            for has, copy in self.copies(0, chunk, True):
                pl.when(has)(copy.wait_send)

        def waits(step, carry):
            for chunk in range(self.chunks):
                for has, copy in self.copies(step, chunk, False):
                    pl.when(has)(copy.wait_send)
            return carry

        lax.fori_loop(1, self.n - 1, waits, 0)

    def forward_all(self):
        def step_of(step, carry):
            self.forward(step)
            return carry

        lax.fori_loop(1, self.n - 1, step_of, 0)


def gather_sems(n, chunks):
    return [pltpu.SemaphoreType.DMA(((n - 1) * chunks,))] * 4


class Exchange:
    def __init__(self, n_dp, n_mp, sems):
        self.n_dp, self.n_mp = n_dp, n_mp
        self.s_mp, self.r_mp, self.s_dp, self.r_dp = sems
        self.dp, self.mp = lax.axis_index("dp"), lax.axis_index("mp")

    def barrier(self):
        barrier = pltpu.get_barrier_semaphore()
        for axis, here, count in (("mp", self.mp, self.n_mp), ("dp", self.dp, self.n_dp)):
            for k in range(1, count):
                pl.semaphore_signal(
                    barrier,
                    inc=1,
                    device_id={axis: lax.rem(here + k, count)},
                    device_id_type=MESH,
                )
        pl.semaphore_wait(barrier, self.n_mp + self.n_dp - 2)

    def swap(self, axis, source_of, target):
        if axis == "mp":
            here, count, send, recv = self.mp, self.n_mp, self.s_mp, self.r_mp
        else:
            here, count, send, recv = self.dp, self.n_dp, self.s_dp, self.r_dp
        copies = []
        for k in range(1, count):
            peer = lax.rem(here + k, count)
            copies.append(
                pltpu.make_async_remote_copy(
                    src_ref=source_of(peer),
                    dst_ref=target.at[here],
                    send_sem=send.at[k - 1],
                    recv_sem=recv.at[k - 1],
                    device_id={axis: peer},
                    device_id_type=MESH,
                )
            )
        for copy in copies:
            copy.start()
        return copies


def exchange_sems(n_dp, n_mp):
    return [pltpu.SemaphoreType.DMA((n_mp - 1,))] * 2 + [pltpu.SemaphoreType.DMA((n_dp - 1,))] * 2


def tile_of(dp, mp, n_mp, local):
    return (dp * n_mp + mp) * local // 128


def flat_pairs(x):
    high, parts, wide = x.shape
    return x.reshape(high, parts, wide // 128, 128).transpose(0, 2, 1, 3).reshape(-1, 128)


def round_shares(w_gu, w_down):
    high, parts, hidden = w_gu.shape
    tiles = hidden // 128
    step = 128
    turn = min(256, hidden)

    def kernel(gu_ref, down_ref, out_ref):
        for part in range(parts):
            for tile in range(tiles):
                cols = pl.ds(part * hidden + tile * 128, 128)
                out_ref[:, cols] = gu_ref[
                    pl.ds(tile * parts + part, step, stride=tiles * parts), :
                ].astype(jnp.bfloat16)
        for i in range(hidden // turn):
            piece = down_ref[pl.ds(i * turn, turn), :]
            out_ref[:, pl.ds(parts * hidden + i * turn, turn)] = piece.T.astype(jnp.bfloat16)

    return pl.pallas_call(
        kernel,
        grid=(high // step,),
        out_shape=jax.ShapeDtypeStruct((high, (parts + 1) * hidden), jnp.bfloat16),
        in_specs=[
            pl.BlockSpec((step * tiles * parts, 128), lambda i: (i, 0)),
            pl.BlockSpec((hidden, step), lambda i: (0, i)),
        ],
        out_specs=pl.BlockSpec((step, (parts + 1) * hidden), lambda i: (i, 0)),
        compiler_params=pltpu.CompilerParams(vmem_limit_bytes=VMEM_LIMIT),
        cost_estimate=pl.CostEstimate(
            flops=0, bytes_accessed=6 * (w_gu.size + w_down.size), transcendentals=0
        ),
        name="round_shares",
    )(flat_pairs(w_gu), w_down)


def gather_first(n_dp, n_mp, own, gains, cotangent, live, collective_id, chunks=2):
    rows, width = own.shape
    local = gains.shape[1]
    lanes = jnp.arange(128, dtype=jnp.int32) // local
    place = lax.rem(lax.axis_index("mp"), 128 // local)
    if n_mp * local < 128:
        place = lax.rem(lax.axis_index("dp") * n_mp + lax.axis_index("mp"), 128 // local)
    tile = jnp.where(
        (lanes == place)[None, :], jnp.tile(gains, (1, 128 // local)), 0.0
    )
    tile = jnp.concatenate([tile, jnp.zeros((6, 128), jnp.float32)], axis=0)

    block = 64 if rows % 64 == 0 else rows

    def kernel(
        own_ref,
        tile_ref,
        cotangent_ref,
        live_ref,
        normed_ref,
        gain_ref,
        base_ref,
        branch_ref,
        all_ref,
        first,
        second,
        *sems,
    ):
        me = lax.axis_index("mp")
        exchange = Exchange(n_dp, n_mp, sems[:4])
        stream = LineGather(n_mp, rows, chunks, own_ref, all_ref, sems[4:])
        exchange.barrier()
        first[me] = tile_ref[...]
        copies = exchange.swap("mp", lambda peer: tile_ref, first)
        for chunk in range(chunks):
            stream.send_own(chunk)
        all_ref[rows_at(me * rows, rows), :] = own_ref[...]
        for copy in copies:
            copy.wait()
        dp = lax.axis_index("dp")
        second[dp] = first[...]
        copies = exchange.swap("dp", lambda peer: first, second)

        def enter(i, carry):
            span = rows_at(i * block, block)
            value = cotangent_ref[span, :].astype(jnp.float32) * live_ref[span, :]
            base_ref[span, :] = value
            branch_ref[span, :] = value.astype(jnp.bfloat16)
            return carry

        lax.fori_loop(0, rows // block, enter, 0)
        for copy in copies:
            copy.wait()
        gain_ref[...] = jnp.zeros_like(gain_ref)
        for d in range(n_dp):
            for m in range(n_mp):
                cols = pl.ds(tile_of(d, m, n_mp, local) * 128, 128)
                gain_ref[:, cols] += second[d, m]
        def norm(block_id):
            def body(i, carry):
                span = rows_at(block_id * rows + i * block, block)
                value = all_ref[span, :].astype(jnp.float32)
                inverse = lax.rsqrt(jnp.mean(value * value, axis=1, keepdims=True) + norm_eps)
                normed_ref[span, :] = (value * inverse * gain_ref[0:1, :]).astype(jnp.bfloat16)
                return carry

            lax.fori_loop(0, rows // block, body, 0)

        def step_of(step, carry):
            @pl.when(step > 0)
            def _():
                for chunk in range(chunks):
                    stream.forward_chunk(step, chunk, step < n_mp - 1)

            @pl.when(me + step < n_mp)
            def _():
                norm(me + step)

            @pl.when((me - step >= 0) & (step > 0))
            def _():
                norm(me - step)

            return carry

        lax.fori_loop(0, n_mp, step_of, 0)
        stream.finish(False)

    half = jnp.bfloat16
    return pl.pallas_call(
        kernel,
        out_shape=[
            jax.ShapeDtypeStruct((n_mp * rows, width), half),
            jax.ShapeDtypeStruct((8, width), jnp.float32),
            jax.ShapeDtypeStruct((rows, width), jnp.float32),
            jax.ShapeDtypeStruct((rows, width), half),
        ],
        in_specs=[VMEM] * 4,
        out_specs=[VMEM] * 4,
        scratch_shapes=[
            pltpu.VMEM((n_mp * rows, width), half),
            pltpu.VMEM((n_mp, 8, 128), jnp.float32),
            pltpu.VMEM((n_dp, n_mp, 8, 128), jnp.float32),
        ]
        + exchange_sems(n_dp, n_mp)
        + gather_sems(n_mp, chunks),
        compiler_params=pltpu.CompilerParams(
            collective_id=collective_id, has_side_effects=True, vmem_limit_bytes=VMEM_LIMIT
        ),
        cost_estimate=pl.CostEstimate(
            flops=0, bytes_accessed=200 * own.size * own.dtype.itemsize, transcendentals=0
        ),
        name="gather_first",
    )(own, tile, cotangent, live)


def dot_t(left, right):
    return lax.dot_general(
        left, right, (((1,), (1,)), ((), ())), preferred_element_type=jnp.float32
    )


def t_dot(left, right):
    return lax.dot_general(
        left, right, (((0,), (0,)), ((), ())), preferred_element_type=jnp.float32
    )


def dot(left, right):
    return jnp.dot(left, right, preferred_element_type=jnp.float32)


def probability(raw):
    return 1.0 / (1.0 + jnp.exp(math.log(SEQ) - raw * (1.0 / math.sqrt(HDIM))))


def rotated(values, cosine, sine, backward=False):
    turned = pltpu.roll(values, HDIM // 2, 1) * sine
    return values * cosine - turned if backward else values * cosine + turned


def scatter_rows(
    n,
    lhs,
    rhs,
    rhs_start,
    own_rows,
    epilogue,
    gains_row,
    collective_id,
    heads=None,
    extra=None,
    extra_right=None,
    other_gain=None,
    grad_lefts=None,
    grad_right=None,
    n_dp=1,
    chunks=2,
):
    total_rows = lhs[0].shape[0]
    rows = total_rows // n
    width = gains_row.shape[1]
    size = rows // chunks
    tile = 512
    has_norm, has_gain = epilogue in ("forward", "backward"), epilogue in ("backward", "last")
    count = len(lhs)
    block = 32
    if heads is not None:
        inner_width = rhs_start // 3
        head_count = inner_width // HDIM
        pieces = [inner_width]
    else:
        pieces = [a.shape[1] for a in lhs]
    depth = sum(pieces)
    if extra_right is not None:
        extra_width = extra_right[0].shape[1] - extra_right[1]

    def kernel(*refs):
        refs = list(refs)

        def take(k):
            return [refs.pop(0) for _ in range(k)]

        left_refs = take(count)
        (right_hbm,) = take(1)
        (gain_ref,) = take(1)
        own_hbm = take(len(own_rows))
        if heads is not None:
            cosine_ref, sine_ref, mask_ref = take(3)
        if other_gain is not None:
            (other_ref,) = take(1)
            grad_hbm = take(3)
        extra_ref = take(1)[0] if extra is not None else None
        extra_right_hbm = take(1)[0] if extra_right is not None else None
        outs = take(1 + has_gain)
        owned_ref = take(1)[0] if other_gain is not None else None
        normed = take(1)[0] if has_norm else None
        if heads is not None:
            query_ref, key_ref, value_ref, mixed_ref = take(4)
        extra_whole = take(1)[0] if extra is not None else None
        if extra_right is not None:
            (extra_out,) = take(1)
        right, held, sent, part = take(4)
        joined_ref = take(1)[0] if heads is not None else None
        right_sem, send_sems, recv_sems = take(3)
        own, own_sems = take(len(own_rows)), take(1)[0]
        own_loads = [
            pltpu.make_async_copy(hbm, ref, own_sems.at[k])
            for k, (hbm, ref) in enumerate(zip(own_hbm, own))
        ]
        me = lax.axis_index("mp")
        fetch = pltpu.make_async_copy(
            right_hbm.at[:, pl.ds(rhs_start, depth)], right, right_sem
        )
        fetch.start()
        if heads is not None:
            (joined_sem,) = take(1)
            fetch_joined = pltpu.make_async_copy(
                right_hbm.at[:, pl.ds(0, rhs_start)], joined_ref, joined_sem
            )
            fetch_joined.start()
        if extra is not None:
            (extra_sem,) = take(1)
            extra_sems = take(4)
            if extra_right is None:
                extra_gather = LineGather(n, rows, 1, extra_ref, extra_whole, extra_sems)
                extra_local = pltpu.make_async_copy(extra_ref, extra_gather.at(me, 0), extra_sem)
                extra_local.start()
            else:
                extra_all, extra_right_ref, extra_right_sem = take(3)
                extra_gather = LineGather(n, rows, 1, extra_ref, extra_all, extra_sems)
                extra_fetch = pltpu.make_async_copy(
                    extra_right_hbm.at[:, pl.ds(extra_right[1], extra_width)],
                    extra_right_ref,
                    extra_right_sem,
                )
                extra_fetch.start()

                def extra_product(block_id):
                    @pl.when((block_id >= 0) & (block_id < n))
                    def _():
                        span = rows_at(block_id * rows, rows)
                        extra_out[span, :] = dot(
                            extra_all[span, :], extra_right_ref[...]
                        ).astype(jnp.bfloat16)
        if other_gain is not None:
            gain_sum, table, first, middle, second = take(5)
            exchange = Exchange(n_dp, n, take(4))
            *grad_left_refs, grad_right_ref, grad_load_sems = take(4)
            grad_loads = [
                pltpu.make_async_copy(hbm, ref, grad_load_sems.at[k])
                for k, (hbm, ref) in enumerate(zip(grad_hbm, [*grad_left_refs, grad_right_ref]))
            ]
            for load in grad_loads:
                load.start()
            grads, paired, landed = take(3)
            pair_send, pair_recv, land_send, land_recv = take(4)
            dp = lax.axis_index("dp")
            core, chip = lax.rem(dp, 2), dp // 2
            chips, share = n_dp // 2, landed.shape[1]
            exchange.barrier()
            pair_copies = [
                pltpu.make_async_remote_copy(
                    src_ref=grads.at[rows_at((2 * q + 1 - core) * share, share)],
                    dst_ref=paired.at[q],
                    send_sem=pair_send.at[q],
                    recv_sem=pair_recv.at[q],
                    device_id={"dp": dp + 1 - 2 * core},
                    device_id_type=MESH,
                )
                for q in range(chips)
            ]
            land_copies = [
                pltpu.make_async_remote_copy(
                    src_ref=paired.at[lax.rem(chip + k, chips)],
                    dst_ref=landed.at[k - 1],
                    send_sem=land_send.at[k - 1],
                    recv_sem=land_recv.at[k - 1],
                    device_id={"dp": 2 * lax.rem(chip + k, chips) + core},
                    device_id_type=MESH,
                )
                for k in range(1, chips)
            ]

            def make_grads():
                for load in grad_loads:
                    load.wait()
                start, narrow = 0, 256
                for k, right_ref in enumerate([*left_refs, grad_right_ref]):
                    left_ref = grad_left_refs[0 if k < count else 1]

                    def column(i, carry, start=start, left_ref=left_ref, right_ref=right_ref):
                        grads[:, rows_at(start + i * narrow, narrow)] = t_dot(
                            left_ref[...], right_ref[:, rows_at(i * narrow, narrow)]
                        ).astype(jnp.bfloat16)
                        return carry

                    lax.fori_loop(0, right_ref.shape[1] // narrow, column, 0)
                    start += right_ref.shape[1]
                for copy in pair_copies:
                    copy.start()
                for copy in pair_copies:
                    copy.wait()

                def add(i, carry):
                    span = rows_at(i * block, block)
                    for q in range(chips):
                        own_span = rows_at((2 * q + core) * share + i * block, block)
                        paired[q, span, :] = (
                            paired[q, span, :].astype(jnp.float32)
                            + grads[own_span, :].astype(jnp.float32)
                        ).astype(jnp.bfloat16)
                    return carry

                lax.fori_loop(0, share // block, add, 0)
                for copy in land_copies:
                    copy.start()

            def land():
                for copy in land_copies:
                    copy.wait()

                def add(i, carry):
                    span = rows_at(i * block, block)
                    total = paired[chip, span, :].astype(jnp.float32)
                    for k in range(chips - 1):
                        total = total + landed[k, span, :].astype(jnp.float32)
                    owned_ref[span, :] = total
                    return carry

                lax.fori_loop(0, share // block, add, 0)

        else:
            gain_sum = outs[1] if has_gain else None
            neighbour_barrier(n)
        if extra is not None:
            extra_gather.send_own(0)
        if extra_right is not None:
            extra_all[rows_at(me * rows, rows), :] = extra_ref[...]
            extra_fetch.wait()
        if heads is not None:
            turn = 256
            fetch_joined.wait()

            def enter(i, carry):
                span = rows_at(i * turn, turn)
                cosine, sine = cosine_ref[span, :], sine_ref[span, :]
                row_vals = left_refs[0][span, :]
                for k, target in ((0, query_ref), (1, key_ref), (2, value_ref)):
                    piece = dot(row_vals, joined_ref[:, pl.ds(k * inner_width, inner_width)])
                    for h in range(head_count):
                        value = piece[:, h * HDIM : (h + 1) * HDIM]
                        if k < 2:
                            value = rotated(value, cosine, sine)
                        target[span, pl.ds(h * HDIM, HDIM)] = value.astype(jnp.bfloat16)
                return carry

            lax.fori_loop(0, total_rows // turn, enter, 0)
        for load in own_loads:
            load.start()
        fetch.wait()

        def attend(block_id):
            span = rows_at(block_id * rows, rows)
            row_pos = block_id * rows + lax.broadcasted_iota(jnp.int32, (rows, rows), 0)

            def against(kb, totals):
                other = rows_at(kb * rows, rows)
                col_pos = kb * rows + lax.broadcasted_iota(jnp.int32, (rows, rows), 1)
                allowed = jnp.where(col_pos <= row_pos, mask_ref[:, other], 0.0)
                out = []
                for h in range(head_count):
                    cols = pl.ds(h * HDIM, HDIM)
                    raw = dot_t(query_ref[span, cols], key_ref[other, cols])
                    prob = probability(raw) * allowed
                    out.append(
                        totals[h]
                        + jnp.dot(
                            prob.astype(jnp.bfloat16),
                            value_ref[other, cols],
                            preferred_element_type=jnp.float32,
                        )
                    )
                return tuple(out)

            start = tuple(jnp.zeros((rows, HDIM), jnp.float32) for _ in range(head_count))
            totals = lax.fori_loop(0, block_id + 1, against, start)
            for h in range(head_count):
                mixed_ref[span, pl.ds(h * HDIM, HDIM)] = totals[h].astype(jnp.bfloat16)

        def product(block_id):
            if heads is not None:
                attend(block_id)
            sources = [mixed_ref] if heads is not None else left_refs

            def column(ct, carry):
                cols = rows_at(ct * tile, tile)
                total, start = None, 0
                for source, piece in zip(sources, pieces):
                    term = dot_t(
                        source[rows_at(block_id * rows, rows), :],
                        right[cols, pl.ds(start, piece)],
                    )
                    start += piece
                    total = term if total is None else total + term
                part[:, cols] = total
                return carry

            lax.fori_loop(0, width // tile, column, 0)

        def hop(block_id, chunk, rightward):
            peer = me + 1 if rightward else me - 1
            slot = block_id if rightward else jnp.where(block_id == peer, n, block_id)
            return remote(
                sent.at[block_id, pl.ds(chunk * size, size)],
                held.at[slot, pl.ds(chunk * size, size)],
                send_sems.at[block_id * chunks + chunk],
                recv_sems.at[slot * chunks + chunk],
                peer,
            )

        def arrival(slot, chunk):
            ref = held.at[slot, pl.ds(chunk * size, size)]
            return remote(
                ref, ref, send_sems.at[chunk], recv_sems.at[slot * chunks + chunk], me
            )

        def add_rows(block_id, chunk, slots):
            def body(i, carry):
                span = rows_at(chunk * size + i * block, block)
                value = part[span, :]
                for slot in slots:
                    value = value + held[slot, span, :].astype(jnp.float32)
                sent[block_id, span, :] = value.astype(jnp.bfloat16)
                return carry

            lax.fori_loop(0, size // block, body, 0)

        def relay(block_id, rightward, inner):
            product(block_id)
            for chunk in range(chunks):

                @pl.when(inner)
                def _():
                    arrival(block_id, chunk).wait_recv()
                    add_rows(block_id, chunk, [block_id])

                @pl.when(jnp.logical_not(inner))
                def _():
                    add_rows(block_id, chunk, [])

                hop(block_id, chunk, rightward).start()

        def step_of(step, carry):
            @pl.when((step >= me + 1) & (me < n - 1))
            def _():
                relay(me + n - step, True, me > 0)

            @pl.when((step >= n - me) & (me > 0))
            def _():
                relay(me - n + step, False, me < n - 1)

            if extra is not None:

                @pl.when(step < n - 1)
                def _():
                    extra_gather.forward(step)
                    if extra_right is not None:
                        extra_product(me - step)
                        extra_product(me + step)

            if other_gain is not None:
                pl.when(step == 1)(make_grads)

            return carry

        lax.fori_loop(1, n, step_of, 0)
        product(me)
        if extra_right is not None:
            extra_product(me)
        for load in own_loads:
            load.wait()
        if has_gain:
            gain_sum[...] = jnp.zeros_like(gain_sum)
        for chunk in range(chunks):

            @pl.when(me > 0)
            def _():
                arrival(me, chunk).wait_recv()

            @pl.when(me < n - 1)
            def _():
                arrival(n, chunk).wait_recv()

            def body(i, carry):
                span = rows_at(chunk * size + i * block, block)
                total = part[span, :]
                zero = jnp.zeros_like(total)
                total = total + jnp.where(me > 0, held[me, span, :].astype(jnp.float32), zero)
                total = total + jnp.where(
                    me < n - 1, held[n, span, :].astype(jnp.float32), zero
                )
                gain = gain_ref[...]
                if epilogue == "residual":
                    outs[0][span, :] = (own[0][span, :] + total).astype(jnp.bfloat16)
                elif epilogue == "forward":
                    value = own[0][span, :].astype(jnp.float32) + total
                    outs[0][span, :] = value
                    inverse = lax.rsqrt(
                        jnp.mean(value * value, axis=1, keepdims=True) + norm_eps
                    )
                    normed[span, :] = (value * inverse * gain).astype(jnp.bfloat16)
                else:
                    value = own[0][span, :].astype(jnp.float32)
                    inverse = lax.rsqrt(
                        jnp.mean(value * value, axis=1, keepdims=True) + norm_eps
                    )
                    unit = value * inverse
                    scaled = total * gain
                    inner = jnp.mean(scaled * unit, axis=1, keepdims=True)
                    result = own[1][span, :] + inverse * (scaled - unit * inner)
                    outs[0][span, :] = result
                    gain_sum[...] += jnp.sum(
                        (total * unit).reshape(block // 8, 8, width), axis=0
                    )
                    if has_norm:
                        normed[span, :] = result.astype(jnp.bfloat16)
                return carry

            lax.fori_loop(0, size // block, body, 0)
        if extra is not None:
            extra_gather.finish()
        if extra_right is not None:
            extra_local = pltpu.make_async_copy(extra_all, extra_whole, extra_sem)
            extra_local.start()
            extra_product(me - (n - 1))
            extra_product(me + (n - 1))
        if extra is not None:
            extra_local.wait()
        if other_gain is not None:
            local = width // (n * n_dp)
            for source, rows_of in ((gain_sum, pl.ds(0, 8)), (other_ref, pl.ds(8, 8))):
                for d in range(n_dp):
                    for m in range(n):
                        cols = pl.ds(tile_of(d, m, n, local) * 128, 128)
                        table[m, d, rows_of, :] = source[:, cols]
            copies = exchange.swap("mp", lambda peer: table.at[peer], first)
            first[me] = table[me]
            for copy in copies:
                copy.wait()
            total = first[0]
            for m in range(1, n):
                total = total + first[m]
            middle[...] = total
            copies = exchange.swap("dp", lambda peer: middle.at[peer], second)
            second[dp] = middle[dp]
            land()
            for copy in copies:
                copy.wait()
            total = second[0]
            for d in range(1, n_dp):
                total = total + second[d]
            outs[1][...] = total

        def sends(step, carry):
            for chunk in range(chunks):

                @pl.when((step >= me + 1) & (me < n - 1))
                def _():
                    hop(me + n - step, chunk, True).wait_send()

                @pl.when((step >= n - me) & (me > 0))
                def _():
                    hop(me - n + step, chunk, False).wait_send()

            return carry

        lax.fori_loop(1, n, sends, 0)

    out_type = jnp.bfloat16 if epilogue == "residual" else jnp.float32
    out_shape = [jax.ShapeDtypeStruct((rows, width), out_type)]
    out_specs = [VMEM]
    if has_gain:
        out_shape.append(
            jax.ShapeDtypeStruct((8, width) if other_gain is None else (16, 128), jnp.float32)
        )
        out_specs.append(VMEM)
    if other_gain is not None:
        share = width // n_dp
        grad_width = sum(pieces) + grad_right.shape[1]
        out_shape.append(jax.ShapeDtypeStruct((share, grad_width), jnp.float32))
        out_specs.append(VMEM)
    scratch = [
        pltpu.VMEM((width, depth), jnp.bfloat16),
        pltpu.VMEM((n + 1, rows, width), jnp.bfloat16),
        pltpu.VMEM((n, rows, width), jnp.bfloat16),
        pltpu.VMEM((rows, width), jnp.float32),
    ]
    if heads is not None:
        scratch.append(pltpu.VMEM((width, rhs_start), jnp.bfloat16))
    if has_norm:
        out_shape.append(jax.ShapeDtypeStruct((rows, width), jnp.bfloat16))
        out_specs.append(VMEM)
    scratch += [
        pltpu.SemaphoreType.DMA,
        pltpu.SemaphoreType.DMA((n * chunks,)),
        pltpu.SemaphoreType.DMA(((n + 1) * chunks,)),
    ]
    scratch += [pltpu.VMEM(x.shape, x.dtype) for x in own_rows]
    scratch.append(pltpu.SemaphoreType.DMA((len(own_rows),)))
    head_args = []
    if heads is not None:
        scratch.append(pltpu.SemaphoreType.DMA)
        head_args = list(heads)
        out_shape += [jax.ShapeDtypeStruct((total_rows, inner_width), jnp.bfloat16)] * 4
        out_specs += [VMEM] * 4
    extra_args = []
    if extra is not None:
        out_shape.append(jax.ShapeDtypeStruct((total_rows, width), jnp.bfloat16))
        out_specs.append(ANY)
        scratch += [pltpu.SemaphoreType.DMA] + gather_sems(n, 1)
        extra_args = [extra]
    if extra_right is not None:
        out_shape.append(jax.ShapeDtypeStruct((total_rows, extra_width), jnp.bfloat16))
        out_specs.append(VMEM)
        scratch += [
            pltpu.VMEM((total_rows, width), jnp.bfloat16),
            pltpu.VMEM((width, extra_width), jnp.bfloat16),
            pltpu.SemaphoreType.DMA,
        ]
        extra_args.append(extra_right[0])
    late_args = []
    if other_gain is not None:
        head_args.append(other_gain)
        late_args = [*grad_lefts, grad_right]
        scratch += [
            pltpu.VMEM((8, width), jnp.float32),
            pltpu.VMEM((n, n_dp, 16, 128), jnp.float32),
            pltpu.VMEM((n, n_dp, 16, 128), jnp.float32),
            pltpu.VMEM((n_dp, 16, 128), jnp.float32),
            pltpu.VMEM((n_dp, 16, 128), jnp.float32),
        ] + exchange_sems(n_dp, n)
        scratch += [pltpu.VMEM(x.shape, x.dtype) for x in late_args]
        scratch.append(pltpu.SemaphoreType.DMA((len(late_args),)))
        chips = n_dp // 2
        scratch.append(pltpu.VMEM((width, grad_width), jnp.bfloat16))
        scratch.append(pltpu.VMEM((chips, share, grad_width), jnp.bfloat16))
        scratch.append(pltpu.VMEM((chips - 1, share, grad_width), jnp.bfloat16))
        scratch += [pltpu.SemaphoreType.DMA((chips,))] * 2
        scratch += [pltpu.SemaphoreType.DMA((chips - 1,))] * 2
    flops = 2 * total_rows * depth * width
    return pl.pallas_call(
        kernel,
        out_shape=out_shape,
        in_specs=[VMEM] * count
        + [ANY]
        + [VMEM]
        + [ANY] * len(own_rows)
        + [VMEM] * len(head_args)
        + [ANY] * len(late_args)
        + [VMEM if extra_right is not None else ANY] * min(1, len(extra_args))
        + [ANY] * max(0, len(extra_args) - 1),
        out_specs=out_specs,
        scratch_shapes=scratch,
        compiler_params=pltpu.CompilerParams(
            collective_id=collective_id, has_side_effects=True, vmem_limit_bytes=VMEM_LIMIT
        ),
        cost_estimate=pl.CostEstimate(
            flops=flops, bytes_accessed=300_000_000, transcendentals=0
        ),
        name="scatter_" + epilogue,
    )(*lhs, rhs, gains_row, *own_rows, *head_args, *late_args, *extra_args)


def feed_forward(n, normed, branch_grad, weights, second, gains_row, collective_id, halves=1, hops=4):
    rows, width = normed.shape
    total_rows = n * rows
    hidden = weights.shape[1] // 3
    count, parcels = hops, halves
    part_size = rows // hops
    tile = min(1024, hidden)
    block = min(32, part_size)
    narrow = min(256, hidden)
    per = hidden // narrow
    pieces = 3 * per
    before = pieces // 6
    between = (pieces - 2 * before) // (count + 1)
    tall = min(1024, width)

    def kernel(
        normed_ref,
        branch_hbm,
        weights_hbm,
        second_ref,
        gain_ref,
        result_ref,
        rounded_ref,
        gain_sum,
        grads_hbm,
        act_hbm,
        gate_hbm,
        up_hbm,
        weight_ref,
        branch_ref,
        all_ref,
        held,
        sent,
        own_part,
        act_ref,
        gate_ref,
        up_ref,
        piece_ref,
        load_sems,
        stage_sems,
        piece_sems,
        grad_sems,
        send_sems,
        recv_sems,
        *gather_refs,
    ):
        me = lax.axis_index("mp")
        middle = (me > 0) & (me < n - 1)
        loads = [
            pltpu.make_async_copy(weights_hbm, weight_ref, load_sems.at[0]),
            pltpu.make_async_copy(branch_hbm, branch_ref, load_sems.at[1]),
        ]
        for load in loads:
            load.start()
        gather = LineGather(n, rows, parcels, normed_ref, all_ref, gather_refs)
        neighbour_barrier(n)
        for parcel in range(parcels):
            gather.send_own(parcel)
        all_ref[rows_at(me * rows, rows), :] = normed_ref[...]
        for load in loads:
            load.wait()

        def hop(block_id, chunk, rightward):
            peer = me + 1 if rightward else me - 1
            slot = block_id if rightward else jnp.where(block_id == peer, n, block_id)
            return remote(
                sent.at[block_id, pl.ds(chunk * part_size, part_size)],
                held.at[slot, pl.ds(chunk * part_size, part_size)],
                send_sems.at[block_id * count + chunk],
                recv_sems.at[slot * count + chunk],
                peer,
            )

        def arrival(slot, chunk):
            ref = held.at[slot, pl.ds(chunk * part_size, part_size)]
            return remote(
                ref, ref, send_sems.at[chunk], recv_sems.at[slot * count + chunk], me
            )

        def stages(block_id, chunk, size):
            span = rows_at(block_id * rows + chunk * size, size)
            return [
                pltpu.make_async_copy(
                    ref.at[pl.ds(chunk * size, size)], hbm.at[span], stage_sems.at[chunk * 3 + k]
                )
                for k, (ref, hbm) in enumerate(
                    ((act_ref, act_hbm), (gate_ref, gate_hbm), (up_ref, up_hbm))
                )
            ]

        def compute(block_id, chunk, size, first):
            here = pl.ds(chunk * size, size)
            span = rows_at(block_id * rows + chunk * size, size)

            @pl.when(jnp.logical_not(first))
            def _():
                for stage in stages(block_id, chunk, size):
                    stage.wait()

            def units(ct, carry):
                cols = rows_at(ct * tile, tile)
                row_vals, branch = all_ref[span, :], branch_ref[span, :]
                gate = dot(row_vals, weight_ref[:, cols])
                up = dot(row_vals, weight_ref[:, rows_at(hidden + ct * tile, tile)])
                act_grad = dot(branch, weight_ref[:, rows_at(2 * hidden + ct * tile, tile)])
                sigma = 1.0 / (1.0 + jnp.exp(-gate))
                silu = gate * sigma
                act_ref[here, cols] = (silu * up).astype(jnp.bfloat16)
                gate_ref[here, cols] = (
                    act_grad * up * sigma * (1.0 + gate * (1.0 - sigma))
                ).astype(jnp.bfloat16)
                up_ref[here, cols] = (act_grad * silu).astype(jnp.bfloat16)
                return carry

            lax.fori_loop(0, hidden // tile, units, 0)
            for stage in stages(block_id, chunk, size):
                stage.start()

            def columns(ct, carry):
                cols = rows_at(ct * tile, tile)
                total = dot_t(gate_ref[here, :], weight_ref[cols, pl.ds(0, hidden)])
                total += dot_t(up_ref[here, :], weight_ref[cols, pl.ds(hidden, hidden)])

                @pl.when(block_id == me)
                def _():
                    own_part[here, cols] = total

                @pl.when(block_id != me)
                def _():
                    sent[block_id, here, cols] = total.astype(jnp.bfloat16)

                return carry

            lax.fori_loop(0, width // tile, columns, 0)

            @pl.when((me == 0) & (block_id > me))
            def _():
                for k in range(size // part_size):
                    hop(block_id, chunk * (size // part_size) + k, True).start()

            @pl.when((me == n - 1) & (block_id < me))
            def _():
                for k in range(size // part_size):
                    hop(block_id, chunk * (size // part_size) + k, False).start()

        def forward(step, parcel):
            gather.forward_chunk(step, parcel, step < n - 1)

        def forward_whole(step):
            for parcel in range(parcels):
                forward(step, parcel)

        def step_of(step, carry):
            def side_of(side, carry):
                block_id = me + (1 - 2 * side) * step
                valid = (block_id >= 0) & (block_id < n) & ((step > 0) | (side == 0))

                @pl.when(middle & (step > 0) & (step < n - 1) & (side == 1))
                def _():
                    forward_whole(step + 1)

                @pl.when(middle & valid)
                def _():
                    compute(block_id, 0, rows, step == 0)

                @pl.when(middle & (step == 0) & (side == 0))
                def _():
                    forward_whole(1)

                for half in range(halves):

                    @pl.when(jnp.logical_not(middle) & valid)
                    def _():
                        pl.when(step > 0)(lambda: forward(step, half))
                        compute(block_id, half, rows // halves, step == 0)

                return carry

            return lax.fori_loop(0, 2, side_of, carry)

        lax.fori_loop(0, n, step_of, 0)
        @pl.when(middle)
        def _():
            for stage in stages(me, 0, rows):
                stage.wait()

        @pl.when(jnp.logical_not(middle))
        def _():
            for half in range(halves):
                for stage in stages(me, half, rows // halves):
                    stage.wait()


        def load_of(source, index, slot):
            return pltpu.make_async_copy(
                source.at[:, rows_at(lax.rem(index, per) * narrow, narrow)],
                piece_ref.at[slot],
                piece_sems.at[slot],
            )

        def load_piece(index):
            for k, source in enumerate((gate_hbm, up_hbm, act_hbm)):

                @pl.when(index // per == k)
                def _():
                    load_of(source, index, lax.rem(index, 2)).start()

        def grad_copy(index):
            cols = rows_at(index * narrow, narrow)
            return pltpu.make_async_copy(
                weight_ref.at[:, cols], grads_hbm.at[:, cols], grad_sems.at[index]
            )

        def grad_piece(index, carry):
            slot = lax.rem(index, 2)
            load_of(gate_hbm, index, slot).wait()

            @pl.when(index + 1 < pieces)
            def _():
                load_piece(index + 1)

            cols = rows_at(index * narrow, narrow)
            for start in range(0, width, tall):
                span = pl.ds(start, tall)

                @pl.when(index < 2 * per)
                def _():
                    weight_ref[span, cols] = t_dot(all_ref[:, span], piece_ref[slot]).astype(
                        jnp.bfloat16
                    )

                @pl.when(index >= 2 * per)
                def _():
                    weight_ref[span, cols] = t_dot(branch_ref[:, span], piece_ref[slot]).astype(
                        jnp.bfloat16
                    )

            grad_copy(index).start()
            return carry

        load_piece(0)

        def add_rows(block_id, chunk):
            def body(i, carry):
                span = rows_at(chunk * part_size + i * block, block)
                value = sent[block_id, span, :].astype(jnp.float32)
                value = value + held[block_id, span, :].astype(jnp.float32)
                sent[block_id, span, :] = value.astype(jnp.bfloat16)
                return carry

            lax.fori_loop(0, part_size // block, body, 0)

        def relay_side(step, chunk, rightward):
            block_id = step if rightward else n - 1 - step
            has = (me > 0) & (step > me) if rightward else (me < n - 1) & (n - 1 - step < me)

            @pl.when(has)
            def _():
                arrival(block_id, chunk).wait_recv()
                add_rows(block_id, chunk)
                hop(block_id, chunk, rightward).start()

        def relay_chunk(step, chunk, near):
            rightward_first = 2 * me < n

            @pl.when(rightward_first)
            def _():
                relay_side(step, chunk, near)

            @pl.when(jnp.logical_not(rightward_first))
            def _():
                relay_side(step, chunk, not near)

        def relay_of(step, carry):
            for chunk in range(count):
                relay_chunk(step, chunk, True)
            for chunk in range(count):
                relay_chunk(step, chunk, False)
            return carry

        lax.fori_loop(1, n - 1, relay_of, 0)
        lax.fori_loop(0, before, grad_piece, 0)

        def last_relay(chunk, carry):
            @pl.when(chunk < count)
            def _():
                relay_chunk(n - 1, chunk, True)

            start = before + chunk * between
            lax.fori_loop(start, start + between, grad_piece, 0)

            @pl.when(chunk > 0)
            def _():
                relay_chunk(n - 1, chunk - 1, False)

            return carry

        lax.fori_loop(0, count + 1, last_relay, 0)
        lax.fori_loop(before + (count + 1) * between, pieces, grad_piece, 0)
        gain_sum[...] = jnp.zeros_like(gain_sum)
        for chunk in range(count):

            @pl.when(me > 0)
            def _():
                arrival(me, chunk).wait_recv()

            @pl.when(me < n - 1)
            def _():
                arrival(n, chunk).wait_recv()

            def body(i, carry):
                span = rows_at(chunk * part_size + i * block, block)
                total = own_part[span, :]
                zero = jnp.zeros_like(total)
                total = total + jnp.where(me > 0, held[me, span, :].astype(jnp.float32), zero)
                total = total + jnp.where(
                    me < n - 1, held[n, span, :].astype(jnp.float32), zero
                )
                value = second_ref[span, :]
                inverse = lax.rsqrt(jnp.mean(value * value, axis=1, keepdims=True) + norm_eps)
                unit = value * inverse
                scaled = total * gain_ref[...]
                inner = jnp.mean(scaled * unit, axis=1, keepdims=True)
                base = branch_ref[
                    rows_at(me * rows + chunk * part_size + i * block, block), :
                ].astype(jnp.float32)
                result = base + inverse * (scaled - unit * inner)
                result_ref[span, :] = result
                rounded_ref[span, :] = result.astype(jnp.bfloat16)
                gain_sum[...] += jnp.sum((total * unit).reshape(block // 8, 8, width), axis=0)
                return carry

            lax.fori_loop(0, part_size // block, body, 0)
        gather.finish(False)

        def sends(block_id, carry):
            for chunk in range(count):

                @pl.when((block_id > me) & (me < n - 1))
                def _():
                    hop(block_id, chunk, True).wait_send()

                @pl.when((block_id < me) & (me > 0))
                def _():
                    hop(block_id, chunk, False).wait_send()

            return carry

        lax.fori_loop(0, n, sends, 0)

        def grads_out(index, carry):
            grad_copy(index).wait()
            return carry

        lax.fori_loop(0, pieces, grads_out, 0)

    half = jnp.bfloat16
    return pl.pallas_call(
        kernel,
        out_shape=[
            jax.ShapeDtypeStruct((rows, width), jnp.float32),
            jax.ShapeDtypeStruct((rows, width), half),
            jax.ShapeDtypeStruct((8, width), jnp.float32),
            jax.ShapeDtypeStruct((width, 3 * hidden), half),
        ]
        + [jax.ShapeDtypeStruct((total_rows, hidden), half)] * 3,
        in_specs=[VMEM, ANY, ANY, VMEM, VMEM],
        out_specs=[VMEM] * 3 + [ANY] * 4,
        scratch_shapes=[
            pltpu.VMEM((width, 3 * hidden), half),
            pltpu.VMEM((total_rows, width), half),
            pltpu.VMEM((total_rows, width), half),
            pltpu.VMEM((n + 1, rows, width), half),
            pltpu.VMEM((n, rows, width), half),
            pltpu.VMEM((rows, width), jnp.float32),
        ]
        + [pltpu.VMEM((rows, hidden), half)] * 3
        + [
            pltpu.VMEM((2, total_rows, narrow), half),
            pltpu.SemaphoreType.DMA((2,)),
            pltpu.SemaphoreType.DMA((halves * 3,)),
            pltpu.SemaphoreType.DMA((2,)),
            pltpu.SemaphoreType.DMA((pieces,)),
            pltpu.SemaphoreType.DMA((n * count,)),
            pltpu.SemaphoreType.DMA(((n + 1) * count,)),
        ]
        + gather_sems(n, parcels),
        compiler_params=pltpu.CompilerParams(
            collective_id=collective_id, has_side_effects=True, vmem_limit_bytes=VMEM_LIMIT
        ),
        cost_estimate=pl.CostEstimate(
            flops=16 * total_rows * width * hidden, bytes_accessed=300_000_000, transcendentals=0
        ),
        name="feed_forward",
    )(normed, branch_grad, weights, second, gains_row)


def attention_backward(queries, keys, values, mixed_grad, cosine, sine, key_mask):
    total_rows, inner_width = queries.shape
    block = min(256, total_rows)

    def kernel(q_ref, k_ref, v_ref, do_ref, cos_ref, sin_ref, mask_ref, dq_out, dk_out, dv_out, dk_ref, dv_ref):
        dk_ref[...] = jnp.zeros_like(dk_ref)
        dv_ref[...] = jnp.zeros_like(dv_ref)
        for i in range(total_rows // block):
            span = pl.ds(i * block, block)
            upto = (i + 1) * block
            shape = (upto, block)
            key_pos = lax.broadcasted_iota(jnp.int32, shape, 0)
            query_pos = i * block + lax.broadcasted_iota(jnp.int32, shape, 1)
            allowed = jnp.where(key_pos <= query_pos, mask_ref[:upto, :], 0.0)
            query, grad = q_ref[span, :], do_ref[span, :]
            key = k_ref[:upto, :]
            prob = probability(dot_t(key, query)) * allowed
            prob_grad = dot_t(v_ref[:upto, :], grad)
            dv_ref[:upto, :] += jnp.dot(
                prob.astype(jnp.bfloat16), grad, preferred_element_type=jnp.float32
            )
            score_grad = (prob_grad * prob * (1.0 - prob) * (1.0 / math.sqrt(HDIM))).astype(
                jnp.bfloat16
            )
            dk_ref[:upto, :] += jnp.dot(score_grad, query, preferred_element_type=jnp.float32)
            dq = t_dot(score_grad, key)
            dq_out[span, :] = rotated(
                dq, cos_ref[span, :], sin_ref[span, :], True
            ).astype(jnp.bfloat16)
        dk_out[...] = rotated(dk_ref[...], cos_ref[...], sin_ref[...], True).astype(jnp.bfloat16)
        dv_out[...] = dv_ref[...].astype(jnp.bfloat16)

    head = pl.BlockSpec((total_rows, HDIM), lambda h: (0, h))
    table = pl.BlockSpec((total_rows, HDIM), lambda h: (0, 0))
    return pl.pallas_call(
        kernel,
        grid=(inner_width // HDIM,),
        out_shape=[jax.ShapeDtypeStruct((total_rows, inner_width), jnp.bfloat16)] * 3,
        in_specs=[head] * 4 + [table] * 2 + [pl.BlockSpec((total_rows, 1), lambda h: (0, 0))],
        out_specs=[head] * 3,
        scratch_shapes=[pltpu.VMEM((total_rows, HDIM), jnp.float32)] * 2,
        compiler_params=pltpu.CompilerParams(vmem_limit_bytes=VMEM_LIMIT),
        cost_estimate=pl.CostEstimate(
            flops=8 * total_rows * total_rows * inner_width,
            bytes_accessed=14 * total_rows * inner_width,
            transcendentals=0,
        ),
        name="attention_backward",
    )(queries, keys, values, mixed_grad, cosine, sine, key_mask)


def updated(weight, moment, average, gradient, rate):
    moment_new = momentum_decay * moment + (1.0 - momentum_decay) * gradient
    weight_new = weight - rate * (
        (1.0 - momentum_decay) * gradient + momentum_decay * moment_new
    )
    average_new = average_decay * average + (1.0 - average_decay) * weight_new
    return weight_new, moment_new, average_new


def store_update(ins, gradient, outs, rate):
    weight, moment, average = updated(*[ref[...] for ref in ins], gradient, rate)
    outs[0][...] = weight
    outs[1][...] = moment
    outs[2][...] = average
    outs[3][...] = weight.astype(jnp.bfloat16)


def update_call(body, grid, arrays, spec, total, total_spec, scratch, name):
    kinds = [jnp.float32] * 3 + [jnp.bfloat16]
    shape = arrays[0].shape
    return pl.pallas_call(
        body,
        grid=grid,
        out_shape=[jax.ShapeDtypeStruct(shape, kind) for kind in kinds],
        in_specs=[spec] * 3 + [total_spec],
        out_specs=[spec] * 4,
        scratch_shapes=scratch,
        compiler_params=pltpu.CompilerParams(vmem_limit_bytes=VMEM_LIMIT),
        cost_estimate=pl.CostEstimate(
            flops=10 * arrays[0].size, bytes_accessed=28 * arrays[0].size, transcendentals=0
        ),
        name=name,
    )(*arrays, total)


def update_flipped(arrays, total, start, rate, name):
    high, wide = arrays[0].shape
    step = min(512, high)

    def body(w, m, a, g, *outs):
        store_update((w, m, a), g[...].astype(jnp.float32).T, outs, rate)

    return update_call(
        body,
        (high // step,),
        arrays,
        pl.BlockSpec((step, wide), lambda i: (i, 0)),
        total,
        pl.BlockSpec((wide, step), lambda i: (0, start // step + i)),
        [],
        name,
    )


def update_parts(arrays, total, rate, name):
    high, parts, wide = arrays[0].shape

    def body(w, m, a, g, *outs):
        store_update((w, m, a), g[...].astype(jnp.float32), outs, rate)

    turns = 1
    outs = update_call(
        body,
        (parts, turns),
        [x.transpose(1, 0, 2) for x in arrays],
        pl.BlockSpec((None, high // turns, wide), lambda i, j: (i, j, 0)),
        total,
        pl.BlockSpec((high // turns, wide), lambda i, j: (j, i)),
        [],
        name,
    )
    return [x.transpose(1, 0, 2) for x in outs]


def update_pairs(arrays, total, rate, name):
    high, parts, wide = arrays[0].shape
    tiles = wide // 128
    step = min(64, high)
    stride = tiles * parts

    def body(w, m, a, g, *rest):
        outs, spread = rest[:4], rest[4]
        for part in range(parts):
            for tile in range(tiles):
                cols = pl.ds(part * wide + tile * 128, 128)
                spread[pl.ds(tile * parts + part, step, stride=stride), :] = g[:, cols].astype(
                    jnp.float32
                )
        store_update((w, m, a), spread[...], outs, rate)

    outs = update_call(
        body,
        (high // step,),
        [flat_pairs(x) for x in arrays],
        pl.BlockSpec((step * stride, 128), lambda i: (i, 0)),
        total,
        pl.BlockSpec((step, parts * wide), lambda i: (i, 0)),
        [pltpu.VMEM((step * stride, 128), jnp.float32)],
        name,
    )
    return [
        x.reshape(high, tiles, parts, 128).transpose(0, 2, 1, 3).reshape(high, parts, wide)
        for x in outs
    ]


def rope_tables(length, half_dim):
    positions = np.arange(length, dtype=np.float32)[:, None]
    inverse_freq = np.power(
        np.float32(rope_base), -np.arange(half_dim, dtype=np.float32) / np.float32(half_dim)
    )
    angles = positions * inverse_freq[None, :]
    cosine, sine = np.cos(angles), np.sin(angles)
    return np.concatenate([cosine, cosine], axis=1), np.concatenate([-sine, sine], axis=1)


def per_device(
    n_dp,
    n_mp,
    tokens,
    cotangent,
    valid_counts,
    w_qkv,
    w_out,
    w_gu,
    w_down,
    gains,
    mom_qkv,
    mom_out,
    mom_gu,
    mom_down,
    mom_gains,
    avg_qkv,
    avg_out,
    avg_gu,
    avg_down,
    avg_gains,
):
    half = jnp.bfloat16
    row_count, width = tokens.shape
    owned, _, local_width = w_qkv.shape
    hidden = w_gu.shape[2]
    valid_len = valid_counts[0]

    attn_part = jnp.concatenate(
        [w_qkv.reshape(owned, 3 * local_width), w_out.T], axis=1
    ).astype(half)
    attn_w = lax.all_gather(attn_part, "dp", axis=0, tiled=True)
    row_ids = lax.axis_index("mp") * row_count + jnp.arange(row_count, dtype=jnp.int32)
    live_rows = (row_ids < valid_len).astype(jnp.float32)[:, None]
    key_mask = (jnp.arange(SEQ, dtype=jnp.int32) < valid_len).astype(jnp.float32)
    ffn_part, tokens_in = lax.optimization_barrier((round_shares(w_gu, w_down), tokens))
    h_first, gain_all, out_grad, own_branch = gather_first(
        n_dp, n_mp, tokens_in, gains, cotangent, live_rows, 1
    )
    ffn_w = lax.all_gather(ffn_part, "dp", axis=0, tiled=True)
    cosine, sine = (jnp.asarray(x, jnp.float32) for x in rope_tables(SEQ, HDIM // 2))

    second, normed_second, queries, keys, values, mixed, branch_grad = scatter_rows(
        n_mp,
        [h_first],
        attn_w,
        3 * local_width,
        [tokens],
        "forward",
        gain_all[1:2],
        2,
        heads=(cosine, sine, key_mask[None, :]),
        extra=own_branch,
    )

    second_grad, own_grad, gain_two, grad_ffn, act, _, _ = feed_forward(
        n_mp, normed_second, branch_grad, ffn_w, second, gain_all[1:2], 3
    )
    sum_ffn = lax.psum_scatter(grad_ffn, "dp", scatter_dimension=0, tiled=True)
    block_out, attn_grad, mixed_grad = scatter_rows(
        n_mp,
        [act],
        ffn_w,
        2 * hidden,
        [second],
        "residual",
        gain_all[1:2],
        7,
        extra=own_grad,
        extra_right=(attn_w, 3 * local_width),
    )

    joined_grad = attention_backward(
        queries, keys, values, mixed_grad, cosine, sine, key_mask[:, None]
    )
    input_grad, gain_tile, sum_attn = scatter_rows(
        n_mp,
        list(joined_grad),
        attn_w,
        0,
        [tokens, second_grad],
        "last",
        gain_all[0:1],
        4,
        other_gain=gain_two,
        grad_lefts=[h_first, attn_grad],
        grad_right=mixed,
        n_dp=n_dp,
    )

    total_rows = SEQ * n_dp
    matrix_rate = step_rate / math.sqrt(total_rows)
    scale_rate = gain_rate / math.sqrt(total_rows)
    local = gains.shape[1]
    place = lax.rem((lax.axis_index("dp") * n_mp + lax.axis_index("mp")) * local, 128)
    sum_gains = lax.dynamic_slice(gain_tile.reshape(2, 8, 128).sum(axis=1), (0, place), (2, local))
    new_gu, next_mom_gu, next_avg_gu, copy_gu = update_pairs(
        [w_gu, mom_gu, avg_gu], sum_ffn, matrix_rate, "update_gu"
    )
    new_down, next_mom_down, next_avg_down, copy_down = update_flipped(
        [w_down, mom_down, avg_down], sum_ffn, 2 * hidden, matrix_rate, "update_down"
    )
    new_qkv, next_mom_qkv, next_avg_qkv, copy_qkv = update_parts(
        [w_qkv, mom_qkv, avg_qkv], sum_attn, matrix_rate, "update_qkv"
    )
    new_out, next_mom_out, next_avg_out, copy_out = update_flipped(
        [w_out, mom_out, avg_out], sum_attn, 3 * local_width, matrix_rate, "update_out"
    )
    new_gains, next_mom_gains, next_avg_gains = updated(
        gains, mom_gains, avg_gains, sum_gains, scale_rate
    )
    return (
        block_out,
        input_grad,
        new_qkv,
        new_out,
        new_gu,
        new_down,
        new_gains,
        next_mom_qkv,
        next_mom_out,
        next_mom_gu,
        next_mom_down,
        next_mom_gains,
        next_avg_qkv,
        next_avg_out,
        next_avg_gu,
        next_avg_down,
        next_avg_gains,
        copy_qkv,
        copy_out,
        copy_gu,
        copy_down,
    )


def solution(mesh):
    rows, one = P(("dp", "mp"), None), P("dp")
    tall, wide, spread = P("dp", None, "mp"), P("mp", "dp"), P(None, ("dp", "mp"))
    weights = (tall, wide, tall, wide)
    return jax.shard_map(
        functools.partial(per_device, mesh.shape["dp"], mesh.shape["mp"]),
        mesh=mesh,
        in_specs=(rows, rows, one, *((*weights, spread) * 3)),
        out_specs=(rows, rows, *((*weights, spread) * 3), *weights),
        check_vma=False,
    )
```

```python
import functools
import math

import jax
import jax.numpy as jnp
from jax import lax
from jax.experimental import pallas as pl
from jax.experimental.pallas import tpu as pltpu
import numpy as np
from jax.sharding import PartitionSpec as P

HDIM = 128
SEQ = 1024
MESH = pl.DeviceIdType.MESH
ANY = pl.BlockSpec(memory_space=pl.ANY)
VMEM = pl.BlockSpec(memory_space=pltpu.VMEM)
VMEM_LIMIT = 60 * 1024 * 1024

norm_eps = 1e-05
rope_base = 10000.0
momentum_decay = 0.9
average_decay = 0.9
step_rate = 0.05
gain_rate = 0.5


def rows_at(start, size):
    return pl.ds(pl.multiple_of(start, size), size)


def remote(src, dst, send_sem, recv_sem, peer):
    return pltpu.make_async_remote_copy(
        src_ref=src,
        dst_ref=dst,
        send_sem=send_sem,
        recv_sem=recv_sem,
        device_id={"mp": peer},
        device_id_type=MESH,
    )


def neighbour_barrier(n):
    me = lax.axis_index("mp")
    barrier = pltpu.get_barrier_semaphore()

    @pl.when(me > 0)
    def _():
        pl.semaphore_signal(barrier, inc=1, device_id={"mp": me - 1}, device_id_type=MESH)

    @pl.when(me < n - 1)
    def _():
        pl.semaphore_signal(barrier, inc=1, device_id={"mp": me + 1}, device_id_type=MESH)

    pl.semaphore_wait(barrier, jnp.where(me > 0, 1, 0) + jnp.where(me < n - 1, 1, 0))


class LineGather:
    def __init__(self, n, rows, chunks, own, whole, sems):
        self.n, self.rows, self.chunks = n, rows, chunks
        self.size = rows // chunks
        self.own, self.whole, self.sems = own, whole, sems
        self.me = lax.axis_index("mp")

    def at(self, block, chunk):
        return self.whole.at[rows_at(block * self.rows + chunk * self.size, self.size)]

    def copies(self, step, chunk, first):
        me, n = self.me, self.n
        send_r, recv_r, send_l, recv_l = self.sems
        out = []
        for block, peer, has, send, recv in (
            (me - step, me + 1, (me - step >= 0) & (me < n - 1), send_r, recv_r),
            (me + step, me - 1, (me + step <= n - 1) & (me > 0), send_l, recv_l),
        ):
            src = (
                self.own.at[pl.ds(chunk * self.size, self.size)]
                if first
                else self.at(block, chunk)
            )
            index = step * self.chunks + chunk
            out.append(
                (has, remote(src, self.at(block, chunk), send.at[index], recv.at[index], peer))
            )
        return out

    def arrivals(self, step, chunk):
        me, n = self.me, self.n
        send_r, recv_r, send_l, recv_l = self.sems
        index = step * self.chunks + chunk
        out = []
        for block, has, send, recv in (
            (me - 1 - step, me - 1 - step >= 0, send_r, recv_r),
            (me + 1 + step, me + 1 + step <= n - 1, send_l, recv_l),
        ):
            ref = self.at(block, chunk)
            out.append((has, remote(ref, ref, send.at[index], recv.at[index], me)))
        return out

    def send_own(self, chunk):
        for has, copy in self.copies(0, chunk, True):
            pl.when(has)(copy.start)

    def forward(self, step):
        for chunk in range(self.chunks):
            self.forward_chunk(step, chunk, True)

    def forward_chunk(self, step, chunk, more):
        for (got, arrival), (has, copy) in zip(
            self.arrivals(step - 1, chunk), self.copies(step, chunk, False)
        ):
            pl.when(got)(arrival.wait_recv)
            pl.when(has & more)(copy.start)

    def finish(self, arrivals=True):
        for chunk in range(self.chunks if arrivals else 0):
            for got, arrival in self.arrivals(self.n - 2, chunk):
                pl.when(got)(arrival.wait_recv)
        for chunk in range(self.chunks):
            for has, copy in self.copies(0, chunk, True):
                pl.when(has)(copy.wait_send)

        def waits(step, carry):
            for chunk in range(self.chunks):
                for has, copy in self.copies(step, chunk, False):
                    pl.when(has)(copy.wait_send)
            return carry

        lax.fori_loop(1, self.n - 1, waits, 0)

    def forward_all(self):
        def step_of(step, carry):
            self.forward(step)
            return carry

        lax.fori_loop(1, self.n - 1, step_of, 0)


def gather_sems(n, chunks):
    return [pltpu.SemaphoreType.DMA(((n - 1) * chunks,))] * 4


class Exchange:
    def __init__(self, n_dp, n_mp, sems):
        self.n_dp, self.n_mp = n_dp, n_mp
        self.s_mp, self.r_mp, self.s_dp, self.r_dp = sems
        self.dp, self.mp = lax.axis_index("dp"), lax.axis_index("mp")

    def barrier(self):
        barrier = pltpu.get_barrier_semaphore()
        for axis, here, count in (("mp", self.mp, self.n_mp), ("dp", self.dp, self.n_dp)):
            for k in range(1, count):
                pl.semaphore_signal(
                    barrier,
                    inc=1,
                    device_id={axis: lax.rem(here + k, count)},
                    device_id_type=MESH,
                )
        pl.semaphore_wait(barrier, self.n_mp + self.n_dp - 2)

    def swap(self, axis, source_of, target):
        if axis == "mp":
            here, count, send, recv = self.mp, self.n_mp, self.s_mp, self.r_mp
        else:
            here, count, send, recv = self.dp, self.n_dp, self.s_dp, self.r_dp
        copies = []
        for k in range(1, count):
            peer = lax.rem(here + k, count)
            copies.append(
                pltpu.make_async_remote_copy(
                    src_ref=source_of(peer),
                    dst_ref=target.at[here],
                    send_sem=send.at[k - 1],
                    recv_sem=recv.at[k - 1],
                    device_id={axis: peer},
                    device_id_type=MESH,
                )
            )
        for copy in copies:
            copy.start()
        return copies


def exchange_sems(n_dp, n_mp):
    return [pltpu.SemaphoreType.DMA((n_mp - 1,))] * 2 + [pltpu.SemaphoreType.DMA((n_dp - 1,))] * 2


def tile_of(dp, mp, n_mp, local):
    return (dp * n_mp + mp) * local // 128


def flat_pairs(x):
    high, parts, wide = x.shape
    return x.reshape(high, parts, wide // 128, 128).transpose(0, 2, 1, 3).reshape(-1, 128)


def round_shares(w_gu, w_down):
    high, parts, hidden = w_gu.shape
    tiles = hidden // 128
    step = 128
    turn = min(256, hidden)

    def kernel(gu_ref, down_ref, out_ref):
        for part in range(parts):
            for tile in range(tiles):
                cols = pl.ds(part * hidden + tile * 128, 128)
                out_ref[:, cols] = gu_ref[
                    pl.ds(tile * parts + part, step, stride=tiles * parts), :
                ].astype(jnp.bfloat16)
        for i in range(hidden // turn):
            piece = down_ref[pl.ds(i * turn, turn), :]
            out_ref[:, pl.ds(parts * hidden + i * turn, turn)] = piece.T.astype(jnp.bfloat16)

    return pl.pallas_call(
        kernel,
        grid=(high // step,),
        out_shape=jax.ShapeDtypeStruct((high, (parts + 1) * hidden), jnp.bfloat16),
        in_specs=[
            pl.BlockSpec((step * tiles * parts, 128), lambda i: (i, 0)),
            pl.BlockSpec((hidden, step), lambda i: (0, i)),
        ],
        out_specs=pl.BlockSpec((step, (parts + 1) * hidden), lambda i: (i, 0)),
        compiler_params=pltpu.CompilerParams(vmem_limit_bytes=VMEM_LIMIT),
        cost_estimate=pl.CostEstimate(
            flops=0, bytes_accessed=6 * (w_gu.size + w_down.size), transcendentals=0
        ),
        name="round_shares",
    )(flat_pairs(w_gu), w_down)


def gather_first(n_dp, n_mp, own, gains, cotangent, live, collective_id, chunks=2):
    rows, width = own.shape
    local = gains.shape[1]
    lanes = jnp.arange(128, dtype=jnp.int32) // local
    place = lax.rem(lax.axis_index("mp"), 128 // local)
    if n_mp * local < 128:
        place = lax.rem(lax.axis_index("dp") * n_mp + lax.axis_index("mp"), 128 // local)
    tile = jnp.where(
        (lanes == place)[None, :], jnp.tile(gains, (1, 128 // local)), 0.0
    )
    tile = jnp.concatenate([tile, jnp.zeros((6, 128), jnp.float32)], axis=0)

    block = 64 if rows % 64 == 0 else rows

    def kernel(
        own_ref,
        tile_ref,
        cotangent_ref,
        live_ref,
        normed_ref,
        gain_ref,
        base_ref,
        branch_ref,
        all_ref,
        first,
        second,
        *sems,
    ):
        me = lax.axis_index("mp")
        exchange = Exchange(n_dp, n_mp, sems[:4])
        stream = LineGather(n_mp, rows, chunks, own_ref, all_ref, sems[4:])
        exchange.barrier()
        first[me] = tile_ref[...]
        copies = exchange.swap("mp", lambda peer: tile_ref, first)
        for chunk in range(chunks):
            stream.send_own(chunk)
        all_ref[rows_at(me * rows, rows), :] = own_ref[...]
        for copy in copies:
            copy.wait()
        dp = lax.axis_index("dp")
        second[dp] = first[...]
        copies = exchange.swap("dp", lambda peer: first, second)

        def enter(i, carry):
            span = rows_at(i * block, block)
            value = cotangent_ref[span, :].astype(jnp.float32) * live_ref[span, :]
            base_ref[span, :] = value
            branch_ref[span, :] = value.astype(jnp.bfloat16)
            return carry

        lax.fori_loop(0, rows // block, enter, 0)
        for copy in copies:
            copy.wait()
        gain_ref[...] = jnp.zeros_like(gain_ref)
        for d in range(n_dp):
            for m in range(n_mp):
                cols = pl.ds(tile_of(d, m, n_mp, local) * 128, 128)
                gain_ref[:, cols] += second[d, m]
        def norm(block_id):
            def body(i, carry):
                span = rows_at(block_id * rows + i * block, block)
                value = all_ref[span, :].astype(jnp.float32)
                inverse = lax.rsqrt(jnp.mean(value * value, axis=1, keepdims=True) + norm_eps)
                normed_ref[span, :] = (value * inverse * gain_ref[0:1, :]).astype(jnp.bfloat16)
                return carry

            lax.fori_loop(0, rows // block, body, 0)

        def step_of(step, carry):
            @pl.when(step > 0)
            def _():
                for chunk in range(chunks):
                    stream.forward_chunk(step, chunk, step < n_mp - 1)

            @pl.when(me + step < n_mp)
            def _():
                norm(me + step)

            @pl.when((me - step >= 0) & (step > 0))
            def _():
                norm(me - step)

            return carry

        lax.fori_loop(0, n_mp, step_of, 0)
        stream.finish(False)

    half = jnp.bfloat16
    return pl.pallas_call(
        kernel,
        out_shape=[
            jax.ShapeDtypeStruct((n_mp * rows, width), half),
            jax.ShapeDtypeStruct((8, width), jnp.float32),
            jax.ShapeDtypeStruct((rows, width), jnp.float32),
            jax.ShapeDtypeStruct((rows, width), half),
        ],
        in_specs=[VMEM] * 4,
        out_specs=[VMEM] * 4,
        scratch_shapes=[
            pltpu.VMEM((n_mp * rows, width), half),
            pltpu.VMEM((n_mp, 8, 128), jnp.float32),
            pltpu.VMEM((n_dp, n_mp, 8, 128), jnp.float32),
        ]
        + exchange_sems(n_dp, n_mp)
        + gather_sems(n_mp, chunks),
        compiler_params=pltpu.CompilerParams(
            collective_id=collective_id, has_side_effects=True, vmem_limit_bytes=VMEM_LIMIT
        ),
        cost_estimate=pl.CostEstimate(
            flops=0, bytes_accessed=200 * own.size * own.dtype.itemsize, transcendentals=0
        ),
        name="gather_first",
    )(own, tile, cotangent, live)


def dot_t(left, right):
    return lax.dot_general(
        left, right, (((1,), (1,)), ((), ())), preferred_element_type=jnp.float32
    )


def t_dot(left, right):
    return lax.dot_general(
        left, right, (((0,), (0,)), ((), ())), preferred_element_type=jnp.float32
    )


def dot(left, right):
    return jnp.dot(left, right, preferred_element_type=jnp.float32)


def probability(raw):
    return 1.0 / (1.0 + jnp.exp(math.log(SEQ) - raw * (1.0 / math.sqrt(HDIM))))


def rotated(values, cosine, sine, backward=False):
    turned = pltpu.roll(values, HDIM // 2, 1) * sine
    return values * cosine - turned if backward else values * cosine + turned


def scatter_rows(
    n,
    lhs,
    rhs,
    rhs_start,
    own_rows,
    epilogue,
    gains,
    gain_row,
    collective_id,
    heads=None,
    extra=None,
    extra_right=None,
    other_gain=None,
    grad_lefts=None,
    grad_right=None,
    n_dp=1,
    chunks=2,
):
    total_rows = lhs[0].shape[0]
    rows = total_rows // n
    width = gains.shape[1]
    size = rows // chunks
    tile = 512
    has_norm, has_gain = epilogue in ("forward", "backward"), epilogue in ("backward", "last")
    count = len(lhs)
    block = 32
    if heads is not None:
        inner_width = rhs_start // 3
        head_count = inner_width // HDIM
        pieces = [inner_width]
    else:
        pieces = [a.shape[1] for a in lhs]
    depth = sum(pieces)
    if extra_right is not None:
        extra_width = extra_right[0].shape[1] - extra_right[1]

    def kernel(*refs):
        refs = list(refs)

        def take(k):
            return [refs.pop(0) for _ in range(k)]

        left_refs = take(count)
        (right_hbm,) = take(1)
        (gain_ref,) = take(1)
        own_hbm = take(len(own_rows))
        if heads is not None:
            cosine_ref, sine_ref, mask_ref = take(3)
        if other_gain is not None:
            (other_ref,) = take(1)
            grad_hbm = take(3)
        extra_ref = take(1)[0] if extra is not None else None
        extra_right_hbm = take(1)[0] if extra_right is not None else None
        outs = take(1 + has_gain)
        owned_ref = take(1)[0] if other_gain is not None else None
        normed = take(1)[0] if has_norm else None
        if heads is not None:
            query_ref, key_ref, value_ref, mixed_ref = take(4)
        extra_whole = take(1)[0] if extra is not None else None
        if extra_right is not None:
            (extra_out,) = take(1)
        right, held, sent, part = take(4)
        joined_ref = take(1)[0] if heads is not None else None
        right_sem, send_sems, recv_sems = take(3)
        own, own_sems = take(len(own_rows)), take(1)[0]
        own_loads = [
            pltpu.make_async_copy(hbm, ref, own_sems.at[k])
            for k, (hbm, ref) in enumerate(zip(own_hbm, own))
        ]
        me = lax.axis_index("mp")
        fetch = pltpu.make_async_copy(
            right_hbm.at[:, pl.ds(rhs_start, depth)], right, right_sem
        )
        fetch.start()
        if heads is not None:
            (joined_sem,) = take(1)
            fetch_joined = pltpu.make_async_copy(
                right_hbm.at[:, pl.ds(0, rhs_start)], joined_ref, joined_sem
            )
            fetch_joined.start()
        if extra is not None:
            (extra_sem,) = take(1)
            extra_sems = take(4)
            if extra_right is None:
                extra_gather = LineGather(n, rows, 1, extra_ref, extra_whole, extra_sems)
                extra_local = pltpu.make_async_copy(extra_ref, extra_gather.at(me, 0), extra_sem)
                extra_local.start()
            else:
                extra_all, extra_right_ref, extra_right_sem = take(3)
                extra_gather = LineGather(n, rows, 1, extra_ref, extra_all, extra_sems)
                extra_fetch = pltpu.make_async_copy(
                    extra_right_hbm.at[:, pl.ds(extra_right[1], extra_width)],
                    extra_right_ref,
                    extra_right_sem,
                )
                extra_fetch.start()

                def extra_product(block_id):
                    @pl.when((block_id >= 0) & (block_id < n))
                    def _():
                        span = rows_at(block_id * rows, rows)
                        extra_out[span, :] = dot(
                            extra_all[span, :], extra_right_ref[...]
                        ).astype(jnp.bfloat16)
        if other_gain is not None:
            gain_sum, table, first, middle, second = take(5)
            exchange = Exchange(n_dp, n, take(4))
            *grad_left_refs, grad_right_ref, grad_load_sems = take(4)
            grad_loads = [
                pltpu.make_async_copy(hbm, ref, grad_load_sems.at[k])
                for k, (hbm, ref) in enumerate(zip(grad_hbm, [*grad_left_refs, grad_right_ref]))
            ]
            for load in grad_loads:
                load.start()
            grads, paired, landed = take(3)
            pair_send, pair_recv, land_send, land_recv = take(4)
            dp = lax.axis_index("dp")
            core, chip = lax.rem(dp, 2), dp // 2
            chips, share = n_dp // 2, landed.shape[1]
            exchange.barrier()
            pair_copies = [
                pltpu.make_async_remote_copy(
                    src_ref=grads.at[rows_at((2 * q + 1 - core) * share, share)],
                    dst_ref=paired.at[q],
                    send_sem=pair_send.at[q],
                    recv_sem=pair_recv.at[q],
                    device_id={"dp": dp + 1 - 2 * core},
                    device_id_type=MESH,
                )
                for q in range(chips)
            ]
            land_copies = [
                pltpu.make_async_remote_copy(
                    src_ref=paired.at[lax.rem(chip + k, chips)],
                    dst_ref=landed.at[k - 1],
                    send_sem=land_send.at[k - 1],
                    recv_sem=land_recv.at[k - 1],
                    device_id={"dp": 2 * lax.rem(chip + k, chips) + core},
                    device_id_type=MESH,
                )
                for k in range(1, chips)
            ]

            def make_grads():
                for load in grad_loads:
                    load.wait()
                start, narrow = 0, 256
                for k, right_ref in enumerate([*left_refs, grad_right_ref]):
                    left_ref = grad_left_refs[0 if k < count else 1]

                    def column(i, carry, start=start, left_ref=left_ref, right_ref=right_ref):
                        grads[:, rows_at(start + i * narrow, narrow)] = t_dot(
                            left_ref[...], right_ref[:, rows_at(i * narrow, narrow)]
                        ).astype(jnp.bfloat16)
                        return carry

                    lax.fori_loop(0, right_ref.shape[1] // narrow, column, 0)
                    start += right_ref.shape[1]
                for copy in pair_copies:
                    copy.start()
                for copy in pair_copies:
                    copy.wait()

                def add(i, carry):
                    span = rows_at(i * block, block)
                    for q in range(chips):
                        own_span = rows_at((2 * q + core) * share + i * block, block)
                        paired[q, span, :] = (
                            paired[q, span, :].astype(jnp.float32)
                            + grads[own_span, :].astype(jnp.float32)
                        ).astype(jnp.bfloat16)
                    return carry

                lax.fori_loop(0, share // block, add, 0)
                for copy in land_copies:
                    copy.start()

            def land():
                for copy in land_copies:
                    copy.wait()

                def add(i, carry):
                    span = rows_at(i * block, block)
                    total = paired[chip, span, :].astype(jnp.float32)
                    for k in range(chips - 1):
                        total = total + landed[k, span, :].astype(jnp.float32)
                    owned_ref[span, :] = total
                    return carry

                lax.fori_loop(0, share // block, add, 0)

        else:
            gain_sum = outs[1] if has_gain else None
            neighbour_barrier(n)
        if extra is not None:
            extra_gather.send_own(0)
        if extra_right is not None:
            extra_all[rows_at(me * rows, rows), :] = extra_ref[...]
            extra_fetch.wait()
        if heads is not None:
            turn = 256
            fetch_joined.wait()

            def enter(i, carry):
                span = rows_at(i * turn, turn)
                cosine, sine = cosine_ref[span, :], sine_ref[span, :]
                row_vals = left_refs[0][span, :]
                for k, target in ((0, query_ref), (1, key_ref), (2, value_ref)):
                    piece = dot(row_vals, joined_ref[:, pl.ds(k * inner_width, inner_width)])
                    for h in range(head_count):
                        value = piece[:, h * HDIM : (h + 1) * HDIM]
                        if k < 2:
                            value = rotated(value, cosine, sine)
                        target[span, pl.ds(h * HDIM, HDIM)] = value.astype(jnp.bfloat16)
                return carry

            lax.fori_loop(0, total_rows // turn, enter, 0)
        for load in own_loads:
            load.start()
        fetch.wait()

        def attend(block_id):
            span = rows_at(block_id * rows, rows)
            row_pos = block_id * rows + lax.broadcasted_iota(jnp.int32, (rows, rows), 0)

            def against(kb, totals):
                other = rows_at(kb * rows, rows)
                col_pos = kb * rows + lax.broadcasted_iota(jnp.int32, (rows, rows), 1)
                allowed = jnp.where(col_pos <= row_pos, mask_ref[:, other], 0.0)
                out = []
                for h in range(head_count):
                    cols = pl.ds(h * HDIM, HDIM)
                    raw = dot_t(query_ref[span, cols], key_ref[other, cols])
                    prob = probability(raw) * allowed
                    out.append(
                        totals[h]
                        + jnp.dot(
                            prob.astype(jnp.bfloat16),
                            value_ref[other, cols],
                            preferred_element_type=jnp.float32,
                        )
                    )
                return tuple(out)

            start = tuple(jnp.zeros((rows, HDIM), jnp.float32) for _ in range(head_count))
            totals = lax.fori_loop(0, block_id + 1, against, start)
            for h in range(head_count):
                mixed_ref[span, pl.ds(h * HDIM, HDIM)] = totals[h].astype(jnp.bfloat16)

        def product(block_id):
            if heads is not None:
                attend(block_id)
            sources = [mixed_ref] if heads is not None else left_refs

            def column(ct, carry):
                cols = rows_at(ct * tile, tile)
                total, start = None, 0
                for source, piece in zip(sources, pieces):
                    term = dot_t(
                        source[rows_at(block_id * rows, rows), :],
                        right[cols, pl.ds(start, piece)],
                    )
                    start += piece
                    total = term if total is None else total + term
                part[:, cols] = total
                return carry

            lax.fori_loop(0, width // tile, column, 0)

        def hop(block_id, chunk, rightward):
            peer = me + 1 if rightward else me - 1
            slot = block_id if rightward else jnp.where(block_id == peer, n, block_id)
            return remote(
                sent.at[block_id, pl.ds(chunk * size, size)],
                held.at[slot, pl.ds(chunk * size, size)],
                send_sems.at[block_id * chunks + chunk],
                recv_sems.at[slot * chunks + chunk],
                peer,
            )

        def arrival(slot, chunk):
            ref = held.at[slot, pl.ds(chunk * size, size)]
            return remote(
                ref, ref, send_sems.at[chunk], recv_sems.at[slot * chunks + chunk], me
            )

        def add_rows(block_id, chunk, slots):
            def body(i, carry):
                span = rows_at(chunk * size + i * block, block)
                value = part[span, :]
                for slot in slots:
                    value = value + held[slot, span, :].astype(jnp.float32)
                sent[block_id, span, :] = value.astype(jnp.bfloat16)
                return carry

            lax.fori_loop(0, size // block, body, 0)

        def relay(block_id, rightward, inner):
            product(block_id)
            for chunk in range(chunks):

                @pl.when(inner)
                def _():
                    arrival(block_id, chunk).wait_recv()
                    add_rows(block_id, chunk, [block_id])

                @pl.when(jnp.logical_not(inner))
                def _():
                    add_rows(block_id, chunk, [])

                hop(block_id, chunk, rightward).start()

        def step_of(step, carry):
            @pl.when((step >= me + 1) & (me < n - 1))
            def _():
                relay(me + n - step, True, me > 0)

            @pl.when((step >= n - me) & (me > 0))
            def _():
                relay(me - n + step, False, me < n - 1)

            if extra is not None:

                @pl.when(step < n - 1)
                def _():
                    extra_gather.forward(step)
                    if extra_right is not None:
                        extra_product(me - step)
                        extra_product(me + step)

            if other_gain is not None:
                pl.when(step == 1)(make_grads)

            return carry

        lax.fori_loop(1, n, step_of, 0)
        product(me)
        if extra_right is not None:
            extra_product(me)
        for load in own_loads:
            load.wait()
        if has_gain:
            gain_sum[...] = jnp.zeros_like(gain_sum)
        for chunk in range(chunks):

            @pl.when(me > 0)
            def _():
                arrival(me, chunk).wait_recv()

            @pl.when(me < n - 1)
            def _():
                arrival(n, chunk).wait_recv()

            def body(i, carry):
                span = rows_at(chunk * size + i * block, block)
                total = part[span, :]
                zero = jnp.zeros_like(total)
                total = total + jnp.where(me > 0, held[me, span, :].astype(jnp.float32), zero)
                total = total + jnp.where(
                    me < n - 1, held[n, span, :].astype(jnp.float32), zero
                )
                gain = gain_ref[gain_row : gain_row + 1, :]
                if epilogue == "residual":
                    outs[0][span, :] = (own[0][span, :] + total).astype(jnp.bfloat16)
                elif epilogue == "forward":
                    value = own[0][span, :].astype(jnp.float32) + total
                    outs[0][span, :] = value
                    inverse = lax.rsqrt(
                        jnp.mean(value * value, axis=1, keepdims=True) + norm_eps
                    )
                    normed[span, :] = (value * inverse * gain).astype(jnp.bfloat16)
                else:
                    value = own[0][span, :].astype(jnp.float32)
                    inverse = lax.rsqrt(
                        jnp.mean(value * value, axis=1, keepdims=True) + norm_eps
                    )
                    unit = value * inverse
                    scaled = total * gain
                    inner = jnp.mean(scaled * unit, axis=1, keepdims=True)
                    result = own[1][span, :] + inverse * (scaled - unit * inner)
                    outs[0][span, :] = result
                    gain_sum[...] += jnp.sum(
                        (total * unit).reshape(block // 8, 8, width), axis=0
                    )
                    if has_norm:
                        normed[span, :] = result.astype(jnp.bfloat16)
                return carry

            lax.fori_loop(0, size // block, body, 0)
        if extra is not None:
            extra_gather.finish()
        if extra_right is not None:
            extra_local = pltpu.make_async_copy(extra_all, extra_whole, extra_sem)
            extra_local.start()
            extra_product(me - (n - 1))
            extra_product(me + (n - 1))
        if extra is not None:
            extra_local.wait()
        if other_gain is not None:
            local = width // (n * n_dp)
            for row, source in ((0, gain_sum), (1, other_ref)):
                total = jnp.sum(source[...], axis=0, keepdims=True)
                for d in range(n_dp):
                    for m in range(n):
                        start = tile_of(d, m, n, local) * 128
                        table[m, d, row : row + 1, :] = total[:, start : start + 128]
            copies = exchange.swap("mp", lambda peer: table.at[peer], first)
            first[me] = table[me]
            for copy in copies:
                copy.wait()
            total = first[0]
            for m in range(1, n):
                total = total + first[m]
            middle[...] = total
            copies = exchange.swap("dp", lambda peer: middle.at[peer], second)
            second[dp] = middle[dp]
            land()
            for copy in copies:
                copy.wait()
            total = second[0]
            for d in range(1, n_dp):
                total = total + second[d]
            outs[1][...] = total

        def sends(step, carry):
            for chunk in range(chunks):

                @pl.when((step >= me + 1) & (me < n - 1))
                def _():
                    hop(me + n - step, chunk, True).wait_send()

                @pl.when((step >= n - me) & (me > 0))
                def _():
                    hop(me - n + step, chunk, False).wait_send()

            return carry

        lax.fori_loop(1, n, sends, 0)

    out_type = jnp.bfloat16 if epilogue == "residual" else jnp.float32
    out_shape = [jax.ShapeDtypeStruct((rows, width), out_type)]
    out_specs = [VMEM]
    if has_gain:
        out_shape.append(
            jax.ShapeDtypeStruct((8, width) if other_gain is None else (2, 128), jnp.float32)
        )
        out_specs.append(VMEM)
    if other_gain is not None:
        share = width // n_dp
        grad_width = sum(pieces) + grad_right.shape[1]
        out_shape.append(jax.ShapeDtypeStruct((share, grad_width), jnp.float32))
        out_specs.append(VMEM)
    scratch = [
        pltpu.VMEM((width, depth), jnp.bfloat16),
        pltpu.VMEM((n + 1, rows, width), jnp.bfloat16),
        pltpu.VMEM((n, rows, width), jnp.bfloat16),
        pltpu.VMEM((rows, width), jnp.float32),
    ]
    if heads is not None:
        scratch.append(pltpu.VMEM((width, rhs_start), jnp.bfloat16))
    if has_norm:
        out_shape.append(jax.ShapeDtypeStruct((rows, width), jnp.bfloat16))
        out_specs.append(VMEM)
    scratch += [
        pltpu.SemaphoreType.DMA,
        pltpu.SemaphoreType.DMA((n * chunks,)),
        pltpu.SemaphoreType.DMA(((n + 1) * chunks,)),
    ]
    scratch += [pltpu.VMEM(x.shape, x.dtype) for x in own_rows]
    scratch.append(pltpu.SemaphoreType.DMA((len(own_rows),)))
    head_args = []
    if heads is not None:
        scratch.append(pltpu.SemaphoreType.DMA)
        head_args = list(heads)
        out_shape += [jax.ShapeDtypeStruct((total_rows, inner_width), jnp.bfloat16)] * 4
        out_specs += [VMEM] * 4
    extra_args = []
    if extra is not None:
        out_shape.append(jax.ShapeDtypeStruct((total_rows, width), jnp.bfloat16))
        out_specs.append(ANY)
        scratch += [pltpu.SemaphoreType.DMA] + gather_sems(n, 1)
        extra_args = [extra]
    if extra_right is not None:
        out_shape.append(jax.ShapeDtypeStruct((total_rows, extra_width), jnp.bfloat16))
        out_specs.append(VMEM)
        scratch += [
            pltpu.VMEM((total_rows, width), jnp.bfloat16),
            pltpu.VMEM((width, extra_width), jnp.bfloat16),
            pltpu.SemaphoreType.DMA,
        ]
        extra_args.append(extra_right[0])
    late_args = []
    if other_gain is not None:
        head_args.append(other_gain)
        late_args = [*grad_lefts, grad_right]
        scratch += [
            pltpu.VMEM((8, width), jnp.float32),
            pltpu.VMEM((n, n_dp, 2, 128), jnp.float32),
            pltpu.VMEM((n, n_dp, 2, 128), jnp.float32),
            pltpu.VMEM((n_dp, 2, 128), jnp.float32),
            pltpu.VMEM((n_dp, 2, 128), jnp.float32),
        ] + exchange_sems(n_dp, n)
        scratch += [pltpu.VMEM(x.shape, x.dtype) for x in late_args]
        scratch.append(pltpu.SemaphoreType.DMA((len(late_args),)))
        chips = n_dp // 2
        scratch.append(pltpu.VMEM((width, grad_width), jnp.bfloat16))
        scratch.append(pltpu.VMEM((chips, share, grad_width), jnp.bfloat16))
        scratch.append(pltpu.VMEM((chips - 1, share, grad_width), jnp.bfloat16))
        scratch += [pltpu.SemaphoreType.DMA((chips,))] * 2
        scratch += [pltpu.SemaphoreType.DMA((chips - 1,))] * 2
    flops = 2 * total_rows * depth * width
    return pl.pallas_call(
        kernel,
        out_shape=out_shape,
        in_specs=[VMEM] * count
        + [ANY]
        + [VMEM]
        + [ANY] * len(own_rows)
        + [VMEM] * len(head_args)
        + [ANY] * len(late_args)
        + [VMEM if extra_right is not None else ANY] * min(1, len(extra_args))
        + [ANY] * max(0, len(extra_args) - 1),
        out_specs=out_specs,
        scratch_shapes=scratch,
        compiler_params=pltpu.CompilerParams(
            collective_id=collective_id, has_side_effects=True, vmem_limit_bytes=VMEM_LIMIT
        ),
        cost_estimate=pl.CostEstimate(
            flops=flops, bytes_accessed=300_000_000, transcendentals=0
        ),
        name="scatter_" + epilogue,
    )(*lhs, rhs, gains, *own_rows, *head_args, *late_args, *extra_args)


def feed_forward(n, normed, branch_grad, weights, second, gains, collective_id, halves=1, hops=4):
    rows, width = normed.shape
    total_rows = n * rows
    hidden = weights.shape[1] // 3
    count, parcels = hops, halves
    part_size = rows // hops
    tile = min(1024, hidden)
    block = min(32, part_size)
    narrow = min(256, hidden)
    per = hidden // narrow
    pieces = 3 * per
    before = pieces // 6
    between = (pieces - 2 * before) // (count + 1)
    tall = min(1024, width)

    def kernel(
        normed_ref,
        branch_hbm,
        weights_hbm,
        second_ref,
        gain_ref,
        result_ref,
        rounded_ref,
        gain_sum,
        grads_hbm,
        act_hbm,
        gate_hbm,
        up_hbm,
        weight_ref,
        branch_ref,
        all_ref,
        held,
        sent,
        own_part,
        act_ref,
        gate_ref,
        up_ref,
        piece_ref,
        load_sems,
        stage_sems,
        piece_sems,
        grad_sems,
        send_sems,
        recv_sems,
        *gather_refs,
    ):
        me = lax.axis_index("mp")
        middle = (me > 0) & (me < n - 1)
        loads = [
            pltpu.make_async_copy(weights_hbm, weight_ref, load_sems.at[0]),
            pltpu.make_async_copy(branch_hbm, branch_ref, load_sems.at[1]),
        ]
        for load in loads:
            load.start()
        gather = LineGather(n, rows, parcels, normed_ref, all_ref, gather_refs)
        neighbour_barrier(n)
        for parcel in range(parcels):
            gather.send_own(parcel)
        all_ref[rows_at(me * rows, rows), :] = normed_ref[...]
        for load in loads:
            load.wait()

        def hop(block_id, chunk, rightward):
            peer = me + 1 if rightward else me - 1
            slot = block_id if rightward else jnp.where(block_id == peer, n, block_id)
            return remote(
                sent.at[block_id, pl.ds(chunk * part_size, part_size)],
                held.at[slot, pl.ds(chunk * part_size, part_size)],
                send_sems.at[block_id * count + chunk],
                recv_sems.at[slot * count + chunk],
                peer,
            )

        def arrival(slot, chunk):
            ref = held.at[slot, pl.ds(chunk * part_size, part_size)]
            return remote(
                ref, ref, send_sems.at[chunk], recv_sems.at[slot * count + chunk], me
            )

        def stages(block_id, chunk, size):
            span = rows_at(block_id * rows + chunk * size, size)
            return [
                pltpu.make_async_copy(
                    ref.at[pl.ds(chunk * size, size)], hbm.at[span], stage_sems.at[chunk * 3 + k]
                )
                for k, (ref, hbm) in enumerate(
                    ((act_ref, act_hbm), (gate_ref, gate_hbm), (up_ref, up_hbm))
                )
            ]

        def compute(block_id, chunk, size, first):
            here = pl.ds(chunk * size, size)
            span = rows_at(block_id * rows + chunk * size, size)

            @pl.when(jnp.logical_not(first))
            def _():
                for stage in stages(block_id, chunk, size):
                    stage.wait()

            def units(ct, carry):
                cols = rows_at(ct * tile, tile)
                row_vals, branch = all_ref[span, :], branch_ref[span, :]
                gate = dot(row_vals, weight_ref[:, cols])
                up = dot(row_vals, weight_ref[:, rows_at(hidden + ct * tile, tile)])
                act_grad = dot(branch, weight_ref[:, rows_at(2 * hidden + ct * tile, tile)])
                sigma = 1.0 / (1.0 + jnp.exp(-gate))
                silu = gate * sigma
                act_ref[here, cols] = (silu * up).astype(jnp.bfloat16)
                gate_ref[here, cols] = (
                    act_grad * up * sigma * (1.0 + gate * (1.0 - sigma))
                ).astype(jnp.bfloat16)
                up_ref[here, cols] = (act_grad * silu).astype(jnp.bfloat16)
                return carry

            lax.fori_loop(0, hidden // tile, units, 0)
            for stage in stages(block_id, chunk, size):
                stage.start()

            def columns(ct, carry):
                cols = rows_at(ct * tile, tile)
                total = dot_t(gate_ref[here, :], weight_ref[cols, pl.ds(0, hidden)])
                total += dot_t(up_ref[here, :], weight_ref[cols, pl.ds(hidden, hidden)])

                @pl.when(block_id == me)
                def _():
                    own_part[here, cols] = total

                @pl.when(block_id != me)
                def _():
                    sent[block_id, here, cols] = total.astype(jnp.bfloat16)

                return carry

            lax.fori_loop(0, width // tile, columns, 0)

            @pl.when((me == 0) & (block_id > me))
            def _():
                for k in range(size // part_size):
                    hop(block_id, chunk * (size // part_size) + k, True).start()

            @pl.when((me == n - 1) & (block_id < me))
            def _():
                for k in range(size // part_size):
                    hop(block_id, chunk * (size // part_size) + k, False).start()

        def forward(step, parcel):
            gather.forward_chunk(step, parcel, step < n - 1)

        def forward_whole(step):
            for parcel in range(parcels):
                forward(step, parcel)

        def step_of(step, carry):
            def side_of(side, carry):
                block_id = me + (1 - 2 * side) * step
                valid = (block_id >= 0) & (block_id < n) & ((step > 0) | (side == 0))

                @pl.when(middle & (step > 0) & (step < n - 1) & (side == 1))
                def _():
                    forward_whole(step + 1)

                @pl.when(middle & valid)
                def _():
                    compute(block_id, 0, rows, step == 0)

                @pl.when(middle & (step == 0) & (side == 0))
                def _():
                    forward_whole(1)

                for half in range(halves):

                    @pl.when(jnp.logical_not(middle) & valid)
                    def _():
                        pl.when(step > 0)(lambda: forward(step, half))
                        compute(block_id, half, rows // halves, step == 0)

                return carry

            return lax.fori_loop(0, 2, side_of, carry)

        lax.fori_loop(0, n, step_of, 0)
        @pl.when(middle)
        def _():
            for stage in stages(me, 0, rows):
                stage.wait()

        @pl.when(jnp.logical_not(middle))
        def _():
            for half in range(halves):
                for stage in stages(me, half, rows // halves):
                    stage.wait()


        def load_of(source, index, slot):
            return pltpu.make_async_copy(
                source.at[:, rows_at(lax.rem(index, per) * narrow, narrow)],
                piece_ref.at[slot],
                piece_sems.at[slot],
            )

        def load_piece(index):
            for k, source in enumerate((gate_hbm, up_hbm, act_hbm)):

                @pl.when(index // per == k)
                def _():
                    load_of(source, index, lax.rem(index, 2)).start()

        def grad_copy(index):
            cols = rows_at(index * narrow, narrow)
            return pltpu.make_async_copy(
                weight_ref.at[:, cols], grads_hbm.at[:, cols], grad_sems.at[index]
            )

        def grad_piece(index, carry):
            slot = lax.rem(index, 2)
            load_of(gate_hbm, index, slot).wait()

            @pl.when(index + 1 < pieces)
            def _():
                load_piece(index + 1)

            cols = rows_at(index * narrow, narrow)
            for start in range(0, width, tall):
                span = pl.ds(start, tall)

                @pl.when(index < 2 * per)
                def _():
                    weight_ref[span, cols] = t_dot(all_ref[:, span], piece_ref[slot]).astype(
                        jnp.bfloat16
                    )

                @pl.when(index >= 2 * per)
                def _():
                    weight_ref[span, cols] = t_dot(branch_ref[:, span], piece_ref[slot]).astype(
                        jnp.bfloat16
                    )

            grad_copy(index).start()
            return carry

        load_piece(0)

        def add_rows(block_id, chunk):
            def body(i, carry):
                span = rows_at(chunk * part_size + i * block, block)
                value = sent[block_id, span, :].astype(jnp.float32)
                value = value + held[block_id, span, :].astype(jnp.float32)
                sent[block_id, span, :] = value.astype(jnp.bfloat16)
                return carry

            lax.fori_loop(0, part_size // block, body, 0)

        def relay_side(step, chunk, rightward):
            block_id = step if rightward else n - 1 - step
            has = (me > 0) & (step > me) if rightward else (me < n - 1) & (n - 1 - step < me)

            @pl.when(has)
            def _():
                arrival(block_id, chunk).wait_recv()
                add_rows(block_id, chunk)
                hop(block_id, chunk, rightward).start()

        def relay_chunk(step, chunk, near):
            rightward_first = 2 * me < n

            @pl.when(rightward_first)
            def _():
                relay_side(step, chunk, near)

            @pl.when(jnp.logical_not(rightward_first))
            def _():
                relay_side(step, chunk, not near)

        def relay_of(step, carry):
            for chunk in range(count):
                relay_chunk(step, chunk, True)
            for chunk in range(count):
                relay_chunk(step, chunk, False)
            return carry

        lax.fori_loop(1, n - 1, relay_of, 0)
        lax.fori_loop(0, before, grad_piece, 0)

        def last_relay(chunk, carry):
            @pl.when(chunk < count)
            def _():
                relay_chunk(n - 1, chunk, True)

            start = before + chunk * between
            lax.fori_loop(start, start + between, grad_piece, 0)

            @pl.when(chunk > 0)
            def _():
                relay_chunk(n - 1, chunk - 1, False)

            return carry

        lax.fori_loop(0, count + 1, last_relay, 0)
        lax.fori_loop(before + (count + 1) * between, pieces, grad_piece, 0)
        gain_sum[...] = jnp.zeros_like(gain_sum)
        for chunk in range(count):

            @pl.when(me > 0)
            def _():
                arrival(me, chunk).wait_recv()

            @pl.when(me < n - 1)
            def _():
                arrival(n, chunk).wait_recv()

            def body(i, carry):
                span = rows_at(chunk * part_size + i * block, block)
                total = own_part[span, :]
                zero = jnp.zeros_like(total)
                total = total + jnp.where(me > 0, held[me, span, :].astype(jnp.float32), zero)
                total = total + jnp.where(
                    me < n - 1, held[n, span, :].astype(jnp.float32), zero
                )
                value = second_ref[span, :]
                inverse = lax.rsqrt(jnp.mean(value * value, axis=1, keepdims=True) + norm_eps)
                unit = value * inverse
                scaled = total * gain_ref[1:2, :]
                inner = jnp.mean(scaled * unit, axis=1, keepdims=True)
                base = branch_ref[
                    rows_at(me * rows + chunk * part_size + i * block, block), :
                ].astype(jnp.float32)
                result = base + inverse * (scaled - unit * inner)
                result_ref[span, :] = result
                rounded_ref[span, :] = result.astype(jnp.bfloat16)
                gain_sum[...] += jnp.sum((total * unit).reshape(block // 8, 8, width), axis=0)
                return carry

            lax.fori_loop(0, part_size // block, body, 0)
        gather.finish(False)

        def sends(block_id, carry):
            for chunk in range(count):

                @pl.when((block_id > me) & (me < n - 1))
                def _():
                    hop(block_id, chunk, True).wait_send()

                @pl.when((block_id < me) & (me > 0))
                def _():
                    hop(block_id, chunk, False).wait_send()

            return carry

        lax.fori_loop(0, n, sends, 0)

        def grads_out(index, carry):
            grad_copy(index).wait()
            return carry

        lax.fori_loop(0, pieces, grads_out, 0)

    half = jnp.bfloat16
    return pl.pallas_call(
        kernel,
        out_shape=[
            jax.ShapeDtypeStruct((rows, width), jnp.float32),
            jax.ShapeDtypeStruct((rows, width), half),
            jax.ShapeDtypeStruct((8, width), jnp.float32),
            jax.ShapeDtypeStruct((width, 3 * hidden), half),
        ]
        + [jax.ShapeDtypeStruct((total_rows, hidden), half)] * 3,
        in_specs=[VMEM, ANY, ANY, VMEM, VMEM],
        out_specs=[VMEM] * 3 + [ANY] * 4,
        scratch_shapes=[
            pltpu.VMEM((width, 3 * hidden), half),
            pltpu.VMEM((total_rows, width), half),
            pltpu.VMEM((total_rows, width), half),
            pltpu.VMEM((n + 1, rows, width), half),
            pltpu.VMEM((n, rows, width), half),
            pltpu.VMEM((rows, width), jnp.float32),
        ]
        + [pltpu.VMEM((rows, hidden), half)] * 3
        + [
            pltpu.VMEM((2, total_rows, narrow), half),
            pltpu.SemaphoreType.DMA((2,)),
            pltpu.SemaphoreType.DMA((halves * 3,)),
            pltpu.SemaphoreType.DMA((2,)),
            pltpu.SemaphoreType.DMA((pieces,)),
            pltpu.SemaphoreType.DMA((n * count,)),
            pltpu.SemaphoreType.DMA(((n + 1) * count,)),
        ]
        + gather_sems(n, parcels),
        compiler_params=pltpu.CompilerParams(
            collective_id=collective_id, has_side_effects=True, vmem_limit_bytes=VMEM_LIMIT
        ),
        cost_estimate=pl.CostEstimate(
            flops=16 * total_rows * width * hidden, bytes_accessed=300_000_000, transcendentals=0
        ),
        name="feed_forward",
    )(normed, branch_grad, weights, second, gains)


def attention_backward(queries, keys, values, mixed_grad, cosine, sine, valid_counts):
    total_rows, inner_width = queries.shape
    block = min(256, total_rows)

    def kernel(q_ref, k_ref, v_ref, do_ref, cos_ref, sin_ref, valid_ref, dq_out, dk_out, dv_out, dk_ref, dv_ref):
        dk_ref[...] = jnp.zeros_like(dk_ref)
        dv_ref[...] = jnp.zeros_like(dv_ref)
        for i in range(total_rows // block):
            span = pl.ds(i * block, block)
            upto = (i + 1) * block
            shape = (upto, block)
            key_pos = lax.broadcasted_iota(jnp.int32, shape, 0)
            query_pos = i * block + lax.broadcasted_iota(jnp.int32, shape, 1)
            allowed = jnp.where((key_pos <= query_pos) & (key_pos < valid_ref[0]), 1.0, 0.0)
            query, grad = q_ref[span, :], do_ref[span, :]
            key = k_ref[:upto, :]
            prob = probability(dot_t(key, query)) * allowed
            prob_grad = dot_t(v_ref[:upto, :], grad)
            dv_ref[:upto, :] += jnp.dot(
                prob.astype(jnp.bfloat16), grad, preferred_element_type=jnp.float32
            )
            score_grad = (prob_grad * prob * (1.0 - prob) * (1.0 / math.sqrt(HDIM))).astype(
                jnp.bfloat16
            )
            dk_ref[:upto, :] += jnp.dot(score_grad, query, preferred_element_type=jnp.float32)
            dq = t_dot(score_grad, key)
            dq_out[span, :] = rotated(
                dq, cos_ref[span, :], sin_ref[span, :], True
            ).astype(jnp.bfloat16)
        dk_out[...] = rotated(dk_ref[...], cos_ref[...], sin_ref[...], True).astype(jnp.bfloat16)
        dv_out[...] = dv_ref[...].astype(jnp.bfloat16)

    head = pl.BlockSpec((total_rows, HDIM), lambda h: (0, h))
    table = pl.BlockSpec((total_rows, HDIM), lambda h: (0, 0))
    return pl.pallas_call(
        kernel,
        grid=(inner_width // HDIM,),
        out_shape=[jax.ShapeDtypeStruct((total_rows, inner_width), jnp.bfloat16)] * 3,
        in_specs=[head] * 4 + [table] * 2 + [pl.BlockSpec(memory_space=pltpu.SMEM)],
        out_specs=[head] * 3,
        scratch_shapes=[pltpu.VMEM((total_rows, HDIM), jnp.float32)] * 2,
        compiler_params=pltpu.CompilerParams(vmem_limit_bytes=VMEM_LIMIT),
        cost_estimate=pl.CostEstimate(
            flops=8 * total_rows * total_rows * inner_width,
            bytes_accessed=14 * total_rows * inner_width,
            transcendentals=0,
        ),
        name="attention_backward",
    )(queries, keys, values, mixed_grad, cosine, sine, valid_counts)


def updated(weight, moment, average, gradient, rate):
    moment_new = momentum_decay * moment + (1.0 - momentum_decay) * gradient
    weight_new = weight - rate * (
        (1.0 - momentum_decay) * gradient + momentum_decay * moment_new
    )
    average_new = average_decay * average + (1.0 - average_decay) * weight_new
    return weight_new, moment_new, average_new


def store_update(ins, gradient, outs, rate):
    weight, moment, average = updated(*[ref[...] for ref in ins], gradient, rate)
    outs[0][...] = weight
    outs[1][...] = moment
    outs[2][...] = average
    outs[3][...] = weight.astype(jnp.bfloat16)


def update_all(pairs, parts, flips, sum_ffn, sum_attn, passed, rate):
    jobs = []

    high, two, wide = pairs[0].shape
    tiles = wide // 128
    step = min(64, high)
    stride = tiles * two

    def spread_gradient(g, spread):
        for part in range(two):
            for tile in range(tiles):
                cols = pl.ds(part * wide + tile * 128, 128)
                spread[pl.ds(tile * two + part, step, stride=stride), :] = g[:, cols].astype(
                    jnp.float32
                )
        return spread[...]

    jobs.append(
        (
            [flat_pairs(x) for x in pairs],
            ((step * stride, 128), lambda i: (i, 0)),
            (sum_ffn, (step, two * wide), lambda i: (i, 0)),
            high // step,
            spread_gradient,
        )
    )
    for arrays, total, start in ((flips[0][0], sum_ffn, flips[0][1]), (flips[1][0], sum_attn, flips[1][1])):
        tall, narrow = arrays[0].shape
        rows = min(512, tall)
        jobs.append(
            (
                arrays,
                ((rows, narrow), lambda i: (i, 0)),
                (total, (narrow, rows), lambda i, first=start // rows: (0, first + i)),
                tall // rows,
                lambda g, spread: g[...].astype(jnp.float32).T,
            )
        )
    deep, count, across = parts[0].shape
    jobs.append(
        (
            [x.transpose(1, 0, 2) for x in parts],
            ((None, deep, across), lambda i: (i, 0, 0)),
            (sum_attn, (deep, across), lambda i: (0, i)),
            count,
            lambda g, spread: g[...].astype(jnp.float32),
        )
    )
    starts = [sum(job[3] for job in jobs[:k]) for k in range(len(jobs))]
    steps = sum(job[3] for job in jobs)

    def within(k, index_map):
        return lambda i: index_map(jnp.clip(i - starts[k], 0, jobs[k][3] - 1))

    in_specs, out_specs, args, out_shape = [], [], [], []
    kinds = [jnp.float32] * 3 + [jnp.bfloat16]
    for k, (arrays, (shape, index_map), (total, total_shape, total_map), _, _) in enumerate(jobs):
        spec = pl.BlockSpec(shape, within(k, index_map))
        in_specs += [spec] * 3 + [pl.BlockSpec(total_shape, within(k, total_map))]
        args += [*arrays, total]
        out_specs += [spec] * 4
        out_shape += [jax.ShapeDtypeStruct(arrays[0].shape, kind) for kind in kinds]
    in_specs += [ANY] * len(passed)
    out_specs += [ANY] * len(passed)
    out_shape += [jax.ShapeDtypeStruct(x.shape, x.dtype) for x in passed]

    def body(*refs):
        ins, refs = refs[: len(in_specs)], refs[len(in_specs) :]
        outs, (spread, sems) = refs[: len(out_specs)], refs[len(out_specs) :]
        i = pl.program_id(0)
        copies = [
            pltpu.make_async_copy(ins[4 * len(jobs) + k], outs[4 * len(jobs) + k], sems.at[k])
            for k in range(len(passed))
        ]

        @pl.when(i == 0)
        def _():
            for copy in copies:
                copy.start()

        for k, job in enumerate(jobs):

            @pl.when((i >= starts[k]) & (i < starts[k] + job[3]))
            def _():
                gradient = job[4](ins[4 * k + 3], spread)
                store_update(ins[4 * k : 4 * k + 3], gradient, outs[4 * k : 4 * k + 4], rate)

        @pl.when(i == steps - 1)
        def _():
            for copy in copies:
                copy.wait()

    size = sum(job[0][0].size for job in jobs)
    outs = pl.pallas_call(
        body,
        grid=(steps,),
        out_shape=out_shape,
        in_specs=in_specs,
        out_specs=out_specs,
        scratch_shapes=[
            pltpu.VMEM((step * stride, 128), jnp.float32),
            pltpu.SemaphoreType.DMA((len(passed),)),
        ],
        compiler_params=pltpu.CompilerParams(vmem_limit_bytes=VMEM_LIMIT),
        cost_estimate=pl.CostEstimate(
            flops=10 * size, bytes_accessed=28 * size, transcendentals=0
        ),
        name="update_all",
    )(*args, *passed)
    gu = [
        x.reshape(high, tiles, two, 128).transpose(0, 2, 1, 3).reshape(high, two, wide)
        for x in outs[:4]
    ]
    qkv = [x.transpose(1, 0, 2) for x in outs[12:16]]
    return gu, outs[4:8], outs[8:12], qkv, outs[16:]


def rope_tables(length, half_dim):
    positions = np.arange(length, dtype=np.float32)[:, None]
    inverse_freq = np.power(
        np.float32(rope_base), -np.arange(half_dim, dtype=np.float32) / np.float32(half_dim)
    )
    angles = positions * inverse_freq[None, :]
    cosine, sine = np.cos(angles), np.sin(angles)
    return np.concatenate([cosine, cosine], axis=1), np.concatenate([-sine, sine], axis=1)


def per_device(
    n_dp,
    n_mp,
    tokens,
    cotangent,
    valid_counts,
    w_qkv,
    w_out,
    w_gu,
    w_down,
    gains,
    mom_qkv,
    mom_out,
    mom_gu,
    mom_down,
    mom_gains,
    avg_qkv,
    avg_out,
    avg_gu,
    avg_down,
    avg_gains,
):
    half = jnp.bfloat16
    row_count, width = tokens.shape
    owned, _, local_width = w_qkv.shape
    hidden = w_gu.shape[2]
    valid_len = valid_counts[0]

    attn_part = jnp.concatenate(
        [w_qkv.reshape(owned, 3 * local_width), w_out.T], axis=1
    ).astype(half)
    attn_w = lax.all_gather(attn_part, "dp", axis=0, tiled=True)
    row_ids = lax.axis_index("mp") * row_count + jnp.arange(row_count, dtype=jnp.int32)
    live_rows = (row_ids < valid_len).astype(jnp.float32)[:, None]
    key_mask = (jnp.arange(SEQ, dtype=jnp.int32) < valid_len).astype(jnp.float32)
    ffn_part, tokens_in = lax.optimization_barrier((round_shares(w_gu, w_down), tokens))
    h_first, gain_all, out_grad, own_branch = gather_first(
        n_dp, n_mp, tokens_in, gains, cotangent, live_rows, 1
    )
    ffn_w = lax.all_gather(ffn_part, "dp", axis=0, tiled=True)
    cosine, sine = (jnp.asarray(x, jnp.float32) for x in rope_tables(SEQ, HDIM // 2))

    second, normed_second, queries, keys, values, mixed, branch_grad = scatter_rows(
        n_mp,
        [h_first],
        attn_w,
        3 * local_width,
        [tokens],
        "forward",
        gain_all,
        1,
        2,
        heads=(cosine, sine, key_mask[None, :]),
        extra=own_branch,
    )

    second_grad, own_grad, gain_two, grad_ffn, act, _, _ = feed_forward(
        n_mp, normed_second, branch_grad, ffn_w, second, gain_all, 3
    )
    sum_ffn = lax.psum_scatter(grad_ffn, "dp", scatter_dimension=0, tiled=True)
    block_out, attn_grad, mixed_grad = scatter_rows(
        n_mp,
        [act],
        ffn_w,
        2 * hidden,
        [second],
        "residual",
        gain_all,
        1,
        7,
        extra=own_grad,
        extra_right=(attn_w, 3 * local_width),
    )

    joined_grad = attention_backward(
        queries, keys, values, mixed_grad, cosine, sine, valid_counts
    )
    input_grad, gain_tile, sum_attn = scatter_rows(
        n_mp,
        list(joined_grad),
        attn_w,
        0,
        [tokens, second_grad],
        "last",
        gain_all,
        0,
        4,
        other_gain=gain_two,
        grad_lefts=[h_first, attn_grad],
        grad_right=mixed,
        n_dp=n_dp,
    )

    total_rows = SEQ * n_dp
    matrix_rate = step_rate / math.sqrt(total_rows)
    scale_rate = gain_rate / math.sqrt(total_rows)
    local = gains.shape[1]
    place = lax.rem((lax.axis_index("dp") * n_mp + lax.axis_index("mp")) * local, 128)
    sum_gains = lax.dynamic_slice(gain_tile, (0, place), (2, local))
    gu, down, out, qkv, (block_out, input_grad) = update_all(
        [w_gu, mom_gu, avg_gu],
        [w_qkv, mom_qkv, avg_qkv],
        (
            ([w_down, mom_down, avg_down], 2 * hidden),
            ([w_out, mom_out, avg_out], 3 * local_width),
        ),
        sum_ffn,
        sum_attn,
        [block_out, input_grad],
        matrix_rate,
    )
    new_gu, next_mom_gu, next_avg_gu, copy_gu = gu
    new_down, next_mom_down, next_avg_down, copy_down = down
    new_out, next_mom_out, next_avg_out, copy_out = out
    new_qkv, next_mom_qkv, next_avg_qkv, copy_qkv = qkv
    new_gains, next_mom_gains, next_avg_gains = updated(
        gains, mom_gains, avg_gains, sum_gains, scale_rate
    )
    return (
        block_out,
        input_grad,
        new_qkv,
        new_out,
        new_gu,
        new_down,
        new_gains,
        next_mom_qkv,
        next_mom_out,
        next_mom_gu,
        next_mom_down,
        next_mom_gains,
        next_avg_qkv,
        next_avg_out,
        next_avg_gu,
        next_avg_down,
        next_avg_gains,
        copy_qkv,
        copy_out,
        copy_gu,
        copy_down,
    )


def solution(mesh):
    rows, one = P(("dp", "mp"), None), P("dp")
    tall, wide, spread = P("dp", None, "mp"), P("mp", "dp"), P(None, ("dp", "mp"))
    weights = (tall, wide, tall, wide)
    return jax.shard_map(
        functools.partial(per_device, mesh.shape["dp"], mesh.shape["mp"]),
        mesh=mesh,
        in_specs=(rows, rows, one, *((*weights, spread) * 3)),
        out_specs=(rows, rows, *((*weights, spread) * 3), *weights),
        check_vma=False,
    )
```

```python
import functools
import math

import jax
import jax.numpy as jnp
from jax import lax
from jax.experimental import pallas as pl
from jax.experimental.pallas import tpu as pltpu
import numpy as np
from jax.sharding import PartitionSpec as P

HDIM = 128
SEQ = 1024
MESH = pl.DeviceIdType.MESH
ANY = pl.BlockSpec(memory_space=pl.ANY)
VMEM = pl.BlockSpec(memory_space=pltpu.VMEM)
VMEM_LIMIT = 60 * 1024 * 1024

norm_eps = 1e-05
rope_base = 10000.0
momentum_decay = 0.9
average_decay = 0.9
step_rate = 0.05
gain_rate = 0.5


def rows_at(start, size):
    return pl.ds(pl.multiple_of(start, size), size)


def remote(src, dst, send_sem, recv_sem, peer):
    return pltpu.make_async_remote_copy(
        src_ref=src,
        dst_ref=dst,
        send_sem=send_sem,
        recv_sem=recv_sem,
        device_id={"mp": peer},
        device_id_type=MESH,
    )


def neighbour_barrier(n):
    me = lax.axis_index("mp")
    barrier = pltpu.get_barrier_semaphore()

    @pl.when(me > 0)
    def _():
        pl.semaphore_signal(barrier, inc=1, device_id={"mp": me - 1}, device_id_type=MESH)

    @pl.when(me < n - 1)
    def _():
        pl.semaphore_signal(barrier, inc=1, device_id={"mp": me + 1}, device_id_type=MESH)

    pl.semaphore_wait(barrier, jnp.where(me > 0, 1, 0) + jnp.where(me < n - 1, 1, 0))


class LineGather:
    def __init__(self, n, rows, chunks, own, whole, sems):
        self.n, self.rows, self.chunks = n, rows, chunks
        self.size = rows // chunks
        self.own, self.whole, self.sems = own, whole, sems
        self.me = lax.axis_index("mp")

    def at(self, block, chunk):
        return self.whole.at[rows_at(block * self.rows + chunk * self.size, self.size)]

    def copies(self, step, chunk, first):
        me, n = self.me, self.n
        send_r, recv_r, send_l, recv_l = self.sems
        out = []
        for block, peer, has, send, recv in (
            (me - step, me + 1, (me - step >= 0) & (me < n - 1), send_r, recv_r),
            (me + step, me - 1, (me + step <= n - 1) & (me > 0), send_l, recv_l),
        ):
            src = (
                self.own.at[pl.ds(chunk * self.size, self.size)]
                if first
                else self.at(block, chunk)
            )
            index = step * self.chunks + chunk
            out.append(
                (has, remote(src, self.at(block, chunk), send.at[index], recv.at[index], peer))
            )
        return out

    def arrivals(self, step, chunk):
        me, n = self.me, self.n
        send_r, recv_r, send_l, recv_l = self.sems
        index = step * self.chunks + chunk
        out = []
        for block, has, send, recv in (
            (me - 1 - step, me - 1 - step >= 0, send_r, recv_r),
            (me + 1 + step, me + 1 + step <= n - 1, send_l, recv_l),
        ):
            ref = self.at(block, chunk)
            out.append((has, remote(ref, ref, send.at[index], recv.at[index], me)))
        return out

    def send_own(self, chunk):
        for has, copy in self.copies(0, chunk, True):
            pl.when(has)(copy.start)

    def forward(self, step):
        for chunk in range(self.chunks):
            self.forward_chunk(step, chunk, True)

    def forward_chunk(self, step, chunk, more):
        for (got, arrival), (has, copy) in zip(
            self.arrivals(step - 1, chunk), self.copies(step, chunk, False)
        ):
            pl.when(got)(arrival.wait_recv)
            pl.when(has & more)(copy.start)

    def finish(self, arrivals=True):
        for chunk in range(self.chunks if arrivals else 0):
            for got, arrival in self.arrivals(self.n - 2, chunk):
                pl.when(got)(arrival.wait_recv)
        for chunk in range(self.chunks):
            for has, copy in self.copies(0, chunk, True):
                pl.when(has)(copy.wait_send)

        def waits(step, carry):
            for chunk in range(self.chunks):
                for has, copy in self.copies(step, chunk, False):
                    pl.when(has)(copy.wait_send)
            return carry

        lax.fori_loop(1, self.n - 1, waits, 0)

    def forward_all(self):
        def step_of(step, carry):
            self.forward(step)
            return carry

        lax.fori_loop(1, self.n - 1, step_of, 0)


def gather_sems(n, chunks):
    return [pltpu.SemaphoreType.DMA(((n - 1) * chunks,))] * 4


class Exchange:
    def __init__(self, n_dp, n_mp, sems):
        self.n_dp, self.n_mp = n_dp, n_mp
        self.s_mp, self.r_mp, self.s_dp, self.r_dp = sems
        self.dp, self.mp = lax.axis_index("dp"), lax.axis_index("mp")

    def barrier(self):
        barrier = pltpu.get_barrier_semaphore()
        for axis, here, count in (("mp", self.mp, self.n_mp), ("dp", self.dp, self.n_dp)):
            for k in range(1, count):
                pl.semaphore_signal(
                    barrier,
                    inc=1,
                    device_id={axis: lax.rem(here + k, count)},
                    device_id_type=MESH,
                )
        pl.semaphore_wait(barrier, self.n_mp + self.n_dp - 2)

    def swap(self, axis, source_of, target):
        if axis == "mp":
            here, count, send, recv = self.mp, self.n_mp, self.s_mp, self.r_mp
        else:
            here, count, send, recv = self.dp, self.n_dp, self.s_dp, self.r_dp
        copies = []
        for k in range(1, count):
            peer = lax.rem(here + k, count)
            copies.append(
                pltpu.make_async_remote_copy(
                    src_ref=source_of(peer),
                    dst_ref=target.at[here],
                    send_sem=send.at[k - 1],
                    recv_sem=recv.at[k - 1],
                    device_id={axis: peer},
                    device_id_type=MESH,
                )
            )
        for copy in copies:
            copy.start()
        return copies


def exchange_sems(n_dp, n_mp):
    return [pltpu.SemaphoreType.DMA((n_mp - 1,))] * 2 + [pltpu.SemaphoreType.DMA((n_dp - 1,))] * 2


def tile_of(dp, mp, n_mp, local):
    return (dp * n_mp + mp) * local // 128


def flat_pairs(x):
    high, parts, wide = x.shape
    return x.reshape(high, parts, wide // 128, 128).transpose(0, 2, 1, 3).reshape(-1, 128)


def round_shares(w_gu, w_down):
    high, parts, hidden = w_gu.shape
    tiles = hidden // 128
    step = 128
    turn = min(256, hidden)

    def kernel(gu_ref, down_ref, out_ref):
        for part in range(parts):
            for tile in range(tiles):
                cols = pl.ds(part * hidden + tile * 128, 128)
                out_ref[:, cols] = gu_ref[
                    pl.ds(tile * parts + part, step, stride=tiles * parts), :
                ].astype(jnp.bfloat16)
        for i in range(hidden // turn):
            piece = down_ref[pl.ds(i * turn, turn), :]
            out_ref[:, pl.ds(parts * hidden + i * turn, turn)] = piece.T.astype(jnp.bfloat16)

    return pl.pallas_call(
        kernel,
        grid=(high // step,),
        out_shape=jax.ShapeDtypeStruct((high, (parts + 1) * hidden), jnp.bfloat16),
        in_specs=[
            pl.BlockSpec((step * tiles * parts, 128), lambda i: (i, 0)),
            pl.BlockSpec((hidden, step), lambda i: (0, i)),
        ],
        out_specs=pl.BlockSpec((step, (parts + 1) * hidden), lambda i: (i, 0)),
        compiler_params=pltpu.CompilerParams(vmem_limit_bytes=VMEM_LIMIT),
        cost_estimate=pl.CostEstimate(
            flops=0, bytes_accessed=6 * (w_gu.size + w_down.size), transcendentals=0
        ),
        name="round_shares",
    )(flat_pairs(w_gu), w_down)


def gather_first(n_dp, n_mp, own, gains, cotangent, live, collective_id, chunks=2):
    rows, width = own.shape
    local = gains.shape[1]
    lanes = jnp.arange(128, dtype=jnp.int32) // local
    place = lax.rem(lax.axis_index("mp"), 128 // local)
    if n_mp * local < 128:
        place = lax.rem(lax.axis_index("dp") * n_mp + lax.axis_index("mp"), 128 // local)
    tile = jnp.where(
        (lanes == place)[None, :], jnp.tile(gains, (1, 128 // local)), 0.0
    )
    tile = jnp.concatenate([tile, jnp.zeros((6, 128), jnp.float32)], axis=0)

    block = 64 if rows % 64 == 0 else rows

    def kernel(
        own_ref,
        tile_ref,
        cotangent_ref,
        live_ref,
        normed_ref,
        gain_ref,
        base_ref,
        branch_ref,
        all_ref,
        first,
        second,
        *sems,
    ):
        me = lax.axis_index("mp")
        exchange = Exchange(n_dp, n_mp, sems[:4])
        stream = LineGather(n_mp, rows, chunks, own_ref, all_ref, sems[4:])
        exchange.barrier()
        first[me] = tile_ref[...]
        copies = exchange.swap("mp", lambda peer: tile_ref, first)
        for chunk in range(chunks):
            stream.send_own(chunk)
        all_ref[rows_at(me * rows, rows), :] = own_ref[...]
        for copy in copies:
            copy.wait()
        dp = lax.axis_index("dp")
        second[dp] = first[...]
        copies = exchange.swap("dp", lambda peer: first, second)

        def enter(i, carry):
            span = rows_at(i * block, block)
            value = cotangent_ref[span, :].astype(jnp.float32) * live_ref[span, :]
            base_ref[span, :] = value
            branch_ref[span, :] = value.astype(jnp.bfloat16)
            return carry

        lax.fori_loop(0, rows // block, enter, 0)
        for copy in copies:
            copy.wait()
        gain_ref[...] = jnp.zeros_like(gain_ref)
        for d in range(n_dp):
            for m in range(n_mp):
                cols = pl.ds(tile_of(d, m, n_mp, local) * 128, 128)
                gain_ref[:, cols] += second[d, m]
        def norm(block_id):
            def body(i, carry):
                span = rows_at(block_id * rows + i * block, block)
                value = all_ref[span, :].astype(jnp.float32)
                inverse = lax.rsqrt(jnp.mean(value * value, axis=1, keepdims=True) + norm_eps)
                normed_ref[span, :] = (value * inverse * gain_ref[0:1, :]).astype(jnp.bfloat16)
                return carry

            lax.fori_loop(0, rows // block, body, 0)

        def step_of(step, carry):
            @pl.when(step > 0)
            def _():
                for chunk in range(chunks):
                    stream.forward_chunk(step, chunk, step < n_mp - 1)

            @pl.when(me + step < n_mp)
            def _():
                norm(me + step)

            @pl.when((me - step >= 0) & (step > 0))
            def _():
                norm(me - step)

            return carry

        lax.fori_loop(0, n_mp, step_of, 0)
        stream.finish(False)

    half = jnp.bfloat16
    return pl.pallas_call(
        kernel,
        out_shape=[
            jax.ShapeDtypeStruct((n_mp * rows, width), half),
            jax.ShapeDtypeStruct((8, width), jnp.float32),
            jax.ShapeDtypeStruct((rows, width), jnp.float32),
            jax.ShapeDtypeStruct((rows, width), half),
        ],
        in_specs=[VMEM] * 4,
        out_specs=[VMEM] * 4,
        scratch_shapes=[
            pltpu.VMEM((n_mp * rows, width), half),
            pltpu.VMEM((n_mp, 8, 128), jnp.float32),
            pltpu.VMEM((n_dp, n_mp, 8, 128), jnp.float32),
        ]
        + exchange_sems(n_dp, n_mp)
        + gather_sems(n_mp, chunks),
        compiler_params=pltpu.CompilerParams(
            collective_id=collective_id, has_side_effects=True, vmem_limit_bytes=VMEM_LIMIT
        ),
        cost_estimate=pl.CostEstimate(
            flops=0, bytes_accessed=200 * own.size * own.dtype.itemsize, transcendentals=0
        ),
        name="gather_first",
    )(own, tile, cotangent, live)


def dot_t(left, right):
    return lax.dot_general(
        left, right, (((1,), (1,)), ((), ())), preferred_element_type=jnp.float32
    )


def t_dot(left, right):
    return lax.dot_general(
        left, right, (((0,), (0,)), ((), ())), preferred_element_type=jnp.float32
    )


def dot(left, right):
    return jnp.dot(left, right, preferred_element_type=jnp.float32)


def probability(raw):
    return 1.0 / (1.0 + jnp.exp(math.log(SEQ) - raw * (1.0 / math.sqrt(HDIM))))


def rotated(values, cosine, sine, backward=False):
    turned = pltpu.roll(values, HDIM // 2, 1) * sine
    return values * cosine - turned if backward else values * cosine + turned


def scatter_rows(
    n,
    lhs,
    rhs,
    rhs_start,
    own_rows,
    epilogue,
    gains,
    gain_row,
    collective_id,
    heads=None,
    extra=None,
    extra_right=None,
    other_gain=None,
    grad_lefts=None,
    grad_right=None,
    n_dp=1,
    chunks=2,
):
    total_rows = lhs[0].shape[0]
    rows = total_rows // n
    width = gains.shape[1]
    size = rows // chunks
    tile = 512
    has_norm, has_gain = epilogue in ("forward", "backward"), epilogue in ("backward", "last")
    count = len(lhs)
    block = 32
    if heads is not None:
        inner_width = rhs_start // 3
        head_count = inner_width // HDIM
        pieces = [inner_width]
    else:
        pieces = [a.shape[1] for a in lhs]
    depth = sum(pieces)
    if extra_right is not None:
        extra_width = extra_right[0].shape[1] - extra_right[1]

    def kernel(*refs):
        refs = list(refs)

        def take(k):
            return [refs.pop(0) for _ in range(k)]

        left_refs = take(count)
        (right_hbm,) = take(1)
        (gain_ref,) = take(1)
        own_hbm = take(len(own_rows))
        if heads is not None:
            cosine_ref, sine_ref, mask_ref = take(3)
        if other_gain is not None:
            (other_ref,) = take(1)
            grad_hbm = take(3)
        extra_ref = take(1)[0] if extra is not None else None
        extra_right_hbm = take(1)[0] if extra_right is not None else None
        outs = take(1 + has_gain)
        owned_ref = take(1)[0] if other_gain is not None else None
        normed = take(1)[0] if has_norm else None
        if heads is not None:
            query_ref, key_ref, value_ref, mixed_ref = take(4)
        extra_whole = take(1)[0] if extra is not None else None
        if extra_right is not None:
            (extra_out,) = take(1)
        right, held, sent, part = take(4)
        joined_ref = take(1)[0] if heads is not None else None
        right_sem, send_sems, recv_sems = take(3)
        own, own_sems = take(len(own_rows)), take(1)[0]
        own_loads = [
            pltpu.make_async_copy(hbm, ref, own_sems.at[k])
            for k, (hbm, ref) in enumerate(zip(own_hbm, own))
        ]
        me = lax.axis_index("mp")
        fetch = pltpu.make_async_copy(
            right_hbm.at[:, pl.ds(rhs_start, depth)], right, right_sem
        )
        fetch.start()
        if heads is not None:
            (joined_sem,) = take(1)
            fetch_joined = pltpu.make_async_copy(
                right_hbm.at[:, pl.ds(0, rhs_start)], joined_ref, joined_sem
            )
            fetch_joined.start()
        if extra is not None:
            (extra_sem,) = take(1)
            extra_sems = take(4)
            if extra_right is None:
                extra_gather = LineGather(n, rows, 1, extra_ref, extra_whole, extra_sems)
                extra_local = pltpu.make_async_copy(extra_ref, extra_gather.at(me, 0), extra_sem)
                extra_local.start()
            else:
                extra_all, extra_right_ref, extra_right_sem = take(3)
                extra_gather = LineGather(n, rows, 1, extra_ref, extra_all, extra_sems)
                extra_fetch = pltpu.make_async_copy(
                    extra_right_hbm.at[:, pl.ds(extra_right[1], extra_width)],
                    extra_right_ref,
                    extra_right_sem,
                )
                extra_fetch.start()

                def extra_product(block_id):
                    @pl.when((block_id >= 0) & (block_id < n))
                    def _():
                        span = rows_at(block_id * rows, rows)
                        extra_out[span, :] = dot(
                            extra_all[span, :], extra_right_ref[...]
                        ).astype(jnp.bfloat16)
        if other_gain is not None:
            gain_sum, table, first, middle, second = take(5)
            exchange = Exchange(n_dp, n, take(4))
            *grad_left_refs, grad_right_ref, grad_load_sems = take(4)
            grad_loads = [
                pltpu.make_async_copy(hbm, ref, grad_load_sems.at[k])
                for k, (hbm, ref) in enumerate(zip(grad_hbm, [*grad_left_refs, grad_right_ref]))
            ]
            for load in grad_loads:
                load.start()
            grads, paired, landed = take(3)
            pair_send, pair_recv, land_send, land_recv = take(4)
            dp = lax.axis_index("dp")
            core, chip = lax.rem(dp, 2), dp // 2
            chips, share = n_dp // 2, landed.shape[1]
            exchange.barrier()
            pair_copies = [
                pltpu.make_async_remote_copy(
                    src_ref=grads.at[rows_at((2 * q + 1 - core) * share, share)],
                    dst_ref=paired.at[q],
                    send_sem=pair_send.at[q],
                    recv_sem=pair_recv.at[q],
                    device_id={"dp": dp + 1 - 2 * core},
                    device_id_type=MESH,
                )
                for q in range(chips)
            ]
            land_copies = [
                pltpu.make_async_remote_copy(
                    src_ref=paired.at[lax.rem(chip + k, chips)],
                    dst_ref=landed.at[k - 1],
                    send_sem=land_send.at[k - 1],
                    recv_sem=land_recv.at[k - 1],
                    device_id={"dp": 2 * lax.rem(chip + k, chips) + core},
                    device_id_type=MESH,
                )
                for k in range(1, chips)
            ]

            def make_grads():
                for load in grad_loads:
                    load.wait()
                start, narrow = 0, 256
                for k, right_ref in enumerate([*left_refs, grad_right_ref]):
                    left_ref = grad_left_refs[0 if k < count else 1]

                    def column(i, carry, start=start, left_ref=left_ref, right_ref=right_ref):
                        grads[:, rows_at(start + i * narrow, narrow)] = t_dot(
                            left_ref[...], right_ref[:, rows_at(i * narrow, narrow)]
                        ).astype(jnp.bfloat16)
                        return carry

                    lax.fori_loop(0, right_ref.shape[1] // narrow, column, 0)
                    start += right_ref.shape[1]
                for copy in pair_copies:
                    copy.start()
                for copy in pair_copies:
                    copy.wait()

                def add(i, carry):
                    span = rows_at(i * block, block)
                    for q in range(chips):
                        own_span = rows_at((2 * q + core) * share + i * block, block)
                        paired[q, span, :] = (
                            paired[q, span, :].astype(jnp.float32)
                            + grads[own_span, :].astype(jnp.float32)
                        ).astype(jnp.bfloat16)
                    return carry

                lax.fori_loop(0, share // block, add, 0)
                for copy in land_copies:
                    copy.start()

            def land():
                for copy in land_copies:
                    copy.wait()

                def add(i, carry):
                    span = rows_at(i * block, block)
                    total = paired[chip, span, :].astype(jnp.float32)
                    for k in range(chips - 1):
                        total = total + landed[k, span, :].astype(jnp.float32)
                    owned_ref[span, :] = total
                    return carry

                lax.fori_loop(0, share // block, add, 0)

        else:
            gain_sum = outs[1] if has_gain else None
            neighbour_barrier(n)
        if extra is not None:
            extra_gather.send_own(0)
        if extra_right is not None:
            extra_all[rows_at(me * rows, rows), :] = extra_ref[...]
            extra_fetch.wait()
        if heads is not None:
            turn = 256
            fetch_joined.wait()

            def enter(i, carry):
                span = rows_at(i * turn, turn)
                cosine, sine = cosine_ref[span, :], sine_ref[span, :]
                row_vals = left_refs[0][span, :]
                for k, target in ((0, query_ref), (1, key_ref), (2, value_ref)):
                    piece = dot(row_vals, joined_ref[:, pl.ds(k * inner_width, inner_width)])
                    for h in range(head_count):
                        value = piece[:, h * HDIM : (h + 1) * HDIM]
                        if k < 2:
                            value = rotated(value, cosine, sine)
                        target[span, pl.ds(h * HDIM, HDIM)] = value.astype(jnp.bfloat16)
                return carry

            lax.fori_loop(0, total_rows // turn, enter, 0)
        for load in own_loads:
            load.start()
        fetch.wait()

        def attend(block_id):
            span = rows_at(block_id * rows, rows)
            row_pos = block_id * rows + lax.broadcasted_iota(jnp.int32, (rows, rows), 0)

            def against(kb, totals):
                other = rows_at(kb * rows, rows)
                col_pos = kb * rows + lax.broadcasted_iota(jnp.int32, (rows, rows), 1)
                allowed = jnp.where(col_pos <= row_pos, mask_ref[:, other], 0.0)
                out = []
                for h in range(head_count):
                    cols = pl.ds(h * HDIM, HDIM)
                    raw = dot_t(query_ref[span, cols], key_ref[other, cols])
                    prob = probability(raw) * allowed
                    out.append(
                        totals[h]
                        + jnp.dot(
                            prob.astype(jnp.bfloat16),
                            value_ref[other, cols],
                            preferred_element_type=jnp.float32,
                        )
                    )
                return tuple(out)

            start = tuple(jnp.zeros((rows, HDIM), jnp.float32) for _ in range(head_count))
            totals = lax.fori_loop(0, block_id + 1, against, start)
            for h in range(head_count):
                mixed_ref[span, pl.ds(h * HDIM, HDIM)] = totals[h].astype(jnp.bfloat16)

        def product(block_id):
            if heads is not None:
                attend(block_id)
            sources = [mixed_ref] if heads is not None else left_refs

            def column(ct, carry):
                cols = rows_at(ct * tile, tile)
                total, start = None, 0
                for source, piece in zip(sources, pieces):
                    term = dot_t(
                        source[rows_at(block_id * rows, rows), :],
                        right[cols, pl.ds(start, piece)],
                    )
                    start += piece
                    total = term if total is None else total + term
                part[:, cols] = total
                return carry

            lax.fori_loop(0, width // tile, column, 0)

        def hop(block_id, chunk, rightward):
            peer = me + 1 if rightward else me - 1
            slot = block_id if rightward else jnp.where(block_id == peer, n, block_id)
            return remote(
                sent.at[block_id, pl.ds(chunk * size, size)],
                held.at[slot, pl.ds(chunk * size, size)],
                send_sems.at[block_id * chunks + chunk],
                recv_sems.at[slot * chunks + chunk],
                peer,
            )

        def arrival(slot, chunk):
            ref = held.at[slot, pl.ds(chunk * size, size)]
            return remote(
                ref, ref, send_sems.at[chunk], recv_sems.at[slot * chunks + chunk], me
            )

        def add_rows(block_id, chunk, slots):
            def body(i, carry):
                span = rows_at(chunk * size + i * block, block)
                value = part[span, :]
                for slot in slots:
                    value = value + held[slot, span, :].astype(jnp.float32)
                sent[block_id, span, :] = value.astype(jnp.bfloat16)
                return carry

            lax.fori_loop(0, size // block, body, 0)

        def relay(block_id, rightward, inner):
            product(block_id)
            for chunk in range(chunks):

                @pl.when(inner)
                def _():
                    arrival(block_id, chunk).wait_recv()
                    add_rows(block_id, chunk, [block_id])

                @pl.when(jnp.logical_not(inner))
                def _():
                    add_rows(block_id, chunk, [])

                hop(block_id, chunk, rightward).start()

        def step_of(step, carry):
            @pl.when((step >= me + 1) & (me < n - 1))
            def _():
                relay(me + n - step, True, me > 0)

            @pl.when((step >= n - me) & (me > 0))
            def _():
                relay(me - n + step, False, me < n - 1)

            if extra is not None:

                @pl.when(step < n - 1)
                def _():
                    extra_gather.forward(step)
                    if extra_right is not None:
                        extra_product(me - step)
                        extra_product(me + step)

            if other_gain is not None:
                pl.when(step == 1)(make_grads)

            return carry

        lax.fori_loop(1, n, step_of, 0)
        product(me)
        if extra_right is not None:
            extra_product(me)
        for load in own_loads:
            load.wait()
        if has_gain:
            gain_sum[...] = jnp.zeros_like(gain_sum)
        for chunk in range(chunks):

            @pl.when(me > 0)
            def _():
                arrival(me, chunk).wait_recv()

            @pl.when(me < n - 1)
            def _():
                arrival(n, chunk).wait_recv()

            def body(i, carry):
                span = rows_at(chunk * size + i * block, block)
                total = part[span, :]
                zero = jnp.zeros_like(total)
                total = total + jnp.where(me > 0, held[me, span, :].astype(jnp.float32), zero)
                total = total + jnp.where(
                    me < n - 1, held[n, span, :].astype(jnp.float32), zero
                )
                gain = gain_ref[gain_row : gain_row + 1, :]
                if epilogue == "residual":
                    outs[0][span, :] = (own[0][span, :] + total).astype(jnp.bfloat16)
                elif epilogue == "forward":
                    value = own[0][span, :].astype(jnp.float32) + total
                    outs[0][span, :] = value
                    inverse = lax.rsqrt(
                        jnp.mean(value * value, axis=1, keepdims=True) + norm_eps
                    )
                    normed[span, :] = (value * inverse * gain).astype(jnp.bfloat16)
                else:
                    value = own[0][span, :].astype(jnp.float32)
                    inverse = lax.rsqrt(
                        jnp.mean(value * value, axis=1, keepdims=True) + norm_eps
                    )
                    unit = value * inverse
                    scaled = total * gain
                    inner = jnp.mean(scaled * unit, axis=1, keepdims=True)
                    result = own[1][span, :] + inverse * (scaled - unit * inner)
                    outs[0][span, :] = result
                    gain_sum[...] += jnp.sum(
                        (total * unit).reshape(block // 8, 8, width), axis=0
                    )
                    if has_norm:
                        normed[span, :] = result.astype(jnp.bfloat16)
                return carry

            lax.fori_loop(0, size // block, body, 0)
        if extra is not None:
            extra_gather.finish()
        if extra_right is not None:
            extra_local = pltpu.make_async_copy(extra_all, extra_whole, extra_sem)
            extra_local.start()
            extra_product(me - (n - 1))
            extra_product(me + (n - 1))
        if extra is not None:
            extra_local.wait()
        if other_gain is not None:
            local = width // (n * n_dp)
            for row, source in ((0, gain_sum), (1, other_ref)):
                total = jnp.sum(source[...], axis=0, keepdims=True)
                for d in range(n_dp):
                    for m in range(n):
                        start = tile_of(d, m, n, local) * 128
                        table[m, d, row : row + 1, :] = total[:, start : start + 128]
            copies = exchange.swap("mp", lambda peer: table.at[peer], first)
            first[me] = table[me]
            for copy in copies:
                copy.wait()
            total = first[0]
            for m in range(1, n):
                total = total + first[m]
            middle[...] = total
            copies = exchange.swap("dp", lambda peer: middle.at[peer], second)
            second[dp] = middle[dp]
            land()
            for copy in copies:
                copy.wait()
            total = second[0]
            for d in range(1, n_dp):
                total = total + second[d]
            outs[1][...] = total

        def sends(step, carry):
            for chunk in range(chunks):

                @pl.when((step >= me + 1) & (me < n - 1))
                def _():
                    hop(me + n - step, chunk, True).wait_send()

                @pl.when((step >= n - me) & (me > 0))
                def _():
                    hop(me - n + step, chunk, False).wait_send()

            return carry

        lax.fori_loop(1, n, sends, 0)

    out_type = jnp.bfloat16 if epilogue == "residual" else jnp.float32
    out_shape = [jax.ShapeDtypeStruct((rows, width), out_type)]
    out_specs = [VMEM]
    if has_gain:
        out_shape.append(
            jax.ShapeDtypeStruct((8, width) if other_gain is None else (2, 128), jnp.float32)
        )
        out_specs.append(VMEM)
    if other_gain is not None:
        share = width // n_dp
        grad_width = sum(pieces) + grad_right.shape[1]
        out_shape.append(jax.ShapeDtypeStruct((share, grad_width), jnp.float32))
        out_specs.append(VMEM)
    scratch = [
        pltpu.VMEM((width, depth), jnp.bfloat16),
        pltpu.VMEM((n + 1, rows, width), jnp.bfloat16),
        pltpu.VMEM((n, rows, width), jnp.bfloat16),
        pltpu.VMEM((rows, width), jnp.float32),
    ]
    if heads is not None:
        scratch.append(pltpu.VMEM((width, rhs_start), jnp.bfloat16))
    if has_norm:
        out_shape.append(jax.ShapeDtypeStruct((rows, width), jnp.bfloat16))
        out_specs.append(VMEM)
    scratch += [
        pltpu.SemaphoreType.DMA,
        pltpu.SemaphoreType.DMA((n * chunks,)),
        pltpu.SemaphoreType.DMA(((n + 1) * chunks,)),
    ]
    scratch += [pltpu.VMEM(x.shape, x.dtype) for x in own_rows]
    scratch.append(pltpu.SemaphoreType.DMA((len(own_rows),)))
    head_args = []
    if heads is not None:
        scratch.append(pltpu.SemaphoreType.DMA)
        head_args = list(heads)
        out_shape += [jax.ShapeDtypeStruct((total_rows, inner_width), jnp.bfloat16)] * 4
        out_specs += [VMEM] * 4
    extra_args = []
    if extra is not None:
        out_shape.append(jax.ShapeDtypeStruct((total_rows, width), jnp.bfloat16))
        out_specs.append(ANY)
        scratch += [pltpu.SemaphoreType.DMA] + gather_sems(n, 1)
        extra_args = [extra]
    if extra_right is not None:
        out_shape.append(jax.ShapeDtypeStruct((total_rows, extra_width), jnp.bfloat16))
        out_specs.append(VMEM)
        scratch += [
            pltpu.VMEM((total_rows, width), jnp.bfloat16),
            pltpu.VMEM((width, extra_width), jnp.bfloat16),
            pltpu.SemaphoreType.DMA,
        ]
        extra_args.append(extra_right[0])
    late_args = []
    if other_gain is not None:
        head_args.append(other_gain)
        late_args = [*grad_lefts, grad_right]
        scratch += [
            pltpu.VMEM((8, width), jnp.float32),
            pltpu.VMEM((n, n_dp, 2, 128), jnp.float32),
            pltpu.VMEM((n, n_dp, 2, 128), jnp.float32),
            pltpu.VMEM((n_dp, 2, 128), jnp.float32),
            pltpu.VMEM((n_dp, 2, 128), jnp.float32),
        ] + exchange_sems(n_dp, n)
        scratch += [pltpu.VMEM(x.shape, x.dtype) for x in late_args]
        scratch.append(pltpu.SemaphoreType.DMA((len(late_args),)))
        chips = n_dp // 2
        scratch.append(pltpu.VMEM((width, grad_width), jnp.bfloat16))
        scratch.append(pltpu.VMEM((chips, share, grad_width), jnp.bfloat16))
        scratch.append(pltpu.VMEM((chips - 1, share, grad_width), jnp.bfloat16))
        scratch += [pltpu.SemaphoreType.DMA((chips,))] * 2
        scratch += [pltpu.SemaphoreType.DMA((chips - 1,))] * 2
    flops = 2 * total_rows * depth * width
    return pl.pallas_call(
        kernel,
        out_shape=out_shape,
        in_specs=[VMEM] * count
        + [ANY]
        + [VMEM]
        + [ANY] * len(own_rows)
        + [VMEM] * len(head_args)
        + [ANY] * len(late_args)
        + [VMEM if extra_right is not None else ANY] * min(1, len(extra_args))
        + [ANY] * max(0, len(extra_args) - 1),
        out_specs=out_specs,
        scratch_shapes=scratch,
        compiler_params=pltpu.CompilerParams(
            collective_id=collective_id, has_side_effects=True, vmem_limit_bytes=VMEM_LIMIT
        ),
        cost_estimate=pl.CostEstimate(
            flops=flops, bytes_accessed=300_000_000, transcendentals=0
        ),
        name="scatter_" + epilogue,
    )(*lhs, rhs, gains, *own_rows, *head_args, *late_args, *extra_args)


def feed_forward(n, normed, branch_grad, weights, second, gains, collective_id, halves=1, hops=4):
    rows, width = normed.shape
    total_rows = n * rows
    hidden = weights.shape[1] // 3
    count, parcels = hops, halves
    part_size = rows // hops
    tile = min(1024, hidden)
    block = min(32, part_size)
    narrow = min(256, hidden)
    per = hidden // narrow
    pieces = 3 * per
    before = pieces // 6
    between = (pieces - 2 * before) // (count + 1)
    tall = min(1024, width)

    def kernel(
        normed_ref,
        branch_hbm,
        weights_hbm,
        second_ref,
        gain_ref,
        result_ref,
        rounded_ref,
        gain_sum,
        grads_hbm,
        act_hbm,
        gate_hbm,
        up_hbm,
        weight_ref,
        branch_ref,
        all_ref,
        held,
        sent,
        own_part,
        act_ref,
        gate_ref,
        up_ref,
        piece_ref,
        load_sems,
        stage_sems,
        piece_sems,
        grad_sems,
        send_sems,
        recv_sems,
        *gather_refs,
    ):
        me = lax.axis_index("mp")
        middle = (me > 0) & (me < n - 1)
        loads = [
            pltpu.make_async_copy(weights_hbm, weight_ref, load_sems.at[0]),
            pltpu.make_async_copy(branch_hbm, branch_ref, load_sems.at[1]),
        ]
        for load in loads:
            load.start()
        gather = LineGather(n, rows, parcels, normed_ref, all_ref, gather_refs)
        neighbour_barrier(n)
        for parcel in range(parcels):
            gather.send_own(parcel)
        all_ref[rows_at(me * rows, rows), :] = normed_ref[...]
        for load in loads:
            load.wait()

        def hop(block_id, chunk, rightward):
            peer = me + 1 if rightward else me - 1
            slot = block_id if rightward else jnp.where(block_id == peer, n, block_id)
            return remote(
                sent.at[block_id, pl.ds(chunk * part_size, part_size)],
                held.at[slot, pl.ds(chunk * part_size, part_size)],
                send_sems.at[block_id * count + chunk],
                recv_sems.at[slot * count + chunk],
                peer,
            )

        def arrival(slot, chunk):
            ref = held.at[slot, pl.ds(chunk * part_size, part_size)]
            return remote(
                ref, ref, send_sems.at[chunk], recv_sems.at[slot * count + chunk], me
            )

        def stages(block_id, chunk, size):
            span = rows_at(block_id * rows + chunk * size, size)
            return [
                pltpu.make_async_copy(
                    ref.at[pl.ds(chunk * size, size)], hbm.at[span], stage_sems.at[chunk * 3 + k]
                )
                for k, (ref, hbm) in enumerate(
                    ((act_ref, act_hbm), (gate_ref, gate_hbm), (up_ref, up_hbm))
                )
            ]

        def compute(block_id, chunk, size, first):
            here = pl.ds(chunk * size, size)
            span = rows_at(block_id * rows + chunk * size, size)

            @pl.when(jnp.logical_not(first))
            def _():
                for stage in stages(block_id, chunk, size):
                    stage.wait()

            def units(ct, carry):
                cols = rows_at(ct * tile, tile)
                row_vals, branch = all_ref[span, :], branch_ref[span, :]
                gate = dot(row_vals, weight_ref[:, cols])
                up = dot(row_vals, weight_ref[:, rows_at(hidden + ct * tile, tile)])
                act_grad = dot(branch, weight_ref[:, rows_at(2 * hidden + ct * tile, tile)])
                sigma = 1.0 / (1.0 + jnp.exp(-gate))
                silu = gate * sigma
                act_ref[here, cols] = (silu * up).astype(jnp.bfloat16)
                gate_ref[here, cols] = (
                    act_grad * up * sigma * (1.0 + gate * (1.0 - sigma))
                ).astype(jnp.bfloat16)
                up_ref[here, cols] = (act_grad * silu).astype(jnp.bfloat16)
                return carry

            lax.fori_loop(0, hidden // tile, units, 0)
            for stage in stages(block_id, chunk, size):
                stage.start()

            def columns(ct, carry):
                cols = rows_at(ct * tile, tile)
                total = dot_t(gate_ref[here, :], weight_ref[cols, pl.ds(0, hidden)])
                total += dot_t(up_ref[here, :], weight_ref[cols, pl.ds(hidden, hidden)])

                @pl.when(block_id == me)
                def _():
                    own_part[here, cols] = total

                @pl.when(block_id != me)
                def _():
                    sent[block_id, here, cols] = total.astype(jnp.bfloat16)

                return carry

            lax.fori_loop(0, width // tile, columns, 0)

            @pl.when((me == 0) & (block_id > me))
            def _():
                for k in range(size // part_size):
                    hop(block_id, chunk * (size // part_size) + k, True).start()

            @pl.when((me == n - 1) & (block_id < me))
            def _():
                for k in range(size // part_size):
                    hop(block_id, chunk * (size // part_size) + k, False).start()

        def forward(step, parcel):
            gather.forward_chunk(step, parcel, step < n - 1)

        def forward_whole(step):
            for parcel in range(parcels):
                forward(step, parcel)

        def step_of(step, carry):
            def side_of(side, carry):
                block_id = me + (1 - 2 * side) * step
                valid = (block_id >= 0) & (block_id < n) & ((step > 0) | (side == 0))

                @pl.when(middle & (step > 0) & (step < n - 1) & (side == 1))
                def _():
                    forward_whole(step + 1)

                @pl.when(middle & valid)
                def _():
                    compute(block_id, 0, rows, step == 0)

                @pl.when(middle & (step == 0) & (side == 0))
                def _():
                    forward_whole(1)

                for half in range(halves):

                    @pl.when(jnp.logical_not(middle) & valid)
                    def _():
                        pl.when(step > 0)(lambda: forward(step, half))
                        compute(block_id, half, rows // halves, step == 0)

                return carry

            return lax.fori_loop(0, 2, side_of, carry)

        lax.fori_loop(0, n, step_of, 0)
        @pl.when(middle)
        def _():
            for stage in stages(me, 0, rows):
                stage.wait()

        @pl.when(jnp.logical_not(middle))
        def _():
            for half in range(halves):
                for stage in stages(me, half, rows // halves):
                    stage.wait()


        def load_of(source, index, slot):
            return pltpu.make_async_copy(
                source.at[:, rows_at(lax.rem(index, per) * narrow, narrow)],
                piece_ref.at[slot],
                piece_sems.at[slot],
            )

        def load_piece(index):
            for k, source in enumerate((gate_hbm, up_hbm, act_hbm)):

                @pl.when(index // per == k)
                def _():
                    load_of(source, index, lax.rem(index, 2)).start()

        def grad_copy(index):
            cols = rows_at(index * narrow, narrow)
            return pltpu.make_async_copy(
                weight_ref.at[:, cols], grads_hbm.at[:, cols], grad_sems.at[index]
            )

        def grad_piece(index, carry):
            slot = lax.rem(index, 2)
            load_of(gate_hbm, index, slot).wait()

            @pl.when(index + 1 < pieces)
            def _():
                load_piece(index + 1)

            cols = rows_at(index * narrow, narrow)
            for start in range(0, width, tall):
                span = pl.ds(start, tall)

                @pl.when(index < 2 * per)
                def _():
                    weight_ref[span, cols] = t_dot(all_ref[:, span], piece_ref[slot]).astype(
                        jnp.bfloat16
                    )

                @pl.when(index >= 2 * per)
                def _():
                    weight_ref[span, cols] = t_dot(branch_ref[:, span], piece_ref[slot]).astype(
                        jnp.bfloat16
                    )

            grad_copy(index).start()
            return carry

        load_piece(0)

        def add_rows(block_id, chunk):
            def body(i, carry):
                span = rows_at(chunk * part_size + i * block, block)
                value = sent[block_id, span, :].astype(jnp.float32)
                value = value + held[block_id, span, :].astype(jnp.float32)
                sent[block_id, span, :] = value.astype(jnp.bfloat16)
                return carry

            lax.fori_loop(0, part_size // block, body, 0)

        def relay_side(step, chunk, rightward):
            block_id = step if rightward else n - 1 - step
            has = (me > 0) & (step > me) if rightward else (me < n - 1) & (n - 1 - step < me)

            @pl.when(has)
            def _():
                arrival(block_id, chunk).wait_recv()
                add_rows(block_id, chunk)
                hop(block_id, chunk, rightward).start()

        def relay_chunk(step, chunk, near):
            rightward_first = 2 * me < n

            @pl.when(rightward_first)
            def _():
                relay_side(step, chunk, near)

            @pl.when(jnp.logical_not(rightward_first))
            def _():
                relay_side(step, chunk, not near)

        def relay_of(step, carry):
            for chunk in range(count):
                relay_chunk(step, chunk, True)
            for chunk in range(count):
                relay_chunk(step, chunk, False)
            return carry

        lax.fori_loop(1, n - 1, relay_of, 0)
        lax.fori_loop(0, before, grad_piece, 0)

        def last_relay(chunk, carry):
            @pl.when(chunk < count)
            def _():
                relay_chunk(n - 1, chunk, True)

            start = before + chunk * between
            lax.fori_loop(start, start + between, grad_piece, 0)

            @pl.when(chunk > 0)
            def _():
                relay_chunk(n - 1, chunk - 1, False)

            return carry

        lax.fori_loop(0, count + 1, last_relay, 0)
        lax.fori_loop(before + (count + 1) * between, pieces, grad_piece, 0)
        gain_sum[...] = jnp.zeros_like(gain_sum)
        for chunk in range(count):

            @pl.when(me > 0)
            def _():
                arrival(me, chunk).wait_recv()

            @pl.when(me < n - 1)
            def _():
                arrival(n, chunk).wait_recv()

            def body(i, carry):
                span = rows_at(chunk * part_size + i * block, block)
                total = own_part[span, :]
                zero = jnp.zeros_like(total)
                total = total + jnp.where(me > 0, held[me, span, :].astype(jnp.float32), zero)
                total = total + jnp.where(
                    me < n - 1, held[n, span, :].astype(jnp.float32), zero
                )
                value = second_ref[span, :]
                inverse = lax.rsqrt(jnp.mean(value * value, axis=1, keepdims=True) + norm_eps)
                unit = value * inverse
                scaled = total * gain_ref[1:2, :]
                inner = jnp.mean(scaled * unit, axis=1, keepdims=True)
                base = branch_ref[
                    rows_at(me * rows + chunk * part_size + i * block, block), :
                ].astype(jnp.float32)
                result = base + inverse * (scaled - unit * inner)
                result_ref[span, :] = result
                rounded_ref[span, :] = result.astype(jnp.bfloat16)
                gain_sum[...] += jnp.sum((total * unit).reshape(block // 8, 8, width), axis=0)
                return carry

            lax.fori_loop(0, part_size // block, body, 0)
        gather.finish(False)

        def sends(block_id, carry):
            for chunk in range(count):

                @pl.when((block_id > me) & (me < n - 1))
                def _():
                    hop(block_id, chunk, True).wait_send()

                @pl.when((block_id < me) & (me > 0))
                def _():
                    hop(block_id, chunk, False).wait_send()

            return carry

        lax.fori_loop(0, n, sends, 0)

        def grads_out(index, carry):
            grad_copy(index).wait()
            return carry

        lax.fori_loop(0, pieces, grads_out, 0)

    half = jnp.bfloat16
    return pl.pallas_call(
        kernel,
        out_shape=[
            jax.ShapeDtypeStruct((rows, width), jnp.float32),
            jax.ShapeDtypeStruct((rows, width), half),
            jax.ShapeDtypeStruct((8, width), jnp.float32),
            jax.ShapeDtypeStruct((width, 3 * hidden), half),
        ]
        + [jax.ShapeDtypeStruct((total_rows, hidden), half)] * 3,
        in_specs=[VMEM, ANY, ANY, VMEM, VMEM],
        out_specs=[VMEM] * 3 + [ANY] * 4,
        scratch_shapes=[
            pltpu.VMEM((width, 3 * hidden), half),
            pltpu.VMEM((total_rows, width), half),
            pltpu.VMEM((total_rows, width), half),
            pltpu.VMEM((n + 1, rows, width), half),
            pltpu.VMEM((n, rows, width), half),
            pltpu.VMEM((rows, width), jnp.float32),
        ]
        + [pltpu.VMEM((rows, hidden), half)] * 3
        + [
            pltpu.VMEM((2, total_rows, narrow), half),
            pltpu.SemaphoreType.DMA((2,)),
            pltpu.SemaphoreType.DMA((halves * 3,)),
            pltpu.SemaphoreType.DMA((2,)),
            pltpu.SemaphoreType.DMA((pieces,)),
            pltpu.SemaphoreType.DMA((n * count,)),
            pltpu.SemaphoreType.DMA(((n + 1) * count,)),
        ]
        + gather_sems(n, parcels),
        compiler_params=pltpu.CompilerParams(
            collective_id=collective_id, has_side_effects=True, vmem_limit_bytes=VMEM_LIMIT
        ),
        cost_estimate=pl.CostEstimate(
            flops=16 * total_rows * width * hidden, bytes_accessed=300_000_000, transcendentals=0
        ),
        name="feed_forward",
    )(normed, branch_grad, weights, second, gains)


def attention_backward(queries, keys, values, mixed_grad, cosine, sine, valid_counts):
    total_rows, inner_width = queries.shape
    block = min(256, total_rows)

    def kernel(q_ref, k_ref, v_ref, do_ref, cos_ref, sin_ref, valid_ref, dq_out, dk_out, dv_out, dk_ref, dv_ref):
        dk_ref[...] = jnp.zeros_like(dk_ref)
        dv_ref[...] = jnp.zeros_like(dv_ref)
        for i in range(total_rows // block):
            span = pl.ds(i * block, block)
            upto = (i + 1) * block
            shape = (upto, block)
            key_pos = lax.broadcasted_iota(jnp.int32, shape, 0)
            query_pos = i * block + lax.broadcasted_iota(jnp.int32, shape, 1)
            allowed = jnp.where((key_pos <= query_pos) & (key_pos < valid_ref[0]), 1.0, 0.0)
            query, grad = q_ref[span, :], do_ref[span, :]
            key = k_ref[:upto, :]
            prob = probability(dot_t(key, query)) * allowed
            prob_grad = dot_t(v_ref[:upto, :], grad)
            dv_ref[:upto, :] += jnp.dot(
                prob.astype(jnp.bfloat16), grad, preferred_element_type=jnp.float32
            )
            score_grad = (prob_grad * prob * (1.0 - prob) * (1.0 / math.sqrt(HDIM))).astype(
                jnp.bfloat16
            )
            dk_ref[:upto, :] += jnp.dot(score_grad, query, preferred_element_type=jnp.float32)
            dq = t_dot(score_grad, key)
            dq_out[span, :] = rotated(
                dq, cos_ref[span, :], sin_ref[span, :], True
            ).astype(jnp.bfloat16)
        dk_out[...] = rotated(dk_ref[...], cos_ref[...], sin_ref[...], True).astype(jnp.bfloat16)
        dv_out[...] = dv_ref[...].astype(jnp.bfloat16)

    head = pl.BlockSpec((total_rows, HDIM), lambda h: (0, h))
    table = pl.BlockSpec((total_rows, HDIM), lambda h: (0, 0))
    return pl.pallas_call(
        kernel,
        grid=(inner_width // HDIM,),
        out_shape=[jax.ShapeDtypeStruct((total_rows, inner_width), jnp.bfloat16)] * 3,
        in_specs=[head] * 4 + [table] * 2 + [pl.BlockSpec(memory_space=pltpu.SMEM)],
        out_specs=[head] * 3,
        scratch_shapes=[pltpu.VMEM((total_rows, HDIM), jnp.float32)] * 2,
        compiler_params=pltpu.CompilerParams(vmem_limit_bytes=VMEM_LIMIT),
        cost_estimate=pl.CostEstimate(
            flops=8 * total_rows * total_rows * inner_width,
            bytes_accessed=14 * total_rows * inner_width,
            transcendentals=0,
        ),
        name="attention_backward",
    )(queries, keys, values, mixed_grad, cosine, sine, valid_counts)


def updated(weight, moment, average, gradient, rate):
    moment_new = momentum_decay * moment + (1.0 - momentum_decay) * gradient
    weight_new = weight - rate * (
        (1.0 - momentum_decay) * gradient + momentum_decay * moment_new
    )
    average_new = average_decay * average + (1.0 - average_decay) * weight_new
    return weight_new, moment_new, average_new


def store_update(ins, gradient, outs, rate):
    weight, moment, average = updated(*[ref[...] for ref in ins], gradient, rate)
    outs[0][...] = weight
    outs[1][...] = moment
    outs[2][...] = average
    outs[3][...] = weight.astype(jnp.bfloat16)


def update_all(pairs, parts, flips, sum_ffn, sum_attn, passed, rate):
    jobs = []

    high, two, wide = pairs[0].shape
    tiles = wide // 128
    step = min(64, high)
    stride = tiles * two

    def spread_gradient(g, spread):
        for part in range(two):
            for tile in range(tiles):
                cols = pl.ds(part * wide + tile * 128, 128)
                spread[pl.ds(tile * two + part, step, stride=stride), :] = g[:, cols].astype(
                    jnp.float32
                )
        return spread[...]

    jobs.append(
        (
            [flat_pairs(x) for x in pairs],
            ((step * stride, 128), lambda i: (i, 0)),
            (sum_ffn, (step, two * wide), lambda i: (i, 0)),
            high // step,
            spread_gradient,
        )
    )
    for arrays, total, start in ((flips[0][0], sum_ffn, flips[0][1]), (flips[1][0], sum_attn, flips[1][1])):
        tall, narrow = arrays[0].shape
        rows = min(512, tall)
        jobs.append(
            (
                arrays,
                ((rows, narrow), lambda i: (i, 0)),
                (total, (narrow, rows), lambda i, first=start // rows: (0, first + i)),
                tall // rows,
                lambda g, spread: g[...].astype(jnp.float32).T,
            )
        )
    deep, count, across = parts[0].shape
    jobs.append(
        (
            [x.transpose(1, 0, 2) for x in parts],
            ((None, deep, across), lambda i: (i, 0, 0)),
            (sum_attn, (deep, across), lambda i: (0, i)),
            count,
            lambda g, spread: g[...].astype(jnp.float32),
        )
    )
    starts = [sum(job[3] for job in jobs[:k]) for k in range(len(jobs))]
    steps = sum(job[3] for job in jobs)

    def within(k, index_map):
        return lambda i: index_map(jnp.clip(i - starts[k], 0, jobs[k][3] - 1))

    in_specs, out_specs, args, out_shape = [], [], [], []
    kinds = [jnp.float32] * 3 + [jnp.bfloat16]
    for k, (arrays, (shape, index_map), (total, total_shape, total_map), _, _) in enumerate(jobs):
        spec = pl.BlockSpec(shape, within(k, index_map))
        in_specs += [spec] * 3 + [pl.BlockSpec(total_shape, within(k, total_map))]
        args += [*arrays, total]
        out_specs += [spec] * 4
        out_shape += [jax.ShapeDtypeStruct(arrays[0].shape, kind) for kind in kinds]
    in_specs += [ANY] * len(passed)
    out_specs += [ANY] * len(passed)
    out_shape += [jax.ShapeDtypeStruct(x.shape, x.dtype) for x in passed]

    def body(*refs):
        ins, refs = refs[: len(in_specs)], refs[len(in_specs) :]
        outs, (spread, sems, *kept) = refs[: len(out_specs)], refs[len(out_specs) :]
        i = pl.program_id(0)
        entering = [
            pltpu.make_async_copy(ins[4 * len(jobs) + k], ref, sems.at[0, k])
            for k, ref in enumerate(kept)
        ]
        leaving = [
            pltpu.make_async_copy(ref, outs[4 * len(jobs) + k], sems.at[1, k])
            for k, ref in enumerate(kept)
        ]

        @pl.when(i == 0)
        def _():
            for copy in entering:
                copy.start()

        @pl.when(i == 1)
        def _():
            for arrived, copy in zip(entering, leaving):
                arrived.wait()
                copy.start()

        for k, job in enumerate(jobs):

            @pl.when((i >= starts[k]) & (i < starts[k] + job[3]))
            def _():
                gradient = job[4](ins[4 * k + 3], spread)
                store_update(ins[4 * k : 4 * k + 3], gradient, outs[4 * k : 4 * k + 4], rate)

        @pl.when(i == steps - 1)
        def _():
            for copy in leaving:
                copy.wait()

    size = sum(job[0][0].size for job in jobs)
    outs = pl.pallas_call(
        body,
        grid=(steps,),
        out_shape=out_shape,
        in_specs=in_specs,
        out_specs=out_specs,
        scratch_shapes=[
            pltpu.VMEM((step * stride, 128), jnp.float32),
            pltpu.SemaphoreType.DMA((2, len(passed))),
        ]
        + [pltpu.VMEM(x.shape, x.dtype) for x in passed],
        compiler_params=pltpu.CompilerParams(vmem_limit_bytes=VMEM_LIMIT),
        cost_estimate=pl.CostEstimate(
            flops=10 * size, bytes_accessed=28 * size, transcendentals=0
        ),
        name="update_all",
    )(*args, *passed)
    gu = [
        x.reshape(high, tiles, two, 128).transpose(0, 2, 1, 3).reshape(high, two, wide)
        for x in outs[:4]
    ]
    qkv = [x.transpose(1, 0, 2) for x in outs[12:16]]
    return gu, outs[4:8], outs[8:12], qkv, outs[16:]


def rope_tables(length, half_dim):
    positions = np.arange(length, dtype=np.float32)[:, None]
    inverse_freq = np.power(
        np.float32(rope_base), -np.arange(half_dim, dtype=np.float32) / np.float32(half_dim)
    )
    angles = positions * inverse_freq[None, :]
    cosine, sine = np.cos(angles), np.sin(angles)
    return np.concatenate([cosine, cosine], axis=1), np.concatenate([-sine, sine], axis=1)


def per_device(
    n_dp,
    n_mp,
    tokens,
    cotangent,
    valid_counts,
    w_qkv,
    w_out,
    w_gu,
    w_down,
    gains,
    mom_qkv,
    mom_out,
    mom_gu,
    mom_down,
    mom_gains,
    avg_qkv,
    avg_out,
    avg_gu,
    avg_down,
    avg_gains,
):
    half = jnp.bfloat16
    row_count, width = tokens.shape
    owned, _, local_width = w_qkv.shape
    hidden = w_gu.shape[2]
    valid_len = valid_counts[0]

    attn_part = jnp.concatenate(
        [w_qkv.reshape(owned, 3 * local_width), w_out.T], axis=1
    ).astype(half)
    attn_w = lax.all_gather(attn_part, "dp", axis=0, tiled=True)
    row_ids = lax.axis_index("mp") * row_count + jnp.arange(row_count, dtype=jnp.int32)
    live_rows = (row_ids < valid_len).astype(jnp.float32)[:, None]
    key_mask = (jnp.arange(SEQ, dtype=jnp.int32) < valid_len).astype(jnp.float32)
    ffn_part, tokens_in = lax.optimization_barrier((round_shares(w_gu, w_down), tokens))
    h_first, gain_all, out_grad, own_branch = gather_first(
        n_dp, n_mp, tokens_in, gains, cotangent, live_rows, 1
    )
    ffn_w = lax.all_gather(ffn_part, "dp", axis=0, tiled=True)
    cosine, sine = (jnp.asarray(x, jnp.float32) for x in rope_tables(SEQ, HDIM // 2))

    second, normed_second, queries, keys, values, mixed, branch_grad = scatter_rows(
        n_mp,
        [h_first],
        attn_w,
        3 * local_width,
        [tokens],
        "forward",
        gain_all,
        1,
        2,
        heads=(cosine, sine, key_mask[None, :]),
        extra=own_branch,
    )

    second_grad, own_grad, gain_two, grad_ffn, act, _, _ = feed_forward(
        n_mp, normed_second, branch_grad, ffn_w, second, gain_all, 3
    )
    sum_ffn = lax.psum_scatter(grad_ffn, "dp", scatter_dimension=0, tiled=True)
    block_out, attn_grad, mixed_grad = scatter_rows(
        n_mp,
        [act],
        ffn_w,
        2 * hidden,
        [second],
        "residual",
        gain_all,
        1,
        7,
        extra=own_grad,
        extra_right=(attn_w, 3 * local_width),
    )

    joined_grad = attention_backward(
        queries, keys, values, mixed_grad, cosine, sine, valid_counts
    )
    input_grad, gain_tile, sum_attn = scatter_rows(
        n_mp,
        list(joined_grad),
        attn_w,
        0,
        [tokens, second_grad],
        "last",
        gain_all,
        0,
        4,
        other_gain=gain_two,
        grad_lefts=[h_first, attn_grad],
        grad_right=mixed,
        n_dp=n_dp,
    )

    total_rows = SEQ * n_dp
    matrix_rate = step_rate / math.sqrt(total_rows)
    scale_rate = gain_rate / math.sqrt(total_rows)
    local = gains.shape[1]
    place = lax.rem((lax.axis_index("dp") * n_mp + lax.axis_index("mp")) * local, 128)
    sum_gains = lax.dynamic_slice(gain_tile, (0, place), (2, local))
    gu, down, out, qkv, (block_out, input_grad) = update_all(
        [w_gu, mom_gu, avg_gu],
        [w_qkv, mom_qkv, avg_qkv],
        (
            ([w_down, mom_down, avg_down], 2 * hidden),
            ([w_out, mom_out, avg_out], 3 * local_width),
        ),
        sum_ffn,
        sum_attn,
        [block_out, input_grad],
        matrix_rate,
    )
    new_gu, next_mom_gu, next_avg_gu, copy_gu = gu
    new_down, next_mom_down, next_avg_down, copy_down = down
    new_out, next_mom_out, next_avg_out, copy_out = out
    new_qkv, next_mom_qkv, next_avg_qkv, copy_qkv = qkv
    new_gains, next_mom_gains, next_avg_gains = updated(
        gains, mom_gains, avg_gains, sum_gains, scale_rate
    )
    return (
        block_out,
        input_grad,
        new_qkv,
        new_out,
        new_gu,
        new_down,
        new_gains,
        next_mom_qkv,
        next_mom_out,
        next_mom_gu,
        next_mom_down,
        next_mom_gains,
        next_avg_qkv,
        next_avg_out,
        next_avg_gu,
        next_avg_down,
        next_avg_gains,
        copy_qkv,
        copy_out,
        copy_gu,
        copy_down,
    )


def solution(mesh):
    rows, one = P(("dp", "mp"), None), P("dp")
    tall, wide, spread = P("dp", None, "mp"), P("mp", "dp"), P(None, ("dp", "mp"))
    weights = (tall, wide, tall, wide)
    return jax.shard_map(
        functools.partial(per_device, mesh.shape["dp"], mesh.shape["mp"]),
        mesh=mesh,
        in_specs=(rows, rows, one, *((*weights, spread) * 3)),
        out_specs=(rows, rows, *((*weights, spread) * 3), *weights),
        check_vma=False,
    )
```

```python
import functools
import math

import jax
import jax.numpy as jnp
from jax import lax
from jax.experimental import pallas as pl
from jax.experimental.pallas import tpu as pltpu
import numpy as np
from jax.sharding import PartitionSpec as P

HDIM = 128
SEQ = 1024
MESH = pl.DeviceIdType.MESH
ANY = pl.BlockSpec(memory_space=pl.ANY)
VMEM = pl.BlockSpec(memory_space=pltpu.VMEM)
VMEM_LIMIT = 60 * 1024 * 1024

norm_eps = 1e-05
rope_base = 10000.0
momentum_decay = 0.9
average_decay = 0.9
step_rate = 0.05
gain_rate = 0.5


def rows_at(start, size):
    return pl.ds(pl.multiple_of(start, size), size)


def remote(src, dst, send_sem, recv_sem, peer):
    return pltpu.make_async_remote_copy(
        src_ref=src,
        dst_ref=dst,
        send_sem=send_sem,
        recv_sem=recv_sem,
        device_id={"mp": peer},
        device_id_type=MESH,
    )


def neighbour_barrier(n):
    me = lax.axis_index("mp")
    barrier = pltpu.get_barrier_semaphore()

    @pl.when(me > 0)
    def _():
        pl.semaphore_signal(barrier, inc=1, device_id={"mp": me - 1}, device_id_type=MESH)

    @pl.when(me < n - 1)
    def _():
        pl.semaphore_signal(barrier, inc=1, device_id={"mp": me + 1}, device_id_type=MESH)

    pl.semaphore_wait(barrier, jnp.where(me > 0, 1, 0) + jnp.where(me < n - 1, 1, 0))


class LineGather:
    def __init__(self, n, rows, chunks, own, whole, sems):
        self.n, self.rows, self.chunks = n, rows, chunks
        self.size = rows // chunks
        self.own, self.whole, self.sems = own, whole, sems
        self.me = lax.axis_index("mp")

    def at(self, block, chunk):
        return self.whole.at[rows_at(block * self.rows + chunk * self.size, self.size)]

    def copies(self, step, chunk, first):
        me, n = self.me, self.n
        send_r, recv_r, send_l, recv_l = self.sems
        out = []
        for block, peer, has, send, recv in (
            (me - step, me + 1, (me - step >= 0) & (me < n - 1), send_r, recv_r),
            (me + step, me - 1, (me + step <= n - 1) & (me > 0), send_l, recv_l),
        ):
            src = (
                self.own.at[pl.ds(chunk * self.size, self.size)]
                if first
                else self.at(block, chunk)
            )
            index = step * self.chunks + chunk
            out.append(
                (has, remote(src, self.at(block, chunk), send.at[index], recv.at[index], peer))
            )
        return out

    def arrivals(self, step, chunk):
        me, n = self.me, self.n
        send_r, recv_r, send_l, recv_l = self.sems
        index = step * self.chunks + chunk
        out = []
        for block, has, send, recv in (
            (me - 1 - step, me - 1 - step >= 0, send_r, recv_r),
            (me + 1 + step, me + 1 + step <= n - 1, send_l, recv_l),
        ):
            ref = self.at(block, chunk)
            out.append((has, remote(ref, ref, send.at[index], recv.at[index], me)))
        return out

    def send_own(self, chunk):
        for has, copy in self.copies(0, chunk, True):
            pl.when(has)(copy.start)

    def forward(self, step):
        for chunk in range(self.chunks):
            self.forward_chunk(step, chunk, True)

    def forward_chunk(self, step, chunk, more):
        for (got, arrival), (has, copy) in zip(
            self.arrivals(step - 1, chunk), self.copies(step, chunk, False)
        ):
            pl.when(got)(arrival.wait_recv)
            pl.when(has & more)(copy.start)

    def finish(self, arrivals=True):
        for chunk in range(self.chunks if arrivals else 0):
            for got, arrival in self.arrivals(self.n - 2, chunk):
                pl.when(got)(arrival.wait_recv)
        for chunk in range(self.chunks):
            for has, copy in self.copies(0, chunk, True):
                pl.when(has)(copy.wait_send)

        def waits(step, carry):
            for chunk in range(self.chunks):
                for has, copy in self.copies(step, chunk, False):
                    pl.when(has)(copy.wait_send)
            return carry

        lax.fori_loop(1, self.n - 1, waits, 0)

    def forward_all(self):
        def step_of(step, carry):
            self.forward(step)
            return carry

        lax.fori_loop(1, self.n - 1, step_of, 0)


def gather_sems(n, chunks):
    return [pltpu.SemaphoreType.DMA(((n - 1) * chunks,))] * 4


class Exchange:
    def __init__(self, n_dp, n_mp, sems):
        self.n_dp, self.n_mp = n_dp, n_mp
        self.s_mp, self.r_mp, self.s_dp, self.r_dp = sems
        self.dp, self.mp = lax.axis_index("dp"), lax.axis_index("mp")

    def barrier(self):
        barrier = pltpu.get_barrier_semaphore()
        for axis, here, count in (("mp", self.mp, self.n_mp), ("dp", self.dp, self.n_dp)):
            for k in range(1, count):
                pl.semaphore_signal(
                    barrier,
                    inc=1,
                    device_id={axis: lax.rem(here + k, count)},
                    device_id_type=MESH,
                )
        pl.semaphore_wait(barrier, self.n_mp + self.n_dp - 2)

    def swap(self, axis, source_of, target):
        if axis == "mp":
            here, count, send, recv = self.mp, self.n_mp, self.s_mp, self.r_mp
        else:
            here, count, send, recv = self.dp, self.n_dp, self.s_dp, self.r_dp
        copies = []
        for k in range(1, count):
            peer = lax.rem(here + k, count)
            copies.append(
                pltpu.make_async_remote_copy(
                    src_ref=source_of(peer),
                    dst_ref=target.at[here],
                    send_sem=send.at[k - 1],
                    recv_sem=recv.at[k - 1],
                    device_id={axis: peer},
                    device_id_type=MESH,
                )
            )
        for copy in copies:
            copy.start()
        return copies


def exchange_sems(n_dp, n_mp):
    return [pltpu.SemaphoreType.DMA((n_mp - 1,))] * 2 + [pltpu.SemaphoreType.DMA((n_dp - 1,))] * 2


def tile_of(dp, mp, n_mp, local):
    return (dp * n_mp + mp) * local // 128


def flat_pairs(x):
    high, parts, wide = x.shape
    return x.reshape(high, parts, wide // 128, 128).transpose(0, 2, 1, 3).reshape(-1, 128)


def round_shares(w_gu, w_down):
    high, parts, hidden = w_gu.shape
    tiles = hidden // 128
    step = 128
    turn = min(256, hidden)

    def kernel(gu_ref, down_ref, out_ref):
        for part in range(parts):
            for tile in range(tiles):
                cols = pl.ds(part * hidden + tile * 128, 128)
                out_ref[:, cols] = gu_ref[
                    pl.ds(tile * parts + part, step, stride=tiles * parts), :
                ].astype(jnp.bfloat16)
        for i in range(hidden // turn):
            piece = down_ref[pl.ds(i * turn, turn), :]
            out_ref[:, pl.ds(parts * hidden + i * turn, turn)] = piece.T.astype(jnp.bfloat16)

    return pl.pallas_call(
        kernel,
        grid=(high // step,),
        out_shape=jax.ShapeDtypeStruct((high, (parts + 1) * hidden), jnp.bfloat16),
        in_specs=[
            pl.BlockSpec((step * tiles * parts, 128), lambda i: (i, 0)),
            pl.BlockSpec((hidden, step), lambda i: (0, i)),
        ],
        out_specs=pl.BlockSpec((step, (parts + 1) * hidden), lambda i: (i, 0)),
        compiler_params=pltpu.CompilerParams(vmem_limit_bytes=VMEM_LIMIT),
        cost_estimate=pl.CostEstimate(
            flops=0, bytes_accessed=6 * (w_gu.size + w_down.size), transcendentals=0
        ),
        name="round_shares",
    )(flat_pairs(w_gu), w_down)


def gather_first(n_dp, n_mp, own, gains, cotangent, live, collective_id, chunks=2):
    rows, width = own.shape
    local = gains.shape[1]
    lanes = jnp.arange(128, dtype=jnp.int32) // local
    place = lax.rem(lax.axis_index("mp"), 128 // local)
    if n_mp * local < 128:
        place = lax.rem(lax.axis_index("dp") * n_mp + lax.axis_index("mp"), 128 // local)
    tile = jnp.where(
        (lanes == place)[None, :], jnp.tile(gains, (1, 128 // local)), 0.0
    )
    tile = jnp.concatenate([tile, jnp.zeros((6, 128), jnp.float32)], axis=0)

    block = 64 if rows % 64 == 0 else rows

    def kernel(
        own_ref,
        tile_ref,
        cotangent_ref,
        live_ref,
        normed_hbm,
        gain_ref,
        base_hbm,
        branch_hbm,
        all_ref,
        first,
        second,
        normed_ref,
        base_ref,
        branch_ref,
        out_sems,
        *sems,
    ):
        me = lax.axis_index("mp")
        exchange = Exchange(n_dp, n_mp, sems[:4])
        stream = LineGather(n_mp, rows, chunks, own_ref, all_ref, sems[4:])
        exchange.barrier()
        first[me] = tile_ref[...]
        copies = exchange.swap("mp", lambda peer: tile_ref, first)
        for chunk in range(chunks):
            stream.send_own(chunk)
        all_ref[rows_at(me * rows, rows), :] = own_ref[...]
        for copy in copies:
            copy.wait()
        dp = lax.axis_index("dp")
        second[dp] = first[...]
        copies = exchange.swap("dp", lambda peer: first, second)

        def enter(i, carry):
            span = rows_at(i * block, block)
            value = cotangent_ref[span, :].astype(jnp.float32) * live_ref[span, :]
            base_ref[span, :] = value
            branch_ref[span, :] = value.astype(jnp.bfloat16)
            return carry

        lax.fori_loop(0, rows // block, enter, 0)
        leaving = [
            pltpu.make_async_copy(base_ref, base_hbm, out_sems.at[n_mp]),
            pltpu.make_async_copy(branch_ref, branch_hbm, out_sems.at[n_mp + 1]),
        ]
        for copy in leaving:
            copy.start()
        for copy in copies:
            copy.wait()
        gain_ref[...] = jnp.zeros_like(gain_ref)
        for d in range(n_dp):
            for m in range(n_mp):
                cols = pl.ds(tile_of(d, m, n_mp, local) * 128, 128)
                gain_ref[:, cols] += second[d, m]
        def leave(block_id):
            span = rows_at(block_id * rows, rows)
            return pltpu.make_async_copy(
                normed_ref.at[span], normed_hbm.at[span], out_sems.at[block_id]
            )

        def norm(block_id):
            def body(i, carry):
                span = rows_at(block_id * rows + i * block, block)
                value = all_ref[span, :].astype(jnp.float32)
                inverse = lax.rsqrt(jnp.mean(value * value, axis=1, keepdims=True) + norm_eps)
                normed_ref[span, :] = (value * inverse * gain_ref[0:1, :]).astype(jnp.bfloat16)
                return carry

            lax.fori_loop(0, rows // block, body, 0)
            leave(block_id).start()

        def step_of(step, carry):
            @pl.when(step > 0)
            def _():
                for chunk in range(chunks):
                    stream.forward_chunk(step, chunk, step < n_mp - 1)

            @pl.when(me + step < n_mp)
            def _():
                norm(me + step)

            @pl.when((me - step >= 0) & (step > 0))
            def _():
                norm(me - step)

            return carry

        lax.fori_loop(0, n_mp, step_of, 0)
        stream.finish(False)
        for block_id in range(n_mp):
            leave(block_id).wait()
        for copy in leaving:
            copy.wait()

    half = jnp.bfloat16
    return pl.pallas_call(
        kernel,
        out_shape=[
            jax.ShapeDtypeStruct((n_mp * rows, width), half),
            jax.ShapeDtypeStruct((8, width), jnp.float32),
            jax.ShapeDtypeStruct((rows, width), jnp.float32),
            jax.ShapeDtypeStruct((rows, width), half),
        ],
        in_specs=[VMEM] * 4,
        out_specs=[ANY, VMEM, ANY, ANY],
        scratch_shapes=[
            pltpu.VMEM((n_mp * rows, width), half),
            pltpu.VMEM((n_mp, 8, 128), jnp.float32),
            pltpu.VMEM((n_dp, n_mp, 8, 128), jnp.float32),
            pltpu.VMEM((n_mp * rows, width), half),
            pltpu.VMEM((rows, width), jnp.float32),
            pltpu.VMEM((rows, width), half),
            pltpu.SemaphoreType.DMA((n_mp + 2,)),
        ]
        + exchange_sems(n_dp, n_mp)
        + gather_sems(n_mp, chunks),
        compiler_params=pltpu.CompilerParams(
            collective_id=collective_id, has_side_effects=True, vmem_limit_bytes=VMEM_LIMIT
        ),
        cost_estimate=pl.CostEstimate(
            flops=0, bytes_accessed=200 * own.size * own.dtype.itemsize, transcendentals=0
        ),
        name="gather_first",
    )(own, tile, cotangent, live)


def dot_t(left, right):
    return lax.dot_general(
        left, right, (((1,), (1,)), ((), ())), preferred_element_type=jnp.float32
    )


def t_dot(left, right):
    return lax.dot_general(
        left, right, (((0,), (0,)), ((), ())), preferred_element_type=jnp.float32
    )


def dot(left, right):
    return jnp.dot(left, right, preferred_element_type=jnp.float32)


def probability(raw):
    return 1.0 / (1.0 + jnp.exp(math.log(SEQ) - raw * (1.0 / math.sqrt(HDIM))))


def rotated(values, cosine, sine, backward=False):
    turned = pltpu.roll(values, HDIM // 2, 1) * sine
    return values * cosine - turned if backward else values * cosine + turned


def scatter_rows(
    n,
    lhs,
    rhs,
    rhs_start,
    own_rows,
    epilogue,
    gains,
    gain_row,
    collective_id,
    heads=None,
    extra=None,
    extra_right=None,
    other_gain=None,
    grad_lefts=None,
    grad_right=None,
    n_dp=1,
    chunks=2,
):
    total_rows = lhs[0].shape[0]
    rows = total_rows // n
    width = gains.shape[1]
    size = rows // chunks
    tile = 512
    has_norm, has_gain = epilogue in ("forward", "backward"), epilogue in ("backward", "last")
    count = len(lhs)
    block = 32
    if heads is not None:
        inner_width = rhs_start // 3
        head_count = inner_width // HDIM
        pieces = [inner_width]
    else:
        pieces = [a.shape[1] for a in lhs]
    depth = sum(pieces)
    if extra_right is not None:
        extra_width = extra_right[0].shape[1] - extra_right[1]

    def kernel(*refs):
        refs = list(refs)

        def take(k):
            return [refs.pop(0) for _ in range(k)]

        left_hbm = take(count)
        (right_hbm,) = take(1)
        (gain_ref,) = take(1)
        own_hbm = take(len(own_rows))
        if heads is not None:
            (mask_ref,) = take(1)
            table_hbm = take(2)
        if other_gain is not None:
            (other_ref,) = take(1)
            grad_hbm = take(3)
        extra_ref = take(1)[0] if extra is not None else None
        extra_right_hbm = take(1)[0] if extra_right is not None else None
        outs = take(1 + has_gain)
        owned_ref = take(1)[0] if other_gain is not None else None
        normed = take(1)[0] if has_norm else None
        if heads is not None:
            head_hbm = take(4)
        extra_whole = take(1)[0] if extra is not None else None
        if extra_right is not None:
            (extra_out,) = take(1)
        right, held, sent, part = take(4)
        joined_ref = take(1)[0] if heads is not None else None
        right_sem, send_sems, recv_sems = take(3)
        own, own_sems = take(len(own_rows)), take(1)[0]
        left_refs, left_sems = take(count), take(1)[0]
        left_loads = [
            pltpu.make_async_copy(hbm, ref, left_sems.at[k])
            for k, (hbm, ref) in enumerate(zip(left_hbm, left_refs))
        ]
        for load in left_loads:
            load.start()
        if heads is not None:
            cosine_ref, sine_ref = take(2)
            query_ref, key_ref, value_ref, mixed_ref = take(4)
            table_sems, head_sems = take(2)
            tables = [
                pltpu.make_async_copy(hbm, ref, table_sems.at[k])
                for k, (hbm, ref) in enumerate(zip(table_hbm, (cosine_ref, sine_ref)))
            ]
            for load in tables:
                load.start()
            heads_out = [
                pltpu.make_async_copy(ref, hbm, head_sems.at[k])
                for k, (ref, hbm) in enumerate(
                    zip((query_ref, key_ref, value_ref, mixed_ref), head_hbm)
                )
            ]
        own_loads = [
            pltpu.make_async_copy(hbm, ref, own_sems.at[k])
            for k, (hbm, ref) in enumerate(zip(own_hbm, own))
        ]
        me = lax.axis_index("mp")
        fetch = pltpu.make_async_copy(
            right_hbm.at[:, pl.ds(rhs_start, depth)], right, right_sem
        )
        fetch.start()
        if heads is not None:
            (joined_sem,) = take(1)
            fetch_joined = pltpu.make_async_copy(
                right_hbm.at[:, pl.ds(0, rhs_start)], joined_ref, joined_sem
            )
            fetch_joined.start()
        if extra is not None:
            (extra_sem,) = take(1)
            extra_sems = take(4)
            if extra_right is None:
                extra_gather = LineGather(n, rows, 1, extra_ref, extra_whole, extra_sems)
                extra_local = pltpu.make_async_copy(extra_ref, extra_gather.at(me, 0), extra_sem)
                extra_local.start()
            else:
                extra_all, extra_right_ref, extra_right_sem = take(3)
                extra_gather = LineGather(n, rows, 1, extra_ref, extra_all, extra_sems)
                extra_fetch = pltpu.make_async_copy(
                    extra_right_hbm.at[:, pl.ds(extra_right[1], extra_width)],
                    extra_right_ref,
                    extra_right_sem,
                )
                extra_fetch.start()

                def extra_product(block_id):
                    @pl.when((block_id >= 0) & (block_id < n))
                    def _():
                        span = rows_at(block_id * rows, rows)
                        extra_out[span, :] = dot(
                            extra_all[span, :], extra_right_ref[...]
                        ).astype(jnp.bfloat16)
        if other_gain is not None:
            gain_sum, table, first, middle, second = take(5)
            exchange = Exchange(n_dp, n, take(4))
            *grad_left_refs, grad_right_ref, grad_load_sems = take(4)
            grad_loads = [
                pltpu.make_async_copy(hbm, ref, grad_load_sems.at[k])
                for k, (hbm, ref) in enumerate(zip(grad_hbm, [*grad_left_refs, grad_right_ref]))
            ]
            for load in grad_loads:
                load.start()
            grads, paired, landed = take(3)
            pair_send, pair_recv, land_send, land_recv = take(4)
            dp = lax.axis_index("dp")
            core, chip = lax.rem(dp, 2), dp // 2
            chips, share = n_dp // 2, landed.shape[1]
            exchange.barrier()
            pair_copies = [
                pltpu.make_async_remote_copy(
                    src_ref=grads.at[rows_at((2 * q + 1 - core) * share, share)],
                    dst_ref=paired.at[q],
                    send_sem=pair_send.at[q],
                    recv_sem=pair_recv.at[q],
                    device_id={"dp": dp + 1 - 2 * core},
                    device_id_type=MESH,
                )
                for q in range(chips)
            ]
            land_copies = [
                pltpu.make_async_remote_copy(
                    src_ref=paired.at[lax.rem(chip + k, chips)],
                    dst_ref=landed.at[k - 1],
                    send_sem=land_send.at[k - 1],
                    recv_sem=land_recv.at[k - 1],
                    device_id={"dp": 2 * lax.rem(chip + k, chips) + core},
                    device_id_type=MESH,
                )
                for k in range(1, chips)
            ]

            def make_grads():
                for load in grad_loads:
                    load.wait()
                start, narrow = 0, 256
                for k, right_ref in enumerate([*left_refs, grad_right_ref]):
                    left_ref = grad_left_refs[0 if k < count else 1]

                    def column(i, carry, start=start, left_ref=left_ref, right_ref=right_ref):
                        grads[:, rows_at(start + i * narrow, narrow)] = t_dot(
                            left_ref[...], right_ref[:, rows_at(i * narrow, narrow)]
                        ).astype(jnp.bfloat16)
                        return carry

                    lax.fori_loop(0, right_ref.shape[1] // narrow, column, 0)
                    start += right_ref.shape[1]
                for copy in pair_copies:
                    copy.start()
                for copy in pair_copies:
                    copy.wait()

                def add(i, carry):
                    span = rows_at(i * block, block)
                    for q in range(chips):
                        own_span = rows_at((2 * q + core) * share + i * block, block)
                        paired[q, span, :] = (
                            paired[q, span, :].astype(jnp.float32)
                            + grads[own_span, :].astype(jnp.float32)
                        ).astype(jnp.bfloat16)
                    return carry

                lax.fori_loop(0, share // block, add, 0)
                for copy in land_copies:
                    copy.start()

            def land():
                for copy in land_copies:
                    copy.wait()

                def add(i, carry):
                    span = rows_at(i * block, block)
                    total = paired[chip, span, :].astype(jnp.float32)
                    for k in range(chips - 1):
                        total = total + landed[k, span, :].astype(jnp.float32)
                    owned_ref[span, :] = total
                    return carry

                lax.fori_loop(0, share // block, add, 0)

        else:
            gain_sum = outs[1] if has_gain else None
            neighbour_barrier(n)
        if extra is not None:
            extra_gather.send_own(0)
        if extra_right is not None:
            extra_all[rows_at(me * rows, rows), :] = extra_ref[...]
            extra_fetch.wait()
        if heads is not None:
            turn = 256
            fetch_joined.wait()
            for load in [*tables, *left_loads]:
                load.wait()

            def enter(i, carry):
                span = rows_at(i * turn, turn)
                cosine, sine = cosine_ref[span, :], sine_ref[span, :]
                row_vals = left_refs[0][span, :]
                for k, target in ((0, query_ref), (1, key_ref), (2, value_ref)):
                    piece = dot(row_vals, joined_ref[:, pl.ds(k * inner_width, inner_width)])
                    for h in range(head_count):
                        value = piece[:, h * HDIM : (h + 1) * HDIM]
                        if k < 2:
                            value = rotated(value, cosine, sine)
                        target[span, pl.ds(h * HDIM, HDIM)] = value.astype(jnp.bfloat16)
                return carry

            lax.fori_loop(0, total_rows // turn, enter, 0)
            for copy in heads_out[:3]:
                copy.start()
        for load in own_loads:
            load.start()
        fetch.wait()
        if heads is None:
            for load in left_loads:
                load.wait()

        def attend(block_id):
            span = rows_at(block_id * rows, rows)
            row_pos = block_id * rows + lax.broadcasted_iota(jnp.int32, (rows, rows), 0)

            def against(kb, totals):
                other = rows_at(kb * rows, rows)
                col_pos = kb * rows + lax.broadcasted_iota(jnp.int32, (rows, rows), 1)
                allowed = jnp.where(col_pos <= row_pos, mask_ref[:, other], 0.0)
                out = []
                for h in range(head_count):
                    cols = pl.ds(h * HDIM, HDIM)
                    raw = dot_t(query_ref[span, cols], key_ref[other, cols])
                    prob = probability(raw) * allowed
                    out.append(
                        totals[h]
                        + jnp.dot(
                            prob.astype(jnp.bfloat16),
                            value_ref[other, cols],
                            preferred_element_type=jnp.float32,
                        )
                    )
                return tuple(out)

            start = tuple(jnp.zeros((rows, HDIM), jnp.float32) for _ in range(head_count))
            totals = lax.fori_loop(0, block_id + 1, against, start)
            for h in range(head_count):
                mixed_ref[span, pl.ds(h * HDIM, HDIM)] = totals[h].astype(jnp.bfloat16)

        def product(block_id):
            if heads is not None:
                attend(block_id)
            sources = [mixed_ref] if heads is not None else left_refs

            def column(ct, carry):
                cols = rows_at(ct * tile, tile)
                total, start = None, 0
                for source, piece in zip(sources, pieces):
                    term = dot_t(
                        source[rows_at(block_id * rows, rows), :],
                        right[cols, pl.ds(start, piece)],
                    )
                    start += piece
                    total = term if total is None else total + term
                part[:, cols] = total
                return carry

            lax.fori_loop(0, width // tile, column, 0)

        def hop(block_id, chunk, rightward):
            peer = me + 1 if rightward else me - 1
            slot = block_id if rightward else jnp.where(block_id == peer, n, block_id)
            return remote(
                sent.at[block_id, pl.ds(chunk * size, size)],
                held.at[slot, pl.ds(chunk * size, size)],
                send_sems.at[block_id * chunks + chunk],
                recv_sems.at[slot * chunks + chunk],
                peer,
            )

        def arrival(slot, chunk):
            ref = held.at[slot, pl.ds(chunk * size, size)]
            return remote(
                ref, ref, send_sems.at[chunk], recv_sems.at[slot * chunks + chunk], me
            )

        def add_rows(block_id, chunk, slots):
            def body(i, carry):
                span = rows_at(chunk * size + i * block, block)
                value = part[span, :]
                for slot in slots:
                    value = value + held[slot, span, :].astype(jnp.float32)
                sent[block_id, span, :] = value.astype(jnp.bfloat16)
                return carry

            lax.fori_loop(0, size // block, body, 0)

        def relay(block_id, rightward, inner):
            product(block_id)
            for chunk in range(chunks):

                @pl.when(inner)
                def _():
                    arrival(block_id, chunk).wait_recv()
                    add_rows(block_id, chunk, [block_id])

                @pl.when(jnp.logical_not(inner))
                def _():
                    add_rows(block_id, chunk, [])

                hop(block_id, chunk, rightward).start()

        def step_of(step, carry):
            @pl.when((step >= me + 1) & (me < n - 1))
            def _():
                relay(me + n - step, True, me > 0)

            @pl.when((step >= n - me) & (me > 0))
            def _():
                relay(me - n + step, False, me < n - 1)

            if extra is not None:

                @pl.when(step < n - 1)
                def _():
                    extra_gather.forward(step)
                    if extra_right is not None:
                        extra_product(me - step)
                        extra_product(me + step)

            if other_gain is not None:
                pl.when(step == 1)(make_grads)

            return carry

        lax.fori_loop(1, n, step_of, 0)
        product(me)
        if heads is not None:
            heads_out[3].start()
        if extra_right is not None:
            extra_product(me)
        for load in own_loads:
            load.wait()
        if has_gain:
            gain_sum[...] = jnp.zeros_like(gain_sum)
        for chunk in range(chunks):

            @pl.when(me > 0)
            def _():
                arrival(me, chunk).wait_recv()

            @pl.when(me < n - 1)
            def _():
                arrival(n, chunk).wait_recv()

            def body(i, carry):
                span = rows_at(chunk * size + i * block, block)
                total = part[span, :]
                zero = jnp.zeros_like(total)
                total = total + jnp.where(me > 0, held[me, span, :].astype(jnp.float32), zero)
                total = total + jnp.where(
                    me < n - 1, held[n, span, :].astype(jnp.float32), zero
                )
                gain = gain_ref[gain_row : gain_row + 1, :]
                if epilogue == "residual":
                    outs[0][span, :] = (own[0][span, :] + total).astype(jnp.bfloat16)
                elif epilogue == "forward":
                    value = own[0][span, :].astype(jnp.float32) + total
                    outs[0][span, :] = value
                    inverse = lax.rsqrt(
                        jnp.mean(value * value, axis=1, keepdims=True) + norm_eps
                    )
                    normed[span, :] = (value * inverse * gain).astype(jnp.bfloat16)
                else:
                    value = own[0][span, :].astype(jnp.float32)
                    inverse = lax.rsqrt(
                        jnp.mean(value * value, axis=1, keepdims=True) + norm_eps
                    )
                    unit = value * inverse
                    scaled = total * gain
                    inner = jnp.mean(scaled * unit, axis=1, keepdims=True)
                    result = own[1][span, :] + inverse * (scaled - unit * inner)
                    outs[0][span, :] = result
                    gain_sum[...] += jnp.sum(
                        (total * unit).reshape(block // 8, 8, width), axis=0
                    )
                    if has_norm:
                        normed[span, :] = result.astype(jnp.bfloat16)
                return carry

            lax.fori_loop(0, size // block, body, 0)
        if extra is not None:
            extra_gather.finish()
        if extra_right is not None:
            extra_local = pltpu.make_async_copy(extra_all, extra_whole, extra_sem)
            extra_local.start()
            extra_product(me - (n - 1))
            extra_product(me + (n - 1))
        if extra is not None:
            extra_local.wait()
        if other_gain is not None:
            local = width // (n * n_dp)
            for row, source in ((0, gain_sum), (1, other_ref)):
                total = jnp.sum(source[...], axis=0, keepdims=True)
                for d in range(n_dp):
                    for m in range(n):
                        start = tile_of(d, m, n, local) * 128
                        table[m, d, row : row + 1, :] = total[:, start : start + 128]
            copies = exchange.swap("mp", lambda peer: table.at[peer], first)
            first[me] = table[me]
            for copy in copies:
                copy.wait()
            total = first[0]
            for m in range(1, n):
                total = total + first[m]
            middle[...] = total
            copies = exchange.swap("dp", lambda peer: middle.at[peer], second)
            second[dp] = middle[dp]
            land()
            for copy in copies:
                copy.wait()
            total = second[0]
            for d in range(1, n_dp):
                total = total + second[d]
            outs[1][...] = total

        def sends(step, carry):
            for chunk in range(chunks):

                @pl.when((step >= me + 1) & (me < n - 1))
                def _():
                    hop(me + n - step, chunk, True).wait_send()

                @pl.when((step >= n - me) & (me > 0))
                def _():
                    hop(me - n + step, chunk, False).wait_send()

            return carry

        lax.fori_loop(1, n, sends, 0)
        if heads is not None:
            for copy in heads_out:
                copy.wait()

    out_type = jnp.bfloat16 if epilogue == "residual" else jnp.float32
    out_shape = [jax.ShapeDtypeStruct((rows, width), out_type)]
    out_specs = [VMEM]
    if has_gain:
        out_shape.append(
            jax.ShapeDtypeStruct((8, width) if other_gain is None else (2, 128), jnp.float32)
        )
        out_specs.append(VMEM)
    if other_gain is not None:
        share = width // n_dp
        grad_width = sum(pieces) + grad_right.shape[1]
        out_shape.append(jax.ShapeDtypeStruct((share, grad_width), jnp.float32))
        out_specs.append(VMEM)
    scratch = [
        pltpu.VMEM((width, depth), jnp.bfloat16),
        pltpu.VMEM((n + 1, rows, width), jnp.bfloat16),
        pltpu.VMEM((n, rows, width), jnp.bfloat16),
        pltpu.VMEM((rows, width), jnp.float32),
    ]
    if heads is not None:
        scratch.append(pltpu.VMEM((width, rhs_start), jnp.bfloat16))
    if has_norm:
        out_shape.append(jax.ShapeDtypeStruct((rows, width), jnp.bfloat16))
        out_specs.append(VMEM)
    scratch += [
        pltpu.SemaphoreType.DMA,
        pltpu.SemaphoreType.DMA((n * chunks,)),
        pltpu.SemaphoreType.DMA(((n + 1) * chunks,)),
    ]
    scratch += [pltpu.VMEM(x.shape, x.dtype) for x in own_rows]
    scratch.append(pltpu.SemaphoreType.DMA((len(own_rows),)))
    scratch += [pltpu.VMEM(x.shape, x.dtype) for x in lhs]
    scratch.append(pltpu.SemaphoreType.DMA((count,)))
    if heads is not None:
        scratch += [pltpu.VMEM(x.shape, x.dtype) for x in heads[:2]]
        scratch += [pltpu.VMEM((total_rows, inner_width), jnp.bfloat16)] * 4
        scratch += [pltpu.SemaphoreType.DMA((2,)), pltpu.SemaphoreType.DMA((4,))]
    head_args = []
    if heads is not None:
        scratch.append(pltpu.SemaphoreType.DMA)
        head_args = [heads[2]]
        out_shape += [jax.ShapeDtypeStruct((total_rows, inner_width), jnp.bfloat16)] * 4
        out_specs += [ANY] * 4
    extra_args = []
    if extra is not None:
        out_shape.append(jax.ShapeDtypeStruct((total_rows, width), jnp.bfloat16))
        out_specs.append(ANY)
        scratch += [pltpu.SemaphoreType.DMA] + gather_sems(n, 1)
        extra_args = [extra]
    if extra_right is not None:
        out_shape.append(jax.ShapeDtypeStruct((total_rows, extra_width), jnp.bfloat16))
        out_specs.append(VMEM)
        scratch += [
            pltpu.VMEM((total_rows, width), jnp.bfloat16),
            pltpu.VMEM((width, extra_width), jnp.bfloat16),
            pltpu.SemaphoreType.DMA,
        ]
        extra_args.append(extra_right[0])
    late_args = list(heads[:2]) if heads is not None else []
    if other_gain is not None:
        head_args.append(other_gain)
        late_args = [*grad_lefts, grad_right]
        scratch += [
            pltpu.VMEM((8, width), jnp.float32),
            pltpu.VMEM((n, n_dp, 2, 128), jnp.float32),
            pltpu.VMEM((n, n_dp, 2, 128), jnp.float32),
            pltpu.VMEM((n_dp, 2, 128), jnp.float32),
            pltpu.VMEM((n_dp, 2, 128), jnp.float32),
        ] + exchange_sems(n_dp, n)
        scratch += [pltpu.VMEM(x.shape, x.dtype) for x in late_args]
        scratch.append(pltpu.SemaphoreType.DMA((len(late_args),)))
        chips = n_dp // 2
        scratch.append(pltpu.VMEM((width, grad_width), jnp.bfloat16))
        scratch.append(pltpu.VMEM((chips, share, grad_width), jnp.bfloat16))
        scratch.append(pltpu.VMEM((chips - 1, share, grad_width), jnp.bfloat16))
        scratch += [pltpu.SemaphoreType.DMA((chips,))] * 2
        scratch += [pltpu.SemaphoreType.DMA((chips - 1,))] * 2
    flops = 2 * total_rows * depth * width
    return pl.pallas_call(
        kernel,
        out_shape=out_shape,
        in_specs=[ANY] * (count + 1)
        + [VMEM]
        + [ANY] * len(own_rows)
        + [VMEM] * len(head_args)
        + [ANY] * len(late_args)
        + [VMEM if extra_right is not None else ANY] * min(1, len(extra_args))
        + [ANY] * max(0, len(extra_args) - 1),
        out_specs=out_specs,
        scratch_shapes=scratch,
        compiler_params=pltpu.CompilerParams(
            collective_id=collective_id, has_side_effects=True, vmem_limit_bytes=VMEM_LIMIT
        ),
        cost_estimate=pl.CostEstimate(
            flops=flops, bytes_accessed=300_000_000, transcendentals=0
        ),
        name="scatter_" + epilogue,
    )(*lhs, rhs, gains, *own_rows, *head_args, *late_args, *extra_args)


def feed_forward(n, normed, branch_grad, weights, second, gains, collective_id, halves=1, hops=4):
    rows, width = normed.shape
    total_rows = n * rows
    hidden = weights.shape[1] // 3
    count, parcels = hops, halves
    part_size = rows // hops
    tile = min(1024, hidden)
    block = min(32, part_size)
    narrow = min(256, hidden)
    per = hidden // narrow
    pieces = 3 * per
    before = pieces // 6
    between = (pieces - 2 * before) // (count + 1)
    tall = min(1024, width)

    def kernel(
        normed_ref,
        branch_hbm,
        weights_hbm,
        second_ref,
        gain_ref,
        result_ref,
        rounded_ref,
        gain_sum,
        grads_hbm,
        act_hbm,
        gate_hbm,
        up_hbm,
        weight_ref,
        branch_ref,
        all_ref,
        held,
        sent,
        own_part,
        act_ref,
        gate_ref,
        up_ref,
        piece_ref,
        load_sems,
        stage_sems,
        piece_sems,
        grad_sems,
        send_sems,
        recv_sems,
        *gather_refs,
    ):
        me = lax.axis_index("mp")
        middle = (me > 0) & (me < n - 1)
        loads = [
            pltpu.make_async_copy(weights_hbm, weight_ref, load_sems.at[0]),
            pltpu.make_async_copy(branch_hbm, branch_ref, load_sems.at[1]),
        ]
        for load in loads:
            load.start()
        gather = LineGather(n, rows, parcels, normed_ref, all_ref, gather_refs)
        neighbour_barrier(n)
        for parcel in range(parcels):
            gather.send_own(parcel)
        all_ref[rows_at(me * rows, rows), :] = normed_ref[...]
        for load in loads:
            load.wait()

        def hop(block_id, chunk, rightward):
            peer = me + 1 if rightward else me - 1
            slot = block_id if rightward else jnp.where(block_id == peer, n, block_id)
            return remote(
                sent.at[block_id, pl.ds(chunk * part_size, part_size)],
                held.at[slot, pl.ds(chunk * part_size, part_size)],
                send_sems.at[block_id * count + chunk],
                recv_sems.at[slot * count + chunk],
                peer,
            )

        def arrival(slot, chunk):
            ref = held.at[slot, pl.ds(chunk * part_size, part_size)]
            return remote(
                ref, ref, send_sems.at[chunk], recv_sems.at[slot * count + chunk], me
            )

        def stages(block_id, chunk, size):
            span = rows_at(block_id * rows + chunk * size, size)
            return [
                pltpu.make_async_copy(
                    ref.at[pl.ds(chunk * size, size)], hbm.at[span], stage_sems.at[chunk * 3 + k]
                )
                for k, (ref, hbm) in enumerate(
                    ((act_ref, act_hbm), (gate_ref, gate_hbm), (up_ref, up_hbm))
                )
            ]

        def compute(block_id, chunk, size, first):
            here = pl.ds(chunk * size, size)
            span = rows_at(block_id * rows + chunk * size, size)

            @pl.when(jnp.logical_not(first))
            def _():
                for stage in stages(block_id, chunk, size):
                    stage.wait()

            def units(ct, carry):
                cols = rows_at(ct * tile, tile)
                row_vals, branch = all_ref[span, :], branch_ref[span, :]
                gate = dot(row_vals, weight_ref[:, cols])
                up = dot(row_vals, weight_ref[:, rows_at(hidden + ct * tile, tile)])
                act_grad = dot(branch, weight_ref[:, rows_at(2 * hidden + ct * tile, tile)])
                sigma = 1.0 / (1.0 + jnp.exp(-gate))
                silu = gate * sigma
                act_ref[here, cols] = (silu * up).astype(jnp.bfloat16)
                gate_ref[here, cols] = (
                    act_grad * up * sigma * (1.0 + gate * (1.0 - sigma))
                ).astype(jnp.bfloat16)
                up_ref[here, cols] = (act_grad * silu).astype(jnp.bfloat16)
                return carry

            lax.fori_loop(0, hidden // tile, units, 0)
            for stage in stages(block_id, chunk, size):
                stage.start()

            def columns(ct, carry):
                cols = rows_at(ct * tile, tile)
                total = dot_t(gate_ref[here, :], weight_ref[cols, pl.ds(0, hidden)])
                total += dot_t(up_ref[here, :], weight_ref[cols, pl.ds(hidden, hidden)])

                @pl.when(block_id == me)
                def _():
                    own_part[here, cols] = total

                @pl.when(block_id != me)
                def _():
                    sent[block_id, here, cols] = total.astype(jnp.bfloat16)

                return carry

            lax.fori_loop(0, width // tile, columns, 0)

            @pl.when((me == 0) & (block_id > me))
            def _():
                for k in range(size // part_size):
                    hop(block_id, chunk * (size // part_size) + k, True).start()

            @pl.when((me == n - 1) & (block_id < me))
            def _():
                for k in range(size // part_size):
                    hop(block_id, chunk * (size // part_size) + k, False).start()

        def forward(step, parcel):
            gather.forward_chunk(step, parcel, step < n - 1)

        def forward_whole(step):
            for parcel in range(parcels):
                forward(step, parcel)

        def step_of(step, carry):
            def side_of(side, carry):
                block_id = me + (1 - 2 * side) * step
                valid = (block_id >= 0) & (block_id < n) & ((step > 0) | (side == 0))

                @pl.when(middle & (step > 0) & (step < n - 1) & (side == 1))
                def _():
                    forward_whole(step + 1)

                @pl.when(middle & valid)
                def _():
                    compute(block_id, 0, rows, step == 0)

                @pl.when(middle & (step == 0) & (side == 0))
                def _():
                    forward_whole(1)

                for half in range(halves):

                    @pl.when(jnp.logical_not(middle) & valid)
                    def _():
                        pl.when(step > 0)(lambda: forward(step, half))
                        compute(block_id, half, rows // halves, step == 0)

                return carry

            return lax.fori_loop(0, 2, side_of, carry)

        lax.fori_loop(0, n, step_of, 0)
        @pl.when(middle)
        def _():
            for stage in stages(me, 0, rows):
                stage.wait()

        @pl.when(jnp.logical_not(middle))
        def _():
            for half in range(halves):
                for stage in stages(me, half, rows // halves):
                    stage.wait()


        def load_of(source, index, slot):
            return pltpu.make_async_copy(
                source.at[:, rows_at(lax.rem(index, per) * narrow, narrow)],
                piece_ref.at[slot],
                piece_sems.at[slot],
            )

        def load_piece(index):
            for k, source in enumerate((gate_hbm, up_hbm, act_hbm)):

                @pl.when(index // per == k)
                def _():
                    load_of(source, index, lax.rem(index, 2)).start()

        def grad_copy(index):
            cols = rows_at(index * narrow, narrow)
            return pltpu.make_async_copy(
                weight_ref.at[:, cols], grads_hbm.at[:, cols], grad_sems.at[index]
            )

        def grad_piece(index, carry):
            slot = lax.rem(index, 2)
            load_of(gate_hbm, index, slot).wait()

            @pl.when(index + 1 < pieces)
            def _():
                load_piece(index + 1)

            cols = rows_at(index * narrow, narrow)
            for start in range(0, width, tall):
                span = pl.ds(start, tall)

                @pl.when(index < 2 * per)
                def _():
                    weight_ref[span, cols] = t_dot(all_ref[:, span], piece_ref[slot]).astype(
                        jnp.bfloat16
                    )

                @pl.when(index >= 2 * per)
                def _():
                    weight_ref[span, cols] = t_dot(branch_ref[:, span], piece_ref[slot]).astype(
                        jnp.bfloat16
                    )

            grad_copy(index).start()
            return carry

        load_piece(0)

        def add_rows(block_id, chunk):
            def body(i, carry):
                span = rows_at(chunk * part_size + i * block, block)
                value = sent[block_id, span, :].astype(jnp.float32)
                value = value + held[block_id, span, :].astype(jnp.float32)
                sent[block_id, span, :] = value.astype(jnp.bfloat16)
                return carry

            lax.fori_loop(0, part_size // block, body, 0)

        def relay_side(step, chunk, rightward):
            block_id = step if rightward else n - 1 - step
            has = (me > 0) & (step > me) if rightward else (me < n - 1) & (n - 1 - step < me)

            @pl.when(has)
            def _():
                arrival(block_id, chunk).wait_recv()
                add_rows(block_id, chunk)
                hop(block_id, chunk, rightward).start()

        def relay_chunk(step, chunk, near):
            rightward_first = 2 * me < n

            @pl.when(rightward_first)
            def _():
                relay_side(step, chunk, near)

            @pl.when(jnp.logical_not(rightward_first))
            def _():
                relay_side(step, chunk, not near)

        def relay_of(step, carry):
            for chunk in range(count):
                relay_chunk(step, chunk, True)
            for chunk in range(count):
                relay_chunk(step, chunk, False)
            return carry

        lax.fori_loop(1, n - 1, relay_of, 0)
        lax.fori_loop(0, before, grad_piece, 0)

        def last_relay(chunk, carry):
            @pl.when(chunk < count)
            def _():
                relay_chunk(n - 1, chunk, True)

            start = before + chunk * between
            lax.fori_loop(start, start + between, grad_piece, 0)

            @pl.when(chunk > 0)
            def _():
                relay_chunk(n - 1, chunk - 1, False)

            return carry

        lax.fori_loop(0, count + 1, last_relay, 0)
        lax.fori_loop(before + (count + 1) * between, pieces, grad_piece, 0)
        gain_sum[...] = jnp.zeros_like(gain_sum)
        for chunk in range(count):

            @pl.when(me > 0)
            def _():
                arrival(me, chunk).wait_recv()

            @pl.when(me < n - 1)
            def _():
                arrival(n, chunk).wait_recv()

            def body(i, carry):
                span = rows_at(chunk * part_size + i * block, block)
                total = own_part[span, :]
                zero = jnp.zeros_like(total)
                total = total + jnp.where(me > 0, held[me, span, :].astype(jnp.float32), zero)
                total = total + jnp.where(
                    me < n - 1, held[n, span, :].astype(jnp.float32), zero
                )
                value = second_ref[span, :]
                inverse = lax.rsqrt(jnp.mean(value * value, axis=1, keepdims=True) + norm_eps)
                unit = value * inverse
                scaled = total * gain_ref[1:2, :]
                inner = jnp.mean(scaled * unit, axis=1, keepdims=True)
                base = branch_ref[
                    rows_at(me * rows + chunk * part_size + i * block, block), :
                ].astype(jnp.float32)
                result = base + inverse * (scaled - unit * inner)
                result_ref[span, :] = result
                rounded_ref[span, :] = result.astype(jnp.bfloat16)
                gain_sum[...] += jnp.sum((total * unit).reshape(block // 8, 8, width), axis=0)
                return carry

            lax.fori_loop(0, part_size // block, body, 0)
        gather.finish(False)

        def sends(block_id, carry):
            for chunk in range(count):

                @pl.when((block_id > me) & (me < n - 1))
                def _():
                    hop(block_id, chunk, True).wait_send()

                @pl.when((block_id < me) & (me > 0))
                def _():
                    hop(block_id, chunk, False).wait_send()

            return carry

        lax.fori_loop(0, n, sends, 0)

        def grads_out(index, carry):
            grad_copy(index).wait()
            return carry

        lax.fori_loop(0, pieces, grads_out, 0)

    half = jnp.bfloat16
    return pl.pallas_call(
        kernel,
        out_shape=[
            jax.ShapeDtypeStruct((rows, width), jnp.float32),
            jax.ShapeDtypeStruct((rows, width), half),
            jax.ShapeDtypeStruct((8, width), jnp.float32),
            jax.ShapeDtypeStruct((width, 3 * hidden), half),
        ]
        + [jax.ShapeDtypeStruct((total_rows, hidden), half)] * 3,
        in_specs=[VMEM, ANY, ANY, VMEM, VMEM],
        out_specs=[VMEM] * 3 + [ANY] * 4,
        scratch_shapes=[
            pltpu.VMEM((width, 3 * hidden), half),
            pltpu.VMEM((total_rows, width), half),
            pltpu.VMEM((total_rows, width), half),
            pltpu.VMEM((n + 1, rows, width), half),
            pltpu.VMEM((n, rows, width), half),
            pltpu.VMEM((rows, width), jnp.float32),
        ]
        + [pltpu.VMEM((rows, hidden), half)] * 3
        + [
            pltpu.VMEM((2, total_rows, narrow), half),
            pltpu.SemaphoreType.DMA((2,)),
            pltpu.SemaphoreType.DMA((halves * 3,)),
            pltpu.SemaphoreType.DMA((2,)),
            pltpu.SemaphoreType.DMA((pieces,)),
            pltpu.SemaphoreType.DMA((n * count,)),
            pltpu.SemaphoreType.DMA(((n + 1) * count,)),
        ]
        + gather_sems(n, parcels),
        compiler_params=pltpu.CompilerParams(
            collective_id=collective_id, has_side_effects=True, vmem_limit_bytes=VMEM_LIMIT
        ),
        cost_estimate=pl.CostEstimate(
            flops=16 * total_rows * width * hidden, bytes_accessed=300_000_000, transcendentals=0
        ),
        name="feed_forward",
    )(normed, branch_grad, weights, second, gains)


def attention_backward(queries, keys, values, mixed_grad, cosine, sine, valid_counts):
    total_rows, inner_width = queries.shape
    block = min(256, total_rows)

    def kernel(q_ref, k_ref, v_ref, do_ref, cos_ref, sin_ref, valid_ref, dq_out, dk_out, dv_out, dk_ref, dv_ref):
        dk_ref[...] = jnp.zeros_like(dk_ref)
        dv_ref[...] = jnp.zeros_like(dv_ref)
        for i in range(total_rows // block):
            span = pl.ds(i * block, block)
            upto = (i + 1) * block
            shape = (upto, block)
            key_pos = lax.broadcasted_iota(jnp.int32, shape, 0)
            query_pos = i * block + lax.broadcasted_iota(jnp.int32, shape, 1)
            allowed = jnp.where((key_pos <= query_pos) & (key_pos < valid_ref[0]), 1.0, 0.0)
            query, grad = q_ref[span, :], do_ref[span, :]
            key = k_ref[:upto, :]
            prob = probability(dot_t(key, query)) * allowed
            prob_grad = dot_t(v_ref[:upto, :], grad)
            dv_ref[:upto, :] += jnp.dot(
                prob.astype(jnp.bfloat16), grad, preferred_element_type=jnp.float32
            )
            score_grad = (prob_grad * prob * (1.0 - prob) * (1.0 / math.sqrt(HDIM))).astype(
                jnp.bfloat16
            )
            dk_ref[:upto, :] += jnp.dot(score_grad, query, preferred_element_type=jnp.float32)
            dq = t_dot(score_grad, key)
            dq_out[span, :] = rotated(
                dq, cos_ref[span, :], sin_ref[span, :], True
            ).astype(jnp.bfloat16)
        dk_out[...] = rotated(dk_ref[...], cos_ref[...], sin_ref[...], True).astype(jnp.bfloat16)
        dv_out[...] = dv_ref[...].astype(jnp.bfloat16)

    head = pl.BlockSpec((total_rows, HDIM), lambda h: (0, h))
    table = pl.BlockSpec((total_rows, HDIM), lambda h: (0, 0))
    return pl.pallas_call(
        kernel,
        grid=(inner_width // HDIM,),
        out_shape=[jax.ShapeDtypeStruct((total_rows, inner_width), jnp.bfloat16)] * 3,
        in_specs=[head] * 4 + [table] * 2 + [pl.BlockSpec(memory_space=pltpu.SMEM)],
        out_specs=[head] * 3,
        scratch_shapes=[pltpu.VMEM((total_rows, HDIM), jnp.float32)] * 2,
        compiler_params=pltpu.CompilerParams(vmem_limit_bytes=VMEM_LIMIT),
        cost_estimate=pl.CostEstimate(
            flops=8 * total_rows * total_rows * inner_width,
            bytes_accessed=14 * total_rows * inner_width,
            transcendentals=0,
        ),
        name="attention_backward",
    )(queries, keys, values, mixed_grad, cosine, sine, valid_counts)


def updated(weight, moment, average, gradient, rate):
    moment_new = momentum_decay * moment + (1.0 - momentum_decay) * gradient
    weight_new = weight - rate * (
        (1.0 - momentum_decay) * gradient + momentum_decay * moment_new
    )
    average_new = average_decay * average + (1.0 - average_decay) * weight_new
    return weight_new, moment_new, average_new


def store_update(ins, gradient, outs, rate):
    weight, moment, average = updated(*[ref[...] for ref in ins], gradient, rate)
    outs[0][...] = weight
    outs[1][...] = moment
    outs[2][...] = average
    outs[3][...] = weight.astype(jnp.bfloat16)


def update_all(pairs, parts, flips, sum_ffn, sum_attn, passed, rate):
    jobs = []

    high, two, wide = pairs[0].shape
    tiles = wide // 128
    step = min(64, high)
    stride = tiles * two

    def spread_gradient(g, spread):
        for part in range(two):
            for tile in range(tiles):
                cols = pl.ds(part * wide + tile * 128, 128)
                spread[pl.ds(tile * two + part, step, stride=stride), :] = g[:, cols].astype(
                    jnp.float32
                )
        return spread[...]

    jobs.append(
        (
            [flat_pairs(x) for x in pairs],
            ((step * stride, 128), lambda i: (i, 0)),
            (sum_ffn, (step, two * wide), lambda i: (i, 0)),
            high // step,
            spread_gradient,
        )
    )
    for arrays, total, start in ((flips[0][0], sum_ffn, flips[0][1]), (flips[1][0], sum_attn, flips[1][1])):
        tall, narrow = arrays[0].shape
        rows = min(512, tall)
        jobs.append(
            (
                arrays,
                ((rows, narrow), lambda i: (i, 0)),
                (total, (narrow, rows), lambda i, first=start // rows: (0, first + i)),
                tall // rows,
                lambda g, spread: g[...].astype(jnp.float32).T,
            )
        )
    deep, count, across = parts[0].shape
    jobs.append(
        (
            [x.transpose(1, 0, 2) for x in parts],
            ((None, deep, across), lambda i: (i, 0, 0)),
            (sum_attn, (deep, across), lambda i: (0, i)),
            count,
            lambda g, spread: g[...].astype(jnp.float32),
        )
    )
    starts = [sum(job[3] for job in jobs[:k]) for k in range(len(jobs))]
    steps = sum(job[3] for job in jobs)

    def within(k, index_map):
        return lambda i: index_map(jnp.clip(i - starts[k], 0, jobs[k][3] - 1))

    in_specs, out_specs, args, out_shape = [], [], [], []
    kinds = [jnp.float32] * 3 + [jnp.bfloat16]
    for k, (arrays, (shape, index_map), (total, total_shape, total_map), _, _) in enumerate(jobs):
        spec = pl.BlockSpec(shape, within(k, index_map))
        in_specs += [spec] * 3 + [pl.BlockSpec(total_shape, within(k, total_map))]
        args += [*arrays, total]
        out_specs += [spec] * 4
        out_shape += [jax.ShapeDtypeStruct(arrays[0].shape, kind) for kind in kinds]
    in_specs += [ANY] * len(passed)
    out_specs += [ANY] * len(passed)
    out_shape += [jax.ShapeDtypeStruct(x.shape, x.dtype) for x in passed]

    def body(*refs):
        ins, refs = refs[: len(in_specs)], refs[len(in_specs) :]
        outs, (spread, sems, *kept) = refs[: len(out_specs)], refs[len(out_specs) :]
        i = pl.program_id(0)
        entering = [
            pltpu.make_async_copy(ins[4 * len(jobs) + k], ref, sems.at[0, k])
            for k, ref in enumerate(kept)
        ]
        leaving = [
            pltpu.make_async_copy(ref, outs[4 * len(jobs) + k], sems.at[1, k])
            for k, ref in enumerate(kept)
        ]

        @pl.when(i == 0)
        def _():
            for copy in entering:
                copy.start()

        @pl.when(i == 1)
        def _():
            for arrived, copy in zip(entering, leaving):
                arrived.wait()
                copy.start()

        for k, job in enumerate(jobs):

            @pl.when((i >= starts[k]) & (i < starts[k] + job[3]))
            def _():
                gradient = job[4](ins[4 * k + 3], spread)
                store_update(ins[4 * k : 4 * k + 3], gradient, outs[4 * k : 4 * k + 4], rate)

        @pl.when(i == steps - 1)
        def _():
            for copy in leaving:
                copy.wait()

    size = sum(job[0][0].size for job in jobs)
    outs = pl.pallas_call(
        body,
        grid=(steps,),
        out_shape=out_shape,
        in_specs=in_specs,
        out_specs=out_specs,
        scratch_shapes=[
            pltpu.VMEM((step * stride, 128), jnp.float32),
            pltpu.SemaphoreType.DMA((2, len(passed))),
        ]
        + [pltpu.VMEM(x.shape, x.dtype) for x in passed],
        compiler_params=pltpu.CompilerParams(vmem_limit_bytes=VMEM_LIMIT),
        cost_estimate=pl.CostEstimate(
            flops=10 * size, bytes_accessed=28 * size, transcendentals=0
        ),
        name="update_all",
    )(*args, *passed)
    gu = [
        x.reshape(high, tiles, two, 128).transpose(0, 2, 1, 3).reshape(high, two, wide)
        for x in outs[:4]
    ]
    qkv = [x.transpose(1, 0, 2) for x in outs[12:16]]
    return gu, outs[4:8], outs[8:12], qkv, outs[16:]


def rope_tables(length, half_dim):
    positions = np.arange(length, dtype=np.float32)[:, None]
    inverse_freq = np.power(
        np.float32(rope_base), -np.arange(half_dim, dtype=np.float32) / np.float32(half_dim)
    )
    angles = positions * inverse_freq[None, :]
    cosine, sine = np.cos(angles), np.sin(angles)
    return np.concatenate([cosine, cosine], axis=1), np.concatenate([-sine, sine], axis=1)


def per_device(
    n_dp,
    n_mp,
    tokens,
    cotangent,
    valid_counts,
    w_qkv,
    w_out,
    w_gu,
    w_down,
    gains,
    mom_qkv,
    mom_out,
    mom_gu,
    mom_down,
    mom_gains,
    avg_qkv,
    avg_out,
    avg_gu,
    avg_down,
    avg_gains,
):
    half = jnp.bfloat16
    row_count, width = tokens.shape
    owned, _, local_width = w_qkv.shape
    hidden = w_gu.shape[2]
    valid_len = valid_counts[0]

    attn_part = jnp.concatenate(
        [w_qkv.reshape(owned, 3 * local_width), w_out.T], axis=1
    ).astype(half)
    attn_w = lax.all_gather(attn_part, "dp", axis=0, tiled=True)
    row_ids = lax.axis_index("mp") * row_count + jnp.arange(row_count, dtype=jnp.int32)
    live_rows = (row_ids < valid_len).astype(jnp.float32)[:, None]
    key_mask = (jnp.arange(SEQ, dtype=jnp.int32) < valid_len).astype(jnp.float32)
    ffn_part, tokens_in = lax.optimization_barrier((round_shares(w_gu, w_down), tokens))
    h_first, gain_all, out_grad, own_branch = gather_first(
        n_dp, n_mp, tokens_in, gains, cotangent, live_rows, 1
    )
    ffn_w = lax.all_gather(ffn_part, "dp", axis=0, tiled=True)
    cosine, sine = (jnp.asarray(x, jnp.float32) for x in rope_tables(SEQ, HDIM // 2))

    second, normed_second, queries, keys, values, mixed, branch_grad = scatter_rows(
        n_mp,
        [h_first],
        attn_w,
        3 * local_width,
        [tokens],
        "forward",
        gain_all,
        1,
        2,
        heads=(cosine, sine, key_mask[None, :]),
        extra=own_branch,
    )

    second_grad, own_grad, gain_two, grad_ffn, act, _, _ = feed_forward(
        n_mp, normed_second, branch_grad, ffn_w, second, gain_all, 3
    )
    sum_ffn = lax.psum_scatter(grad_ffn, "dp", scatter_dimension=0, tiled=True)
    block_out, attn_grad, mixed_grad = scatter_rows(
        n_mp,
        [act],
        ffn_w,
        2 * hidden,
        [second],
        "residual",
        gain_all,
        1,
        7,
        extra=own_grad,
        extra_right=(attn_w, 3 * local_width),
    )

    joined_grad = attention_backward(
        queries, keys, values, mixed_grad, cosine, sine, valid_counts
    )
    input_grad, gain_tile, sum_attn = scatter_rows(
        n_mp,
        list(joined_grad),
        attn_w,
        0,
        [tokens, second_grad],
        "last",
        gain_all,
        0,
        4,
        other_gain=gain_two,
        grad_lefts=[h_first, attn_grad],
        grad_right=mixed,
        n_dp=n_dp,
    )

    total_rows = SEQ * n_dp
    matrix_rate = step_rate / math.sqrt(total_rows)
    scale_rate = gain_rate / math.sqrt(total_rows)
    local = gains.shape[1]
    place = lax.rem((lax.axis_index("dp") * n_mp + lax.axis_index("mp")) * local, 128)
    sum_gains = lax.dynamic_slice(gain_tile, (0, place), (2, local))
    gu, down, out, qkv, (block_out, input_grad) = update_all(
        [w_gu, mom_gu, avg_gu],
        [w_qkv, mom_qkv, avg_qkv],
        (
            ([w_down, mom_down, avg_down], 2 * hidden),
            ([w_out, mom_out, avg_out], 3 * local_width),
        ),
        sum_ffn,
        sum_attn,
        [block_out, input_grad],
        matrix_rate,
    )
    new_gu, next_mom_gu, next_avg_gu, copy_gu = gu
    new_down, next_mom_down, next_avg_down, copy_down = down
    new_out, next_mom_out, next_avg_out, copy_out = out
    new_qkv, next_mom_qkv, next_avg_qkv, copy_qkv = qkv
    new_gains, next_mom_gains, next_avg_gains = updated(
        gains, mom_gains, avg_gains, sum_gains, scale_rate
    )
    return (
        block_out,
        input_grad,
        new_qkv,
        new_out,
        new_gu,
        new_down,
        new_gains,
        next_mom_qkv,
        next_mom_out,
        next_mom_gu,
        next_mom_down,
        next_mom_gains,
        next_avg_qkv,
        next_avg_out,
        next_avg_gu,
        next_avg_down,
        next_avg_gains,
        copy_qkv,
        copy_out,
        copy_gu,
        copy_down,
    )


def solution(mesh):
    rows, one = P(("dp", "mp"), None), P("dp")
    tall, wide, spread = P("dp", None, "mp"), P("mp", "dp"), P(None, ("dp", "mp"))
    weights = (tall, wide, tall, wide)
    return jax.shard_map(
        functools.partial(per_device, mesh.shape["dp"], mesh.shape["mp"]),
        mesh=mesh,
        in_specs=(rows, rows, one, *((*weights, spread) * 3)),
        out_specs=(rows, rows, *((*weights, spread) * 3), *weights),
        check_vma=False,
    )
```

```python
import functools
import math

import jax
import jax.numpy as jnp
from jax import lax
from jax.experimental import pallas as pl
from jax.experimental.pallas import tpu as pltpu
import numpy as np
from jax.sharding import PartitionSpec as P

HDIM = 128
SEQ = 1024
MESH = pl.DeviceIdType.MESH
ANY = pl.BlockSpec(memory_space=pl.ANY)
VMEM = pl.BlockSpec(memory_space=pltpu.VMEM)
VMEM_LIMIT = 60 * 1024 * 1024

norm_eps = 1e-05
rope_base = 10000.0
momentum_decay = 0.9
average_decay = 0.9
step_rate = 0.05
gain_rate = 0.5


def rows_at(start, size):
    return pl.ds(pl.multiple_of(start, size), size)


def remote(src, dst, send_sem, recv_sem, peer):
    return pltpu.make_async_remote_copy(
        src_ref=src,
        dst_ref=dst,
        send_sem=send_sem,
        recv_sem=recv_sem,
        device_id={"mp": peer},
        device_id_type=MESH,
    )


def neighbour_barrier(n):
    me = lax.axis_index("mp")
    barrier = pltpu.get_barrier_semaphore()

    @pl.when(me > 0)
    def _():
        pl.semaphore_signal(barrier, inc=1, device_id={"mp": me - 1}, device_id_type=MESH)

    @pl.when(me < n - 1)
    def _():
        pl.semaphore_signal(barrier, inc=1, device_id={"mp": me + 1}, device_id_type=MESH)

    pl.semaphore_wait(barrier, jnp.where(me > 0, 1, 0) + jnp.where(me < n - 1, 1, 0))


class LineGather:
    def __init__(self, n, rows, chunks, own, whole, sems):
        self.n, self.rows, self.chunks = n, rows, chunks
        self.size = rows // chunks
        self.own, self.whole, self.sems = own, whole, sems
        self.me = lax.axis_index("mp")

    def at(self, block, chunk):
        return self.whole.at[rows_at(block * self.rows + chunk * self.size, self.size)]

    def copies(self, step, chunk, first):
        me, n = self.me, self.n
        send_r, recv_r, send_l, recv_l = self.sems
        out = []
        for block, peer, has, send, recv in (
            (me - step, me + 1, (me - step >= 0) & (me < n - 1), send_r, recv_r),
            (me + step, me - 1, (me + step <= n - 1) & (me > 0), send_l, recv_l),
        ):
            src = (
                self.own.at[pl.ds(chunk * self.size, self.size)]
                if first
                else self.at(block, chunk)
            )
            index = step * self.chunks + chunk
            out.append(
                (has, remote(src, self.at(block, chunk), send.at[index], recv.at[index], peer))
            )
        return out

    def arrivals(self, step, chunk):
        me, n = self.me, self.n
        send_r, recv_r, send_l, recv_l = self.sems
        index = step * self.chunks + chunk
        out = []
        for block, has, send, recv in (
            (me - 1 - step, me - 1 - step >= 0, send_r, recv_r),
            (me + 1 + step, me + 1 + step <= n - 1, send_l, recv_l),
        ):
            ref = self.at(block, chunk)
            out.append((has, remote(ref, ref, send.at[index], recv.at[index], me)))
        return out

    def send_own(self, chunk):
        for has, copy in self.copies(0, chunk, True):
            pl.when(has)(copy.start)

    def forward(self, step):
        for chunk in range(self.chunks):
            self.forward_chunk(step, chunk, True)

    def forward_chunk(self, step, chunk, more):
        for (got, arrival), (has, copy) in zip(
            self.arrivals(step - 1, chunk), self.copies(step, chunk, False)
        ):
            pl.when(got)(arrival.wait_recv)
            pl.when(has & more)(copy.start)

    def finish(self, arrivals=True):
        for chunk in range(self.chunks if arrivals else 0):
            for got, arrival in self.arrivals(self.n - 2, chunk):
                pl.when(got)(arrival.wait_recv)
        for chunk in range(self.chunks):
            for has, copy in self.copies(0, chunk, True):
                pl.when(has)(copy.wait_send)

        def waits(step, carry):
            for chunk in range(self.chunks):
                for has, copy in self.copies(step, chunk, False):
                    pl.when(has)(copy.wait_send)
            return carry

        lax.fori_loop(1, self.n - 1, waits, 0)

    def forward_all(self):
        def step_of(step, carry):
            self.forward(step)
            return carry

        lax.fori_loop(1, self.n - 1, step_of, 0)


def gather_sems(n, chunks):
    return [pltpu.SemaphoreType.DMA(((n - 1) * chunks,))] * 4


class Exchange:
    def __init__(self, n_dp, n_mp, sems):
        self.n_dp, self.n_mp = n_dp, n_mp
        self.s_mp, self.r_mp, self.s_dp, self.r_dp = sems
        self.dp, self.mp = lax.axis_index("dp"), lax.axis_index("mp")

    def barrier(self):
        barrier = pltpu.get_barrier_semaphore()
        for axis, here, count in (("mp", self.mp, self.n_mp), ("dp", self.dp, self.n_dp)):
            for k in range(1, count):
                pl.semaphore_signal(
                    barrier,
                    inc=1,
                    device_id={axis: lax.rem(here + k, count)},
                    device_id_type=MESH,
                )
        pl.semaphore_wait(barrier, self.n_mp + self.n_dp - 2)

    def swap(self, axis, source_of, target):
        if axis == "mp":
            here, count, send, recv = self.mp, self.n_mp, self.s_mp, self.r_mp
        else:
            here, count, send, recv = self.dp, self.n_dp, self.s_dp, self.r_dp
        copies = []
        for k in range(1, count):
            peer = lax.rem(here + k, count)
            copies.append(
                pltpu.make_async_remote_copy(
                    src_ref=source_of(peer),
                    dst_ref=target.at[here],
                    send_sem=send.at[k - 1],
                    recv_sem=recv.at[k - 1],
                    device_id={axis: peer},
                    device_id_type=MESH,
                )
            )
        for copy in copies:
            copy.start()
        return copies


def exchange_sems(n_dp, n_mp):
    return [pltpu.SemaphoreType.DMA((n_mp - 1,))] * 2 + [pltpu.SemaphoreType.DMA((n_dp - 1,))] * 2


def tile_of(dp, mp, n_mp, local):
    return (dp * n_mp + mp) * local // 128


def flat_pairs(x):
    high, parts, wide = x.shape
    return x.reshape(high, parts, wide // 128, 128).transpose(0, 2, 1, 3).reshape(-1, 128)


def round_shares(w_gu, w_down):
    high, parts, hidden = w_gu.shape
    tiles = hidden // 128
    step = 128
    turn = min(256, hidden)

    def kernel(gu_ref, down_ref, out_ref):
        for part in range(parts):
            for tile in range(tiles):
                cols = pl.ds(part * hidden + tile * 128, 128)
                out_ref[:, cols] = gu_ref[
                    pl.ds(tile * parts + part, step, stride=tiles * parts), :
                ].astype(jnp.bfloat16)
        for i in range(hidden // turn):
            piece = down_ref[pl.ds(i * turn, turn), :]
            out_ref[:, pl.ds(parts * hidden + i * turn, turn)] = piece.T.astype(jnp.bfloat16)

    return pl.pallas_call(
        kernel,
        grid=(high // step,),
        out_shape=jax.ShapeDtypeStruct((high, (parts + 1) * hidden), jnp.bfloat16),
        in_specs=[
            pl.BlockSpec((step * tiles * parts, 128), lambda i: (i, 0)),
            pl.BlockSpec((hidden, step), lambda i: (0, i)),
        ],
        out_specs=pl.BlockSpec((step, (parts + 1) * hidden), lambda i: (i, 0)),
        compiler_params=pltpu.CompilerParams(vmem_limit_bytes=VMEM_LIMIT),
        cost_estimate=pl.CostEstimate(
            flops=0, bytes_accessed=6 * (w_gu.size + w_down.size), transcendentals=0
        ),
        name="round_shares",
    )(flat_pairs(w_gu), w_down)


def gather_first(n_dp, n_mp, own, gains, cotangent, live, collective_id, chunks=2):
    rows, width = own.shape
    local = gains.shape[1]
    lanes = jnp.arange(128, dtype=jnp.int32) // local
    place = lax.rem(lax.axis_index("mp"), 128 // local)
    if n_mp * local < 128:
        place = lax.rem(lax.axis_index("dp") * n_mp + lax.axis_index("mp"), 128 // local)
    tile = jnp.where(
        (lanes == place)[None, :], jnp.tile(gains, (1, 128 // local)), 0.0
    )
    tile = jnp.concatenate([tile, jnp.zeros((6, 128), jnp.float32)], axis=0)

    block = 64 if rows % 64 == 0 else rows

    def kernel(
        own_ref,
        tile_ref,
        cotangent_ref,
        live_ref,
        normed_hbm,
        gain_ref,
        base_hbm,
        branch_hbm,
        all_ref,
        first,
        second,
        normed_ref,
        base_ref,
        branch_ref,
        out_sems,
        *sems,
    ):
        me = lax.axis_index("mp")
        exchange = Exchange(n_dp, n_mp, sems[:4])
        stream = LineGather(n_mp, rows, chunks, own_ref, all_ref, sems[4:])
        exchange.barrier()
        first[me] = tile_ref[...]
        copies = exchange.swap("mp", lambda peer: tile_ref, first)
        for chunk in range(chunks):
            stream.send_own(chunk)
        all_ref[rows_at(me * rows, rows), :] = own_ref[...]
        for copy in copies:
            copy.wait()
        dp = lax.axis_index("dp")
        second[dp] = first[...]
        copies = exchange.swap("dp", lambda peer: first, second)

        def enter(i, carry):
            span = rows_at(i * block, block)
            value = cotangent_ref[span, :].astype(jnp.float32) * live_ref[span, :]
            base_ref[span, :] = value
            branch_ref[span, :] = value.astype(jnp.bfloat16)
            return carry

        lax.fori_loop(0, rows // block, enter, 0)
        leaving = [
            pltpu.make_async_copy(base_ref, base_hbm, out_sems.at[n_mp]),
            pltpu.make_async_copy(branch_ref, branch_hbm, out_sems.at[n_mp + 1]),
        ]
        for copy in leaving:
            copy.start()
        for copy in copies:
            copy.wait()
        gain_ref[...] = jnp.zeros_like(gain_ref)
        for d in range(n_dp):
            for m in range(n_mp):
                cols = pl.ds(tile_of(d, m, n_mp, local) * 128, 128)
                gain_ref[:, cols] += second[d, m]
        def leave(block_id):
            span = rows_at(block_id * rows, rows)
            return pltpu.make_async_copy(
                normed_ref.at[span], normed_hbm.at[span], out_sems.at[block_id]
            )

        def norm(block_id):
            def body(i, carry):
                span = rows_at(block_id * rows + i * block, block)
                value = all_ref[span, :].astype(jnp.float32)
                inverse = lax.rsqrt(jnp.mean(value * value, axis=1, keepdims=True) + norm_eps)
                normed_ref[span, :] = (value * inverse * gain_ref[0:1, :]).astype(jnp.bfloat16)
                return carry

            lax.fori_loop(0, rows // block, body, 0)
            leave(block_id).start()

        def step_of(step, carry):
            @pl.when(step > 0)
            def _():
                for chunk in range(chunks):
                    stream.forward_chunk(step, chunk, step < n_mp - 1)

            @pl.when(me + step < n_mp)
            def _():
                norm(me + step)

            @pl.when((me - step >= 0) & (step > 0))
            def _():
                norm(me - step)

            return carry

        lax.fori_loop(0, n_mp, step_of, 0)
        stream.finish(False)
        for block_id in range(n_mp):
            leave(block_id).wait()
        for copy in leaving:
            copy.wait()

    half = jnp.bfloat16
    return pl.pallas_call(
        kernel,
        out_shape=[
            jax.ShapeDtypeStruct((n_mp * rows, width), half),
            jax.ShapeDtypeStruct((8, width), jnp.float32),
            jax.ShapeDtypeStruct((rows, width), jnp.float32),
            jax.ShapeDtypeStruct((rows, width), half),
        ],
        in_specs=[VMEM] * 4,
        out_specs=[ANY, VMEM, ANY, ANY],
        scratch_shapes=[
            pltpu.VMEM((n_mp * rows, width), half),
            pltpu.VMEM((n_mp, 8, 128), jnp.float32),
            pltpu.VMEM((n_dp, n_mp, 8, 128), jnp.float32),
            pltpu.VMEM((n_mp * rows, width), half),
            pltpu.VMEM((rows, width), jnp.float32),
            pltpu.VMEM((rows, width), half),
            pltpu.SemaphoreType.DMA((n_mp + 2,)),
        ]
        + exchange_sems(n_dp, n_mp)
        + gather_sems(n_mp, chunks),
        compiler_params=pltpu.CompilerParams(
            collective_id=collective_id, has_side_effects=True, vmem_limit_bytes=VMEM_LIMIT
        ),
        cost_estimate=pl.CostEstimate(
            flops=0, bytes_accessed=200 * own.size * own.dtype.itemsize, transcendentals=0
        ),
        name="gather_first",
    )(own, tile, cotangent, live)


def dot_t(left, right):
    return lax.dot_general(
        left, right, (((1,), (1,)), ((), ())), preferred_element_type=jnp.float32
    )


def t_dot(left, right):
    return lax.dot_general(
        left, right, (((0,), (0,)), ((), ())), preferred_element_type=jnp.float32
    )


def dot(left, right):
    return jnp.dot(left, right, preferred_element_type=jnp.float32)


def probability(raw):
    return 1.0 / (1.0 + jnp.exp(math.log(SEQ) - raw * (1.0 / math.sqrt(HDIM))))


def rotated(values, cosine, sine, backward=False):
    turned = pltpu.roll(values, HDIM // 2, 1) * sine
    return values * cosine - turned if backward else values * cosine + turned


def scatter_rows(
    n,
    lhs,
    rhs,
    rhs_start,
    own_rows,
    epilogue,
    gains,
    gain_row,
    collective_id,
    heads=None,
    extra=None,
    extra_right=None,
    other_gain=None,
    grad_lefts=None,
    grad_right=None,
    n_dp=1,
    chunks=2,
):
    total_rows = lhs[0].shape[0]
    rows = total_rows // n
    width = gains.shape[1]
    size = rows // chunks
    tile = 512
    has_norm, has_gain = epilogue in ("forward", "backward"), epilogue in ("backward", "last")
    count = len(lhs)
    block = 32
    if heads is not None:
        inner_width = rhs_start // 3
        head_count = inner_width // HDIM
        pieces = [inner_width]
    else:
        pieces = [a.shape[1] for a in lhs]
    depth = sum(pieces)
    if extra_right is not None:
        extra_width = extra_right[0].shape[1] - extra_right[1]

    def kernel(*refs):
        refs = list(refs)

        def take(k):
            return [refs.pop(0) for _ in range(k)]

        left_refs = take(count)
        (right_hbm,) = take(1)
        (gain_ref,) = take(1)
        own_hbm = take(len(own_rows))
        if heads is not None:
            cosine_ref, sine_ref, mask_ref = take(3)
        if other_gain is not None:
            (other_ref,) = take(1)
            grad_hbm = take(3)
        extra_ref = take(1)[0] if extra is not None else None
        extra_right_hbm = take(1)[0] if extra_right is not None else None
        outs = take(1 + has_gain)
        owned_ref = take(1)[0] if other_gain is not None else None
        normed = take(1)[0] if has_norm else None
        if heads is not None:
            query_ref, key_ref, value_ref, mixed_ref = take(4)
        extra_whole = take(1)[0] if extra is not None else None
        if extra_right is not None:
            (extra_out,) = take(1)
        right, held, sent, part = take(4)
        joined_ref = take(1)[0] if heads is not None else None
        right_sem, send_sems, recv_sems = take(3)
        own, own_sems = take(len(own_rows)), take(1)[0]
        own_loads = [
            pltpu.make_async_copy(hbm, ref, own_sems.at[k])
            for k, (hbm, ref) in enumerate(zip(own_hbm, own))
        ]
        me = lax.axis_index("mp")
        fetch = pltpu.make_async_copy(
            right_hbm.at[:, pl.ds(rhs_start, depth)], right, right_sem
        )
        fetch.start()
        if heads is not None:
            (joined_sem,) = take(1)
            fetch_joined = pltpu.make_async_copy(
                right_hbm.at[:, pl.ds(0, rhs_start)], joined_ref, joined_sem
            )
            fetch_joined.start()
        if extra is not None:
            (extra_sem,) = take(1)
            extra_sems = take(4)
            if extra_right is None:
                extra_gather = LineGather(n, rows, 1, extra_ref, extra_whole, extra_sems)
                extra_local = pltpu.make_async_copy(extra_ref, extra_gather.at(me, 0), extra_sem)
                extra_local.start()
            else:
                extra_all, extra_right_ref, extra_right_sem = take(3)
                extra_gather = LineGather(n, rows, 1, extra_ref, extra_all, extra_sems)
                extra_fetch = pltpu.make_async_copy(
                    extra_right_hbm.at[:, pl.ds(extra_right[1], extra_width)],
                    extra_right_ref,
                    extra_right_sem,
                )
                extra_fetch.start()

                def extra_product(block_id):
                    @pl.when((block_id >= 0) & (block_id < n))
                    def _():
                        span = rows_at(block_id * rows, rows)
                        extra_out[span, :] = dot(
                            extra_all[span, :], extra_right_ref[...]
                        ).astype(jnp.bfloat16)
        if other_gain is not None:
            gain_sum, table, first, middle, second = take(5)
            exchange = Exchange(n_dp, n, take(4))
            *grad_left_refs, grad_right_ref, grad_load_sems = take(4)
            grad_loads = [
                pltpu.make_async_copy(hbm, ref, grad_load_sems.at[k])
                for k, (hbm, ref) in enumerate(zip(grad_hbm, [*grad_left_refs, grad_right_ref]))
            ]
            for load in grad_loads:
                load.start()
            grads, paired, landed = take(3)
            pair_send, pair_recv, land_send, land_recv = take(4)
            dp = lax.axis_index("dp")
            core, chip = lax.rem(dp, 2), dp // 2
            chips, share = n_dp // 2, landed.shape[1]
            exchange.barrier()
            pair_copies = [
                pltpu.make_async_remote_copy(
                    src_ref=grads.at[rows_at((2 * q + 1 - core) * share, share)],
                    dst_ref=paired.at[q],
                    send_sem=pair_send.at[q],
                    recv_sem=pair_recv.at[q],
                    device_id={"dp": dp + 1 - 2 * core},
                    device_id_type=MESH,
                )
                for q in range(chips)
            ]
            land_copies = [
                pltpu.make_async_remote_copy(
                    src_ref=paired.at[lax.rem(chip + k, chips)],
                    dst_ref=landed.at[k - 1],
                    send_sem=land_send.at[k - 1],
                    recv_sem=land_recv.at[k - 1],
                    device_id={"dp": 2 * lax.rem(chip + k, chips) + core},
                    device_id_type=MESH,
                )
                for k in range(1, chips)
            ]

            def make_grads():
                for load in grad_loads:
                    load.wait()
                start, narrow = 0, 256
                for k, right_ref in enumerate([*left_refs, grad_right_ref]):
                    left_ref = grad_left_refs[0 if k < count else 1]

                    def column(i, carry, start=start, left_ref=left_ref, right_ref=right_ref):
                        grads[:, rows_at(start + i * narrow, narrow)] = t_dot(
                            left_ref[...], right_ref[:, rows_at(i * narrow, narrow)]
                        ).astype(jnp.bfloat16)
                        return carry

                    lax.fori_loop(0, right_ref.shape[1] // narrow, column, 0)
                    start += right_ref.shape[1]
                for copy in pair_copies:
                    copy.start()
                for copy in pair_copies:
                    copy.wait()

                def add(i, carry):
                    span = rows_at(i * block, block)
                    for q in range(chips):
                        own_span = rows_at((2 * q + core) * share + i * block, block)
                        paired[q, span, :] = (
                            paired[q, span, :].astype(jnp.float32)
                            + grads[own_span, :].astype(jnp.float32)
                        ).astype(jnp.bfloat16)
                    return carry

                lax.fori_loop(0, share // block, add, 0)
                for copy in land_copies:
                    copy.start()

            def land():
                for copy in land_copies:
                    copy.wait()

                def add(i, carry):
                    span = rows_at(i * block, block)
                    total = paired[chip, span, :].astype(jnp.float32)
                    for k in range(chips - 1):
                        total = total + landed[k, span, :].astype(jnp.float32)
                    owned_ref[span, :] = total
                    return carry

                lax.fori_loop(0, share // block, add, 0)

        else:
            gain_sum = outs[1] if has_gain else None
            neighbour_barrier(n)
        if extra is not None:
            extra_gather.send_own(0)
        if extra_right is not None:
            extra_all[rows_at(me * rows, rows), :] = extra_ref[...]
            extra_fetch.wait()
        if heads is not None:
            turn = 256
            fetch_joined.wait()

            def enter(i, carry):
                span = rows_at(i * turn, turn)
                cosine, sine = cosine_ref[span, :], sine_ref[span, :]
                row_vals = left_refs[0][span, :]
                for k, target in ((0, query_ref), (1, key_ref), (2, value_ref)):
                    piece = dot(row_vals, joined_ref[:, pl.ds(k * inner_width, inner_width)])
                    for h in range(head_count):
                        value = piece[:, h * HDIM : (h + 1) * HDIM]
                        if k < 2:
                            value = rotated(value, cosine, sine)
                        target[span, pl.ds(h * HDIM, HDIM)] = value.astype(jnp.bfloat16)
                return carry

            lax.fori_loop(0, total_rows // turn, enter, 0)
        for load in own_loads:
            load.start()
        fetch.wait()

        def attend(block_id):
            span = rows_at(block_id * rows, rows)
            row_pos = block_id * rows + lax.broadcasted_iota(jnp.int32, (rows, rows), 0)

            def against(kb, totals):
                other = rows_at(kb * rows, rows)
                col_pos = kb * rows + lax.broadcasted_iota(jnp.int32, (rows, rows), 1)
                allowed = jnp.where(col_pos <= row_pos, mask_ref[:, other], 0.0)
                out = []
                for h in range(head_count):
                    cols = pl.ds(h * HDIM, HDIM)
                    raw = dot_t(query_ref[span, cols], key_ref[other, cols])
                    prob = probability(raw) * allowed
                    out.append(
                        totals[h]
                        + jnp.dot(
                            prob.astype(jnp.bfloat16),
                            value_ref[other, cols],
                            preferred_element_type=jnp.float32,
                        )
                    )
                return tuple(out)

            start = tuple(jnp.zeros((rows, HDIM), jnp.float32) for _ in range(head_count))
            totals = lax.fori_loop(0, block_id + 1, against, start)
            for h in range(head_count):
                mixed_ref[span, pl.ds(h * HDIM, HDIM)] = totals[h].astype(jnp.bfloat16)

        def product(block_id):
            if heads is not None:
                attend(block_id)
            sources = [mixed_ref] if heads is not None else left_refs

            def column(ct, carry):
                cols = rows_at(ct * tile, tile)
                total, start = None, 0
                for source, piece in zip(sources, pieces):
                    term = dot_t(
                        source[rows_at(block_id * rows, rows), :],
                        right[cols, pl.ds(start, piece)],
                    )
                    start += piece
                    total = term if total is None else total + term
                part[:, cols] = total
                return carry

            lax.fori_loop(0, width // tile, column, 0)

        def hop(block_id, chunk, rightward):
            peer = me + 1 if rightward else me - 1
            slot = block_id if rightward else jnp.where(block_id == peer, n, block_id)
            return remote(
                sent.at[block_id, pl.ds(chunk * size, size)],
                held.at[slot, pl.ds(chunk * size, size)],
                send_sems.at[block_id * chunks + chunk],
                recv_sems.at[slot * chunks + chunk],
                peer,
            )

        def arrival(slot, chunk):
            ref = held.at[slot, pl.ds(chunk * size, size)]
            return remote(
                ref, ref, send_sems.at[chunk], recv_sems.at[slot * chunks + chunk], me
            )

        def add_rows(block_id, chunk, slots):
            def body(i, carry):
                span = rows_at(chunk * size + i * block, block)
                value = part[span, :]
                for slot in slots:
                    value = value + held[slot, span, :].astype(jnp.float32)
                sent[block_id, span, :] = value.astype(jnp.bfloat16)
                return carry

            lax.fori_loop(0, size // block, body, 0)

        def relay(block_id, rightward, inner):
            product(block_id)
            for chunk in range(chunks):

                @pl.when(inner)
                def _():
                    arrival(block_id, chunk).wait_recv()
                    add_rows(block_id, chunk, [block_id])

                @pl.when(jnp.logical_not(inner))
                def _():
                    add_rows(block_id, chunk, [])

                hop(block_id, chunk, rightward).start()

        def step_of(step, carry):
            @pl.when((step >= me + 1) & (me < n - 1))
            def _():
                relay(me + n - step, True, me > 0)

            @pl.when((step >= n - me) & (me > 0))
            def _():
                relay(me - n + step, False, me < n - 1)

            if extra is not None:

                @pl.when(step < n - 1)
                def _():
                    extra_gather.forward(step)
                    if extra_right is not None:
                        extra_product(me - step)
                        extra_product(me + step)

            if other_gain is not None:
                pl.when(step == 1)(make_grads)

            return carry

        lax.fori_loop(1, n, step_of, 0)
        product(me)
        if extra_right is not None:
            extra_product(me)
        for load in own_loads:
            load.wait()
        if has_gain:
            gain_sum[...] = jnp.zeros_like(gain_sum)
        for chunk in range(chunks):

            @pl.when(me > 0)
            def _():
                arrival(me, chunk).wait_recv()

            @pl.when(me < n - 1)
            def _():
                arrival(n, chunk).wait_recv()

            def body(i, carry):
                span = rows_at(chunk * size + i * block, block)
                total = part[span, :]
                zero = jnp.zeros_like(total)
                total = total + jnp.where(me > 0, held[me, span, :].astype(jnp.float32), zero)
                total = total + jnp.where(
                    me < n - 1, held[n, span, :].astype(jnp.float32), zero
                )
                gain = gain_ref[gain_row : gain_row + 1, :]
                if epilogue == "residual":
                    outs[0][span, :] = (own[0][span, :] + total).astype(jnp.bfloat16)
                elif epilogue == "forward":
                    value = own[0][span, :].astype(jnp.float32) + total
                    outs[0][span, :] = value
                    inverse = lax.rsqrt(
                        jnp.mean(value * value, axis=1, keepdims=True) + norm_eps
                    )
                    normed[span, :] = (value * inverse * gain).astype(jnp.bfloat16)
                else:
                    value = own[0][span, :].astype(jnp.float32)
                    inverse = lax.rsqrt(
                        jnp.mean(value * value, axis=1, keepdims=True) + norm_eps
                    )
                    unit = value * inverse
                    scaled = total * gain
                    inner = jnp.mean(scaled * unit, axis=1, keepdims=True)
                    result = own[1][span, :] + inverse * (scaled - unit * inner)
                    outs[0][span, :] = result
                    gain_sum[...] += jnp.sum(
                        (total * unit).reshape(block // 8, 8, width), axis=0
                    )
                    if has_norm:
                        normed[span, :] = result.astype(jnp.bfloat16)
                return carry

            lax.fori_loop(0, size // block, body, 0)
        if extra is not None:
            extra_gather.finish()
        if extra_right is not None:
            extra_local = pltpu.make_async_copy(extra_all, extra_whole, extra_sem)
            extra_local.start()
            extra_product(me - (n - 1))
            extra_product(me + (n - 1))
        if extra is not None:
            extra_local.wait()
        if other_gain is not None:
            local = width // (n * n_dp)
            for row, source in ((0, gain_sum), (1, other_ref)):
                total = jnp.sum(source[...], axis=0, keepdims=True)
                for d in range(n_dp):
                    for m in range(n):
                        start = tile_of(d, m, n, local) * 128
                        table[m, d, row : row + 1, :] = total[:, start : start + 128]
            copies = exchange.swap("mp", lambda peer: table.at[peer], first)
            first[me] = table[me]
            for copy in copies:
                copy.wait()
            total = first[0]
            for m in range(1, n):
                total = total + first[m]
            middle[...] = total
            copies = exchange.swap("dp", lambda peer: middle.at[peer], second)
            second[dp] = middle[dp]
            land()
            for copy in copies:
                copy.wait()
            total = second[0]
            for d in range(1, n_dp):
                total = total + second[d]
            outs[1][...] = total

        def sends(step, carry):
            for chunk in range(chunks):

                @pl.when((step >= me + 1) & (me < n - 1))
                def _():
                    hop(me + n - step, chunk, True).wait_send()

                @pl.when((step >= n - me) & (me > 0))
                def _():
                    hop(me - n + step, chunk, False).wait_send()

            return carry

        lax.fori_loop(1, n, sends, 0)

    out_type = jnp.bfloat16 if epilogue == "residual" else jnp.float32
    out_shape = [jax.ShapeDtypeStruct((rows, width), out_type)]
    out_specs = [VMEM]
    if has_gain:
        out_shape.append(
            jax.ShapeDtypeStruct((8, width) if other_gain is None else (2, 128), jnp.float32)
        )
        out_specs.append(VMEM)
    if other_gain is not None:
        share = width // n_dp
        grad_width = sum(pieces) + grad_right.shape[1]
        out_shape.append(jax.ShapeDtypeStruct((share, grad_width), jnp.float32))
        out_specs.append(VMEM)
    scratch = [
        pltpu.VMEM((width, depth), jnp.bfloat16),
        pltpu.VMEM((n + 1, rows, width), jnp.bfloat16),
        pltpu.VMEM((n, rows, width), jnp.bfloat16),
        pltpu.VMEM((rows, width), jnp.float32),
    ]
    if heads is not None:
        scratch.append(pltpu.VMEM((width, rhs_start), jnp.bfloat16))
    if has_norm:
        out_shape.append(jax.ShapeDtypeStruct((rows, width), jnp.bfloat16))
        out_specs.append(VMEM)
    scratch += [
        pltpu.SemaphoreType.DMA,
        pltpu.SemaphoreType.DMA((n * chunks,)),
        pltpu.SemaphoreType.DMA(((n + 1) * chunks,)),
    ]
    scratch += [pltpu.VMEM(x.shape, x.dtype) for x in own_rows]
    scratch.append(pltpu.SemaphoreType.DMA((len(own_rows),)))
    head_args = []
    if heads is not None:
        scratch.append(pltpu.SemaphoreType.DMA)
        head_args = list(heads)
        out_shape += [jax.ShapeDtypeStruct((total_rows, inner_width), jnp.bfloat16)] * 4
        out_specs += [VMEM] * 4
    extra_args = []
    if extra is not None:
        out_shape.append(jax.ShapeDtypeStruct((total_rows, width), jnp.bfloat16))
        out_specs.append(ANY)
        scratch += [pltpu.SemaphoreType.DMA] + gather_sems(n, 1)
        extra_args = [extra]
    if extra_right is not None:
        out_shape.append(jax.ShapeDtypeStruct((total_rows, extra_width), jnp.bfloat16))
        out_specs.append(VMEM)
        scratch += [
            pltpu.VMEM((total_rows, width), jnp.bfloat16),
            pltpu.VMEM((width, extra_width), jnp.bfloat16),
            pltpu.SemaphoreType.DMA,
        ]
        extra_args.append(extra_right[0])
    late_args = []
    if other_gain is not None:
        head_args.append(other_gain)
        late_args = [*grad_lefts, grad_right]
        scratch += [
            pltpu.VMEM((8, width), jnp.float32),
            pltpu.VMEM((n, n_dp, 2, 128), jnp.float32),
            pltpu.VMEM((n, n_dp, 2, 128), jnp.float32),
            pltpu.VMEM((n_dp, 2, 128), jnp.float32),
            pltpu.VMEM((n_dp, 2, 128), jnp.float32),
        ] + exchange_sems(n_dp, n)
        scratch += [pltpu.VMEM(x.shape, x.dtype) for x in late_args]
        scratch.append(pltpu.SemaphoreType.DMA((len(late_args),)))
        chips = n_dp // 2
        scratch.append(pltpu.VMEM((width, grad_width), jnp.bfloat16))
        scratch.append(pltpu.VMEM((chips, share, grad_width), jnp.bfloat16))
        scratch.append(pltpu.VMEM((chips - 1, share, grad_width), jnp.bfloat16))
        scratch += [pltpu.SemaphoreType.DMA((chips,))] * 2
        scratch += [pltpu.SemaphoreType.DMA((chips - 1,))] * 2
    flops = 2 * total_rows * depth * width
    return pl.pallas_call(
        kernel,
        out_shape=out_shape,
        in_specs=[VMEM] * count
        + [ANY]
        + [VMEM]
        + [ANY] * len(own_rows)
        + [VMEM] * len(head_args)
        + [ANY] * len(late_args)
        + [VMEM if extra_right is not None else ANY] * min(1, len(extra_args))
        + [ANY] * max(0, len(extra_args) - 1),
        out_specs=out_specs,
        scratch_shapes=scratch,
        compiler_params=pltpu.CompilerParams(
            collective_id=collective_id, has_side_effects=True, vmem_limit_bytes=VMEM_LIMIT
        ),
        cost_estimate=pl.CostEstimate(
            flops=flops, bytes_accessed=300_000_000, transcendentals=0
        ),
        name="scatter_" + epilogue,
    )(*lhs, rhs, gains, *own_rows, *head_args, *late_args, *extra_args)


def feed_forward(n, normed, branch_grad, weights, second, gains, collective_id, halves=1, hops=4):
    rows, width = normed.shape
    total_rows = n * rows
    hidden = weights.shape[1] // 3
    count, parcels = hops, halves
    part_size = rows // hops
    tile = min(1024, hidden)
    block = min(32, part_size)
    narrow = min(256, hidden)
    per = hidden // narrow
    pieces = 3 * per
    before = pieces // 6
    between = (pieces - 2 * before) // (count + 1)
    tall = min(1024, width)

    def kernel(
        normed_ref,
        branch_hbm,
        weights_hbm,
        second_ref,
        gain_ref,
        result_ref,
        rounded_ref,
        gain_sum,
        grads_hbm,
        act_hbm,
        gate_hbm,
        up_hbm,
        weight_ref,
        branch_ref,
        all_ref,
        held,
        sent,
        own_part,
        act_ref,
        gate_ref,
        up_ref,
        piece_ref,
        load_sems,
        stage_sems,
        piece_sems,
        grad_sems,
        send_sems,
        recv_sems,
        *gather_refs,
    ):
        me = lax.axis_index("mp")
        middle = (me > 0) & (me < n - 1)
        loads = [
            pltpu.make_async_copy(weights_hbm, weight_ref, load_sems.at[0]),
            pltpu.make_async_copy(branch_hbm, branch_ref, load_sems.at[1]),
        ]
        for load in loads:
            load.start()
        gather = LineGather(n, rows, parcels, normed_ref, all_ref, gather_refs)
        neighbour_barrier(n)
        for parcel in range(parcels):
            gather.send_own(parcel)
        all_ref[rows_at(me * rows, rows), :] = normed_ref[...]
        for load in loads:
            load.wait()

        def hop(block_id, chunk, rightward):
            peer = me + 1 if rightward else me - 1
            slot = block_id if rightward else jnp.where(block_id == peer, n, block_id)
            return remote(
                sent.at[block_id, pl.ds(chunk * part_size, part_size)],
                held.at[slot, pl.ds(chunk * part_size, part_size)],
                send_sems.at[block_id * count + chunk],
                recv_sems.at[slot * count + chunk],
                peer,
            )

        def arrival(slot, chunk):
            ref = held.at[slot, pl.ds(chunk * part_size, part_size)]
            return remote(
                ref, ref, send_sems.at[chunk], recv_sems.at[slot * count + chunk], me
            )

        def stages(block_id, chunk, size):
            span = rows_at(block_id * rows + chunk * size, size)
            return [
                pltpu.make_async_copy(
                    ref.at[pl.ds(chunk * size, size)], hbm.at[span], stage_sems.at[chunk * 3 + k]
                )
                for k, (ref, hbm) in enumerate(
                    ((act_ref, act_hbm), (gate_ref, gate_hbm), (up_ref, up_hbm))
                )
            ]

        def compute(block_id, chunk, size, first):
            here = pl.ds(chunk * size, size)
            span = rows_at(block_id * rows + chunk * size, size)

            @pl.when(jnp.logical_not(first))
            def _():
                for stage in stages(block_id, chunk, size):
                    stage.wait()

            def units(ct, carry):
                cols = rows_at(ct * tile, tile)
                row_vals, branch = all_ref[span, :], branch_ref[span, :]
                gate = dot(row_vals, weight_ref[:, cols])
                up = dot(row_vals, weight_ref[:, rows_at(hidden + ct * tile, tile)])
                act_grad = dot(branch, weight_ref[:, rows_at(2 * hidden + ct * tile, tile)])
                sigma = 1.0 / (1.0 + jnp.exp(-gate))
                silu = gate * sigma
                act_ref[here, cols] = (silu * up).astype(jnp.bfloat16)
                gate_ref[here, cols] = (
                    act_grad * up * sigma * (1.0 + gate * (1.0 - sigma))
                ).astype(jnp.bfloat16)
                up_ref[here, cols] = (act_grad * silu).astype(jnp.bfloat16)
                return carry

            lax.fori_loop(0, hidden // tile, units, 0)
            for stage in stages(block_id, chunk, size):
                stage.start()

            def columns(ct, carry):
                cols = rows_at(ct * tile, tile)
                total = dot_t(gate_ref[here, :], weight_ref[cols, pl.ds(0, hidden)])
                total += dot_t(up_ref[here, :], weight_ref[cols, pl.ds(hidden, hidden)])

                @pl.when(block_id == me)
                def _():
                    own_part[here, cols] = total

                @pl.when(block_id != me)
                def _():
                    sent[block_id, here, cols] = total.astype(jnp.bfloat16)

                return carry

            lax.fori_loop(0, width // tile, columns, 0)

            @pl.when((me == 0) & (block_id > me))
            def _():
                for k in range(size // part_size):
                    hop(block_id, chunk * (size // part_size) + k, True).start()

            @pl.when((me == n - 1) & (block_id < me))
            def _():
                for k in range(size // part_size):
                    hop(block_id, chunk * (size // part_size) + k, False).start()

        def forward(step, parcel):
            gather.forward_chunk(step, parcel, step < n - 1)

        def forward_whole(step):
            for parcel in range(parcels):
                forward(step, parcel)

        def step_of(step, carry):
            def side_of(side, carry):
                block_id = me + (1 - 2 * side) * step
                valid = (block_id >= 0) & (block_id < n) & ((step > 0) | (side == 0))

                @pl.when(middle & (step > 0) & (step < n - 1) & (side == 1))
                def _():
                    forward_whole(step + 1)

                @pl.when(middle & valid)
                def _():
                    compute(block_id, 0, rows, step == 0)

                @pl.when(middle & (step == 0) & (side == 0))
                def _():
                    forward_whole(1)

                for half in range(halves):

                    @pl.when(jnp.logical_not(middle) & valid)
                    def _():
                        pl.when(step > 0)(lambda: forward(step, half))
                        compute(block_id, half, rows // halves, step == 0)

                return carry

            return lax.fori_loop(0, 2, side_of, carry)

        lax.fori_loop(0, n, step_of, 0)
        @pl.when(middle)
        def _():
            for stage in stages(me, 0, rows):
                stage.wait()

        @pl.when(jnp.logical_not(middle))
        def _():
            for half in range(halves):
                for stage in stages(me, half, rows // halves):
                    stage.wait()


        def load_of(source, index, slot):
            return pltpu.make_async_copy(
                source.at[:, rows_at(lax.rem(index, per) * narrow, narrow)],
                piece_ref.at[slot],
                piece_sems.at[slot],
            )

        def load_piece(index):
            for k, source in enumerate((gate_hbm, up_hbm, act_hbm)):

                @pl.when(index // per == k)
                def _():
                    load_of(source, index, lax.rem(index, 2)).start()

        def grad_copy(index):
            cols = rows_at(index * narrow, narrow)
            return pltpu.make_async_copy(
                weight_ref.at[:, cols], grads_hbm.at[:, cols], grad_sems.at[index]
            )

        def grad_piece(index, carry):
            slot = lax.rem(index, 2)
            load_of(gate_hbm, index, slot).wait()

            @pl.when(index + 1 < pieces)
            def _():
                load_piece(index + 1)

            cols = rows_at(index * narrow, narrow)
            for start in range(0, width, tall):
                span = pl.ds(start, tall)

                @pl.when(index < 2 * per)
                def _():
                    weight_ref[span, cols] = t_dot(all_ref[:, span], piece_ref[slot]).astype(
                        jnp.bfloat16
                    )

                @pl.when(index >= 2 * per)
                def _():
                    weight_ref[span, cols] = t_dot(branch_ref[:, span], piece_ref[slot]).astype(
                        jnp.bfloat16
                    )

            grad_copy(index).start()
            return carry

        load_piece(0)

        def add_rows(block_id, chunk):
            def body(i, carry):
                span = rows_at(chunk * part_size + i * block, block)
                value = sent[block_id, span, :].astype(jnp.float32)
                value = value + held[block_id, span, :].astype(jnp.float32)
                sent[block_id, span, :] = value.astype(jnp.bfloat16)
                return carry

            lax.fori_loop(0, part_size // block, body, 0)

        def relay_side(step, chunk, rightward):
            block_id = step if rightward else n - 1 - step
            has = (me > 0) & (step > me) if rightward else (me < n - 1) & (n - 1 - step < me)

            @pl.when(has)
            def _():
                arrival(block_id, chunk).wait_recv()
                add_rows(block_id, chunk)
                hop(block_id, chunk, rightward).start()

        def relay_chunk(step, chunk, near):
            rightward_first = 2 * me < n

            @pl.when(rightward_first)
            def _():
                relay_side(step, chunk, near)

            @pl.when(jnp.logical_not(rightward_first))
            def _():
                relay_side(step, chunk, not near)

        def relay_of(step, carry):
            for chunk in range(count):
                relay_chunk(step, chunk, True)
            for chunk in range(count):
                relay_chunk(step, chunk, False)
            return carry

        lax.fori_loop(1, n - 1, relay_of, 0)
        lax.fori_loop(0, before, grad_piece, 0)

        def last_relay(chunk, carry):
            @pl.when(chunk < count)
            def _():
                relay_chunk(n - 1, chunk, True)

            start = before + chunk * between
            lax.fori_loop(start, start + between, grad_piece, 0)

            @pl.when(chunk > 0)
            def _():
                relay_chunk(n - 1, chunk - 1, False)

            return carry

        lax.fori_loop(0, count + 1, last_relay, 0)
        lax.fori_loop(before + (count + 1) * between, pieces, grad_piece, 0)
        gain_sum[...] = jnp.zeros_like(gain_sum)
        for chunk in range(count):

            @pl.when(me > 0)
            def _():
                arrival(me, chunk).wait_recv()

            @pl.when(me < n - 1)
            def _():
                arrival(n, chunk).wait_recv()

            def body(i, carry):
                span = rows_at(chunk * part_size + i * block, block)
                total = own_part[span, :]
                zero = jnp.zeros_like(total)
                total = total + jnp.where(me > 0, held[me, span, :].astype(jnp.float32), zero)
                total = total + jnp.where(
                    me < n - 1, held[n, span, :].astype(jnp.float32), zero
                )
                value = second_ref[span, :]
                inverse = lax.rsqrt(jnp.mean(value * value, axis=1, keepdims=True) + norm_eps)
                unit = value * inverse
                scaled = total * gain_ref[1:2, :]
                inner = jnp.mean(scaled * unit, axis=1, keepdims=True)
                base = branch_ref[
                    rows_at(me * rows + chunk * part_size + i * block, block), :
                ].astype(jnp.float32)
                result = base + inverse * (scaled - unit * inner)
                result_ref[span, :] = result
                rounded_ref[span, :] = result.astype(jnp.bfloat16)
                gain_sum[...] += jnp.sum((total * unit).reshape(block // 8, 8, width), axis=0)
                return carry

            lax.fori_loop(0, part_size // block, body, 0)
        gather.finish(False)

        def sends(block_id, carry):
            for chunk in range(count):

                @pl.when((block_id > me) & (me < n - 1))
                def _():
                    hop(block_id, chunk, True).wait_send()

                @pl.when((block_id < me) & (me > 0))
                def _():
                    hop(block_id, chunk, False).wait_send()

            return carry

        lax.fori_loop(0, n, sends, 0)

        def grads_out(index, carry):
            grad_copy(index).wait()
            return carry

        lax.fori_loop(0, pieces, grads_out, 0)

    half = jnp.bfloat16
    return pl.pallas_call(
        kernel,
        out_shape=[
            jax.ShapeDtypeStruct((rows, width), jnp.float32),
            jax.ShapeDtypeStruct((rows, width), half),
            jax.ShapeDtypeStruct((8, width), jnp.float32),
            jax.ShapeDtypeStruct((width, 3 * hidden), half),
        ]
        + [jax.ShapeDtypeStruct((total_rows, hidden), half)] * 3,
        in_specs=[VMEM, ANY, ANY, VMEM, VMEM],
        out_specs=[VMEM] * 3 + [ANY] * 4,
        scratch_shapes=[
            pltpu.VMEM((width, 3 * hidden), half),
            pltpu.VMEM((total_rows, width), half),
            pltpu.VMEM((total_rows, width), half),
            pltpu.VMEM((n + 1, rows, width), half),
            pltpu.VMEM((n, rows, width), half),
            pltpu.VMEM((rows, width), jnp.float32),
        ]
        + [pltpu.VMEM((rows, hidden), half)] * 3
        + [
            pltpu.VMEM((2, total_rows, narrow), half),
            pltpu.SemaphoreType.DMA((2,)),
            pltpu.SemaphoreType.DMA((halves * 3,)),
            pltpu.SemaphoreType.DMA((2,)),
            pltpu.SemaphoreType.DMA((pieces,)),
            pltpu.SemaphoreType.DMA((n * count,)),
            pltpu.SemaphoreType.DMA(((n + 1) * count,)),
        ]
        + gather_sems(n, parcels),
        compiler_params=pltpu.CompilerParams(
            collective_id=collective_id, has_side_effects=True, vmem_limit_bytes=VMEM_LIMIT
        ),
        cost_estimate=pl.CostEstimate(
            flops=16 * total_rows * width * hidden, bytes_accessed=300_000_000, transcendentals=0
        ),
        name="feed_forward",
    )(normed, branch_grad, weights, second, gains)


def attention_backward(queries, keys, values, mixed_grad, cosine, sine, valid_counts):
    total_rows, inner_width = queries.shape
    block = min(256, total_rows)

    def kernel(q_ref, k_ref, v_ref, do_ref, cos_ref, sin_ref, valid_ref, dq_out, dk_out, dv_out, dk_ref, dv_ref):
        dk_ref[...] = jnp.zeros_like(dk_ref)
        dv_ref[...] = jnp.zeros_like(dv_ref)
        for i in range(total_rows // block):
            span = pl.ds(i * block, block)
            upto = (i + 1) * block
            shape = (upto, block)
            key_pos = lax.broadcasted_iota(jnp.int32, shape, 0)
            query_pos = i * block + lax.broadcasted_iota(jnp.int32, shape, 1)
            allowed = jnp.where((key_pos <= query_pos) & (key_pos < valid_ref[0]), 1.0, 0.0)
            query, grad = q_ref[span, :], do_ref[span, :]
            key = k_ref[:upto, :]
            prob = probability(dot_t(key, query)) * allowed
            prob_grad = dot_t(v_ref[:upto, :], grad)
            dv_ref[:upto, :] += jnp.dot(
                prob.astype(jnp.bfloat16), grad, preferred_element_type=jnp.float32
            )
            score_grad = (prob_grad * prob * (1.0 - prob) * (1.0 / math.sqrt(HDIM))).astype(
                jnp.bfloat16
            )
            dk_ref[:upto, :] += jnp.dot(score_grad, query, preferred_element_type=jnp.float32)
            dq = t_dot(score_grad, key)
            dq_out[span, :] = rotated(
                dq, cos_ref[span, :], sin_ref[span, :], True
            ).astype(jnp.bfloat16)
        dk_out[...] = rotated(dk_ref[...], cos_ref[...], sin_ref[...], True).astype(jnp.bfloat16)
        dv_out[...] = dv_ref[...].astype(jnp.bfloat16)

    head = pl.BlockSpec((total_rows, HDIM), lambda h: (0, h))
    table = pl.BlockSpec((total_rows, HDIM), lambda h: (0, 0))
    return pl.pallas_call(
        kernel,
        grid=(inner_width // HDIM,),
        out_shape=[jax.ShapeDtypeStruct((total_rows, inner_width), jnp.bfloat16)] * 3,
        in_specs=[head] * 4 + [table] * 2 + [pl.BlockSpec(memory_space=pltpu.SMEM)],
        out_specs=[head] * 3,
        scratch_shapes=[pltpu.VMEM((total_rows, HDIM), jnp.float32)] * 2,
        compiler_params=pltpu.CompilerParams(vmem_limit_bytes=VMEM_LIMIT),
        cost_estimate=pl.CostEstimate(
            flops=8 * total_rows * total_rows * inner_width,
            bytes_accessed=14 * total_rows * inner_width,
            transcendentals=0,
        ),
        name="attention_backward",
    )(queries, keys, values, mixed_grad, cosine, sine, valid_counts)


def updated(weight, moment, average, gradient, rate):
    moment_new = momentum_decay * moment + (1.0 - momentum_decay) * gradient
    weight_new = weight - rate * (
        (1.0 - momentum_decay) * gradient + momentum_decay * moment_new
    )
    average_new = average_decay * average + (1.0 - average_decay) * weight_new
    return weight_new, moment_new, average_new


def store_update(ins, gradient, outs, rate):
    weight, moment, average = updated(*[ref[...] for ref in ins], gradient, rate)
    outs[0][...] = weight
    outs[1][...] = moment
    outs[2][...] = average
    outs[3][...] = weight.astype(jnp.bfloat16)


def update_all(pairs, parts, flips, sum_ffn, sum_attn, passed, rate):
    jobs = []

    high, two, wide = pairs[0].shape
    tiles = wide // 128
    step = min(64, high)
    stride = tiles * two

    def spread_gradient(g, spread):
        for part in range(two):
            for tile in range(tiles):
                cols = pl.ds(part * wide + tile * 128, 128)
                spread[pl.ds(tile * two + part, step, stride=stride), :] = g[:, cols].astype(
                    jnp.float32
                )
        return spread[...]

    jobs.append(
        (
            [flat_pairs(x) for x in pairs],
            ((step * stride, 128), lambda i: (i, 0)),
            (sum_ffn, (step, two * wide), lambda i: (i, 0)),
            high // step,
            spread_gradient,
        )
    )
    for arrays, total, start in ((flips[0][0], sum_ffn, flips[0][1]), (flips[1][0], sum_attn, flips[1][1])):
        tall, narrow = arrays[0].shape
        rows = min(512, tall)
        jobs.append(
            (
                arrays,
                ((rows, narrow), lambda i: (i, 0)),
                (total, (narrow, rows), lambda i, first=start // rows: (0, first + i)),
                tall // rows,
                lambda g, spread: g[...].astype(jnp.float32).T,
            )
        )
    deep, count, across = parts[0].shape
    jobs.append(
        (
            [x.transpose(1, 0, 2) for x in parts],
            ((None, deep, across), lambda i: (i, 0, 0)),
            (sum_attn, (deep, across), lambda i: (0, i)),
            count,
            lambda g, spread: g[...].astype(jnp.float32),
        )
    )
    starts = [sum(job[3] for job in jobs[:k]) for k in range(len(jobs))]
    steps = sum(job[3] for job in jobs)

    def within(k, index_map):
        return lambda i: index_map(jnp.clip(i - starts[k], 0, jobs[k][3] - 1))

    in_specs, out_specs, args, out_shape = [], [], [], []
    kinds = [jnp.float32] * 3 + [jnp.bfloat16]
    for k, (arrays, (shape, index_map), (total, total_shape, total_map), _, _) in enumerate(jobs):
        spec = pl.BlockSpec(shape, within(k, index_map))
        in_specs += [spec] * 3 + [pl.BlockSpec(total_shape, within(k, total_map))]
        args += [*arrays, total]
        out_specs += [spec] * 4
        out_shape += [jax.ShapeDtypeStruct(arrays[0].shape, kind) for kind in kinds]
    in_specs += [ANY] * len(passed)
    out_specs += [ANY] * len(passed)
    out_shape += [jax.ShapeDtypeStruct(x.shape, x.dtype) for x in passed]

    def body(*refs):
        ins, refs = refs[: len(in_specs)], refs[len(in_specs) :]
        outs, (spread, sems, *kept) = refs[: len(out_specs)], refs[len(out_specs) :]
        i = pl.program_id(0)
        entering = [
            pltpu.make_async_copy(ins[4 * len(jobs) + k], ref, sems.at[0, k])
            for k, ref in enumerate(kept)
        ]
        leaving = [
            pltpu.make_async_copy(ref, outs[4 * len(jobs) + k], sems.at[1, k])
            for k, ref in enumerate(kept)
        ]

        @pl.when(i == 0)
        def _():
            for copy in entering:
                copy.start()

        @pl.when(i == 1)
        def _():
            for arrived, copy in zip(entering, leaving):
                arrived.wait()
                copy.start()

        for k, job in enumerate(jobs):

            @pl.when((i >= starts[k]) & (i < starts[k] + job[3]))
            def _():
                gradient = job[4](ins[4 * k + 3], spread)
                store_update(ins[4 * k : 4 * k + 3], gradient, outs[4 * k : 4 * k + 4], rate)

        @pl.when(i == steps - 1)
        def _():
            for copy in leaving:
                copy.wait()

    size = sum(job[0][0].size for job in jobs)
    outs = pl.pallas_call(
        body,
        grid=(steps,),
        out_shape=out_shape,
        in_specs=in_specs,
        out_specs=out_specs,
        scratch_shapes=[
            pltpu.VMEM((step * stride, 128), jnp.float32),
            pltpu.SemaphoreType.DMA((2, len(passed))),
        ]
        + [pltpu.VMEM(x.shape, x.dtype) for x in passed],
        compiler_params=pltpu.CompilerParams(vmem_limit_bytes=VMEM_LIMIT),
        cost_estimate=pl.CostEstimate(
            flops=10 * size, bytes_accessed=28 * size, transcendentals=0
        ),
        name="update_all",
    )(*args, *passed)
    gu = [
        x.reshape(high, tiles, two, 128).transpose(0, 2, 1, 3).reshape(high, two, wide)
        for x in outs[:4]
    ]
    qkv = [x.transpose(1, 0, 2) for x in outs[12:16]]
    return gu, outs[4:8], outs[8:12], qkv, outs[16:]


def rope_tables(length, half_dim):
    positions = np.arange(length, dtype=np.float32)[:, None]
    inverse_freq = np.power(
        np.float32(rope_base), -np.arange(half_dim, dtype=np.float32) / np.float32(half_dim)
    )
    angles = positions * inverse_freq[None, :]
    cosine, sine = np.cos(angles), np.sin(angles)
    return np.concatenate([cosine, cosine], axis=1), np.concatenate([-sine, sine], axis=1)


def per_device(
    n_dp,
    n_mp,
    tokens,
    cotangent,
    valid_counts,
    w_qkv,
    w_out,
    w_gu,
    w_down,
    gains,
    mom_qkv,
    mom_out,
    mom_gu,
    mom_down,
    mom_gains,
    avg_qkv,
    avg_out,
    avg_gu,
    avg_down,
    avg_gains,
):
    half = jnp.bfloat16
    row_count, width = tokens.shape
    owned, _, local_width = w_qkv.shape
    hidden = w_gu.shape[2]
    valid_len = valid_counts[0]

    attn_part = jnp.concatenate(
        [w_qkv.reshape(owned, 3 * local_width), w_out.T], axis=1
    ).astype(half)
    attn_w = lax.all_gather(attn_part, "dp", axis=0, tiled=True)
    row_ids = lax.axis_index("mp") * row_count + jnp.arange(row_count, dtype=jnp.int32)
    live_rows = (row_ids < valid_len).astype(jnp.float32)[:, None]
    key_mask = (jnp.arange(SEQ, dtype=jnp.int32) < valid_len).astype(jnp.float32)
    ffn_part, tokens_in = lax.optimization_barrier((round_shares(w_gu, w_down), tokens))
    h_first, gain_all, out_grad, own_branch = gather_first(
        n_dp, n_mp, tokens_in, gains, cotangent, live_rows, 1
    )
    ffn_w = lax.all_gather(ffn_part, "dp", axis=0, tiled=True)
    cosine, sine = (jnp.asarray(x, jnp.float32) for x in rope_tables(SEQ, HDIM // 2))

    second, normed_second, queries, keys, values, mixed, branch_grad = scatter_rows(
        n_mp,
        [h_first],
        attn_w,
        3 * local_width,
        [tokens],
        "forward",
        gain_all,
        1,
        2,
        heads=(cosine, sine, key_mask[None, :]),
        extra=own_branch,
    )

    second_grad, own_grad, gain_two, grad_ffn, act, _, _ = feed_forward(
        n_mp, normed_second, branch_grad, ffn_w, second, gain_all, 3
    )
    sum_ffn = lax.psum_scatter(grad_ffn, "dp", scatter_dimension=0, tiled=True)
    block_out, attn_grad, mixed_grad = scatter_rows(
        n_mp,
        [act],
        ffn_w,
        2 * hidden,
        [second],
        "residual",
        gain_all,
        1,
        7,
        extra=own_grad,
        extra_right=(attn_w, 3 * local_width),
    )

    joined_grad = attention_backward(
        queries, keys, values, mixed_grad, cosine, sine, valid_counts
    )
    input_grad, gain_tile, sum_attn = scatter_rows(
        n_mp,
        list(joined_grad),
        attn_w,
        0,
        [tokens, second_grad],
        "last",
        gain_all,
        0,
        4,
        other_gain=gain_two,
        grad_lefts=[h_first, attn_grad],
        grad_right=mixed,
        n_dp=n_dp,
    )

    total_rows = SEQ * n_dp
    matrix_rate = step_rate / math.sqrt(total_rows)
    scale_rate = gain_rate / math.sqrt(total_rows)
    local = gains.shape[1]
    place = lax.rem((lax.axis_index("dp") * n_mp + lax.axis_index("mp")) * local, 128)
    sum_gains = lax.dynamic_slice(gain_tile, (0, place), (2, local))
    gu, down, out, qkv, (block_out, input_grad) = update_all(
        [w_gu, mom_gu, avg_gu],
        [w_qkv, mom_qkv, avg_qkv],
        (
            ([w_down, mom_down, avg_down], 2 * hidden),
            ([w_out, mom_out, avg_out], 3 * local_width),
        ),
        sum_ffn,
        sum_attn,
        [block_out, input_grad],
        matrix_rate,
    )
    new_gu, next_mom_gu, next_avg_gu, copy_gu = gu
    new_down, next_mom_down, next_avg_down, copy_down = down
    new_out, next_mom_out, next_avg_out, copy_out = out
    new_qkv, next_mom_qkv, next_avg_qkv, copy_qkv = qkv
    new_gains, next_mom_gains, next_avg_gains = updated(
        gains, mom_gains, avg_gains, sum_gains, scale_rate
    )
    return (
        block_out,
        input_grad,
        new_qkv,
        new_out,
        new_gu,
        new_down,
        new_gains,
        next_mom_qkv,
        next_mom_out,
        next_mom_gu,
        next_mom_down,
        next_mom_gains,
        next_avg_qkv,
        next_avg_out,
        next_avg_gu,
        next_avg_down,
        next_avg_gains,
        copy_qkv,
        copy_out,
        copy_gu,
        copy_down,
    )


def solution(mesh):
    rows, one = P(("dp", "mp"), None), P("dp")
    tall, wide, spread = P("dp", None, "mp"), P("mp", "dp"), P(None, ("dp", "mp"))
    weights = (tall, wide, tall, wide)
    return jax.shard_map(
        functools.partial(per_device, mesh.shape["dp"], mesh.shape["mp"]),
        mesh=mesh,
        in_specs=(rows, rows, one, *((*weights, spread) * 3)),
        out_specs=(rows, rows, *((*weights, spread) * 3), *weights),
        check_vma=False,
    )
```
